128 devices in a mesh: dp: 64 (over x, y_hi, z, core), tensor: 2 (over y_lo).
Axes of the slice: x: 4, y: 4 (y_hi: 2, y_lo: 2; y = y_hi * 2 + y_lo), z: 4, core: 2. Of those that a mesh axis runs over, the one named last changes fastest.
Arguments:
- hidden_in: bfloat16 [16384, 2048], P(('dp', 'tensor')), may hold values from -6 to 6
- doc_ids: int32 [64, 256], P('dp'), may hold values from 0 to 2, never falling along the last dimension, each value on 1 to 192 neighbouring positions
- expert_ids: int32 [16384, 8], P(('dp', 'tensor')), may hold values from 0 to 127, all different within a row; in each aligned block of 128 rows (0 to 127, 128 to 255, ...) at most 8 rows name the same one
- attn_gain: float32 [2048], replicated, may hold values from 0.1 to 1.9
- query_weight: bfloat16 [2048, 4096], P('dp', 'tensor'), may hold values from -0.125 to 0.125
- key_weight: bfloat16 [2048, 512], P('dp', 'tensor'), may hold values from -0.125 to 0.125
- value_weight: bfloat16 [2048, 512], P('dp', 'tensor'), may hold values from -0.125 to 0.125
- output_weight: bfloat16 [4096, 2048], P('tensor', 'dp'), may hold values from -0.75 to 0.75
- query_gain: float32 [128], replicated, may hold values from 0.1 to 1.9
- key_gain: float32 [128], replicated, may hold values from 0.1 to 1.9
- moe_gain: float32 [2048], replicated, may hold values from 0.1 to 1.9
- router_weight: bfloat16 [2048, 128], replicated, may hold values from -0.0625 to 0.0625
- gate_weight: bfloat16 [128, 2048, 768], P(('dp', 'tensor')), may hold values from -0.125 to 0.125
- up_weight: bfloat16 [128, 2048, 768], P(('dp', 'tensor')), may hold values from -0.125 to 0.125
- down_weight: bfloat16 [128, 768, 2048], P(('dp', 'tensor')), may hold values from -0.625 to 0.625
- cotangent: bfloat16 [16384, 2048], P(('dp', 'tensor')), may hold values from -6 to 6
Outputs:
- layer_out: bfloat16 [16384, 2048], P(('dp', 'tensor'))
- input_grad: float32 [16384, 2048], P(('dp', 'tensor'))
- attngain_grad: float32 [2048], replicated
- qweight_grad: float32 [2048, 4096], P('dp', 'tensor')
- kweight_grad: float32 [2048, 512], P('dp', 'tensor')
- vweight_grad: float32 [2048, 512], P('dp', 'tensor')
- oweight_grad: float32 [4096, 2048], P('tensor', 'dp')
- qgain_grad: float32 [128], replicated
- kgain_grad: float32 [128], replicated
- moegain_grad: float32 [2048], replicated
- router_grad: float32 [2048, 128], replicated
- gate_grad: float32 [128, 2048, 768], P(('dp', 'tensor'))
- up_grad: float32 [128, 2048, 768], P(('dp', 'tensor'))
- down_grad: float32 [128, 768, 2048], P(('dp', 'tensor'))
The draws below stay inside these ranges and needn't reach their ends.
Inputs may be any that keep to these rules, and one draw needn't show every extreme that they name: `doc_ids`: each row is one group of 256 tokens: 3 sequences, ids never falling, each 1 to 192 tokens long, one exactly 192. `expert_ids`: each row names 8 different experts; in the 128 rows of one device every expert is named exactly 8 times.
All inputs are finite; a program needn't handle non-finite values.
Results may differ from the reference program's by a relative error of at most 0.023.
Values may be sent and summed in bfloat16 or wider, within the bound.
A program may use at most 192 MiB of HBM per device.

```python
import math
import jax
import jax.numpy as jnp
import numpy as np
from jax import lax

D = 2048
H = 32
KVH = 4
HD = 128
FF = 768
TOPK = 8
TOK_DEV = 128
BLOCK = 128
NSEG = 3
EXPERTS = 128
GROUP_TOK = 256
SEQ_MAX = 192
CAP = 8
TOKENS = 16384
N_DP = 64
DEVICES = 128


def levels(stream_key, shape, cuts, low, top_value):
    loudness = 1.0
    for dim, shards_of in cuts:
        steps = jax.random.uniform(jax.random.fold_in(jax.random.fold_in(stream_key, 6), dim), (shards_of,), jnp.float32, low / len(cuts), top_value / len(cuts))
        loudness = loudness * jnp.repeat(jnp.exp(steps), shape[dim] // shards_of).reshape((-1,) + (1,) * (len(shape) - 1 - dim))
    return loudness


def split_up(number_of, total, reach, skew):
    weights = [(1 << 20) // math.isqrt(rank ** skew) + 1 for rank in range(2, number_of + 1)]
    rest, counts = total - reach - (number_of - 1), [1] * (number_of - 1)
    while rest > 0:
        candidates = [i for i in range(number_of - 1) if counts[i] < reach]
        mass, remaining = sum([weights[i] for i in candidates]), rest
        for i in candidates:
            extra = min(reach - counts[i], max(1, remaining * weights[i] // mass), rest)
            counts[i] = counts[i] + extra
            rest = rest - extra
    return np.array([reach] + counts)


def uneven_parts(key, count, total, bound, slope):
    if count == 2:
        one = jax.random.randint(key, (), max(1, total - bound), min(bound, total - 1) + 1)
        return jnp.stack([one, total - one])
    lengths = jnp.asarray(split_up(count, total, bound, slope), jnp.int32)
    couples = (count - 1) // 2
    donor, taker = lengths[1:1 + 2 * couples:2], lengths[2:2 + 2 * couples:2]
    room = jnp.minimum(donor - 1, bound - taker)
    passed = jax.random.randint(jax.random.fold_in(key, 1), (couples,), 0, 1 << 20) % (room + 1)
    lengths = lengths.at[1:1 + 2 * couples:2].set(donor - passed).at[2:2 + 2 * couples:2].set(taker + passed)
    return lengths[jax.random.permutation(jax.random.fold_in(key, 2), count)]


def deal_out(rng, own, number, rows, number_of, top, reach, skew):
    order = jax.random.permutation(rng, number_of)
    crowded, common = shares(number_of, rows * top, reach, skew, True), shares(number_of, rows * top, reach, skew, False)
    places = jnp.arange(number_of)

    def named(tallies, offset_by):
        used = int((tallies > 0).sum())
        fixed = max(1, used // 4)
        shifted = fixed + (places - fixed + offset_by * (used - fixed)) % max(1, number_of - fixed)
        return jnp.zeros((number_of,), jnp.int32).at[order[jnp.where(places < fixed, places, shifted)]].set(jnp.asarray(tallies, jnp.int32))

    tallies = jnp.where(number % 4 == 0, named(crowded, number // 4), named(common, number - number // 4 - 1))
    mixed = jax.random.permutation(jax.random.fold_in(own, 3), number_of)
    source_of, receiver = mixed[0:number_of // 2 * 2:2], mixed[1:number_of // 2 * 2:2]
    slack = jnp.minimum(tallies[source_of] - 1, reach - tallies[receiver]) // 2
    slack = jnp.where((source_of == order[0]) | (receiver == order[0]) | (tallies[receiver] == 0), 0, jnp.maximum(slack, 0))
    shifted = jax.random.randint(jax.random.fold_in(own, 4), (number_of // 2,), 0, 1 << 20) % (slack + 1)
    tallies = tallies.at[source_of].add(-shifted).at[receiver].add(shifted)
    items = jnp.searchsorted(jnp.cumsum(tallies), jnp.arange(rows * top), side="right").astype(jnp.int32)
    listing = items.reshape(top, rows).T
    listing = listing[jax.random.permutation(jax.random.fold_in(own, 1), rows)]
    offset_by = jax.random.randint(jax.random.fold_in(own, 2), (rows, 1), 0, top)
    return jnp.take_along_axis(listing, (jnp.arange(top)[None, :] + offset_by) % top, axis=1)


def shares(amount, total, reach, slope, full):
    loads = [(1 << 20) // math.isqrt(grade ** slope) + 1 for grade in range(1, amount + 1)]
    largest = reach if full else min(reach, max(-(-total // amount), total * loads[0] // sum(loads)))
    least = 1 if total - largest >= amount - 1 else 0
    holding, rest = [largest] + [least] * (amount - 1), total - largest - least * (amount - 1)
    while rest > 0:
        free = [i for i in range(1, amount) if holding[i] < largest] or [i for i in range(1, amount) if holding[i] < reach]
        pool, remaining = sum([loads[i] for i in free]), rest
        for i in free:
            addition = min(reach - holding[i], max(1, remaining * loads[i] // pool), rest)
            holding[i] = holding[i] + addition
            rest = rest - addition
    return np.array(holding)


def normal_values(own_key, extent, spread, bound, split=(), held_as=jnp.bfloat16):
    level = levels(own_key, extent, split, -0.22, 0.18) if split else 1.0
    entries = jax.random.normal(own_key, extent, jnp.float32) * spread * level
    return jnp.minimum(jnp.maximum(entries, -bound), bound).astype(held_as)


def setup_inputs(seed: int = 0) -> dict:
    arg_keys = jax.random.split(jax.random.key(seed), 17)
    hidden_in = normal_values(arg_keys[0], (TOKENS, D), 1.0, 6.0, ((0, 128),))
    doc_ids = jax.vmap(lambda own: jnp.searchsorted(jnp.cumsum(uneven_parts(own, NSEG, GROUP_TOK, SEQ_MAX, 0)), jnp.arange(GROUP_TOK), side="right"))(jax.random.split(arg_keys[1], N_DP)).reshape((N_DP, GROUP_TOK)).astype(jnp.int32)
    expert_ids_keys = jax.random.split(jax.random.fold_in(arg_keys[2], 1), TOKENS // TOK_DEV)
    expert_ids_turns = jax.random.permutation(jax.random.fold_in(arg_keys[2], 3), TOKENS // TOK_DEV)
    expert_ids = jax.vmap(lambda own, number: deal_out(jax.random.fold_in(arg_keys[2], 2), own, number, TOK_DEV, EXPERTS, TOPK, CAP, 0))(expert_ids_keys, expert_ids_turns).reshape((TOKENS, TOPK))
    attn_gain = jnp.clip(1.0 + 0.18 * jax.random.normal(arg_keys[3], (D,), jnp.float32), 0.1, 1.9)
    query_weight = normal_values(arg_keys[4], (D, H * HD), D ** -0.5, 0.125, ((0, 64), (1, 2)))
    key_weight = normal_values(arg_keys[5], (D, KVH * HD), D ** -0.5, 0.125, ((0, 64), (1, 2)))
    value_weight = normal_values(arg_keys[6], (D, KVH * HD), D ** -0.5, 0.125, ((0, 64), (1, 2)))
    output_weight = normal_values(arg_keys[7], (H * HD, D), (H * HD // 64) ** -0.5, 0.75, ((0, 2), (1, 64)))
    query_gain = jnp.clip(1.0 + 0.18 * jax.random.normal(arg_keys[8], (HD,), jnp.float32), 0.1, 1.9)
    key_gain = jnp.clip(1.0 + 0.18 * jax.random.normal(arg_keys[9], (HD,), jnp.float32), 0.1, 1.9)
    moe_gain = jnp.clip(1.0 + 0.18 * jax.random.normal(arg_keys[10], (D,), jnp.float32), 0.1, 1.9)
    router_weight = normal_values(arg_keys[11], (D, EXPERTS), (4 * D) ** -0.5, 0.0625)
    gate_weight = normal_values(arg_keys[12], (EXPERTS, D, FF), D ** -0.5, 0.125, ((0, 128),))
    up_weight = normal_values(arg_keys[13], (EXPERTS, D, FF), D ** -0.5, 0.125, ((0, 128),))
    down_weight = normal_values(arg_keys[14], (EXPERTS, FF, D), (FF // 8) ** -0.5, 0.625, ((0, 128),))
    cotangent = normal_values(arg_keys[15], (TOKENS, D), 1.0, 6.0, ((0, 128),))
    return dict(hidden_in=hidden_in, doc_ids=doc_ids, expert_ids=expert_ids, attn_gain=attn_gain, query_weight=query_weight, key_weight=key_weight, value_weight=value_weight, output_weight=output_weight, query_gain=query_gain, key_gain=key_gain, moe_gain=moe_gain, router_weight=router_weight, gate_weight=gate_weight, up_weight=up_weight, down_weight=down_weight, cotangent=cotangent)


@jax.custom_vjp
def low(v):
    return lax.optimization_barrier(v.astype(jnp.bfloat16)).astype(jnp.float32)

@jax.custom_vjp
def low_back(v):
    return v

def low_keep(v):
    return (low(v), None)

def low_pass(kept, grad):
    return (grad,)

def back_keep(v):
    return (v, None)

def back_low(kept, grad):
    return (low(grad),)
low.defvjp(low_keep, low_pass)
low_back.defvjp(back_keep, back_low)
EPSILON = 1e-06
ROPE_BASE = 1000000.0
MASKED = -1e+30
PRECISE = lax.Precision.HIGHEST

def matmul(first_op, second_op):
    return jnp.dot(first_op, second_op, precision=PRECISE, preferred_element_type=jnp.float32)

def rms_scale(values, norm_gain):
    return values * lax.rsqrt(lax.optimization_barrier(jnp.mean(values * values, axis=-1, keepdims=True)) + EPSILON) * norm_gain

def rotate(values, cosine, sine_table):
    half_size = values.shape[-1] // 2
    leading = values[..., :half_size]
    trailing = values[..., half_size:]
    return jnp.concatenate([leading * cosine - trailing * sine_table, trailing * cosine + leading * sine_table], axis=-1)

def layout(doc_row):
    length = doc_row.shape[0]
    indices = jnp.arange(length, dtype=jnp.int32)
    same_doc = doc_row[:, None] == doc_row[None, :]
    earlier = indices[None, :] < indices[:, None]
    position = lax.optimization_barrier(jnp.sum(jnp.where(same_doc & earlier, 1, 0), axis=1)).astype(jnp.int32)
    blocks = position // BLOCK
    allowed = same_doc & (blocks[None, :] <= blocks[:, None])
    return (position, allowed)

def rotary(position, head_size):
    half_size = head_size // 2
    frequency = jnp.exp(-jnp.log(ROPE_BASE) * jnp.arange(half_size, dtype=jnp.float32) * 2.0 / head_size)
    angles = position.astype(jnp.float32)[:, None] * frequency[None, :]
    return (jnp.cos(angles)[:, None, :], jnp.sin(angles)[:, None, :])

def attend(normed, doc_row, query_weight, key_weight, value_weight, output_weight, query_gain, key_gain):
    length = normed.shape[0]
    position, allowed = layout(doc_row)
    cosine, sine_table = rotary(position, HD)
    queries = low_back(matmul(normed, query_weight)).reshape(length, H, HD)
    key_rows = low_back(matmul(normed, key_weight)).reshape(length, KVH, HD)
    values = low(low_back(matmul(normed, value_weight))).reshape(length, KVH, HD)
    queries = low(rotate(rms_scale(queries, query_gain), cosine, sine_table)).reshape(length, KVH, H // KVH, HD)
    key_rows = low(rotate(rms_scale(key_rows, key_gain), cosine, sine_table))
    scores = low_back(jnp.einsum('qkgd,tkd->kgqt', queries, key_rows, precision=PRECISE) * (1.0 / math.sqrt(HD)))
    scores = jnp.where(allowed[None, None], scores, MASKED)
    attention = low(jax.nn.softmax(scores, axis=-1))
    mixed_heads = jnp.einsum('kgqt,tkd->qkgd', attention, values, precision=PRECISE)
    mixed_heads = low(low_back(mixed_heads)).reshape(length, H * HD)
    return low_back(matmul(mixed_heads, output_weight))

def experts(moe_rows, routes, gate_probs, gate_weight, up_weight, down_weight):
    flat_ids = routes.reshape(-1)
    onehot = (flat_ids[:, None] == jnp.arange(EXPERTS, dtype=jnp.int32)[None, :]).astype(jnp.int32)
    ranking = lax.optimization_barrier(jnp.sum((jnp.cumsum(onehot, axis=0) - 1) * onehot, axis=1)).astype(jnp.int32)
    slot_index = flat_ids * CAP + ranking
    owner_row = jnp.zeros((TOK_DEV * TOPK,), jnp.int32).at[slot_index].set(jnp.arange(TOK_DEV * TOPK, dtype=jnp.int32))
    expert_rows = low_back(moe_rows[owner_row // TOPK]).reshape(EXPERTS, CAP, D)
    gate_pre = low_back(jnp.einsum('ecd,edf->ecf', expert_rows, gate_weight, precision=PRECISE))
    up_pre = low_back(jnp.einsum('ecd,edf->ecf', expert_rows, up_weight, precision=PRECISE))
    inner_act = low(jax.nn.silu(gate_pre) * up_pre)
    outputs = low_back(low(jnp.einsum('ecf,efd->ecd', inner_act, down_weight, precision=PRECISE)))
    picked = outputs.reshape(TOK_DEV * TOPK, D)[slot_index].reshape(TOK_DEV, TOPK, D)
    return lax.optimization_barrier(jnp.sum(gate_probs[:, :, None] * picked, axis=1))

def forward(hidden, attn_gain, query_weight, key_weight, value_weight, output_weight, query_gain, key_gain, moe_gain, router_weight, gate_weight, up_weight, down_weight, doc_ids, expert_ids):
    normed = low(rms_scale(hidden, attn_gain))

    def group_step(pieces):
        return attend(pieces[0], pieces[1], query_weight, key_weight, value_weight, output_weight, query_gain, key_gain)
    attn_out = lax.map(jax.checkpoint(group_step), (normed.reshape(N_DP, GROUP_TOK, D), doc_ids)).reshape(TOKENS, D)
    residual = hidden + attn_out
    moe_input = low(rms_scale(residual, moe_gain))
    logits = low_back(matmul(moe_input, router_weight))
    gate_probs = jax.nn.softmax(jnp.take_along_axis(logits, expert_ids, axis=1), axis=-1)

    def source_step(pieces):
        return experts(pieces[0], pieces[1], pieces[2], gate_weight, up_weight, down_weight)
    moe_out = lax.map(jax.checkpoint(source_step), (moe_input.reshape(DEVICES, TOK_DEV, D), expert_ids.reshape(DEVICES, TOK_DEV, TOPK), gate_probs.reshape(DEVICES, TOK_DEV, TOPK))).reshape(TOKENS, D)
    return residual + moe_out

def reference(hidden_in, doc_ids, expert_ids, attn_gain, query_weight, key_weight, value_weight, output_weight, query_gain, key_gain, moe_gain, router_weight, gate_weight, up_weight, down_weight, cotangent):

    def closed(hidden, gain_one, wquery, wkey, wvalue, woutput, gain_query, gain_key, gain_moe, wrouter, wgate, wup, wdown):
        return forward(hidden, gain_one, wquery, wkey, wvalue, woutput, gain_query, gain_key, gain_moe, wrouter, wgate, wup, wdown, doc_ids, expert_ids)
    result, pullback = jax.vjp(closed, hidden_in.astype(jnp.float32), attn_gain, query_weight.astype(jnp.float32), key_weight.astype(jnp.float32), value_weight.astype(jnp.float32), output_weight.astype(jnp.float32), query_gain, key_gain, moe_gain, router_weight.astype(jnp.float32), gate_weight.astype(jnp.float32), up_weight.astype(jnp.float32), down_weight.astype(jnp.float32))
    grads = pullback(cotangent.astype(jnp.float32))
    return (result.astype(jnp.bfloat16), grads[0], grads[1], grads[2], grads[3], grads[4], grads[5], grads[6], grads[7], grads[8], grads[9], grads[10], grads[11], grads[12])
```

```python
import math

import jax
import jax.numpy as jnp
from jax import lax
from jax.sharding import PartitionSpec as P

BLOCK = 128
EPSILON = 1e-06
ROPE_BASE = 1000000.0
MASKED = -1e30
F32 = jnp.float32
BF16 = jnp.bfloat16


def dot_nt(a, b):
    return lax.dot_general(a, b, (((1,), (1,)), ((), ())), preferred_element_type=F32)


def dot_tn(a, b):
    return lax.dot_general(a, b, (((0,), (0,)), ((), ())), preferred_element_type=F32)


def dot_nn(a, b):
    return lax.dot_general(a, b, (((1,), (0,)), ((), ())), preferred_element_type=F32)


def rms_recip(values):
    return lax.rsqrt(jnp.mean(values * values, axis=-1, keepdims=True) + EPSILON)


def rms_scale(values, gain):
    return values * rms_recip(values) * gain


def rms_back(values, gain, upstream):
    r = rms_recip(values)
    scaled = upstream * gain
    inner = jnp.mean(scaled * values, axis=-1, keepdims=True)
    grad_values = r * scaled - values * (r * r * r) * inner
    return grad_values, upstream * values * r


def rotate(values, cosine, sine):
    half = values.shape[-1] // 2
    a = values[..., :half]
    b = values[..., half:]
    return jnp.concatenate([a * cosine - b * sine, b * cosine + a * sine], axis=-1)


def layout(doc_row):
    length = doc_row.shape[0]
    indices = jnp.arange(length, dtype=jnp.int32)
    same_doc = doc_row[:, None] == doc_row[None, :]
    earlier = indices[None, :] < indices[:, None]
    position = jnp.sum(jnp.where(same_doc & earlier, 1, 0), axis=1).astype(jnp.int32)
    blocks = position // BLOCK
    allowed = same_doc & (blocks[None, :] <= blocks[:, None])
    return position, allowed


def rotary(position, head_size):
    half = head_size // 2
    frequency = jnp.exp(-jnp.log(ROPE_BASE) * jnp.arange(half, dtype=F32) * 2.0 / head_size)
    angles = position.astype(F32)[:, None] * frequency[None, :]
    return jnp.cos(angles)[:, None, :], jnp.sin(angles)[:, None, :]


def on_device(
    hidden_in,
    doc_ids,
    expert_ids,
    attn_gain,
    query_weight,
    key_weight,
    value_weight,
    output_weight,
    query_gain,
    key_gain,
    moe_gain,
    router_weight,
    gate_weight,
    up_weight,
    down_weight,
    cotangent,
):
    both = ("dp", "tensor")
    tok, width = hidden_in.shape
    hd = query_gain.shape[0]
    nkv = key_weight.shape[1] // hd
    nq = query_weight.shape[1] // hd
    group = nq // nkv
    experts = router_weight.shape[1]
    routes = expert_ids.shape[1]
    cap = tok * routes // experts
    slots = experts * cap
    scale = 1.0 / math.sqrt(hd)
    tokens = doc_ids.shape[1]
    me = lax.axis_index(both)

    lane = lax.broadcasted_iota(jnp.int32, (1, 1, experts), 2)
    chosen = jnp.sum((expert_ids[:, :, None] == lane).astype(F32), axis=1)
    below = (
        lax.broadcasted_iota(jnp.int32, (tok, tok), 1)
        < lax.broadcasted_iota(jnp.int32, (tok, tok), 0)
    ).astype(BF16)
    rank = dot_nn(below, chosen.astype(BF16))
    place = jnp.where(chosen > 0, rank, -1.0).T
    spread = (
        place[:, None, :] == lax.broadcasted_iota(jnp.int32, (1, cap, 1), 1).astype(F32)
    ).astype(BF16).reshape(slots, tok)

    cot_out = dot_nn(spread, jnp.concatenate([cotangent, chosen.astype(BF16)], axis=1)).astype(BF16)
    cot_in = lax.all_to_all(
        cot_out.reshape(experts, cap, width + experts), both, split_axis=0, concat_axis=0, tiled=True
    ).reshape(slots, width + experts)

    hidden = hidden_in.astype(F32)
    normed_local = rms_scale(hidden, attn_gain).astype(BF16)
    normed = lax.all_gather(normed_local, "tensor", axis=0, tiled=True)
    shard = jnp.concatenate([query_weight, key_weight, value_weight, output_weight.T], axis=1)
    weights = lax.all_gather(shard, "dp", axis=0, tiled=True)
    nqkv = (nq + 2 * nkv) * hd
    in_weights = weights[:, :nqkv]
    out_weights = weights[:, nqkv:]

    position, allowed = layout(doc_ids[0])
    cosine, sine = rotary(position, hd)
    raw = dot_nn(normed, in_weights)
    query_raw = raw[:, : nq * hd].reshape(tokens, nq, hd)
    key_raw = raw[:, nq * hd : (nq + nkv) * hd].reshape(tokens, nkv, hd)
    values = raw[:, (nq + nkv) * hd :].astype(BF16).reshape(tokens, nkv, hd)
    query = rotate(rms_scale(query_raw, query_gain), cosine, sine).astype(BF16)
    query = query.reshape(tokens, nkv, group, hd)
    key = rotate(rms_scale(key_raw, key_gain), cosine, sine).astype(BF16)
    scores = jnp.einsum("qkgd,tkd->kgqt", query, key, preferred_element_type=F32) * scale
    scores = jnp.where(allowed[None, None], scores, MASKED)
    weight = jnp.exp(scores - jnp.max(scores, axis=-1, keepdims=True))
    attention = weight / jnp.sum(weight, axis=-1, keepdims=True)
    attention_low = attention.astype(BF16)
    mixed = jnp.einsum("kgqt,tkd->qkgd", attention_low, values, preferred_element_type=F32)
    mixed = mixed.astype(BF16).reshape(tokens, nq * hd)
    attn_out = lax.psum_scatter(
        dot_nt(mixed, out_weights).astype(BF16), "tensor", scatter_dimension=0, tiled=True
    ).astype(F32)

    residual = hidden + attn_out
    moe_input = rms_scale(residual, moe_gain).astype(BF16)
    sent = dot_nn(spread, moe_input).astype(BF16)
    rows = lax.all_to_all(
        sent.reshape(experts, cap, width), both, split_axis=0, concat_axis=0, tiled=True
    ).reshape(slots, width)
    logits = dot_nn(moe_input, router_weight)
    masked = jnp.where(chosen > 0, logits, MASKED)
    probs = jnp.exp(masked - jnp.max(masked, axis=-1, keepdims=True))
    probs = probs / jnp.sum(probs, axis=-1, keepdims=True)

    gate_mat, up_mat, down_mat = gate_weight[0], up_weight[0], down_weight[0]
    cot_rows = cot_in[:, :width]
    inner_up = dot_nt(cot_rows, down_mat)
    row_logits = jnp.where(cot_in[:, width:] > 0, dot_nn(rows, router_weight), MASKED)
    row_probs = jnp.exp(row_logits - jnp.max(row_logits, axis=-1, keepdims=True))
    mine = lax.broadcasted_iota(jnp.int32, (1, experts), 1) == me
    prob = jnp.sum(jnp.where(mine, row_probs, 0.0), axis=-1, keepdims=True) / jnp.sum(
        row_probs, axis=-1, keepdims=True
    )
    gate_pre = dot_nn(rows, gate_mat)
    up_pre = dot_nn(rows, up_mat)
    sigmoid = jax.nn.sigmoid(gate_pre)
    silu = gate_pre * sigmoid
    inner = silu * up_pre
    gate_up = jnp.sum(inner * inner_up, axis=-1, keepdims=True)
    inner_low = (prob * inner).astype(BF16)
    grad_inner = prob * inner_up
    grad_gate = (grad_inner * up_pre * sigmoid * (1.0 + gate_pre * (1.0 - sigmoid))).astype(BF16)
    grad_up = (grad_inner * silu).astype(BF16)
    grad_rows = (dot_nt(grad_gate, gate_mat) + dot_nt(grad_up, up_mat)).astype(BF16)
    gate_up_high = gate_up.astype(BF16)
    gate_up_rest = (gate_up - gate_up_high.astype(F32)).astype(BF16)
    none = jnp.zeros((), BF16)
    home_out = jnp.concatenate(
        [grad_rows, jnp.where(mine, gate_up_high, none), jnp.where(mine, gate_up_rest, none)], axis=1
    )
    home = lax.all_to_all(
        home_out.reshape(experts, cap, width + 2 * experts), both, split_axis=0, concat_axis=0, tiled=True
    ).reshape(slots, width + 2 * experts)
    expert_out = dot_nn(inner_low, down_mat).astype(BF16)
    returned = lax.all_to_all(
        expert_out.reshape(experts, cap, width), both, split_axis=0, concat_axis=0, tiled=True
    ).reshape(slots, width)
    down_grad = dot_tn(inner_low, cot_rows)
    gate_grad = dot_tn(rows, grad_gate)
    up_grad = dot_tn(rows, grad_up)

    upstream = cotangent.astype(F32)
    summed = dot_tn(spread, home)
    gate_upstream = summed[:, width : width + experts] + summed[:, width + experts :]
    grad_chosen = probs * (gate_upstream - jnp.sum(probs * gate_upstream, axis=-1, keepdims=True))
    grad_logits = grad_chosen.astype(BF16)
    grad_moe_input = summed[:, :width] + dot_nt(grad_logits, router_weight)
    router_part = dot_tn(moe_input, grad_logits)
    grad_norm, moegain_rows = rms_back(residual, moe_gain, grad_moe_input)
    moegain_part = jnp.sum(moegain_rows, axis=0)
    grad_residual = upstream + grad_norm
    grad_attn = lax.all_gather(grad_residual.astype(BF16), "tensor", axis=0, tiled=True)
    layer_out = (residual + dot_tn(spread, returned)).astype(BF16)

    grad_mixed = dot_nn(grad_attn, out_weights).astype(BF16).reshape(tokens, nkv, group, hd)
    grad_values = jnp.einsum("kgqt,qkgd->tkd", attention_low, grad_mixed, preferred_element_type=F32)
    grad_soft = jnp.einsum("qkgd,tkd->kgqt", grad_mixed, values, preferred_element_type=F32)
    row_delta = jnp.sum(attention * grad_soft, axis=-1, keepdims=True)
    grad_scores = (attention * (grad_soft - row_delta)).astype(BF16)
    grad_query = jnp.einsum("kgqt,tkd->qkgd", grad_scores, key, preferred_element_type=F32) * scale
    grad_key = jnp.einsum("kgqt,qkgd->tkd", grad_scores, query, preferred_element_type=F32) * scale
    grad_query_raw, qgain_rows = rms_back(
        query_raw, query_gain, rotate(grad_query.reshape(tokens, nq, hd), cosine, -sine)
    )
    grad_key_raw, kgain_rows = rms_back(key_raw, key_gain, rotate(grad_key, cosine, -sine))
    grad_raw = jnp.concatenate(
        [
            grad_query_raw.astype(BF16).reshape(tokens, nq * hd),
            grad_key_raw.astype(BF16).reshape(tokens, nkv * hd),
            grad_values.astype(BF16).reshape(tokens, nkv * hd),
        ],
        axis=1,
    )
    grad_normed = lax.psum_scatter(
        dot_nt(grad_raw, in_weights).astype(BF16), "tensor", scatter_dimension=0, tiled=True
    ).astype(F32)
    weight_part = jnp.concatenate([dot_tn(normed, grad_raw), dot_tn(grad_attn, mixed)], axis=1)
    weight_grad = lax.psum_scatter(weight_part, "dp", scatter_dimension=0, tiled=True)
    grad_hidden, attngain_rows = rms_back(hidden, attn_gain, grad_normed)
    input_grad = grad_residual + grad_hidden
    router_grad, attngain_grad, moegain_grad, qgain_grad, kgain_grad = lax.psum(
        (
            router_part,
            jnp.sum(attngain_rows, axis=0),
            moegain_part,
            jnp.sum(qgain_rows, axis=(0, 1)),
            jnp.sum(kgain_rows, axis=(0, 1)),
        ),
        both,
    )
    return (
        layer_out,
        input_grad,
        attngain_grad,
        weight_grad[:, : nq * hd],
        weight_grad[:, nq * hd : (nq + nkv) * hd],
        weight_grad[:, (nq + nkv) * hd : nqkv],
        weight_grad[:, nqkv:].T,
        qgain_grad,
        kgain_grad,
        moegain_grad,
        router_grad,
        gate_grad[None],
        up_grad[None],
        down_grad[None],
    )


def solution(mesh):
    both = ("dp", "tensor")
    in_specs = (
        P(both, None),
        P("dp", None),
        P(both, None),
        P(),
        P("dp", "tensor"),
        P("dp", "tensor"),
        P("dp", "tensor"),
        P("tensor", "dp"),
        P(),
        P(),
        P(),
        P(),
        P(both, None, None),
        P(both, None, None),
        P(both, None, None),
        P(both, None),
    )
    out_specs = (
        P(both, None),
        P(both, None),
        P(),
        P("dp", "tensor"),
        P("dp", "tensor"),
        P("dp", "tensor"),
        P("tensor", "dp"),
        P(),
        P(),
        P(),
        P(),
        P(both, None, None),
        P(both, None, None),
        P(both, None, None),
    )
    return jax.shard_map(
        on_device, mesh=mesh, in_specs=in_specs, out_specs=out_specs, check_vma=False
    )
```

```python
import math

import jax
import jax.numpy as jnp
from jax import lax
from jax.experimental import pallas as pl
from jax.experimental.pallas import tpu as pltpu
from jax.sharding import PartitionSpec as P

BLOCK = 128
EPSILON = 1e-06
ROPE_BASE = 1000000.0
MASKED = -1e30
F32 = jnp.float32
BF16 = jnp.bfloat16


def dot_nt(a, b):
    return lax.dot_general(a, b, (((1,), (1,)), ((), ())), preferred_element_type=F32)


def dot_tn(a, b):
    return lax.dot_general(a, b, (((0,), (0,)), ((), ())), preferred_element_type=F32)


def dot_nn(a, b):
    return lax.dot_general(a, b, (((1,), (0,)), ((), ())), preferred_element_type=F32)


def rms_recip(values):
    return lax.rsqrt(jnp.mean(values * values, axis=-1, keepdims=True) + EPSILON)


def rms_scale(values, gain):
    return values * rms_recip(values) * gain


def rms_back(values, gain, upstream):
    r = rms_recip(values)
    scaled = upstream * gain
    inner = jnp.mean(scaled * values, axis=-1, keepdims=True)
    grad_values = r * scaled - values * (r * r * r) * inner
    return grad_values, upstream * values * r


def rotate(values, cosine, sine):
    half = values.shape[-1] // 2
    a = values[..., :half]
    b = values[..., half:]
    return jnp.concatenate([a * cosine - b * sine, b * cosine + a * sine], axis=-1)


def layout(doc_row):
    length = doc_row.shape[0]
    indices = jnp.arange(length, dtype=jnp.int32)
    same_doc = doc_row[:, None] == doc_row[None, :]
    earlier = indices[None, :] < indices[:, None]
    position = jnp.sum(jnp.where(same_doc & earlier, 1, 0), axis=1).astype(jnp.int32)
    blocks = position // BLOCK
    allowed = same_doc & (blocks[None, :] <= blocks[:, None])
    return position, allowed


def rotary(position, head_size):
    half = head_size // 2
    frequency = jnp.exp(-jnp.log(ROPE_BASE) * jnp.arange(half, dtype=F32) * 2.0 / head_size)
    angles = position.astype(F32)[:, None] * frequency[None, :]
    return jnp.cos(angles)[:, None, :], jnp.sin(angles)[:, None, :]


MESH = pl.DeviceIdType.MESH
ANY = pl.BlockSpec(memory_space=pl.ANY)
VMEM = pl.BlockSpec(memory_space=pltpu.VMEM)
NX, NYH, NZ, NC = 4, 2, 4, 2
RING = 4


class Place:
    def __init__(self):
        dp = lax.axis_index("dp")
        self.t = lax.axis_index("tensor")
        self.c = lax.rem(dp, NC)
        self.z = lax.rem(dp // NC, NZ)
        self.yh = lax.rem(dp // (NC * NZ), NYH)
        self.x = dp // (NC * NZ * NYH)

    def device(self, x=None, yh=None, z=None, c=None, t=None):
        pick = lambda given, own: own if given is None else given
        x, yh, z, c = pick(x, self.x), pick(yh, self.yh), pick(z, self.z), pick(c, self.c)
        return (((x * NYH + yh) * NZ + z) * NC + c, pick(t, self.t))


def after(i):
    return lax.rem(i + 1, RING)


def before(i):
    return lax.rem(i + RING - 1, RING)


def across(i):
    return lax.rem(i + 2, RING)


def greet(peers):
    barrier = pltpu.get_barrier_semaphore()
    for peer in peers:
        pl.semaphore_signal(barrier, inc=1, device_id=peer, device_id_type=MESH)
    pl.semaphore_wait(barrier, len(peers))


class Copies:
    def __init__(self, send, recv, local):
        self.send, self.recv, self.local = send, recv, local
        self.n = self.m = 0
        self.sent = []

    def put(self, src, dst, peer):
        copy = pltpu.make_async_remote_copy(
            src_ref=src,
            dst_ref=dst,
            send_sem=self.send.at[self.n],
            recv_sem=self.recv.at[self.n],
            device_id=peer,
            device_id_type=MESH,
        )
        self.n += 1
        copy.start()
        self.sent.append(copy)
        return copy

    def keep(self, src, dst):
        copy = pltpu.make_async_copy(src, dst, self.local.at[self.m])
        self.m += 1
        copy.start()
        return copy

    def finish(self):
        for copy in self.sent:
            copy.wait_send()


def gather_kernel(sa, sb, tok, doc, wa, wb, toks, docs, send, recv, local):
    me = Place()
    x, yh, z, c, t = me.x, me.yh, me.z, me.c, me.t
    sibling = me.device(c=1 - c)
    pair = me.device(yh=1 - yh)
    partner = me.device(t=1 - t)
    ring_x = (me.device(x=after(x)), me.device(x=before(x)))
    ring_z = (me.device(z=after(z)), me.device(z=before(z)))
    greet([sibling, pair, partner, *ring_x, *ring_z])
    go = Copies(send, recv, local)

    shards = ((sa, wa), (sb, wb))
    cores = [go.put(s.at[1 - c], w.at[x, yh, z, c], sibling) for s, w in shards]
    kept = [go.keep(s.at[c], w.at[x, yh, z, c]) for s, w in shards]
    to_partner = go.put(tok, toks.at[c, t], partner)
    rest = [go.keep(tok, toks.at[c, t]), go.keep(doc, docs.at[c])]
    tail = [go.put(tok, toks.at[c, t], sibling), go.put(doc, docs.at[c], sibling)]
    for copy in kept:
        copy.wait()
    for copy in cores:
        copy.wait_recv()
    pairs = [go.put(w.at[x, yh, z], w.at[x, yh, z], pair) for _, w in shards]

    ways = (
        (wa, x, z, ring_x, ring_z, lambda w, i, j, y: w.at[i, y, j], lambda w, j, y: w.at[:, y, j]),
        (wb, z, x, ring_z, ring_x, lambda w, i, j, y: w.at[j, y, i], lambda w, j, y: w.at[j, y]),
    )

    def first(y):
        out = []
        for w, i, j, one, two, unit, slab in ways:
            own = unit(w, i, j, y)
            out.append((go.put(own, own, one[0]), go.put(own, own, one[1])))
        return out

    def second(y, firsts):
        out = []
        for (w, i, j, one, two, unit, slab), (up, down) in zip(ways, firsts):
            up.wait_recv()
            low = unit(w, before(i), j, y).at[0]
            a = go.put(low, low, one[0])
            down.wait_recv()
            high = unit(w, after(i), j, y).at[1]
            out.append((a, go.put(high, high, one[1])))
        return out

    def third(y, seconds):
        out = []
        for (w, i, j, one, two, unit, slab), (up, down) in zip(ways, seconds):
            up.wait_recv()
            down.wait_recv()
            own = slab(w, j, y)
            out.append((go.put(own, own, two[0]), go.put(own, own, two[1])))
        return out

    def fourth(y, thirds):
        out = []
        for (w, i, j, one, two, unit, slab), (up, down) in zip(ways, thirds):
            up.wait_recv()
            low = slab(w, before(j), y).at[:, 0]
            a = go.put(low, low, two[0])
            down.wait_recv()
            high = slab(w, after(j), y).at[:, 1]
            out.append((a, go.put(high, high, two[1])))
        return out

    near = first(yh)
    near = second(yh, near)
    for copy in pairs:
        copy.wait_recv()
    far = first(1 - yh)
    near = third(yh, near)
    far = second(1 - yh, far)
    to_partner.wait_recv()
    other = toks.at[c, 1 - t]
    tail.append(go.put(other, other, sibling))
    far = third(1 - yh, far)
    near = fourth(yh, near)
    far = fourth(1 - yh, far)
    for up, down in near + far:
        up.wait_recv()
        down.wait_recv()
    for copy in tail:
        copy.wait_recv()
    for copy in rest:
        copy.wait()
    go.finish()


def gather(shard_a, shard_b, tokens, docs):
    width_a, width_b = shard_a.shape[-1], shard_b.shape[-1]
    rows = shard_a.shape[1]
    lead = (NX, NYH, NZ, NC, rows)
    wa, wb, toks, docs = pl.pallas_call(
        gather_kernel,
        name="gather_weights",
        out_shape=(
            jax.ShapeDtypeStruct((*lead, width_a), BF16),
            jax.ShapeDtypeStruct((*lead, width_b), BF16),
            jax.ShapeDtypeStruct((NC, 2, *tokens.shape), BF16),
            jax.ShapeDtypeStruct((NC, *docs.shape), docs.dtype),
        ),
        in_specs=[ANY] * 4,
        out_specs=(ANY,) * 4,
        scratch_shapes=[
            pltpu.SemaphoreType.DMA((40,)),
            pltpu.SemaphoreType.DMA((40,)),
            pltpu.SemaphoreType.DMA((4,)),
        ],
        compiler_params=pltpu.CompilerParams(collective_id=1, has_side_effects=True),
    )(shard_a, shard_b, tokens, docs)
    depth = NX * NYH * NZ * NC * rows
    return (
        wa.reshape(depth, width_a),
        wb.reshape(depth, width_b),
        toks.reshape(NC * 2 * tokens.shape[0], tokens.shape[1]),
        docs,
    )


def share_kernel(tok, toks, send, recv, local):
    me = Place()
    c, t = me.c, me.t
    sibling, partner = me.device(c=1 - c), me.device(t=1 - t)
    greet([sibling, partner])
    go = Copies(send, recv, local)
    half = tok.shape[0] // 2
    parts = [pl.ds(i * half, half) for i in range(2)]
    over = [go.put(tok.at[p], toks.at[c, t, p], partner) for p in parts]
    near = [go.put(tok, toks.at[c, t], sibling)]
    kept = go.keep(tok, toks.at[c, t])
    for copy, p in zip(over, parts):
        copy.wait_recv()
        other = toks.at[c, 1 - t, p]
        near.append(go.put(other, other, sibling))
    for copy in near:
        copy.wait_recv()
    kept.wait()
    go.finish()


def share(tokens, ident):
    toks = pl.pallas_call(
        share_kernel,
        name=f"share_rows_{ident}",
        out_shape=jax.ShapeDtypeStruct((NC, 2, *tokens.shape), tokens.dtype),
        in_specs=[ANY],
        out_specs=ANY,
        scratch_shapes=[
            pltpu.SemaphoreType.DMA((5,)),
            pltpu.SemaphoreType.DMA((5,)),
            pltpu.SemaphoreType.DMA((1,)),
        ],
        compiler_params=pltpu.CompilerParams(collective_id=ident, has_side_effects=True),
    )(tokens)
    return toks.reshape(NC * 2 * tokens.shape[0], tokens.shape[1])


def reduce_kernel(part, out, near, own, sums, far, send, recv, local):
    me = Place()
    c, t = me.c, me.t
    sibling, partner = me.device(c=1 - c), me.device(t=1 - t)
    greet([sibling, partner])
    go = Copies(send, recv, local)
    half = out.shape[0] // 2
    parts = [pl.ds(i * half, half) for i in range(2)]
    away = [go.put(part.at[1 - c, 1 - t, p], near.at[0, p], sibling) for p in parts]
    home = go.put(part.at[1 - c, t], near.at[1], sibling)
    kept = [go.keep(part.at[c, 1 - t], own.at[0]), go.keep(part.at[c, t], own.at[1])]
    kept[0].wait()
    over = []
    for copy, p in zip(away, parts):
        copy.wait_recv()
        sums[p] = (own[0, p].astype(F32) + near[0, p].astype(F32)).astype(BF16)
        over.append(go.put(sums.at[p], far.at[p], partner))
    kept[1].wait()
    home.wait_recv()
    out[...] = own[1].astype(F32) + near[1].astype(F32)
    for copy, p in zip(over, parts):
        copy.wait_recv()
        out[p] += far[p].astype(F32)
    go.finish()


def reduce(part, ident):
    rows, width = part.shape[0] // (NC * 2), part.shape[1]
    return pl.pallas_call(
        reduce_kernel,
        name=f"reduce_rows_{ident}",
        out_shape=jax.ShapeDtypeStruct((rows, width), F32),
        in_specs=[ANY],
        out_specs=VMEM,
        scratch_shapes=[
            pltpu.VMEM((2, rows, width), BF16),
            pltpu.VMEM((2, rows, width), BF16),
            pltpu.VMEM((rows, width), BF16),
            pltpu.VMEM((rows, width), BF16),
            pltpu.SemaphoreType.DMA((5,)),
            pltpu.SemaphoreType.DMA((5,)),
            pltpu.SemaphoreType.DMA((2,)),
        ],
        compiler_params=pltpu.CompilerParams(
            collective_id=ident, has_side_effects=True, vmem_limit_bytes=24 << 20
        ),
    )(part.reshape(NC, 2, rows, width))


def scatter_kernel(
    ga, gb, oa, ob, ka, kb, ra, rb, qa, qb, sa, sb, ya, yb, ma, mb, ta, tb, ca, cb, send, recv, local
):
    me = Place()
    x, yh, z, c = me.x, me.yh, me.z, me.c
    sibling = me.device(c=1 - c)
    pair = me.device(yh=1 - yh)
    ring_x = (me.device(x=after(x)), me.device(x=before(x)))
    ring_z = (me.device(z=after(z)), me.device(z=before(z)))
    greet([sibling, pair, *ring_x, *ring_z])
    go = Copies(send, recv, local)

    def slab_a(i, r):
        return ga.at[i, :, :, r]

    def slab_b(i, r):
        return gb.at[:, :, i, r]

    ways = ((slab_a, x, ring_x, ka, ra), (slab_b, z, ring_z, kb, rb))
    cross, straight, kept = [], [], []
    for slab, i, ring, k, r in ways:
        cross.append((go.put(slab(across(i), 0), r.at[0], ring[0]), go.put(slab(across(i), 1), r.at[1], ring[1])))
    for slab, i, ring, k, r in ways:
        kept.append(
            [
                go.keep(slab(after(i), 0), k.at[0]),
                go.keep(slab(before(i), 1), k.at[1]),
                go.keep(slab(i, 0), k.at[2]),
                go.keep(slab(i, 1), k.at[3]),
            ]
        )
        straight.append((go.put(slab(after(i), 1), r.at[2], ring[0]), go.put(slab(before(i), 0), r.at[3], ring[1])))
    summed = []
    for (slab, i, ring, k, r), copies, own in zip(ways, cross, kept):
        both = []
        for side in range(2):
            own[side].wait()
            copies[side].wait_recv()

            def add(n, _, k=k, r=r, side=side):
                at = (side, n // k.shape[2], lax.rem(n, k.shape[2]))
                k[at] = (k[at].astype(F32) + r[at].astype(F32)).astype(BF16)
                return 0

            lax.fori_loop(0, k.shape[1] * k.shape[2], add, 0)
            both.append(go.put(k.at[side], r.at[4 + side], ring[side]))
        summed.append(both)
    for (slab, i, ring, k, r), one, two, own in zip(ways, straight, summed, kept):
        own[2].wait()
        own[3].wait()
        one[0].wait_recv()
        one[1].wait_recv()
        two[0].wait_recv()
        two[1].wait_recv()

        def close(n, _, k=k, r=r):
            at = (n // k.shape[2], lax.rem(n, k.shape[2]))
            for own, summed_side, straight_side in ((2, 4, 3), (3, 5, 2)):
                k[(own, *at)] = (
                    k[(own, *at)].astype(F32)
                    + r[(summed_side, *at)].astype(F32)
                    + r[(straight_side, *at)].astype(F32)
                ).astype(BF16)
            return 0

        lax.fori_loop(0, k.shape[1] * k.shape[2], close, 0)

    def part_a(r, j, y):
        return ka.at[r, y, j]

    def part_b(r, j, y):
        return kb.at[r, j, y]

    ways = ((part_a, z, ring_z, qa, sa), (part_b, x, ring_x, qb, sb))
    cross, straight, summed = [], [], []
    for part, j, ring, q, s in ways:
        cross.append(
            [
                [go.put(part(2 + side, across(j), y), q.at[side, y], ring[side]) for y in range(NYH)]
                for side in range(2)
            ]
        )
    for part, j, ring, q, s in ways:
        straight.append(
            [
                [go.put(part(3 - side, (after, before)[side](j), y), q.at[2 + side, y], ring[side]) for y in range(NYH)]
                for side in range(2)
            ]
        )
    for (part, j, ring, q, s), copies in zip(ways, cross):
        both = []
        for side in range(2):
            sent = []
            for y in range(NYH):
                copies[side][y].wait_recv()
                mine = part(2 + side, (after, before)[side](j), y)
                s[side, y] = (mine[...].astype(F32) + q[side, y].astype(F32)).astype(BF16)
                sent.append(go.put(s.at[side, y], q.at[4 + side, y], ring[side]))
            both.append(sent)
        summed.append(both)
    for (part, j, ring, q, s), one, two in zip(ways, straight, summed):
        for copies in (*one, *two):
            for copy in copies:
                copy.wait_recv()

    def total(part, j, q, side, y):
        return part(2 + side, j, y)[...].astype(F32) + q[4 + side, y].astype(F32) + q[3 - side, y].astype(F32)

    ways = ((part_a, z, qa, ya, ma, ta, ca, oa), (part_b, x, qb, yb, mb, tb, cb, ob))
    crossed = []
    for part, j, q, yy, m, tt, cc, o in ways:
        for side in range(2):
            yy[side] = total(part, j, q, side, 1 - yh).astype(BF16)
        crossed.append(go.put(yy, m, pair))
    last = []
    for (part, j, q, yy, m, tt, cc, o), copy in zip(ways, crossed):
        for side in range(2):
            tt[side] = total(part, j, q, side, yh)
        copy.wait_recv()
        tt[...] += m[...].astype(F32)
        last.append(go.put(tt.at[1 - c], cc, sibling))
        o[c] = tt[c]
    for (part, j, q, yy, m, tt, cc, o), copy in zip(ways, last):
        copy.wait_recv()
        o[1 - c] = cc[...]
    go.finish()


def scatter(grad_a, grad_b):
    rows = grad_a.shape[0] // (NX * NYH * NZ * NC)
    lead = (NX, NYH, NZ, NC, rows)
    widths = (grad_a.shape[1], grad_b.shape[1])

    def each(shape, dtype):
        return [pltpu.VMEM((*shape, rows, w), dtype) for w in widths]

    def held(count):
        dims = ((NYH, NZ), (NX, NYH))
        return [pltpu.VMEM((count, *d, rows, w), BF16) for d, w in zip(dims, widths)]

    return pl.pallas_call(
        scatter_kernel,
        name="scatter_weights",
        out_shape=tuple(jax.ShapeDtypeStruct((NC, rows, w), F32) for w in widths),
        in_specs=[ANY, ANY],
        out_specs=(VMEM, VMEM),
        scratch_shapes=[
            *held(4),
            *held(6),
            *each((6, NYH), BF16),
            *each((2, NYH), BF16),
            *each((2,), BF16),
            *each((2,), BF16),
            *each((2,), F32),
            *each((), F32),
            pltpu.SemaphoreType.DMA((40,)),
            pltpu.SemaphoreType.DMA((40,)),
            pltpu.SemaphoreType.DMA((8,)),
        ],
        compiler_params=pltpu.CompilerParams(
            collective_id=5, has_side_effects=True, vmem_limit_bytes=40 << 20
        ),
    )(grad_a.reshape(*lead, widths[0]), grad_b.reshape(*lead, widths[1]))


def on_device(
    hidden_in,
    doc_ids,
    expert_ids,
    attn_gain,
    query_weight,
    key_weight,
    value_weight,
    output_weight,
    query_gain,
    key_gain,
    moe_gain,
    router_weight,
    gate_weight,
    up_weight,
    down_weight,
    cotangent,
):
    both = ("dp", "tensor")
    tok, width = hidden_in.shape
    hd = query_gain.shape[0]
    nkv = key_weight.shape[1] // hd
    nq = query_weight.shape[1] // hd
    group = nq // nkv
    experts = router_weight.shape[1]
    routes = expert_ids.shape[1]
    cap = tok * routes // experts
    slots = experts * cap
    scale = 1.0 / math.sqrt(hd)
    tokens = doc_ids.shape[1]
    me = lax.axis_index(both)

    lane = lax.broadcasted_iota(jnp.int32, (1, 1, experts), 2)
    chosen = jnp.sum((expert_ids[:, :, None] == lane).astype(F32), axis=1)
    below = (
        lax.broadcasted_iota(jnp.int32, (tok, tok), 1)
        < lax.broadcasted_iota(jnp.int32, (tok, tok), 0)
    ).astype(BF16)
    rank = dot_nn(below, chosen.astype(BF16))
    place = jnp.where(chosen > 0, rank, -1.0).T
    spread = (
        place[:, None, :] == lax.broadcasted_iota(jnp.int32, (1, cap, 1), 1).astype(F32)
    ).astype(BF16).reshape(slots, tok)

    cot_out = dot_nn(spread, jnp.concatenate([cotangent, chosen.astype(BF16)], axis=1)).astype(BF16)
    cot_in = lax.all_to_all(
        cot_out.reshape(experts, cap, width + experts), both, split_axis=0, concat_axis=0, tiled=True
    ).reshape(slots, width + experts)

    hidden = hidden_in.astype(F32)
    normed_local = rms_scale(hidden, attn_gain).astype(BF16)

    def core_parts(shards):
        split = [s.reshape(s.shape[0], NC, s.shape[1] // NC) for s in shards]
        return jnp.concatenate(split, axis=2).transpose(1, 0, 2)

    in_weights, out_weights, normed, docs = gather(
        core_parts([query_weight, key_weight, value_weight]),
        core_parts([output_weight.T]),
        normed_local,
        jnp.broadcast_to(doc_ids, (8, tokens)).astype(F32),
    )

    position, allowed = jax.vmap(layout)(docs[:, 0])
    cosine, sine = jax.vmap(lambda p: rotary(p, hd))(position)
    raw = dot_nn(normed, in_weights)
    heads = group * hd
    query_raw = raw[:, :heads].reshape(NC, tokens, group, hd)
    key_raw = raw[:, heads : heads + hd].reshape(NC, tokens, 1, hd)
    values = raw[:, heads + hd :].astype(BF16).reshape(NC, tokens, hd)
    query = rotate(rms_scale(query_raw, query_gain), cosine, sine).astype(BF16)
    key = rotate(rms_scale(key_raw, key_gain), cosine, sine).astype(BF16)[:, :, 0]
    scores = jnp.einsum("bqgd,btd->bgqt", query, key, preferred_element_type=F32) * scale
    scores = jnp.where(allowed[:, None], scores, MASKED)
    weight = jnp.exp(scores - jnp.max(scores, axis=-1, keepdims=True))
    attention = weight / jnp.sum(weight, axis=-1, keepdims=True)
    attention_low = attention.astype(BF16)
    mixed = jnp.einsum("bgqt,btd->bqgd", attention_low, values, preferred_element_type=F32)
    mixed = mixed.astype(BF16).reshape(NC * tokens, heads)
    attn_out = reduce(dot_nt(mixed, out_weights).astype(BF16), 2)

    residual = hidden + attn_out
    moe_input = rms_scale(residual, moe_gain).astype(BF16)
    sent = dot_nn(spread, moe_input).astype(BF16)
    rows = lax.all_to_all(
        sent.reshape(experts, cap, width), both, split_axis=0, concat_axis=0, tiled=True
    ).reshape(slots, width)
    logits = dot_nn(moe_input, router_weight)
    masked = jnp.where(chosen > 0, logits, MASKED)
    probs = jnp.exp(masked - jnp.max(masked, axis=-1, keepdims=True))
    probs = probs / jnp.sum(probs, axis=-1, keepdims=True)

    gate_mat, up_mat, down_mat = gate_weight[0], up_weight[0], down_weight[0]
    cot_rows = cot_in[:, :width]
    inner_up = dot_nt(cot_rows, down_mat)
    row_logits = jnp.where(cot_in[:, width:] > 0, dot_nn(rows, router_weight), MASKED)
    row_probs = jnp.exp(row_logits - jnp.max(row_logits, axis=-1, keepdims=True))
    mine = lax.broadcasted_iota(jnp.int32, (1, experts), 1) == me
    prob = jnp.sum(jnp.where(mine, row_probs, 0.0), axis=-1, keepdims=True) / jnp.sum(
        row_probs, axis=-1, keepdims=True
    )
    gate_pre = dot_nn(rows, gate_mat)
    up_pre = dot_nn(rows, up_mat)
    sigmoid = jax.nn.sigmoid(gate_pre)
    silu = gate_pre * sigmoid
    inner = silu * up_pre
    gate_up = jnp.sum(inner * inner_up, axis=-1, keepdims=True)
    inner_low = (prob * inner).astype(BF16)
    grad_inner = prob * inner_up
    grad_gate = (grad_inner * up_pre * sigmoid * (1.0 + gate_pre * (1.0 - sigmoid))).astype(BF16)
    grad_up = (grad_inner * silu).astype(BF16)
    grad_rows = (dot_nt(grad_gate, gate_mat) + dot_nt(grad_up, up_mat)).astype(BF16)
    gate_up_high = gate_up.astype(BF16)
    gate_up_rest = (gate_up - gate_up_high.astype(F32)).astype(BF16)
    none = jnp.zeros((), BF16)
    home_out = jnp.concatenate(
        [grad_rows, jnp.where(mine, gate_up_high, none), jnp.where(mine, gate_up_rest, none)], axis=1
    )
    home = lax.all_to_all(
        home_out.reshape(experts, cap, width + 2 * experts), both, split_axis=0, concat_axis=0, tiled=True
    ).reshape(slots, width + 2 * experts)
    expert_out = dot_nn(inner_low, down_mat).astype(BF16)
    returned = lax.all_to_all(
        expert_out.reshape(experts, cap, width), both, split_axis=0, concat_axis=0, tiled=True
    ).reshape(slots, width)
    down_grad = dot_tn(inner_low, cot_rows)
    gate_grad = dot_tn(rows, grad_gate)
    up_grad = dot_tn(rows, grad_up)

    upstream = cotangent.astype(F32)
    summed = dot_tn(spread, home)
    gate_upstream = summed[:, width : width + experts] + summed[:, width + experts :]
    grad_chosen = probs * (gate_upstream - jnp.sum(probs * gate_upstream, axis=-1, keepdims=True))
    grad_logits = grad_chosen.astype(BF16)
    grad_moe_input = summed[:, :width] + dot_nt(grad_logits, router_weight)
    router_part = dot_tn(moe_input, grad_logits)
    grad_norm, moegain_rows = rms_back(residual, moe_gain, grad_moe_input)
    moegain_part = jnp.sum(moegain_rows, axis=0)
    grad_residual = upstream + grad_norm
    grad_attn = share(grad_residual.astype(BF16), 3)
    layer_out = (residual + dot_tn(spread, returned)).astype(BF16)

    grad_mixed = dot_nn(grad_attn, out_weights).astype(BF16).reshape(NC, tokens, group, hd)
    grad_values = jnp.einsum("bgqt,bqgd->btd", attention_low, grad_mixed, preferred_element_type=F32)
    grad_soft = jnp.einsum("bqgd,btd->bgqt", grad_mixed, values, preferred_element_type=F32)
    row_delta = jnp.sum(attention * grad_soft, axis=-1, keepdims=True)
    grad_scores = (attention * (grad_soft - row_delta)).astype(BF16)
    grad_query = jnp.einsum("bgqt,btd->bqgd", grad_scores, key, preferred_element_type=F32) * scale
    grad_key = jnp.einsum("bgqt,bqgd->btd", grad_scores, query, preferred_element_type=F32) * scale
    grad_query_raw, qgain_rows = rms_back(query_raw, query_gain, rotate(grad_query, cosine, -sine))
    grad_key_raw, kgain_rows = rms_back(
        key_raw, key_gain, rotate(grad_key[:, :, None], cosine, -sine)
    )
    grad_raw = jnp.concatenate(
        [
            grad_query_raw.astype(BF16).reshape(NC * tokens, heads),
            grad_key_raw.astype(BF16).reshape(NC * tokens, hd),
            grad_values.astype(BF16).reshape(NC * tokens, hd),
        ],
        axis=1,
    )
    grad_normed = reduce(dot_nt(grad_raw, in_weights).astype(BF16), 4)
    in_grad, out_grad = scatter(
        dot_tn(normed, grad_raw).astype(BF16), dot_tn(grad_attn, mixed).astype(BF16)
    )
    grad_hidden, attngain_rows = rms_back(hidden, attn_gain, grad_normed)
    input_grad = grad_residual + grad_hidden

    def all_sum(flat):
        copies = jnp.broadcast_to(flat[None], (experts, *flat.shape))
        return jnp.sum(lax.all_to_all(copies, both, 0, 0, tiled=True), axis=0)

    def all_sum_long(rows):
        pieces = rows.reshape(experts, rows.shape[0] // experts, rows.shape[1])
        piece = jnp.sum(lax.all_to_all(pieces, both, 0, 0, tiled=True), axis=0)
        copies = jnp.broadcast_to(piece[None], pieces.shape)
        return lax.all_to_all(copies, both, 0, 0, tiled=True).reshape(rows.shape)

    router_grad = all_sum_long(router_part)
    gains = all_sum(
        jnp.concatenate(
            [
                jnp.sum(attngain_rows, axis=0),
                moegain_part,
                jnp.sum(qgain_rows, axis=(0, 1, 2)),
                jnp.sum(kgain_rows, axis=(0, 1, 2)),
            ]
        ).reshape(-1, hd)
    ).reshape(-1)
    attngain_grad = gains[:width]
    moegain_grad = gains[width : 2 * width]
    qgain_grad = gains[2 * width : 2 * width + hd]
    kgain_grad = gains[2 * width + hd :]

    def join(parts):
        return jnp.concatenate([parts[i] for i in range(NC)], axis=1)

    return (
        layer_out,
        input_grad,
        attngain_grad,
        join(in_grad[:, :, :heads]),
        join(in_grad[:, :, heads : heads + hd]),
        join(in_grad[:, :, heads + hd :]),
        join(out_grad).T,
        qgain_grad,
        kgain_grad,
        moegain_grad,
        router_grad,
        gate_grad[None],
        up_grad[None],
        down_grad[None],
    )


def solution(mesh):
    both = ("dp", "tensor")
    in_specs = (
        P(both, None),
        P("dp", None),
        P(both, None),
        P(),
        P("dp", "tensor"),
        P("dp", "tensor"),
        P("dp", "tensor"),
        P("tensor", "dp"),
        P(),
        P(),
        P(),
        P(),
        P(both, None, None),
        P(both, None, None),
        P(both, None, None),
        P(both, None),
    )
    out_specs = (
        P(both, None),
        P(both, None),
        P(),
        P("dp", "tensor"),
        P("dp", "tensor"),
        P("dp", "tensor"),
        P("tensor", "dp"),
        P(),
        P(),
        P(),
        P(),
        P(both, None, None),
        P(both, None, None),
        P(both, None, None),
    )
    return jax.shard_map(
        on_device, mesh=mesh, in_specs=in_specs, out_specs=out_specs, check_vma=False
    )
```

```python
import functools
import math

import jax
import jax.numpy as jnp
from jax import lax
from jax.experimental import pallas as pl
from jax.experimental.pallas import tpu as pltpu
from jax.sharding import PartitionSpec as P

BLOCK = 128
EPSILON = 1e-06
ROPE_BASE = 1000000.0
MASKED = -1e30
F32 = jnp.float32
BF16 = jnp.bfloat16


def dot_nt(a, b):
    return lax.dot_general(a, b, (((1,), (1,)), ((), ())), preferred_element_type=F32)


def dot_tn(a, b):
    return lax.dot_general(a, b, (((0,), (0,)), ((), ())), preferred_element_type=F32)


def dot_nn(a, b):
    return lax.dot_general(a, b, (((1,), (0,)), ((), ())), preferred_element_type=F32)


def rms_recip(values):
    return lax.rsqrt(jnp.mean(values * values, axis=-1, keepdims=True) + EPSILON)


def rms_scale(values, gain):
    return values * rms_recip(values) * gain


def rms_back(values, gain, upstream):
    r = rms_recip(values)
    scaled = upstream * gain
    inner = jnp.mean(scaled * values, axis=-1, keepdims=True)
    grad_values = r * scaled - values * (r * r * r) * inner
    return grad_values, upstream * values * r


def rotate(values, cosine, sine):
    half = values.shape[-1] // 2
    a = values[..., :half]
    b = values[..., half:]
    return jnp.concatenate([a * cosine - b * sine, b * cosine + a * sine], axis=-1)


def layout(doc_row):
    length = doc_row.shape[0]
    indices = jnp.arange(length, dtype=jnp.int32)
    same_doc = doc_row[:, None] == doc_row[None, :]
    earlier = indices[None, :] < indices[:, None]
    position = jnp.sum(jnp.where(same_doc & earlier, 1, 0), axis=1).astype(jnp.int32)
    blocks = position // BLOCK
    allowed = same_doc & (blocks[None, :] <= blocks[:, None])
    return position, allowed


def rotary(position, head_size):
    half = head_size // 2
    frequency = jnp.exp(-jnp.log(ROPE_BASE) * jnp.arange(half, dtype=F32) * 2.0 / head_size)
    angles = position.astype(F32)[:, None] * frequency[None, :]
    return jnp.cos(angles), jnp.sin(angles)


MESH = pl.DeviceIdType.MESH
ANY = pl.BlockSpec(memory_space=pl.ANY)
VMEM = pl.BlockSpec(memory_space=pltpu.VMEM)
NX, NYH, NZ, NC = 4, 2, 4, 2
RING = 4


def cost(microseconds):
    return pl.CostEstimate(flops=0, transcendentals=0, bytes_accessed=int(microseconds * 3.6e6))


class Place:
    def __init__(self):
        dp = lax.axis_index("dp")
        self.t = lax.axis_index("tensor")
        self.c = lax.rem(dp, NC)
        self.z = lax.rem(dp // NC, NZ)
        self.yh = lax.rem(dp // (NC * NZ), NYH)
        self.x = dp // (NC * NZ * NYH)

    def device(self, x=None, yh=None, z=None, c=None, t=None):
        pick = lambda given, own: own if given is None else given
        x, yh, z, c = pick(x, self.x), pick(yh, self.yh), pick(z, self.z), pick(c, self.c)
        return (((x * NYH + yh) * NZ + z) * NC + c, pick(t, self.t))


def after(i):
    return lax.rem(i + 1, RING)


def before(i):
    return lax.rem(i + RING - 1, RING)


def across(i):
    return lax.rem(i + 2, RING)


def greet(peers):
    barrier = pltpu.get_barrier_semaphore()
    for peer in peers:
        pl.semaphore_signal(barrier, inc=1, device_id=peer, device_id_type=MESH)
    pl.semaphore_wait(barrier, len(peers))


class Copies:
    def __init__(self, send, recv, local):
        self.send, self.recv, self.local = send, recv, local
        self.n = self.m = 0
        self.sent = []

    def put(self, src, dst, peer):
        copy = pltpu.make_async_remote_copy(
            src_ref=src,
            dst_ref=dst,
            send_sem=self.send.at[self.n],
            recv_sem=self.recv.at[self.n],
            device_id=peer,
            device_id_type=MESH,
        )
        self.n += 1
        copy.start()
        self.sent.append(copy)
        return copy

    def keep(self, src, dst):
        copy = pltpu.make_async_copy(src, dst, self.local.at[self.m])
        self.m += 1
        copy.start()
        return copy

    def finish(self):
        for copy in self.sent:
            copy.wait_send()


def gather_kernel(sa, sb, tok, doc, wa, wb, toks, docs, send, recv, local):
    me = Place()
    x, yh, z, c, t = me.x, me.yh, me.z, me.c, me.t
    sibling = me.device(c=1 - c)
    pair = me.device(yh=1 - yh)
    partner = me.device(t=1 - t)
    ring_x = (me.device(x=after(x)), me.device(x=before(x)))
    ring_z = (me.device(z=after(z)), me.device(z=before(z)))
    greet([sibling, pair, partner, *ring_x, *ring_z])
    go = Copies(send, recv, local)

    shards = ((sa, wa), (sb, wb))
    cores = [go.put(s.at[1 - c], w.at[x, yh, z, c], sibling) for s, w in shards]
    kept = [go.keep(s.at[c], w.at[x, yh, z, c]) for s, w in shards]
    to_partner = go.put(tok, toks.at[c, t], partner)
    rest = [go.keep(tok, toks.at[c, t]), go.keep(doc, docs.at[c])]
    tail = [go.put(tok, toks.at[c, t], sibling), go.put(doc, docs.at[c], sibling)]
    for copy in kept:
        copy.wait()
    for copy in cores:
        copy.wait_recv()
    pairs = [go.put(w.at[x, yh, z], w.at[x, yh, z], pair) for _, w in shards]

    ways = (
        (wa, x, z, ring_x, ring_z, lambda w, i, j, y: w.at[i, y, j], lambda w, j, y: w.at[:, y, j]),
        (wb, z, x, ring_z, ring_x, lambda w, i, j, y: w.at[j, y, i], lambda w, j, y: w.at[j, y]),
    )

    def first(y):
        out = []
        for w, i, j, one, two, unit, slab in ways:
            own = unit(w, i, j, y)
            out.append((go.put(own, own, one[0]), go.put(own, own, one[1])))
        return out

    def second(y, firsts):
        out = []
        for (w, i, j, one, two, unit, slab), (up, down) in zip(ways, firsts):
            up.wait_recv()
            low = unit(w, before(i), j, y).at[0]
            a = go.put(low, low, one[0])
            down.wait_recv()
            high = unit(w, after(i), j, y).at[1]
            out.append((a, go.put(high, high, one[1])))
        return out

    def third(y, seconds):
        out = []
        for (w, i, j, one, two, unit, slab), (up, down) in zip(ways, seconds):
            up.wait_recv()
            down.wait_recv()
            own = slab(w, j, y)
            out.append((go.put(own, own, two[0]), go.put(own, own, two[1])))
        return out

    def fourth(y, thirds):
        out = []
        for (w, i, j, one, two, unit, slab), (up, down) in zip(ways, thirds):
            up.wait_recv()
            low = slab(w, before(j), y).at[:, 0]
            a = go.put(low, low, two[0])
            down.wait_recv()
            high = slab(w, after(j), y).at[:, 1]
            out.append((a, go.put(high, high, two[1])))
        return out

    near = first(yh)
    near = second(yh, near)
    for copy in pairs:
        copy.wait_recv()
    far = first(1 - yh)
    near = third(yh, near)
    far = second(1 - yh, far)
    to_partner.wait_recv()
    other = toks.at[c, 1 - t]
    tail.append(go.put(other, other, sibling))
    far = third(1 - yh, far)
    near = fourth(yh, near)
    far = fourth(1 - yh, far)
    for up, down in near + far:
        up.wait_recv()
        down.wait_recv()
    for copy in tail:
        copy.wait_recv()
    for copy in rest:
        copy.wait()
    go.finish()


def gather(shard_a, shard_b, tokens, docs):
    width_a, width_b = shard_a.shape[-1], shard_b.shape[-1]
    rows = shard_a.shape[1]
    lead = (NX, NYH, NZ, NC, rows)
    wa, wb, toks, docs = pl.pallas_call(
        gather_kernel,
        name="gather_weights",
        cost_estimate=cost(60),
        out_shape=(
            jax.ShapeDtypeStruct((*lead, width_a), BF16),
            jax.ShapeDtypeStruct((*lead, width_b), BF16),
            jax.ShapeDtypeStruct((NC, 2, *tokens.shape), BF16),
            jax.ShapeDtypeStruct((NC, *docs.shape), docs.dtype),
        ),
        in_specs=[ANY] * 4,
        out_specs=(ANY,) * 4,
        scratch_shapes=[
            pltpu.SemaphoreType.DMA((40,)),
            pltpu.SemaphoreType.DMA((40,)),
            pltpu.SemaphoreType.DMA((4,)),
        ],
        compiler_params=pltpu.CompilerParams(collective_id=1, has_side_effects=True),
    )(shard_a, shard_b, tokens, docs)
    depth = NX * NYH * NZ * NC * rows
    return (
        wa.reshape(depth, width_a),
        wb.reshape(depth, width_b),
        toks.reshape(NC * 2 * tokens.shape[0], tokens.shape[1]),
        docs,
    )


def share_kernel(tok, toks, send, recv, local):
    me = Place()
    c, t = me.c, me.t
    sibling, partner = me.device(c=1 - c), me.device(t=1 - t)
    greet([sibling, partner])
    go = Copies(send, recv, local)
    half = tok.shape[0] // 2
    parts = [pl.ds(i * half, half) for i in range(2)]
    over = [go.put(tok.at[p], toks.at[c, t, p], partner) for p in parts]
    near = [go.put(tok, toks.at[c, t], sibling)]
    kept = go.keep(tok, toks.at[c, t])
    for copy, p in zip(over, parts):
        copy.wait_recv()
        other = toks.at[c, 1 - t, p]
        near.append(go.put(other, other, sibling))
    for copy in near:
        copy.wait_recv()
    kept.wait()
    go.finish()


def share(tokens, ident):
    toks = pl.pallas_call(
        share_kernel,
        name=f"share_rows_{ident}",
        cost_estimate=cost(13),
        out_shape=jax.ShapeDtypeStruct((NC, 2, *tokens.shape), tokens.dtype),
        in_specs=[ANY],
        out_specs=ANY,
        scratch_shapes=[
            pltpu.SemaphoreType.DMA((5,)),
            pltpu.SemaphoreType.DMA((5,)),
            pltpu.SemaphoreType.DMA((1,)),
        ],
        compiler_params=pltpu.CompilerParams(collective_id=ident, has_side_effects=True),
    )(tokens)
    return toks.reshape(NC * 2 * tokens.shape[0], tokens.shape[1])


def reduce_kernel(part, out, near, own, sums, far, send, recv, local):
    me = Place()
    c, t = me.c, me.t
    sibling, partner = me.device(c=1 - c), me.device(t=1 - t)
    greet([sibling, partner])
    go = Copies(send, recv, local)
    half = out.shape[0] // 2
    parts = [pl.ds(i * half, half) for i in range(2)]
    away = [go.put(part.at[1 - c, 1 - t, p], near.at[0, p], sibling) for p in parts]
    home = go.put(part.at[1 - c, t], near.at[1], sibling)
    kept = [go.keep(part.at[c, 1 - t], own.at[0]), go.keep(part.at[c, t], own.at[1])]
    kept[0].wait()
    over = []
    for copy, p in zip(away, parts):
        copy.wait_recv()
        sums[p] = (own[0, p].astype(F32) + near[0, p].astype(F32)).astype(BF16)
        over.append(go.put(sums.at[p], far.at[p], partner))
    kept[1].wait()
    home.wait_recv()
    out[...] = own[1].astype(F32) + near[1].astype(F32)
    for copy, p in zip(over, parts):
        copy.wait_recv()
        out[p] += far[p].astype(F32)
    go.finish()


def reduce(part, ident):
    rows, width = part.shape[0] // (NC * 2), part.shape[1]
    return pl.pallas_call(
        reduce_kernel,
        name=f"reduce_rows_{ident}",
        cost_estimate=cost(15),
        out_shape=jax.ShapeDtypeStruct((rows, width), F32),
        in_specs=[ANY],
        out_specs=VMEM,
        scratch_shapes=[
            pltpu.VMEM((2, rows, width), BF16),
            pltpu.VMEM((2, rows, width), BF16),
            pltpu.VMEM((rows, width), BF16),
            pltpu.VMEM((rows, width), BF16),
            pltpu.SemaphoreType.DMA((5,)),
            pltpu.SemaphoreType.DMA((5,)),
            pltpu.SemaphoreType.DMA((2,)),
        ],
        compiler_params=pltpu.CompilerParams(
            collective_id=ident, has_side_effects=True, vmem_limit_bytes=24 << 20
        ),
    )(part.reshape(NC, 2, rows, width))


def scatter_kernel(
    ga, gb, oa, ob, ka, kb, ra, rb, qa, qb, sa, sb, ya, yb, ma, mb, ta, tb, ca, cb, send, recv, local
):
    me = Place()
    x, yh, z, c = me.x, me.yh, me.z, me.c
    sibling = me.device(c=1 - c)
    pair = me.device(yh=1 - yh)
    ring_x = (me.device(x=after(x)), me.device(x=before(x)))
    ring_z = (me.device(z=after(z)), me.device(z=before(z)))
    greet([sibling, pair, *ring_x, *ring_z])
    go = Copies(send, recv, local)

    def slab_a(i, r):
        return ga.at[i, :, :, r]

    def slab_b(i, r):
        return gb.at[:, :, i, r]

    ways = ((slab_a, x, ring_x, ka, ra), (slab_b, z, ring_z, kb, rb))
    cross, straight, kept = [], [], []
    for slab, i, ring, k, r in ways:
        cross.append((go.put(slab(across(i), 0), r.at[0], ring[0]), go.put(slab(across(i), 1), r.at[1], ring[1])))
    for slab, i, ring, k, r in ways:
        kept.append(
            [
                go.keep(slab(after(i), 0), k.at[0]),
                go.keep(slab(before(i), 1), k.at[1]),
                go.keep(slab(i, 0), k.at[2]),
                go.keep(slab(i, 1), k.at[3]),
            ]
        )
        straight.append((go.put(slab(after(i), 1), r.at[2], ring[0]), go.put(slab(before(i), 0), r.at[3], ring[1])))
    summed = []
    for (slab, i, ring, k, r), copies, own in zip(ways, cross, kept):
        both = []
        for side in range(2):
            own[side].wait()
            copies[side].wait_recv()

            def add(n, _, k=k, r=r, side=side):
                at = (side, n // k.shape[2], lax.rem(n, k.shape[2]))
                k[at] = (k[at].astype(F32) + r[at].astype(F32)).astype(BF16)
                return 0

            lax.fori_loop(0, k.shape[1] * k.shape[2], add, 0)
            both.append(go.put(k.at[side], r.at[4 + side], ring[side]))
        summed.append(both)
    for (slab, i, ring, k, r), one, two, own in zip(ways, straight, summed, kept):
        own[2].wait()
        own[3].wait()
        one[0].wait_recv()
        one[1].wait_recv()
        two[0].wait_recv()
        two[1].wait_recv()

        def close(n, _, k=k, r=r):
            at = (n // k.shape[2], lax.rem(n, k.shape[2]))
            for own, summed_side, straight_side in ((2, 4, 3), (3, 5, 2)):
                k[(own, *at)] = (
                    k[(own, *at)].astype(F32)
                    + r[(summed_side, *at)].astype(F32)
                    + r[(straight_side, *at)].astype(F32)
                ).astype(BF16)
            return 0

        lax.fori_loop(0, k.shape[1] * k.shape[2], close, 0)

    def part_a(r, j, y):
        return ka.at[r, y, j]

    def part_b(r, j, y):
        return kb.at[r, j, y]

    ways = ((part_a, z, ring_z, qa, sa), (part_b, x, ring_x, qb, sb))
    cross, straight, summed = [], [], []
    for part, j, ring, q, s in ways:
        cross.append(
            [
                [go.put(part(2 + side, across(j), y), q.at[side, y], ring[side]) for y in range(NYH)]
                for side in range(2)
            ]
        )
    for part, j, ring, q, s in ways:
        straight.append(
            [
                [go.put(part(3 - side, (after, before)[side](j), y), q.at[2 + side, y], ring[side]) for y in range(NYH)]
                for side in range(2)
            ]
        )
    for (part, j, ring, q, s), copies in zip(ways, cross):
        both = []
        for side in range(2):
            sent = []
            for y in range(NYH):
                copies[side][y].wait_recv()
                mine = part(2 + side, (after, before)[side](j), y)
                s[side, y] = (mine[...].astype(F32) + q[side, y].astype(F32)).astype(BF16)
                sent.append(go.put(s.at[side, y], q.at[4 + side, y], ring[side]))
            both.append(sent)
        summed.append(both)
    for (part, j, ring, q, s), one, two in zip(ways, straight, summed):
        for copies in (*one, *two):
            for copy in copies:
                copy.wait_recv()

    def total(part, j, q, side, y):
        return part(2 + side, j, y)[...].astype(F32) + q[4 + side, y].astype(F32) + q[3 - side, y].astype(F32)

    ways = ((part_a, z, qa, ya, ma, ta, ca, oa), (part_b, x, qb, yb, mb, tb, cb, ob))
    crossed = []
    for part, j, q, yy, m, tt, cc, o in ways:
        for side in range(2):
            yy[side] = total(part, j, q, side, 1 - yh).astype(BF16)
        crossed.append(go.put(yy, m, pair))
    last = []
    for (part, j, q, yy, m, tt, cc, o), copy in zip(ways, crossed):
        for side in range(2):
            tt[side] = total(part, j, q, side, yh)
        copy.wait_recv()
        tt[...] += m[...].astype(F32)
        last.append(go.put(tt.at[1 - c], cc, sibling))
        o[c] = tt[c]
    for (part, j, q, yy, m, tt, cc, o), copy in zip(ways, last):
        copy.wait_recv()
        o[1 - c] = cc[...]
    go.finish()


def scatter(grad_a, grad_b):
    rows = grad_a.shape[0] // (NX * NYH * NZ * NC)
    lead = (NX, NYH, NZ, NC, rows)
    widths = (grad_a.shape[1], grad_b.shape[1])

    def each(shape, dtype):
        return [pltpu.VMEM((*shape, rows, w), dtype) for w in widths]

    def held(count):
        dims = ((NYH, NZ), (NX, NYH))
        return [pltpu.VMEM((count, *d, rows, w), BF16) for d, w in zip(dims, widths)]

    return pl.pallas_call(
        scatter_kernel,
        name="scatter_weights",
        cost_estimate=cost(80),
        out_shape=tuple(jax.ShapeDtypeStruct((NC, rows, w), F32) for w in widths),
        in_specs=[ANY, ANY],
        out_specs=(VMEM, VMEM),
        scratch_shapes=[
            *held(4),
            *held(6),
            *each((6, NYH), BF16),
            *each((2, NYH), BF16),
            *each((2,), BF16),
            *each((2,), BF16),
            *each((2,), F32),
            *each((), F32),
            pltpu.SemaphoreType.DMA((40,)),
            pltpu.SemaphoreType.DMA((40,)),
            pltpu.SemaphoreType.DMA((8,)),
        ],
        compiler_params=pltpu.CompilerParams(
            collective_id=5, has_side_effects=True, vmem_limit_bytes=40 << 20
        ),
    )(grad_a.reshape(*lead, widths[0]), grad_b.reshape(*lead, widths[1]))


def unit_rows(values):
    return lax.rsqrt(jnp.mean(values * values, axis=-1, keepdims=True) + EPSILON)


def turn(values, cosine, signed):
    return values * cosine + pltpu.roll(values, values.shape[-1] // 2, 1) * signed


def attend_kernel(scale, raw, bias, cosine, signed, qgain, kgain, query, kv, weights, mixed):
    heads = query.shape[1] // cosine.shape[1]
    hd = cosine.shape[1]
    cos, sig = cosine[...], signed[...]
    key_raw = raw[:, heads * hd : (heads + 1) * hd]
    key = turn(key_raw * unit_rows(key_raw) * kgain[...], cos, sig).astype(BF16)
    value = raw[:, (heads + 1) * hd :].astype(BF16)
    kv[:, :hd] = key
    kv[:, hd:] = value
    for h in range(heads):
        at = slice(h * hd, (h + 1) * hd)
        head = raw[:, at]
        rows = turn(head * unit_rows(head) * qgain[...], cos, sig).astype(BF16)
        query[:, at] = rows
        scores = dot_nt(rows, key) * scale + bias[0]
        peak = jnp.max(scores, axis=-1, keepdims=True)
        weight = jnp.exp(scores - peak)
        weight = weight * (1.0 / jnp.sum(weight, axis=-1, keepdims=True))
        weights[0, h] = weight
        mixed[:, at] = dot_nn(weight.astype(BF16), value).astype(BF16)


def attend(raw, bias, cosine, signed, query_gain, key_gain, scale):
    groups, tokens = bias.shape[0], bias.shape[1]
    hd = cosine.shape[1]
    heads = raw.shape[1] // hd - 2
    rows = groups * tokens

    def block(cols):
        return pl.BlockSpec((tokens, cols), lambda g: (g, 0))

    gain = pl.BlockSpec((1, hd), lambda g: (0, 0))
    square = pl.BlockSpec((1, tokens, tokens), lambda g: (g, 0, 0))
    return pl.pallas_call(
        functools.partial(attend_kernel, scale),
        name="attend",
        cost_estimate=cost(8),
        grid=(groups,),
        out_shape=(
            jax.ShapeDtypeStruct((rows, heads * hd), BF16),
            jax.ShapeDtypeStruct((rows, 2 * hd), BF16),
            jax.ShapeDtypeStruct((groups, heads, tokens, tokens), F32),
            jax.ShapeDtypeStruct((rows, heads * hd), BF16),
        ),
        in_specs=[block((heads + 2) * hd), square, block(hd), block(hd), gain, gain],
        out_specs=(
            block(heads * hd),
            block(2 * hd),
            pl.BlockSpec((1, heads, tokens, tokens), lambda g: (g, 0, 0, 0)),
            block(heads * hd),
        ),
        compiler_params=pltpu.CompilerParams(vmem_limit_bytes=40 << 20),
    )(raw, bias, cosine, signed, query_gain.reshape(1, hd), key_gain.reshape(1, hd))


def norm_back(values, gain, upstream):
    r = unit_rows(values)
    scaled = upstream * gain
    inner = jnp.mean(scaled * values, axis=-1, keepdims=True)
    grad = r * scaled - values * (r * r * r * inner)
    return grad, jnp.sum(upstream * values * r, axis=0, keepdims=True)


def attend_back_kernel(
    scale, raw, cosine, signed, qgain, kgain, query, kv, weights, grad_mixed, grad_raw, grad_gains
):
    hd = cosine.shape[1]
    heads = query.shape[1] // hd
    cos, sig = cosine[...], -signed[...]
    key, value = kv[:, :hd], kv[:, hd:]
    grad_key = jnp.zeros(key.shape, F32)
    grad_value = jnp.zeros(key.shape, F32)
    query_gains = jnp.zeros((1, hd), F32)
    for h in range(heads):
        at = slice(h * hd, (h + 1) * hd)
        weight = weights[0, h]
        grad_head = grad_mixed[:, at]
        grad_value += dot_tn(weight.astype(BF16), grad_head)
        grad_soft = dot_nt(grad_head, value)
        delta = jnp.sum(weight * grad_soft, axis=-1, keepdims=True)
        grad_scores = (weight * (grad_soft - delta)).astype(BF16)
        grad_key += dot_tn(grad_scores, query[:, at])
        turned = turn(dot_nn(grad_scores, key) * scale, cos, sig)
        grad, gains = norm_back(raw[:, at], qgain[...], turned)
        grad_raw[:, at] = grad.astype(BF16)
        query_gains += gains
    at = slice(heads * hd, (heads + 1) * hd)
    grad, key_gains = norm_back(raw[:, at], kgain[...], turn(grad_key * scale, cos, sig))
    grad_raw[:, at] = grad.astype(BF16)
    grad_raw[:, (heads + 1) * hd :] = grad_value.astype(BF16)
    gains = jnp.concatenate([query_gains, key_gains], axis=0)

    @pl.when(pl.program_id(0) == 0)
    def _():
        grad_gains[...] = gains

    @pl.when(pl.program_id(0) > 0)
    def _():
        grad_gains[...] += gains


def attend_back(raw, cosine, signed, query_gain, key_gain, query, kv, weights, grad_mixed, scale):
    groups, heads, tokens, _ = weights.shape
    hd = cosine.shape[1]
    rows = groups * tokens

    def block(cols):
        return pl.BlockSpec((tokens, cols), lambda g: (g, 0))

    gain = pl.BlockSpec((1, hd), lambda g: (0, 0))
    return pl.pallas_call(
        functools.partial(attend_back_kernel, scale),
        name="attend_back",
        cost_estimate=cost(14),
        grid=(groups,),
        out_shape=(
            jax.ShapeDtypeStruct((rows, (heads + 2) * hd), BF16),
            jax.ShapeDtypeStruct((2, hd), F32),
        ),
        in_specs=[
            block((heads + 2) * hd),
            block(hd),
            block(hd),
            gain,
            gain,
            block(heads * hd),
            block(2 * hd),
            pl.BlockSpec((1, heads, tokens, tokens), lambda g: (g, 0, 0, 0)),
            block(heads * hd),
        ],
        out_specs=(block((heads + 2) * hd), pl.BlockSpec((2, hd), lambda g: (0, 0))),
        compiler_params=pltpu.CompilerParams(vmem_limit_bytes=40 << 20),
    )(raw, cosine, signed, query_gain.reshape(1, hd), key_gain.reshape(1, hd), query, kv, weights, grad_mixed)


def on_device(
    hidden_in,
    doc_ids,
    expert_ids,
    attn_gain,
    query_weight,
    key_weight,
    value_weight,
    output_weight,
    query_gain,
    key_gain,
    moe_gain,
    router_weight,
    gate_weight,
    up_weight,
    down_weight,
    cotangent,
):
    both = ("dp", "tensor")
    tok, width = hidden_in.shape
    hd = query_gain.shape[0]
    nkv = key_weight.shape[1] // hd
    nq = query_weight.shape[1] // hd
    group = nq // nkv
    experts = router_weight.shape[1]
    routes = expert_ids.shape[1]
    cap = tok * routes // experts
    slots = experts * cap
    scale = 1.0 / math.sqrt(hd)
    tokens = doc_ids.shape[1]
    me = lax.axis_index(both)

    lane = lax.broadcasted_iota(jnp.int32, (1, 1, experts), 2)
    chosen = jnp.sum((expert_ids[:, :, None] == lane).astype(F32), axis=1)
    below = (
        lax.broadcasted_iota(jnp.int32, (tok, tok), 1)
        < lax.broadcasted_iota(jnp.int32, (tok, tok), 0)
    ).astype(BF16)
    rank = dot_nn(below, chosen.astype(BF16))
    place = jnp.where(chosen > 0, rank, -1.0).T
    spread = (
        place[:, None, :] == lax.broadcasted_iota(jnp.int32, (1, cap, 1), 1).astype(F32)
    ).astype(BF16).reshape(slots, tok)

    hidden = hidden_in.astype(F32)
    normed_local = rms_scale(hidden, attn_gain).astype(BF16)

    def core_parts(shards):
        split = [s.reshape(s.shape[0], NC, s.shape[1] // NC) for s in shards]
        return jnp.concatenate(split, axis=2).transpose(1, 0, 2)

    in_weights, out_weights, normed, docs = gather(
        core_parts([query_weight, key_weight, value_weight]),
        core_parts([output_weight.T]),
        normed_local,
        jnp.broadcast_to(doc_ids, (8, tokens)).astype(F32),
    )

    spread_late, docs = lax.optimization_barrier((spread, docs))
    cot_out = dot_nn(spread_late, jnp.concatenate([cotangent, chosen.astype(BF16)], axis=1)).astype(BF16)
    cot_in = lax.all_to_all(
        cot_out.reshape(experts, cap, width + experts), both, split_axis=0, concat_axis=0, tiled=True
    ).reshape(slots, width + experts)

    position, allowed = jax.vmap(layout)(docs[:, 0])
    cosine, sine = rotary(position.reshape(-1), hd)
    cosine = jnp.concatenate([cosine, cosine], axis=1)
    signed = jnp.concatenate([-sine, sine], axis=1)
    bias = jnp.where(allowed, 0.0, MASKED).astype(F32)
    raw = dot_nn(normed, in_weights)
    heads = group * hd
    query, kv, attention, mixed = attend(raw, bias, cosine, signed, query_gain, key_gain, scale)
    attn_out = reduce(dot_nt(mixed, out_weights).astype(BF16), 2)

    residual = hidden + attn_out
    moe_input = rms_scale(residual, moe_gain).astype(BF16)
    moe_input, cot_in = lax.optimization_barrier((moe_input, cot_in))
    sent = dot_nn(spread, moe_input).astype(BF16)
    rows = lax.all_to_all(
        sent.reshape(experts, cap, width), both, split_axis=0, concat_axis=0, tiled=True
    ).reshape(slots, width)
    logits = dot_nn(moe_input, router_weight)
    masked = jnp.where(chosen > 0, logits, MASKED)
    probs = jnp.exp(masked - jnp.max(masked, axis=-1, keepdims=True))
    probs = probs / jnp.sum(probs, axis=-1, keepdims=True)

    gate_mat, up_mat, down_mat = gate_weight[0], up_weight[0], down_weight[0]
    cot_rows = cot_in[:, :width]
    inner_up = dot_nt(cot_rows, down_mat)
    row_logits = jnp.where(cot_in[:, width:] > 0, dot_nn(rows, router_weight), MASKED)
    row_probs = jnp.exp(row_logits - jnp.max(row_logits, axis=-1, keepdims=True))
    mine = lax.broadcasted_iota(jnp.int32, (1, experts), 1) == me
    prob = jnp.sum(jnp.where(mine, row_probs, 0.0), axis=-1, keepdims=True) / jnp.sum(
        row_probs, axis=-1, keepdims=True
    )
    gate_pre = dot_nn(rows, gate_mat)
    up_pre = dot_nn(rows, up_mat)
    sigmoid = jax.nn.sigmoid(gate_pre)
    silu = gate_pre * sigmoid
    inner = silu * up_pre
    gate_up = jnp.sum(inner * inner_up, axis=-1, keepdims=True)
    inner_low = (prob * inner).astype(BF16)
    grad_inner = prob * inner_up
    grad_gate = (grad_inner * up_pre * sigmoid * (1.0 + gate_pre * (1.0 - sigmoid))).astype(BF16)
    grad_up = (grad_inner * silu).astype(BF16)
    grad_rows = (dot_nt(grad_gate, gate_mat) + dot_nt(grad_up, up_mat)).astype(BF16)
    gate_up_high = gate_up.astype(BF16)
    gate_up_rest = (gate_up - gate_up_high.astype(F32)).astype(BF16)
    none = jnp.zeros((), BF16)
    home_out = jnp.concatenate(
        [grad_rows, jnp.where(mine, gate_up_high, none), jnp.where(mine, gate_up_rest, none)], axis=1
    )
    home = lax.all_to_all(
        home_out.reshape(experts, cap, width + 2 * experts), both, split_axis=0, concat_axis=0, tiled=True
    ).reshape(slots, width + 2 * experts)
    expert_out = dot_nn(inner_low, down_mat).astype(BF16)
    down_grad = dot_tn(inner_low, cot_rows)
    gate_grad = dot_tn(rows, grad_gate)
    up_grad = dot_tn(rows, grad_up)
    home, down_grad, gate_grad, up_grad = lax.optimization_barrier(
        (home, down_grad, gate_grad, up_grad)
    )

    upstream = cotangent.astype(F32)
    summed = dot_tn(spread, home)
    gate_upstream = summed[:, width : width + experts] + summed[:, width + experts :]
    grad_chosen = probs * (gate_upstream - jnp.sum(probs * gate_upstream, axis=-1, keepdims=True))
    grad_logits = grad_chosen.astype(BF16)
    grad_moe_input = summed[:, :width] + dot_nt(grad_logits, router_weight)
    router_part = dot_tn(moe_input, grad_logits)
    grad_norm, moegain_rows = rms_back(residual, moe_gain, grad_moe_input)
    moegain_part = jnp.sum(moegain_rows, axis=0)
    grad_residual = upstream + grad_norm
    grad_attn = share(grad_residual.astype(BF16), 3)
    pieces = router_part.reshape(experts, width // experts, experts)
    piece = jnp.sum(lax.all_to_all(pieces, both, 0, 0, tiled=True), axis=0)
    expert_out, grad_attn, piece = lax.optimization_barrier((expert_out, grad_attn, piece))
    returned = lax.all_to_all(
        expert_out.reshape(experts, cap, width), both, split_axis=0, concat_axis=0, tiled=True
    ).reshape(slots, width)

    grad_mixed = dot_nn(grad_attn, out_weights).astype(BF16)
    grad_raw, head_gains = attend_back(
        raw, cosine, signed, query_gain, key_gain, query, kv, attention, grad_mixed, scale
    )
    grad_normed = reduce(dot_nt(grad_raw, in_weights).astype(BF16), 4)
    in_grad, out_grad = scatter(
        dot_tn(normed, grad_raw).astype(BF16), dot_tn(grad_attn, mixed).astype(BF16)
    )
    grad_hidden, attngain_rows = rms_back(hidden, attn_gain, grad_normed)
    input_grad = grad_residual + grad_hidden

    gains = jnp.concatenate([jnp.sum(attngain_rows, axis=0), moegain_part, head_gains.reshape(-1)])
    term = jnp.concatenate([piece, gains.reshape(-1, experts)], axis=0)
    term, returned = lax.optimization_barrier((term, returned))
    layer_out = (residual + dot_tn(spread, returned)).astype(BF16)
    terms = lax.all_to_all(
        jnp.broadcast_to(term[None], (experts, *term.shape)), both, 0, 0, tiled=True
    )
    router_grad = terms[:, : piece.shape[0]].reshape(width, experts)
    gains = jnp.sum(terms[:, piece.shape[0] :], axis=0).reshape(-1)
    attngain_grad = gains[:width]
    moegain_grad = gains[width : 2 * width]
    qgain_grad = gains[2 * width : 2 * width + hd]
    kgain_grad = gains[2 * width + hd :]

    def join(parts):
        return jnp.concatenate([parts[i] for i in range(NC)], axis=1)

    return (
        layer_out,
        input_grad,
        attngain_grad,
        join(in_grad[:, :, :heads]),
        join(in_grad[:, :, heads : heads + hd]),
        join(in_grad[:, :, heads + hd :]),
        join(out_grad).T,
        qgain_grad,
        kgain_grad,
        moegain_grad,
        router_grad,
        gate_grad[None],
        up_grad[None],
        down_grad[None],
    )


def solution(mesh):
    both = ("dp", "tensor")
    in_specs = (
        P(both, None),
        P("dp", None),
        P(both, None),
        P(),
        P("dp", "tensor"),
        P("dp", "tensor"),
        P("dp", "tensor"),
        P("tensor", "dp"),
        P(),
        P(),
        P(),
        P(),
        P(both, None, None),
        P(both, None, None),
        P(both, None, None),
        P(both, None),
    )
    out_specs = (
        P(both, None),
        P(both, None),
        P(),
        P("dp", "tensor"),
        P("dp", "tensor"),
        P("dp", "tensor"),
        P("tensor", "dp"),
        P(),
        P(),
        P(),
        P(),
        P(both, None, None),
        P(both, None, None),
        P(both, None, None),
    )
    return jax.shard_map(
        on_device, mesh=mesh, in_specs=in_specs, out_specs=out_specs, check_vma=False
    )
```

```python
import functools
import math

import jax
import jax.numpy as jnp
from jax import lax
from jax.experimental import pallas as pl
from jax.experimental.pallas import tpu as pltpu
from jax.sharding import PartitionSpec as P

BLOCK = 128
EPSILON = 1e-06
ROPE_BASE = 1000000.0
MASKED = -1e30
F32 = jnp.float32
BF16 = jnp.bfloat16


def dot_nt(a, b):
    return lax.dot_general(a, b, (((1,), (1,)), ((), ())), preferred_element_type=F32)


def dot_tn(a, b):
    return lax.dot_general(a, b, (((0,), (0,)), ((), ())), preferred_element_type=F32)


def dot_nn(a, b):
    return lax.dot_general(a, b, (((1,), (0,)), ((), ())), preferred_element_type=F32)


def rms_recip(values):
    return lax.rsqrt(jnp.mean(values * values, axis=-1, keepdims=True) + EPSILON)


def rms_scale(values, gain):
    return values * rms_recip(values) * gain


def rms_back(values, gain, upstream):
    r = rms_recip(values)
    scaled = upstream * gain
    inner = jnp.mean(scaled * values, axis=-1, keepdims=True)
    grad_values = r * scaled - values * (r * r * r) * inner
    return grad_values, upstream * values * r


def rotate(values, cosine, sine):
    half = values.shape[-1] // 2
    a = values[..., :half]
    b = values[..., half:]
    return jnp.concatenate([a * cosine - b * sine, b * cosine + a * sine], axis=-1)


def layout(doc_row):
    length = doc_row.shape[0]
    indices = jnp.arange(length, dtype=jnp.int32)
    same_doc = doc_row[:, None] == doc_row[None, :]
    earlier = indices[None, :] < indices[:, None]
    position = jnp.sum(jnp.where(same_doc & earlier, 1, 0), axis=1).astype(jnp.int32)
    blocks = position // BLOCK
    allowed = same_doc & (blocks[None, :] <= blocks[:, None])
    return position, allowed


def rotary(position, head_size):
    half = head_size // 2
    frequency = jnp.exp(-jnp.log(ROPE_BASE) * jnp.arange(half, dtype=F32) * 2.0 / head_size)
    angles = position.astype(F32)[:, None] * frequency[None, :]
    return jnp.cos(angles), jnp.sin(angles)


MESH = pl.DeviceIdType.MESH
ANY = pl.BlockSpec(memory_space=pl.ANY)
VMEM = pl.BlockSpec(memory_space=pltpu.VMEM)
NX, NYH, NZ, NC = 4, 2, 4, 2
RING = 4


def cost(microseconds):
    return pl.CostEstimate(flops=0, transcendentals=0, bytes_accessed=int(microseconds * 3.6e6))


class Place:
    def __init__(self):
        dp = lax.axis_index("dp")
        self.t = lax.axis_index("tensor")
        self.c = lax.rem(dp, NC)
        self.z = lax.rem(dp // NC, NZ)
        self.yh = lax.rem(dp // (NC * NZ), NYH)
        self.x = dp // (NC * NZ * NYH)

    def device(self, x=None, yh=None, z=None, c=None, t=None):
        pick = lambda given, own: own if given is None else given
        x, yh, z, c = pick(x, self.x), pick(yh, self.yh), pick(z, self.z), pick(c, self.c)
        return (((x * NYH + yh) * NZ + z) * NC + c, pick(t, self.t))


def after(i):
    return lax.rem(i + 1, RING)


def before(i):
    return lax.rem(i + RING - 1, RING)


def across(i):
    return lax.rem(i + 2, RING)


def greet(peers):
    barrier = pltpu.get_barrier_semaphore()
    for peer in peers:
        pl.semaphore_signal(barrier, inc=1, device_id=peer, device_id_type=MESH)
    pl.semaphore_wait(barrier, len(peers))


class Copies:
    def __init__(self, send, recv, local):
        self.send, self.recv, self.local = send, recv, local
        self.n = self.m = 0
        self.sent = []

    def put(self, src, dst, peer):
        copy = pltpu.make_async_remote_copy(
            src_ref=src,
            dst_ref=dst,
            send_sem=self.send.at[self.n],
            recv_sem=self.recv.at[self.n],
            device_id=peer,
            device_id_type=MESH,
        )
        self.n += 1
        copy.start()
        self.sent.append(copy)
        return copy

    def keep(self, src, dst):
        copy = pltpu.make_async_copy(src, dst, self.local.at[self.m])
        self.m += 1
        copy.start()
        return copy

    def finish(self):
        for copy in self.sent:
            copy.wait_send()


def gather_kernel(q, k, v, o, tok, doc, wa, wb, toks, docs, send, recv, local):
    me = Place()
    x, yh, z, c, t = me.x, me.yh, me.z, me.c, me.t
    sibling = me.device(c=1 - c)
    pair = me.device(yh=1 - yh)
    partner = me.device(t=1 - t)
    ring_x = (me.device(x=after(x)), me.device(x=before(x)))
    ring_z = (me.device(z=after(z)), me.device(z=before(z)))
    greet([sibling, pair, partner, *ring_x, *ring_z])
    go = Copies(send, recv, local)

    shards, start = [], 0
    for ref, w in ((q, wa), (k, wa), (v, wa), (o, wb)):
        cols = ref.shape[1] // NC
        to = w.at[x, yh, z, c, :, pl.ds(0 if w is wb else start, cols)]
        shards.append((ref, cols, to))
        start += cols

    def part(ref, cols, core):
        return ref.at[:, pl.ds(pl.multiple_of(core * cols, cols), cols)]

    cores = [go.put(part(ref, cols, 1 - c), to, sibling) for ref, cols, to in shards]
    kept = [go.keep(part(ref, cols, c), to) for ref, cols, to in shards]
    for copy in kept:
        copy.wait()
    for copy in cores:
        copy.wait_recv()
    pairs = [go.put(w.at[x, yh, z], w.at[x, yh, z], pair) for w in (wa, wb)]

    ways = (
        (wa, x, z, ring_x, ring_z, lambda w, i, j, y: w.at[i, y, j], lambda w, j, y: w.at[:, y, j]),
        (wb, z, x, ring_z, ring_x, lambda w, i, j, y: w.at[j, y, i], lambda w, j, y: w.at[j, y]),
    )

    def first(y):
        out = []
        for w, i, j, one, two, unit, slab in ways:
            own = unit(w, i, j, y)
            out.append((go.put(own, own, one[0]), go.put(own, own, one[1])))
        return out

    def second(y, firsts):
        out = []
        for (w, i, j, one, two, unit, slab), (up, down) in zip(ways, firsts):
            up.wait_recv()
            low = unit(w, before(i), j, y).at[0]
            a = go.put(low, low, one[0])
            down.wait_recv()
            high = unit(w, after(i), j, y).at[1]
            out.append((a, go.put(high, high, one[1])))
        return out

    def third(y, seconds):
        out = []
        for (w, i, j, one, two, unit, slab), (up, down) in zip(ways, seconds):
            up.wait_recv()
            down.wait_recv()
            own = slab(w, j, y)
            out.append((go.put(own, own, two[0]), go.put(own, own, two[1])))
        return out

    def fourth(y, thirds):
        out = []
        for (w, i, j, one, two, unit, slab), (up, down) in zip(ways, thirds):
            up.wait_recv()
            low = slab(w, before(j), y).at[:, 0]
            a = go.put(low, low, two[0])
            down.wait_recv()
            high = slab(w, after(j), y).at[:, 1]
            out.append((a, go.put(high, high, two[1])))
        return out

    near = first(yh)
    to_partner = go.put(tok, toks.at[c, t], partner)
    rest = [go.keep(tok, toks.at[c, t]), go.keep(doc, docs.at[c])]
    tail = [go.put(tok, toks.at[c, t], sibling), go.put(doc, docs.at[c], sibling)]
    near = second(yh, near)
    near = third(yh, near)
    for copy in pairs:
        copy.wait_recv()
    far = first(1 - yh)
    far = second(1 - yh, far)
    far = third(1 - yh, far)
    near = fourth(yh, near)
    to_partner.wait_recv()
    other = toks.at[c, 1 - t]
    tail.append(go.put(other, other, sibling))
    far = fourth(1 - yh, far)
    for up, down in near + far:
        up.wait_recv()
        down.wait_recv()
    for copy in tail:
        copy.wait_recv()
    for copy in rest:
        copy.wait()
    go.finish()


def gather(query, key, value, out, tokens, docs):
    rows = query.shape[0]
    width_a = (query.shape[1] + key.shape[1] + value.shape[1]) // NC
    width_b = out.shape[1] // NC
    lead = (NX, NYH, NZ, NC, rows)
    wa, wb, toks, docs = pl.pallas_call(
        gather_kernel,
        name="gather_weights",
        cost_estimate=cost(60),
        out_shape=(
            jax.ShapeDtypeStruct((*lead, width_a), BF16),
            jax.ShapeDtypeStruct((*lead, width_b), BF16),
            jax.ShapeDtypeStruct((NC, 2, *tokens.shape), BF16),
            jax.ShapeDtypeStruct((NC, *docs.shape), docs.dtype),
        ),
        in_specs=[ANY] * 6,
        out_specs=(ANY,) * 4,
        scratch_shapes=[
            pltpu.SemaphoreType.DMA((42,)),
            pltpu.SemaphoreType.DMA((42,)),
            pltpu.SemaphoreType.DMA((6,)),
        ],
        compiler_params=pltpu.CompilerParams(collective_id=1, has_side_effects=True),
    )(query, key, value, out, tokens, docs)
    depth = NX * NYH * NZ * NC * rows
    return (
        wa.reshape(depth, width_a),
        wb.reshape(depth, width_b),
        toks.reshape(NC * 2 * tokens.shape[0], tokens.shape[1]),
        docs,
    )


def share_kernel(tok, toks, send, recv, local):
    me = Place()
    c, t = me.c, me.t
    sibling, partner = me.device(c=1 - c), me.device(t=1 - t)
    greet([sibling, partner])
    go = Copies(send, recv, local)
    half = tok.shape[0] // 2
    parts = [pl.ds(i * half, half) for i in range(2)]
    over = [go.put(tok.at[p], toks.at[c, t, p], partner) for p in parts]
    near = [go.put(tok, toks.at[c, t], sibling)]
    kept = go.keep(tok, toks.at[c, t])
    for copy, p in zip(over, parts):
        copy.wait_recv()
        other = toks.at[c, 1 - t, p]
        near.append(go.put(other, other, sibling))
    for copy in near:
        copy.wait_recv()
    kept.wait()
    go.finish()


def share(tokens, ident):
    toks = pl.pallas_call(
        share_kernel,
        name=f"share_rows_{ident}",
        cost_estimate=cost(13),
        out_shape=jax.ShapeDtypeStruct((NC, 2, *tokens.shape), tokens.dtype),
        in_specs=[ANY],
        out_specs=ANY,
        scratch_shapes=[
            pltpu.SemaphoreType.DMA((5,)),
            pltpu.SemaphoreType.DMA((5,)),
            pltpu.SemaphoreType.DMA((1,)),
        ],
        compiler_params=pltpu.CompilerParams(collective_id=ident, has_side_effects=True),
    )(tokens)
    return toks.reshape(NC * 2 * tokens.shape[0], tokens.shape[1])


def reduce_kernel(part, out, near, own, sums, far, send, recv, local):
    me = Place()
    c, t = me.c, me.t
    sibling, partner = me.device(c=1 - c), me.device(t=1 - t)
    greet([sibling, partner])
    go = Copies(send, recv, local)
    half = out.shape[0] // 2
    parts = [pl.ds(i * half, half) for i in range(2)]
    away = [go.put(part.at[1 - c, 1 - t, p], near.at[0, p], sibling) for p in parts]
    home = go.put(part.at[1 - c, t], near.at[1], sibling)
    kept = [go.keep(part.at[c, 1 - t], own.at[0]), go.keep(part.at[c, t], own.at[1])]
    kept[0].wait()
    over = []
    for copy, p in zip(away, parts):
        copy.wait_recv()
        sums[p] = (own[0, p].astype(F32) + near[0, p].astype(F32)).astype(BF16)
        over.append(go.put(sums.at[p], far.at[p], partner))
    kept[1].wait()
    home.wait_recv()
    out[...] = own[1].astype(F32) + near[1].astype(F32)
    for copy, p in zip(over, parts):
        copy.wait_recv()
        out[p] += far[p].astype(F32)
    go.finish()


def reduce(part, ident):
    rows, width = part.shape[0] // (NC * 2), part.shape[1]
    return pl.pallas_call(
        reduce_kernel,
        name=f"reduce_rows_{ident}",
        cost_estimate=cost(15),
        out_shape=jax.ShapeDtypeStruct((rows, width), F32),
        in_specs=[ANY],
        out_specs=VMEM,
        scratch_shapes=[
            pltpu.VMEM((2, rows, width), BF16),
            pltpu.VMEM((2, rows, width), BF16),
            pltpu.VMEM((rows, width), BF16),
            pltpu.VMEM((rows, width), BF16),
            pltpu.SemaphoreType.DMA((5,)),
            pltpu.SemaphoreType.DMA((5,)),
            pltpu.SemaphoreType.DMA((2,)),
        ],
        compiler_params=pltpu.CompilerParams(
            collective_id=ident, has_side_effects=True, vmem_limit_bytes=24 << 20
        ),
    )(part.reshape(NC, 2, rows, width))


def scatter_kernel(
    ga, gb, gains, piece, oq, ok, ov, oo, og, op, ka, kb, ra, rb, qa, qb, sa, sb, ya, yb, ma, mb, ta, tb, ca, cb,
    ring_gains, sum_gains, pair_gains, send, recv, local
):
    me = Place()
    x, yh, z, c = me.x, me.yh, me.z, me.c
    sibling = me.device(c=1 - c)
    pair = me.device(yh=1 - yh)
    partner = me.device(t=1 - me.t)
    ring_x = (me.device(x=after(x)), me.device(x=before(x)))
    ring_z = (me.device(z=after(z)), me.device(z=before(z)))
    round_x = (*ring_x, me.device(x=across(x)))
    round_z = (*ring_z, me.device(z=across(z)))
    greet([sibling, pair, partner, *round_x, *round_z])
    go = Copies(send, recv, local)
    chunks = (1 - yh, yh)

    def around(n, term, own, peers):
        ring_gains[n, own] = term
        return [go.put(ring_gains.at[n, own], ring_gains.at[n, own], peer) for peer in peers]

    def ring_sum(n, copies):
        for copy in copies:
            copy.wait_recv()
        return (ring_gains[n, 0] + ring_gains[n, 1]) + (ring_gains[n, 2] + ring_gains[n, 3])

    def swap(n, term, peer):
        sum_gains[n] = term
        return go.put(sum_gains.at[n], pair_gains.at[n], peer)

    def swapped(n, copy):
        copy.wait_recv()
        return sum_gains[n] + pair_gains[n]


    ways = (
        (lambda i, y, h: ga.at[i, y, :, h], x, z, ring_x, ring_z, ka, ra, qa, sa),
        (lambda i, y, h: gb.at[:, y, i, h], z, x, ring_z, ring_x, kb, rb, qb, sb),
    )

    def cross(n):
        out = []
        for slab, i, j, one, two, k, r, q, s in ways:
            far = across(i)
            out.append(
                [go.put(slab(far, chunks[n], h), r.at[n, h], one[h]) for h in range(2)]
            )
        return out

    def straight(n):
        out = []
        for slab, i, j, one, two, k, r, q, s in ways:
            near = (after(i), before(i))
            out.append(
                [go.put(slab(near[h], chunks[n], 1 - h), r.at[n, 2 + h], one[h]) for h in range(2)]
            )
        return out

    def hold(n):
        out = []
        for slab, i, j, one, two, k, r, q, s in ways:
            parts = ((after(i), 0), (before(i), 1), (i, 0), (i, 1))
            out.append(
                [go.keep(slab(p, chunks[n], h), k.at[n, m]) for m, (p, h) in enumerate(parts)]
            )
        return out

    def add(n, crossed, held):
        out = []
        for (slab, i, j, one, two, k, r, q, s), copies, own in zip(ways, crossed, held):
            both = []
            for h in range(2):
                own[h].wait()
                copies[h].wait_recv()

                def step(m, _, k=k, r=r, h=h):
                    k[n, h, m] = (k[n, h, m].astype(F32) + r[n, h, m].astype(F32)).astype(BF16)
                    return 0

                lax.fori_loop(0, k.shape[2], step, 0)
                both.append(go.put(k.at[n, h], r.at[n, 4 + h], one[h]))
            out.append(both)
        return out

    def close(n, straights, summed, held):
        out = []
        for (slab, i, j, one, two, k, r, q, s), a, b, own in zip(ways, straights, summed, held):
            for h in range(2):
                own[2 + h].wait()
                a[h].wait_recv()
                b[h].wait_recv()

            def step(m, _, k=k, r=r):
                for h in range(2):
                    k[n, 2 + h, m] = (
                        k[n, 2 + h, m].astype(F32)
                        + r[n, 4 + h, m].astype(F32)
                        + r[n, 3 - h, m].astype(F32)
                    ).astype(BF16)
                return 0

            lax.fori_loop(0, k.shape[2], step, 0)
            near = (after(j), before(j))
            over = [go.put(k.at[n, 2 + h, across(j)], q.at[n, h], two[h]) for h in range(2)]
            direct = [go.put(k.at[n, 3 - h, near[h]], q.at[n, 2 + h], two[h]) for h in range(2)]
            out.append((over, direct))
        return out

    def add_second(n, closed):
        out = []
        for (slab, i, j, one, two, k, r, q, s), (over, direct) in zip(ways, closed):
            near = (after(j), before(j))
            both = []
            for h in range(2):
                over[h].wait_recv()
                s[n, h] = (k[n, 2 + h, near[h]].astype(F32) + q[n, h].astype(F32)).astype(BF16)
                both.append(go.put(s.at[n, h], q.at[n, 4 + h], two[h]))
            out.append(both + direct)
        return out

    def total(n, added, w):
        slab, i, j, one, two, k, r, q, s = ways[w]
        for copy in added[w]:
            copy.wait_recv()
        return [
            k[n, 2 + h, j].astype(F32) + q[n, 4 + h].astype(F32) + q[n, 3 - h].astype(F32)
            for h in range(2)
        ]

    t = me.t

    def spread(ref, peers):
        return [go.put(ref, ref, peer) for peer in peers]

    def arrived(copies):
        for copy in copies:
            copy.wait_recv()

    terms = around(0, gains[...], x, round_x)
    mine = op.at[x, yh, z, c, t]
    held_piece = go.keep(piece, mine)
    pieces = [go.put(piece, mine, sibling)]
    cross_0, straight_0 = cross(0), straight(0)
    held_0, held_1 = hold(0), hold(1)
    terms = around(1, ring_sum(0, terms), z, round_z)
    arrived(pieces)
    held_piece.wait()
    pieces = spread(op.at[x, yh, z, :, t], [partner])
    cross_1 = cross(1)
    sums_0 = add(0, cross_0, held_0)
    straight_1 = straight(1)
    arrived(pieces)
    pieces = spread(op.at[x, yh, z], [pair])
    sums_1 = add(1, cross_1, held_1)
    arrived(pieces)
    pieces = spread(op.at[x, :, z], round_x)
    terms = swap(0, ring_sum(1, terms), pair)
    closed_0 = close(0, straight_0, sums_0, held_0)
    terms = swap(1, swapped(0, terms), partner)
    arrived(pieces)
    pieces = spread(op.at[:, :, z], round_z)
    added_0 = add_second(0, closed_0)
    ends = ((ya, ma, ta, ca), (yb, mb, tb, cb))
    pairs = []
    for w, (yy, m, tt, cc) in enumerate(ends):
        for h, part in enumerate(total(0, added_0, w)):
            yy[h] = part.astype(BF16)
        pairs.append(go.put(yy, m, pair))
    terms = swap(2, swapped(1, terms), sibling)
    closed_1 = close(1, straight_1, sums_1, held_1)
    added_1 = add_second(1, closed_1)
    last = []
    for w, (yy, m, tt, cc) in enumerate(ends):
        parts = total(1, added_1, w)
        pairs[w].wait_recv()
        for h, part in enumerate(parts):
            tt[h] = part + m[h].astype(F32)
        last.append(go.put(tt.at[1 - c], cc, sibling))
    og[...] = swapped(2, terms)
    arrived(pieces)

    def write(core, a, b):
        start = 0
        for out, held in ((oq, a), (ok, a), (ov, a), (oo, b)):
            cols = out.shape[1] // NC
            at = 0 if held is b else start
            out[:, pl.ds(pl.multiple_of(core * cols, cols), cols)] = held[:, at : at + cols]
            start += cols

    write(c, ta[c], tb[c])
    for copy in last:
        copy.wait_recv()
    write(1 - c, ca[...], cb[...])
    go.finish()


def scatter(grad_a, grad_b, gains, piece, columns):
    rows = grad_a.shape[0] // (NX * NYH * NZ * NC)
    lead = (NX, NYH, NZ, NC, rows)
    widths = (grad_a.shape[1], grad_b.shape[1])

    def each(shape, dtype):
        return [pltpu.VMEM((*shape, rows, w), dtype) for w in widths]

    return pl.pallas_call(
        scatter_kernel,
        name="scatter_weights",
        cost_estimate=cost(80),
        out_shape=(
            *(jax.ShapeDtypeStruct((rows, w), F32) for w in columns),
            jax.ShapeDtypeStruct(gains.shape, F32),
            jax.ShapeDtypeStruct((NX, NYH, NZ, NC, 2, *piece.shape), piece.dtype),
        ),
        in_specs=[ANY, ANY, VMEM, ANY],
        out_specs=(*(VMEM,) * 5, ANY),
        scratch_shapes=[
            *each((2, 4, RING), BF16),
            *each((2, 6, RING), BF16),
            *each((2, 6), BF16),
            *each((2, 2), BF16),
            *each((2,), BF16),
            *each((2,), BF16),
            *each((2,), F32),
            *each((), F32),
            pltpu.VMEM((2, RING, *gains.shape), F32),
            pltpu.VMEM((3, *gains.shape), F32),
            pltpu.VMEM((3, *gains.shape), F32),
            pltpu.SemaphoreType.DMA((70,)),
            pltpu.SemaphoreType.DMA((70,)),
            pltpu.SemaphoreType.DMA((17,)),
        ],
        compiler_params=pltpu.CompilerParams(
            collective_id=5, has_side_effects=True, vmem_limit_bytes=40 << 20
        ),
    )(grad_a.reshape(*lead, widths[0]), grad_b.reshape(*lead, widths[1]), gains, piece)


def unit_rows(values):
    return lax.rsqrt(jnp.mean(values * values, axis=-1, keepdims=True) + EPSILON)


def turn(values, cosine, signed):
    return values * cosine + pltpu.roll(values, values.shape[-1] // 2, 1) * signed


def attend_kernel(scale, raw, bias, cosine, signed, qgain, kgain, query, kv, weights, mixed):
    heads = query.shape[1] // cosine.shape[1]
    hd = cosine.shape[1]
    cos, sig = cosine[...], signed[...]
    key_raw = raw[:, heads * hd : (heads + 1) * hd]
    key = turn(key_raw * unit_rows(key_raw) * kgain[...], cos, sig).astype(BF16)
    value = raw[:, (heads + 1) * hd :].astype(BF16)
    kv[:, :hd] = key
    kv[:, hd:] = value
    for h in range(heads):
        at = slice(h * hd, (h + 1) * hd)
        head = raw[:, at]
        rows = turn(head * unit_rows(head) * qgain[...], cos, sig).astype(BF16)
        query[:, at] = rows
        scores = dot_nt(rows, key) * scale + bias[0]
        peak = jnp.max(scores, axis=-1, keepdims=True)
        weight = jnp.exp(scores - peak)
        weight = weight * (1.0 / jnp.sum(weight, axis=-1, keepdims=True))
        weights[0, h] = weight
        mixed[:, at] = dot_nn(weight.astype(BF16), value).astype(BF16)


def attend(raw, bias, cosine, signed, query_gain, key_gain, scale):
    groups, tokens = bias.shape[0], bias.shape[1]
    hd = cosine.shape[1]
    heads = raw.shape[1] // hd - 2
    rows = groups * tokens

    def block(cols):
        return pl.BlockSpec((tokens, cols), lambda g: (g, 0))

    gain = pl.BlockSpec((1, hd), lambda g: (0, 0))
    square = pl.BlockSpec((1, tokens, tokens), lambda g: (g, 0, 0))
    return pl.pallas_call(
        functools.partial(attend_kernel, scale),
        name="attend",
        cost_estimate=cost(8),
        grid=(groups,),
        out_shape=(
            jax.ShapeDtypeStruct((rows, heads * hd), BF16),
            jax.ShapeDtypeStruct((rows, 2 * hd), BF16),
            jax.ShapeDtypeStruct((groups, heads, tokens, tokens), F32),
            jax.ShapeDtypeStruct((rows, heads * hd), BF16),
        ),
        in_specs=[block((heads + 2) * hd), square, block(hd), block(hd), gain, gain],
        out_specs=(
            block(heads * hd),
            block(2 * hd),
            pl.BlockSpec((1, heads, tokens, tokens), lambda g: (g, 0, 0, 0)),
            block(heads * hd),
        ),
        compiler_params=pltpu.CompilerParams(vmem_limit_bytes=40 << 20),
    )(raw, bias, cosine, signed, query_gain.reshape(1, hd), key_gain.reshape(1, hd))


def norm_back(values, gain, upstream):
    r = unit_rows(values)
    scaled = upstream * gain
    inner = jnp.mean(scaled * values, axis=-1, keepdims=True)
    grad = r * scaled - values * (r * r * r * inner)
    return grad, jnp.sum(upstream * values * r, axis=0, keepdims=True)


def attend_back_kernel(
    scale, raw, cosine, signed, qgain, kgain, query, kv, weights, grad_mixed, grad_raw, grad_gains
):
    hd = cosine.shape[1]
    heads = query.shape[1] // hd
    cos, sig = cosine[...], -signed[...]
    key, value = kv[:, :hd], kv[:, hd:]
    grad_key = jnp.zeros(key.shape, F32)
    grad_value = jnp.zeros(key.shape, F32)
    query_gains = jnp.zeros((1, hd), F32)
    for h in range(heads):
        at = slice(h * hd, (h + 1) * hd)
        weight = weights[0, h]
        grad_head = grad_mixed[:, at]
        grad_value += dot_tn(weight.astype(BF16), grad_head)
        grad_soft = dot_nt(grad_head, value)
        delta = jnp.sum(weight * grad_soft, axis=-1, keepdims=True)
        grad_scores = (weight * (grad_soft - delta)).astype(BF16)
        grad_key += dot_tn(grad_scores, query[:, at])
        turned = turn(dot_nn(grad_scores, key) * scale, cos, sig)
        grad, gains = norm_back(raw[:, at], qgain[...], turned)
        grad_raw[:, at] = grad.astype(BF16)
        query_gains += gains
    at = slice(heads * hd, (heads + 1) * hd)
    grad, key_gains = norm_back(raw[:, at], kgain[...], turn(grad_key * scale, cos, sig))
    grad_raw[:, at] = grad.astype(BF16)
    grad_raw[:, (heads + 1) * hd :] = grad_value.astype(BF16)
    gains = jnp.concatenate([query_gains, key_gains], axis=0)

    @pl.when(pl.program_id(0) == 0)
    def _():
        grad_gains[...] = gains

    @pl.when(pl.program_id(0) > 0)
    def _():
        grad_gains[...] += gains


def attend_back(raw, cosine, signed, query_gain, key_gain, query, kv, weights, grad_mixed, scale):
    groups, heads, tokens, _ = weights.shape
    hd = cosine.shape[1]
    rows = groups * tokens

    def block(cols):
        return pl.BlockSpec((tokens, cols), lambda g: (g, 0))

    gain = pl.BlockSpec((1, hd), lambda g: (0, 0))
    return pl.pallas_call(
        functools.partial(attend_back_kernel, scale),
        name="attend_back",
        cost_estimate=cost(14),
        grid=(groups,),
        out_shape=(
            jax.ShapeDtypeStruct((rows, (heads + 2) * hd), BF16),
            jax.ShapeDtypeStruct((2, hd), F32),
        ),
        in_specs=[
            block((heads + 2) * hd),
            block(hd),
            block(hd),
            gain,
            gain,
            block(heads * hd),
            block(2 * hd),
            pl.BlockSpec((1, heads, tokens, tokens), lambda g: (g, 0, 0, 0)),
            block(heads * hd),
        ],
        out_specs=(block((heads + 2) * hd), pl.BlockSpec((2, hd), lambda g: (0, 0))),
        compiler_params=pltpu.CompilerParams(vmem_limit_bytes=40 << 20),
    )(raw, cosine, signed, query_gain.reshape(1, hd), key_gain.reshape(1, hd), query, kv, weights, grad_mixed)


def on_device(
    hidden_in,
    doc_ids,
    expert_ids,
    attn_gain,
    query_weight,
    key_weight,
    value_weight,
    output_weight,
    query_gain,
    key_gain,
    moe_gain,
    router_weight,
    gate_weight,
    up_weight,
    down_weight,
    cotangent,
):
    both = ("dp", "tensor")
    tok, width = hidden_in.shape
    hd = query_gain.shape[0]
    nkv = key_weight.shape[1] // hd
    nq = query_weight.shape[1] // hd
    group = nq // nkv
    experts = router_weight.shape[1]
    routes = expert_ids.shape[1]
    cap = tok * routes // experts
    slots = experts * cap
    scale = 1.0 / math.sqrt(hd)
    tokens = doc_ids.shape[1]
    me = lax.axis_index(both)

    lane = lax.broadcasted_iota(jnp.int32, (1, 1, experts), 2)
    chosen = jnp.sum((expert_ids[:, :, None] == lane).astype(F32), axis=1)
    below = (
        lax.broadcasted_iota(jnp.int32, (tok, tok), 1)
        < lax.broadcasted_iota(jnp.int32, (tok, tok), 0)
    ).astype(BF16)
    rank = dot_nn(below, chosen.astype(BF16))
    place = jnp.where(chosen > 0, rank, -1.0).T
    spread = (
        place[:, None, :] == lax.broadcasted_iota(jnp.int32, (1, cap, 1), 1).astype(F32)
    ).astype(BF16).reshape(slots, tok)

    hidden = hidden_in.astype(F32)
    normed_local = rms_scale(hidden, attn_gain).astype(BF16)

    in_weights, out_weights, normed, docs = gather(
        query_weight,
        key_weight,
        value_weight,
        output_weight.T,
        normed_local,
        jnp.broadcast_to(doc_ids, (8, tokens)).astype(F32),
    )

    spread_late, docs = lax.optimization_barrier((spread, docs))
    cot_out = dot_nn(spread_late, jnp.concatenate([cotangent, chosen.astype(BF16)], axis=1)).astype(BF16)
    cot_in = lax.all_to_all(
        cot_out.reshape(experts, cap, width + experts), both, split_axis=0, concat_axis=0, tiled=True
    ).reshape(slots, width + experts)

    position, allowed = jax.vmap(layout)(docs[:, 0])
    cosine, sine = rotary(position.reshape(-1), hd)
    cosine = jnp.concatenate([cosine, cosine], axis=1)
    signed = jnp.concatenate([-sine, sine], axis=1)
    bias = jnp.where(allowed, 0.0, MASKED).astype(F32)
    raw = dot_nn(normed, in_weights)
    heads = group * hd
    query, kv, attention, mixed = attend(raw, bias, cosine, signed, query_gain, key_gain, scale)
    attn_out = reduce(dot_nt(mixed, out_weights).astype(BF16), 2)

    residual = hidden + attn_out
    moe_input = rms_scale(residual, moe_gain).astype(BF16)
    moe_input, cot_in = lax.optimization_barrier((moe_input, cot_in))
    sent = dot_nn(spread, moe_input).astype(BF16)
    rows = lax.all_to_all(
        sent.reshape(experts, cap, width), both, split_axis=0, concat_axis=0, tiled=True
    ).reshape(slots, width)
    logits = dot_nn(moe_input, router_weight)
    masked = jnp.where(chosen > 0, logits, MASKED)
    probs = jnp.exp(masked - jnp.max(masked, axis=-1, keepdims=True))
    probs = probs / jnp.sum(probs, axis=-1, keepdims=True)

    gate_mat, up_mat, down_mat = gate_weight[0], up_weight[0], down_weight[0]
    cot_rows = cot_in[:, :width]
    inner_up = dot_nt(cot_rows, down_mat)
    row_logits = jnp.where(cot_in[:, width:] > 0, dot_nn(rows, router_weight), MASKED)
    row_probs = jnp.exp(row_logits - jnp.max(row_logits, axis=-1, keepdims=True))
    mine = lax.broadcasted_iota(jnp.int32, (1, experts), 1) == me
    prob = jnp.sum(jnp.where(mine, row_probs, 0.0), axis=-1, keepdims=True) / jnp.sum(
        row_probs, axis=-1, keepdims=True
    )
    gate_pre = dot_nn(rows, gate_mat)
    up_pre = dot_nn(rows, up_mat)
    sigmoid = jax.nn.sigmoid(gate_pre)
    silu = gate_pre * sigmoid
    inner = silu * up_pre
    gate_up = jnp.sum(inner * inner_up, axis=-1, keepdims=True)
    inner_low = (prob * inner).astype(BF16)
    grad_inner = prob * inner_up
    grad_gate = (grad_inner * up_pre * sigmoid * (1.0 + gate_pre * (1.0 - sigmoid))).astype(BF16)
    grad_up = (grad_inner * silu).astype(BF16)
    grad_rows = (dot_nt(grad_gate, gate_mat) + dot_nt(grad_up, up_mat)).astype(BF16)
    gate_up_high = gate_up.astype(BF16)
    gate_up_rest = (gate_up - gate_up_high.astype(F32)).astype(BF16)
    none = jnp.zeros((), BF16)
    home_out = jnp.concatenate(
        [grad_rows, jnp.where(mine, gate_up_high, none), jnp.where(mine, gate_up_rest, none)], axis=1
    )
    home = lax.all_to_all(
        home_out.reshape(experts, cap, width + 2 * experts), both, split_axis=0, concat_axis=0, tiled=True
    ).reshape(slots, width + 2 * experts)
    expert_out = dot_nn(inner_low, down_mat).astype(BF16)
    down_grad = dot_tn(inner_low, cot_rows)
    gate_grad = dot_tn(rows, grad_gate)
    up_grad = dot_tn(rows, grad_up)
    home, down_grad, gate_grad, up_grad = lax.optimization_barrier(
        (home, down_grad, gate_grad, up_grad)
    )

    upstream = cotangent.astype(F32)
    summed = dot_tn(spread, home)
    gate_upstream = summed[:, width : width + experts] + summed[:, width + experts :]
    grad_chosen = probs * (gate_upstream - jnp.sum(probs * gate_upstream, axis=-1, keepdims=True))
    grad_logits = grad_chosen.astype(BF16)
    grad_moe_input = summed[:, :width] + dot_nt(grad_logits, router_weight)
    router_part = dot_tn(moe_input, grad_logits)
    grad_norm, moegain_rows = rms_back(residual, moe_gain, grad_moe_input)
    moegain_part = jnp.sum(moegain_rows, axis=0)
    grad_residual = upstream + grad_norm
    grad_attn = share(grad_residual.astype(BF16), 3)
    pieces = router_part.astype(BF16).reshape(experts, width // experts, experts)
    piece = jnp.sum(lax.all_to_all(pieces, both, 0, 0, tiled=True).astype(F32), axis=0)
    expert_out, grad_attn, piece = lax.optimization_barrier((expert_out, grad_attn, piece))
    returned = lax.all_to_all(
        expert_out.reshape(experts, cap, width), both, split_axis=0, concat_axis=0, tiled=True
    ).reshape(slots, width)

    grad_mixed = dot_nn(grad_attn, out_weights).astype(BF16)
    grad_raw, head_gains = attend_back(
        raw, cosine, signed, query_gain, key_gain, query, kv, attention, grad_mixed, scale
    )
    grad_normed = reduce(dot_nt(grad_raw, in_weights).astype(BF16), 4)
    grad_hidden, attngain_rows = rms_back(hidden, attn_gain, grad_normed)
    input_grad = grad_residual + grad_hidden

    gains = jnp.concatenate([jnp.sum(attngain_rows, axis=0), moegain_part]).reshape(-1, hd)
    gains = jnp.concatenate([gains, head_gains, jnp.zeros((6, hd), F32)], axis=0)

    layer_out = (residual + dot_tn(spread, returned)).astype(BF16)
    query_grad, key_grad, value_grad, out_grad, gains, router_grad = scatter(
        dot_tn(normed, grad_raw).astype(BF16),
        dot_tn(grad_attn, mixed).astype(BF16),
        gains,
        piece.astype(BF16),
        (nq * hd, nkv * hd, nkv * hd, nq * hd),
    )
    at = width // hd
    return (
        layer_out,
        input_grad,
        gains[:at].reshape(-1),
        query_grad,
        key_grad,
        value_grad,
        out_grad.T,
        gains[2 * at],
        gains[2 * at + 1],
        gains[at : 2 * at].reshape(-1),
        router_grad.reshape(width, experts).astype(F32),
        gate_grad[None],
        up_grad[None],
        down_grad[None],
    )


def solution(mesh):
    both = ("dp", "tensor")
    in_specs = (
        P(both, None),
        P("dp", None),
        P(both, None),
        P(),
        P("dp", "tensor"),
        P("dp", "tensor"),
        P("dp", "tensor"),
        P("tensor", "dp"),
        P(),
        P(),
        P(),
        P(),
        P(both, None, None),
        P(both, None, None),
        P(both, None, None),
        P(both, None),
    )
    out_specs = (
        P(both, None),
        P(both, None),
        P(),
        P("dp", "tensor"),
        P("dp", "tensor"),
        P("dp", "tensor"),
        P("tensor", "dp"),
        P(),
        P(),
        P(),
        P(),
        P(both, None, None),
        P(both, None, None),
        P(both, None, None),
    )
    return jax.shard_map(
        on_device, mesh=mesh, in_specs=in_specs, out_specs=out_specs, check_vma=False
    )
```

```python
import functools
import math

import jax
import jax.numpy as jnp
from jax import lax
from jax.experimental import pallas as pl
from jax.experimental.pallas import tpu as pltpu
from jax.sharding import PartitionSpec as P

BLOCK = 128
EPSILON = 1e-06
ROPE_BASE = 1000000.0
MASKED = -1e30
F32 = jnp.float32
BF16 = jnp.bfloat16


def dot_nt(a, b):
    return lax.dot_general(a, b, (((1,), (1,)), ((), ())), preferred_element_type=F32)


def dot_tn(a, b):
    return lax.dot_general(a, b, (((0,), (0,)), ((), ())), preferred_element_type=F32)


def dot_nn(a, b):
    return lax.dot_general(a, b, (((1,), (0,)), ((), ())), preferred_element_type=F32)


def rms_recip(values):
    return lax.rsqrt(jnp.mean(values * values, axis=-1, keepdims=True) + EPSILON)


def rms_scale(values, gain):
    return values * rms_recip(values) * gain


def rms_back(values, gain, upstream):
    r = rms_recip(values)
    scaled = upstream * gain
    inner = jnp.mean(scaled * values, axis=-1, keepdims=True)
    grad_values = r * scaled - values * (r * r * r) * inner
    return grad_values, upstream * values * r


def rotate(values, cosine, sine):
    half = values.shape[-1] // 2
    a = values[..., :half]
    b = values[..., half:]
    return jnp.concatenate([a * cosine - b * sine, b * cosine + a * sine], axis=-1)


def layout(doc_row):
    length = doc_row.shape[0]
    indices = jnp.arange(length, dtype=jnp.int32)
    same_doc = doc_row[:, None] == doc_row[None, :]
    earlier = indices[None, :] < indices[:, None]
    position = jnp.sum(jnp.where(same_doc & earlier, 1, 0), axis=1).astype(jnp.int32)
    blocks = position // BLOCK
    allowed = same_doc & (blocks[None, :] <= blocks[:, None])
    return position, allowed


def rotary(position, head_size):
    half = head_size // 2
    frequency = jnp.exp(-jnp.log(ROPE_BASE) * jnp.arange(half, dtype=F32) * 2.0 / head_size)
    angles = position.astype(F32)[:, None] * frequency[None, :]
    return jnp.cos(angles), jnp.sin(angles)


MESH = pl.DeviceIdType.MESH
ANY = pl.BlockSpec(memory_space=pl.ANY)
VMEM = pl.BlockSpec(memory_space=pltpu.VMEM)
NX, NYH, NZ, NC = 4, 2, 4, 2
RING = 4


def cost(microseconds):
    return pl.CostEstimate(flops=0, transcendentals=0, bytes_accessed=int(microseconds * 3.6e6))


class Place:
    def __init__(self):
        dp = lax.axis_index("dp")
        self.t = lax.axis_index("tensor")
        self.c = lax.rem(dp, NC)
        self.z = lax.rem(dp // NC, NZ)
        self.yh = lax.rem(dp // (NC * NZ), NYH)
        self.x = dp // (NC * NZ * NYH)
        self.y = self.yh * 2 + self.t

    def device(self, x=None, yh=None, z=None, c=None, t=None):
        pick = lambda given, own: own if given is None else given
        x, yh, z, c = pick(x, self.x), pick(yh, self.yh), pick(z, self.z), pick(c, self.c)
        return (((x * NYH + yh) * NZ + z) * NC + c, pick(t, self.t))

    def at_y(self, y):
        return self.device(yh=y // 2, t=lax.rem(y, 2))


def after(i):
    return lax.rem(i + 1, RING)


def before(i):
    return lax.rem(i + RING - 1, RING)


def across(i):
    return lax.rem(i + 2, RING)


def greet(peers):
    barrier = pltpu.get_barrier_semaphore()
    for peer in peers:
        pl.semaphore_signal(barrier, inc=1, device_id=peer, device_id_type=MESH)
    pl.semaphore_wait(barrier, len(peers))


class Copies:
    def __init__(self, send, recv, local):
        self.send, self.recv, self.local = send, recv, local
        self.n = self.m = 0
        self.sent = []

    def put(self, src, dst, peer):
        copy = pltpu.make_async_remote_copy(
            src_ref=src,
            dst_ref=dst,
            send_sem=self.send.at[self.n],
            recv_sem=self.recv.at[self.n],
            device_id=peer,
            device_id_type=MESH,
        )
        self.n += 1
        copy.start()
        self.sent.append(copy)
        return copy

    def keep(self, src, dst):
        copy = pltpu.make_async_copy(src, dst, self.local.at[self.m])
        self.m += 1
        copy.start()
        return copy

    def finish(self):
        for copy in self.sent:
            copy.wait_send()


def gather_kernel(q, k, v, o, tok, doc, wa, wb, toks, docs, send, recv, local):
    me = Place()
    x, yh, z, c, p = me.x, me.yh, me.z, me.c, me.y
    sibling = me.device(c=1 - c)
    pair = me.device(yh=1 - yh)
    ring_x = (me.device(x=after(x)), me.device(x=before(x)))
    ring_z = (me.device(z=after(z)), me.device(z=before(z)))
    ring_y = (me.at_y(after(p)), me.at_y(before(p)))
    greet([sibling, pair, *ring_x, *ring_z, *ring_y])
    go = Copies(send, recv, local)

    shards, start = [], 0
    for ref, w in ((q, wa), (k, wa), (v, wa), (o, wb)):
        cols = ref.shape[1] // NYH
        to = w.at[x, yh, z, c, :, pl.ds(0 if w is wb else start, cols)]
        shards.append((ref, cols, to))
        start += cols

    def part(ref, cols, head):
        return ref.at[:, pl.ds(pl.multiple_of(head * cols, cols), cols)]

    pairs = [go.put(part(ref, cols, 1 - yh), to, pair) for ref, cols, to in shards]
    kept = [go.keep(part(ref, cols, yh), to) for ref, cols, to in shards]
    for copy in kept:
        copy.wait()
    for copy in pairs:
        copy.wait_recv()

    ways = (
        (x, z, ring_x, ring_z, lambda i, j: wa.at[i, :, j, c], lambda j: wa.at[:, :, j, c]),
        (z, x, ring_z, ring_x, lambda i, j: wb.at[j, :, i, c], lambda j: wb.at[j, :, :, c]),
    )

    def both(ref, peers):
        return [go.put(ref, ref, peer) for peer in peers]

    def relay(low, high, copies, peers):
        copies[0].wait_recv()
        up = go.put(low.at[0], low.at[0], peers[0])
        copies[1].wait_recv()
        return [up, go.put(high.at[1], high.at[1], peers[1])]

    def arrived(copies):
        for copy in copies:
            copy.wait_recv()

    near = [both(unit(i, j), one) for i, j, one, two, unit, slab in ways]
    own = [both(unit(i, j), two) for i, j, one, two, unit, slab in ways]
    rows = [go.put(tok, toks.at[p], peer) for peer in ring_y]
    rest = [go.keep(tok, toks.at[p]), go.keep(doc, docs.at[yh])]
    tail = [go.put(doc, docs.at[yh], pair)]
    far = [
        relay(unit(before(i), j), unit(after(i), j), copies, one)
        for (i, j, one, two, unit, slab), copies in zip(ways, near)
    ]
    low = [both(unit(before(i), j), two) for i, j, one, two, unit, slab in ways]
    high = [both(unit(after(i), j), two) for i, j, one, two, unit, slab in ways]
    last = []
    for (i, j, one, two, unit, slab), copies in zip(ways, far):
        arrived(copies)
        last.append(both(unit(across(i), j), two))
        tail.append(go.put(slab(j), slab(j), sibling))
    half = tok.shape[0] // 2
    rows[0].wait_recv()
    piece = toks.at[before(p), pl.ds(0, half)]
    tail.append(go.put(piece, piece, ring_y[0]))
    rows[1].wait_recv()
    piece = toks.at[after(p), pl.ds(half, half)]
    tail.append(go.put(piece, piece, ring_y[1]))
    ends = [[], []]
    for place, copies in ((lambda i: i, own), (before, low), (after, high), (across, last)):
        for n, (i, j, one, two, unit, slab) in enumerate(ways):
            u = place(i)
            ends[n] += relay(unit(u, before(j)), unit(u, after(j)), copies[n], two)
    for i, j, one, two, unit, slab in ways:
        tail.append(go.put(slab(before(j)), slab(before(j)), sibling))
        tail.append(go.put(slab(after(j)), slab(after(j)), sibling))
    for (i, j, one, two, unit, slab), copies in zip(ways, ends):
        arrived(copies)
        tail.append(go.put(slab(across(j)), slab(across(j)), sibling))
    arrived(tail)
    for copy in rest:
        copy.wait()
    go.finish()


def gather(query, key, value, out, tokens, docs):
    rows = query.shape[0]
    width_a = (query.shape[1] + key.shape[1] + value.shape[1]) // NYH
    width_b = out.shape[1] // NYH
    lead = (NX, NYH, NZ, NC, rows)
    wa, wb, toks, docs = pl.pallas_call(
        gather_kernel,
        name="gather_weights",
        cost_estimate=cost(60),
        out_shape=(
            jax.ShapeDtypeStruct((*lead, width_a), BF16),
            jax.ShapeDtypeStruct((*lead, width_b), BF16),
            jax.ShapeDtypeStruct((RING, *tokens.shape), BF16),
            jax.ShapeDtypeStruct((NYH, *docs.shape), docs.dtype),
        ),
        in_specs=[ANY] * 6,
        out_specs=(ANY,) * 4,
        scratch_shapes=[
            pltpu.SemaphoreType.DMA((57,)),
            pltpu.SemaphoreType.DMA((57,)),
            pltpu.SemaphoreType.DMA((6,)),
        ],
        compiler_params=pltpu.CompilerParams(collective_id=1, has_side_effects=True),
    )(query, key, value, out, tokens, docs)
    depth = NX * NYH * NZ * NC * rows
    return (
        wa.reshape(depth, width_a),
        wb.reshape(depth, width_b),
        toks.reshape(RING * tokens.shape[0], tokens.shape[1]),
        docs,
    )


def share_kernel(tok, toks, send, recv, local):
    me = Place()
    p = me.y
    ring = (me.at_y(after(p)), me.at_y(before(p)))
    greet(ring)
    go = Copies(send, recv, local)
    half = tok.shape[0] // 2
    direct = [go.put(tok, toks.at[p], peer) for peer in ring]
    kept = go.keep(tok, toks.at[p])
    relays = []
    for h, owner in enumerate((before(p), after(p))):
        direct[h].wait_recv()
        piece = toks.at[owner, pl.ds(h * half, half)]
        relays.append(go.put(piece, piece, ring[h]))
    for copy in relays:
        copy.wait_recv()
    kept.wait()
    go.finish()


def share(tokens, ident):
    toks = pl.pallas_call(
        share_kernel,
        name=f"share_rows_{ident}",
        cost_estimate=cost(13),
        out_shape=jax.ShapeDtypeStruct((RING, *tokens.shape), tokens.dtype),
        in_specs=[ANY],
        out_specs=ANY,
        scratch_shapes=[
            pltpu.SemaphoreType.DMA((4,)),
            pltpu.SemaphoreType.DMA((4,)),
            pltpu.SemaphoreType.DMA((1,)),
        ],
        compiler_params=pltpu.CompilerParams(collective_id=ident, has_side_effects=True),
    )(tokens)
    return toks.reshape(RING * tokens.shape[0], tokens.shape[1])


def reduce_kernel(part, out, held, own, got, send, recv, local):
    me = Place()
    p = me.y
    ring = (me.at_y(after(p)), me.at_y(before(p)))
    greet(ring)
    go = Copies(send, recv, local)
    half = out.shape[0] // 2
    halves = [pl.ds(h * half, half) for h in range(2)]
    near = (after(p), before(p))
    cross = [go.put(part.at[across(p), halves[h]], got.at[h], ring[h]) for h in range(2)]
    kept = [go.keep(part.at[near[h], halves[h]], held.at[h]) for h in range(2)]
    straight = [go.put(part.at[near[h], halves[1 - h]], got.at[2 + h], ring[h]) for h in range(2)]
    mine = go.keep(part.at[p], own)
    sums = []
    for h in range(2):
        kept[h].wait()
        cross[h].wait_recv()
        held[h] = (held[h].astype(F32) + got[h].astype(F32)).astype(BF16)
        sums.append(go.put(held.at[h], got.at[4 + h], ring[h]))
    mine.wait()
    for copy in straight:
        copy.wait_recv()
    for h in range(2):
        sums[h].wait_recv()
        out[halves[h]] = (
            own[halves[h]].astype(F32) + got[4 + h].astype(F32) + got[3 - h].astype(F32)
        )
    go.finish()


def reduce(part, ident):
    rows, width = part.shape[0] // RING, part.shape[1]
    half = rows // 2
    return pl.pallas_call(
        reduce_kernel,
        name=f"reduce_rows_{ident}",
        cost_estimate=cost(15),
        out_shape=jax.ShapeDtypeStruct((rows, width), F32),
        in_specs=[ANY],
        out_specs=VMEM,
        scratch_shapes=[
            pltpu.VMEM((2, half, width), BF16),
            pltpu.VMEM((rows, width), BF16),
            pltpu.VMEM((6, half, width), BF16),
            pltpu.SemaphoreType.DMA((6,)),
            pltpu.SemaphoreType.DMA((6,)),
            pltpu.SemaphoreType.DMA((3,)),
        ],
        compiler_params=pltpu.CompilerParams(
            collective_id=ident, has_side_effects=True, vmem_limit_bytes=24 << 20
        ),
    )(part.reshape(RING, rows, width))


def scatter_kernel(
    ga, gb, gains, piece, oq, ok, ov, oo, og, op, ka, kb, da, db, ra, rb, qa, qb, sa, sb, ta, tb, ua, ub, ma, mb,
    ring_gains, sum_gains, pair_gains, send, recv, local
):
    me = Place()
    x, yh, z, c, t = me.x, me.yh, me.z, me.c, me.t
    sibling = me.device(c=1 - c)
    pair = me.device(yh=1 - yh)
    partner = me.device(t=1 - t)
    ring_x = (me.device(x=after(x)), me.device(x=before(x)))
    ring_z = (me.device(z=after(z)), me.device(z=before(z)))
    round_x = (*ring_x, me.device(x=across(x)))
    round_z = (*ring_z, me.device(z=across(z)))
    greet([sibling, pair, partner, *round_x, *round_z])
    go = Copies(send, recv, local)

    def around(n, term, own, peers):
        ring_gains[n, own] = term
        return [go.put(ring_gains.at[n, own], ring_gains.at[n, own], peer) for peer in peers]

    def ring_sum(n, copies):
        for copy in copies:
            copy.wait_recv()
        return (ring_gains[n, 0] + ring_gains[n, 1]) + (ring_gains[n, 2] + ring_gains[n, 3])

    def swap(n, term, peer):
        sum_gains[n] = term
        return go.put(sum_gains.at[n], pair_gains.at[n], peer)

    def swapped(n, copy):
        copy.wait_recv()
        return sum_gains[n] + pair_gains[n]


    ways = (
        (lambda i, h, n: ga.at[i, h, :, n], x, z, ring_x, ring_z, ka, da, ra, qa, sa, ta),
        (lambda i, h, n: gb.at[:, h, i, n], z, x, ring_z, ring_x, kb, db, rb, qb, sb, tb),
    )
    places = (across, after, before, lambda i: i)

    def spread(ref, peers):
        return [go.put(ref, ref, peer) for peer in peers]

    def arrived(copies):
        for copy in copies:
            copy.wait_recv()

    given, held = [[], []], [[], []]
    for n, place in enumerate(places):
        for w, (slab, i, j, one, two, k, d, r, q, s, u) in enumerate(ways):
            given[w].append([go.put(slab(place(i), h, 1 - c), d.at[n, h], sibling) for h in range(2)])
            held[w].append([go.keep(slab(place(i), h, c), k.at[n, h]) for h in range(2)])

    def ready(w, n, h):
        given[w][n][h].wait_recv()
        held[w][n][h].wait()

    def total(w, n, h, extra):
        slab, i, j, one, two, k, d, r, q, s, u = ways[w]

        def step(m, _):
            value = k[n, h, m].astype(F32) + d[n, h, m].astype(F32)
            for e in extra:
                value += r[e, m].astype(F32)
            k[n, h, m] = value.astype(BF16)
            return 0

        lax.fori_loop(0, k.shape[2], step, 0)

    terms = around(0, gains[...], x, round_x)
    mine = op.at[x, yh, z, c, t]
    held_piece = go.keep(piece, mine)
    pieces = [go.put(piece, mine, sibling)]
    cross, straight, sums = [[], []], [[], []], [[], []]
    for w, (slab, i, j, one, two, k, d, r, q, s, u) in enumerate(ways):
        for h in range(2):
            ready(w, 0, h)
            total(w, 0, h, ())
            cross[w].append(go.put(k.at[0, h], r.at[h], one[h]))
    for w, (slab, i, j, one, two, k, d, r, q, s, u) in enumerate(ways):
        for h in range(2):
            ready(w, 1 + h, 1 - h)
            total(w, 1 + h, 1 - h, ())
            straight[w].append(go.put(k.at[1 + h, 1 - h], r.at[2 + h], one[h]))
    terms = around(1, ring_sum(0, terms), z, round_z)
    arrived(pieces)
    held_piece.wait()
    pieces = spread(op.at[x, yh, z, :, t], [partner])
    for w, (slab, i, j, one, two, k, d, r, q, s, u) in enumerate(ways):
        for h in range(2):
            ready(w, 1 + h, h)
            cross[w][h].wait_recv()
            total(w, 1 + h, h, (h,))
            sums[w].append(go.put(k.at[1 + h, h], r.at[4 + h], one[h]))
    arrived(pieces)
    pieces = spread(op.at[x, yh, z], [pair])
    terms = swap(0, ring_sum(1, terms), pair)
    for w in range(2):
        for h in range(2):
            ready(w, 3, h)
            straight[w][1 - h].wait_recv()
            total(w, 3, h, (3 - h,))
    arrived(pieces)
    pieces = spread(op.at[x, :, z], round_x)
    terms = swap(1, swapped(0, terms), partner)
    over, direct, final = [[], []], [[], []], [[], []]
    for w, (slab, i, j, one, two, k, d, r, q, s, u) in enumerate(ways):
        near = (after(j), before(j))
        for h in range(2):
            sums[w][h].wait_recv()

            def step(m, _, k=k, r=r, h=h):
                k[3, h, m] = (k[3, h, m].astype(F32) + r[4 + h, m].astype(F32)).astype(BF16)
                return 0

            lax.fori_loop(0, k.shape[2], step, 0)
            over[w].append(go.put(k.at[3, h, across(j)], q.at[h], two[h]))
        for h in range(2):
            direct[w].append(go.put(k.at[3, 1 - h, near[h]], q.at[2 + h], two[h]))
    arrived(pieces)
    pieces = spread(op.at[:, :, z], round_z)
    terms = swap(2, swapped(1, terms), sibling)
    for w, (slab, i, j, one, two, k, d, r, q, s, u) in enumerate(ways):
        near = (after(j), before(j))
        for h in range(2):
            over[w][h].wait_recv()
            s[h] = (k[3, h, near[h]].astype(F32) + q[h].astype(F32)).astype(BF16)
            final[w].append(go.put(s.at[h], q.at[4 + h], two[h]))
    last = []
    for w, ((slab, i, j, one, two, k, d, r, q, s, u), v, m) in enumerate(zip(ways, (ua, ub), (ma, mb))):
        arrived(direct[w])
        arrived(final[w])
        for h in range(2):
            u[h] = k[3, h, j].astype(F32) + q[4 + h].astype(F32) + q[3 - h].astype(F32)
        v[...] = u[1 - yh].astype(BF16)
        last.append(go.put(v, m, pair))
    og[...] = swapped(2, terms)

    def write(head, a, b):
        start = 0
        for out, block in ((oq, a), (ok, a), (ov, a), (oo, b)):
            cols = out.shape[1] // NYH
            at = 0 if block is b else start
            out[:, pl.ds(pl.multiple_of(head * cols, cols), cols)] = block[:, at : at + cols]
            start += cols

    write(yh, ta[yh], tb[yh])
    arrived(last)
    write(1 - yh, ma[...].astype(F32), mb[...].astype(F32))
    arrived(pieces)
    go.finish()


def scatter(grad_a, grad_b, gains, piece, columns):
    rows = grad_a.shape[0] // (NX * NYH * NZ * NC)
    lead = (NX, NYH, NZ, NC, rows)
    widths = (grad_a.shape[1], grad_b.shape[1])

    def each(shape, dtype):
        return [pltpu.VMEM((*shape, rows, w), dtype) for w in widths]

    return pl.pallas_call(
        scatter_kernel,
        name="scatter_weights",
        cost_estimate=cost(80),
        out_shape=(
            *(jax.ShapeDtypeStruct((rows, w), F32) for w in columns),
            jax.ShapeDtypeStruct(gains.shape, F32),
            jax.ShapeDtypeStruct((NX, NYH, NZ, NC, 2, *piece.shape), piece.dtype),
        ),
        in_specs=[ANY, ANY, VMEM, ANY],
        out_specs=(*(VMEM,) * 5, ANY),
        scratch_shapes=[
            *each((4, 2, RING), BF16),
            *each((4, 2, RING), BF16),
            *each((6, RING), BF16),
            *each((6,), BF16),
            *each((2,), BF16),
            *each((2,), F32),
            *each((), BF16),
            *each((), BF16),
            pltpu.VMEM((2, RING, *gains.shape), F32),
            pltpu.VMEM((3, *gains.shape), F32),
            pltpu.VMEM((3, *gains.shape), F32),
            pltpu.SemaphoreType.DMA((60,)),
            pltpu.SemaphoreType.DMA((60,)),
            pltpu.SemaphoreType.DMA((17,)),
        ],
        compiler_params=pltpu.CompilerParams(
            collective_id=5, has_side_effects=True, vmem_limit_bytes=40 << 20
        ),
    )(grad_a.reshape(*lead, widths[0]), grad_b.reshape(*lead, widths[1]), gains, piece)


def unit_rows(values):
    return lax.rsqrt(jnp.mean(values * values, axis=-1, keepdims=True) + EPSILON)


def turn(values, cosine, signed):
    return values * cosine + pltpu.roll(values, values.shape[-1] // 2, 1) * signed


def attend_kernel(scale, raw, bias, cosine, signed, qgain, kgain, query, kv, weights, mixed):
    heads = query.shape[1] // cosine.shape[1]
    hd = cosine.shape[1]
    cos, sig = cosine[...], signed[...]
    key_raw = raw[:, heads * hd : (heads + 1) * hd]
    key = turn(key_raw * unit_rows(key_raw) * kgain[...], cos, sig).astype(BF16)
    value = raw[:, (heads + 1) * hd :].astype(BF16)
    kv[:, :hd] = key
    kv[:, hd:] = value
    for h in range(heads):
        at = slice(h * hd, (h + 1) * hd)
        head = raw[:, at]
        rows = turn(head * unit_rows(head) * qgain[...], cos, sig).astype(BF16)
        query[:, at] = rows
        scores = dot_nt(rows, key) * scale + bias[0]
        peak = jnp.max(scores, axis=-1, keepdims=True)
        weight = jnp.exp(scores - peak)
        weight = weight * (1.0 / jnp.sum(weight, axis=-1, keepdims=True))
        weights[0, h] = weight
        mixed[:, at] = dot_nn(weight.astype(BF16), value).astype(BF16)


def attend(raw, bias, cosine, signed, query_gain, key_gain, scale):
    groups, tokens = bias.shape[0], bias.shape[1]
    hd = cosine.shape[1]
    heads = raw.shape[1] // hd - 2
    rows = groups * tokens

    def block(cols):
        return pl.BlockSpec((tokens, cols), lambda g: (g, 0))

    gain = pl.BlockSpec((1, hd), lambda g: (0, 0))
    square = pl.BlockSpec((1, tokens, tokens), lambda g: (g, 0, 0))
    return pl.pallas_call(
        functools.partial(attend_kernel, scale),
        name="attend",
        cost_estimate=cost(8),
        grid=(groups,),
        out_shape=(
            jax.ShapeDtypeStruct((rows, heads * hd), BF16),
            jax.ShapeDtypeStruct((rows, 2 * hd), BF16),
            jax.ShapeDtypeStruct((groups, heads, tokens, tokens), F32),
            jax.ShapeDtypeStruct((rows, heads * hd), BF16),
        ),
        in_specs=[block((heads + 2) * hd), square, block(hd), block(hd), gain, gain],
        out_specs=(
            block(heads * hd),
            block(2 * hd),
            pl.BlockSpec((1, heads, tokens, tokens), lambda g: (g, 0, 0, 0)),
            block(heads * hd),
        ),
        compiler_params=pltpu.CompilerParams(vmem_limit_bytes=40 << 20),
    )(raw, bias, cosine, signed, query_gain.reshape(1, hd), key_gain.reshape(1, hd))


def norm_back(values, gain, upstream):
    r = unit_rows(values)
    scaled = upstream * gain
    inner = jnp.mean(scaled * values, axis=-1, keepdims=True)
    grad = r * scaled - values * (r * r * r * inner)
    return grad, jnp.sum(upstream * values * r, axis=0, keepdims=True)


def attend_back_kernel(
    scale, raw, cosine, signed, qgain, kgain, query, kv, weights, grad_mixed, grad_raw, grad_gains
):
    hd = cosine.shape[1]
    heads = query.shape[1] // hd
    cos, sig = cosine[...], -signed[...]
    key, value = kv[:, :hd], kv[:, hd:]
    grad_key = jnp.zeros(key.shape, F32)
    grad_value = jnp.zeros(key.shape, F32)
    query_gains = jnp.zeros((1, hd), F32)
    for h in range(heads):
        at = slice(h * hd, (h + 1) * hd)
        weight = weights[0, h]
        grad_head = grad_mixed[:, at]
        grad_value += dot_tn(weight.astype(BF16), grad_head)
        grad_soft = dot_nt(grad_head, value)
        delta = jnp.sum(weight * grad_soft, axis=-1, keepdims=True)
        grad_scores = (weight * (grad_soft - delta)).astype(BF16)
        grad_key += dot_tn(grad_scores, query[:, at])
        turned = turn(dot_nn(grad_scores, key) * scale, cos, sig)
        grad, gains = norm_back(raw[:, at], qgain[...], turned)
        grad_raw[:, at] = grad.astype(BF16)
        query_gains += gains
    at = slice(heads * hd, (heads + 1) * hd)
    grad, key_gains = norm_back(raw[:, at], kgain[...], turn(grad_key * scale, cos, sig))
    grad_raw[:, at] = grad.astype(BF16)
    grad_raw[:, (heads + 1) * hd :] = grad_value.astype(BF16)
    gains = jnp.concatenate([query_gains, key_gains], axis=0)

    @pl.when(pl.program_id(0) == 0)
    def _():
        grad_gains[...] = gains

    @pl.when(pl.program_id(0) > 0)
    def _():
        grad_gains[...] += gains


def attend_back(raw, cosine, signed, query_gain, key_gain, query, kv, weights, grad_mixed, scale):
    groups, heads, tokens, _ = weights.shape
    hd = cosine.shape[1]
    rows = groups * tokens

    def block(cols):
        return pl.BlockSpec((tokens, cols), lambda g: (g, 0))

    gain = pl.BlockSpec((1, hd), lambda g: (0, 0))
    return pl.pallas_call(
        functools.partial(attend_back_kernel, scale),
        name="attend_back",
        cost_estimate=cost(14),
        grid=(groups,),
        out_shape=(
            jax.ShapeDtypeStruct((rows, (heads + 2) * hd), BF16),
            jax.ShapeDtypeStruct((2, hd), F32),
        ),
        in_specs=[
            block((heads + 2) * hd),
            block(hd),
            block(hd),
            gain,
            gain,
            block(heads * hd),
            block(2 * hd),
            pl.BlockSpec((1, heads, tokens, tokens), lambda g: (g, 0, 0, 0)),
            block(heads * hd),
        ],
        out_specs=(block((heads + 2) * hd), pl.BlockSpec((2, hd), lambda g: (0, 0))),
        compiler_params=pltpu.CompilerParams(vmem_limit_bytes=40 << 20),
    )(raw, cosine, signed, query_gain.reshape(1, hd), key_gain.reshape(1, hd), query, kv, weights, grad_mixed)


def on_device(
    hidden_in,
    doc_ids,
    expert_ids,
    attn_gain,
    query_weight,
    key_weight,
    value_weight,
    output_weight,
    query_gain,
    key_gain,
    moe_gain,
    router_weight,
    gate_weight,
    up_weight,
    down_weight,
    cotangent,
):
    both = ("dp", "tensor")
    tok, width = hidden_in.shape
    hd = query_gain.shape[0]
    nkv = key_weight.shape[1] // hd
    nq = query_weight.shape[1] // hd
    group = nq // nkv
    experts = router_weight.shape[1]
    routes = expert_ids.shape[1]
    cap = tok * routes // experts
    slots = experts * cap
    scale = 1.0 / math.sqrt(hd)
    tokens = doc_ids.shape[1]
    me = lax.axis_index(both)

    lane = lax.broadcasted_iota(jnp.int32, (1, 1, experts), 2)
    chosen = jnp.sum((expert_ids[:, :, None] == lane).astype(F32), axis=1)
    below = (
        lax.broadcasted_iota(jnp.int32, (tok, tok), 1)
        < lax.broadcasted_iota(jnp.int32, (tok, tok), 0)
    ).astype(BF16)
    rank = dot_nn(below, chosen.astype(BF16))
    place = jnp.where(chosen > 0, rank, -1.0).T
    spread = (
        place[:, None, :] == lax.broadcasted_iota(jnp.int32, (1, cap, 1), 1).astype(F32)
    ).astype(BF16).reshape(slots, tok)

    hidden = hidden_in.astype(F32)
    normed_local = rms_scale(hidden, attn_gain).astype(BF16)

    in_weights, out_weights, normed, docs = gather(
        query_weight,
        key_weight,
        value_weight,
        output_weight.T,
        normed_local,
        jnp.broadcast_to(doc_ids, (8, tokens)).astype(F32),
    )

    spread_late, docs = lax.optimization_barrier((spread, docs))
    cot_out = dot_nn(spread_late, jnp.concatenate([cotangent, chosen.astype(BF16)], axis=1)).astype(BF16)
    cot_in = lax.all_to_all(
        cot_out.reshape(experts, cap, width + experts), both, split_axis=0, concat_axis=0, tiled=True
    ).reshape(slots, width + experts)

    position, allowed = jax.vmap(layout)(docs[:, 0])
    cosine, sine = rotary(position.reshape(-1), hd)
    cosine = jnp.concatenate([cosine, cosine], axis=1)
    signed = jnp.concatenate([-sine, sine], axis=1)
    bias = jnp.where(allowed, 0.0, MASKED).astype(F32)
    raw = dot_nn(normed, in_weights)
    heads = group * hd
    query, kv, attention, mixed = attend(raw, bias, cosine, signed, query_gain, key_gain, scale)
    attn_out = reduce(dot_nt(mixed, out_weights).astype(BF16), 2)

    residual = hidden + attn_out
    moe_input = rms_scale(residual, moe_gain).astype(BF16)
    moe_input, cot_in = lax.optimization_barrier((moe_input, cot_in))
    sent = dot_nn(spread, moe_input).astype(BF16)
    rows = lax.all_to_all(
        sent.reshape(experts, cap, width), both, split_axis=0, concat_axis=0, tiled=True
    ).reshape(slots, width)
    logits = dot_nn(moe_input, router_weight)
    masked = jnp.where(chosen > 0, logits, MASKED)
    probs = jnp.exp(masked - jnp.max(masked, axis=-1, keepdims=True))
    probs = probs / jnp.sum(probs, axis=-1, keepdims=True)

    gate_mat, up_mat, down_mat = gate_weight[0], up_weight[0], down_weight[0]
    cot_rows = cot_in[:, :width]
    inner_up = dot_nt(cot_rows, down_mat)
    row_logits = jnp.where(cot_in[:, width:] > 0, dot_nn(rows, router_weight), MASKED)
    row_probs = jnp.exp(row_logits - jnp.max(row_logits, axis=-1, keepdims=True))
    mine = lax.broadcasted_iota(jnp.int32, (1, experts), 1) == me
    prob = jnp.sum(jnp.where(mine, row_probs, 0.0), axis=-1, keepdims=True) / jnp.sum(
        row_probs, axis=-1, keepdims=True
    )
    gate_pre = dot_nn(rows, gate_mat)
    up_pre = dot_nn(rows, up_mat)
    sigmoid = jax.nn.sigmoid(gate_pre)
    silu = gate_pre * sigmoid
    inner = silu * up_pre
    gate_up = jnp.sum(inner * inner_up, axis=-1, keepdims=True)
    inner_low = (prob * inner).astype(BF16)
    grad_inner = prob * inner_up
    grad_gate = (grad_inner * up_pre * sigmoid * (1.0 + gate_pre * (1.0 - sigmoid))).astype(BF16)
    grad_up = (grad_inner * silu).astype(BF16)
    grad_rows = (dot_nt(grad_gate, gate_mat) + dot_nt(grad_up, up_mat)).astype(BF16)
    gate_up_high = gate_up.astype(BF16)
    gate_up_rest = (gate_up - gate_up_high.astype(F32)).astype(BF16)
    none = jnp.zeros((), BF16)
    home_out = jnp.concatenate(
        [grad_rows, jnp.where(mine, gate_up_high, none), jnp.where(mine, gate_up_rest, none)], axis=1
    )
    home = lax.all_to_all(
        home_out.reshape(experts, cap, width + 2 * experts), both, split_axis=0, concat_axis=0, tiled=True
    ).reshape(slots, width + 2 * experts)
    expert_out = dot_nn(inner_low, down_mat).astype(BF16)
    down_grad = dot_tn(inner_low, cot_rows)
    gate_grad = dot_tn(rows, grad_gate)
    up_grad = dot_tn(rows, grad_up)
    home, down_grad, gate_grad, up_grad = lax.optimization_barrier(
        (home, down_grad, gate_grad, up_grad)
    )

    upstream = cotangent.astype(F32)
    summed = dot_tn(spread, home)
    gate_upstream = summed[:, width : width + experts] + summed[:, width + experts :]
    grad_chosen = probs * (gate_upstream - jnp.sum(probs * gate_upstream, axis=-1, keepdims=True))
    grad_logits = grad_chosen.astype(BF16)
    grad_moe_input = summed[:, :width] + dot_nt(grad_logits, router_weight)
    router_part = dot_tn(moe_input, grad_logits)
    grad_norm, moegain_rows = rms_back(residual, moe_gain, grad_moe_input)
    moegain_part = jnp.sum(moegain_rows, axis=0)
    grad_residual = upstream + grad_norm
    grad_attn = share(grad_residual.astype(BF16), 3)
    pieces = router_part.astype(BF16).reshape(experts, width // experts, experts)
    piece = jnp.sum(lax.all_to_all(pieces, both, 0, 0, tiled=True).astype(F32), axis=0)
    expert_out, grad_attn, piece = lax.optimization_barrier((expert_out, grad_attn, piece))
    returned = lax.all_to_all(
        expert_out.reshape(experts, cap, width), both, split_axis=0, concat_axis=0, tiled=True
    ).reshape(slots, width)

    grad_mixed = dot_nn(grad_attn, out_weights).astype(BF16)
    grad_raw, head_gains = attend_back(
        raw, cosine, signed, query_gain, key_gain, query, kv, attention, grad_mixed, scale
    )
    grad_normed = reduce(dot_nt(grad_raw, in_weights).astype(BF16), 4)
    grad_hidden, attngain_rows = rms_back(hidden, attn_gain, grad_normed)
    input_grad = grad_residual + grad_hidden

    gains = jnp.concatenate([jnp.sum(attngain_rows, axis=0), moegain_part]).reshape(-1, hd)
    gains = jnp.concatenate([gains, head_gains, jnp.zeros((6, hd), F32)], axis=0)

    layer_out = (residual + dot_tn(spread, returned)).astype(BF16)
    query_grad, key_grad, value_grad, out_grad, gains, router_grad = scatter(
        dot_tn(normed, grad_raw).astype(BF16),
        dot_tn(grad_attn, mixed).astype(BF16),
        gains,
        piece.astype(BF16),
        (nq * hd, nkv * hd, nkv * hd, nq * hd),
    )
    at = width // hd
    return (
        layer_out,
        input_grad,
        gains[:at].reshape(-1),
        query_grad,
        key_grad,
        value_grad,
        out_grad.T,
        gains[2 * at],
        gains[2 * at + 1],
        gains[at : 2 * at].reshape(-1),
        router_grad.reshape(width, experts).astype(F32),
        gate_grad[None],
        up_grad[None],
        down_grad[None],
    )


def solution(mesh):
    both = ("dp", "tensor")
    in_specs = (
        P(both, None),
        P("dp", None),
        P(both, None),
        P(),
        P("dp", "tensor"),
        P("dp", "tensor"),
        P("dp", "tensor"),
        P("tensor", "dp"),
        P(),
        P(),
        P(),
        P(),
        P(both, None, None),
        P(both, None, None),
        P(both, None, None),
        P(both, None),
    )
    out_specs = (
        P(both, None),
        P(both, None),
        P(),
        P("dp", "tensor"),
        P("dp", "tensor"),
        P("dp", "tensor"),
        P("tensor", "dp"),
        P(),
        P(),
        P(),
        P(),
        P(both, None, None),
        P(both, None, None),
        P(both, None, None),
    )
    return jax.shard_map(
        on_device, mesh=mesh, in_specs=in_specs, out_specs=out_specs, check_vma=False
    )
```

```python
import functools
import math

import jax
import jax.numpy as jnp
from jax import lax
from jax.experimental import pallas as pl
from jax.experimental.pallas import tpu as pltpu
from jax.sharding import PartitionSpec as P

BLOCK = 128
EPSILON = 1e-06
ROPE_BASE = 1000000.0
MASKED = -1e30
F32 = jnp.float32
BF16 = jnp.bfloat16


def dot_nt(a, b):
    return lax.dot_general(a, b, (((1,), (1,)), ((), ())), preferred_element_type=F32)


def dot_tn(a, b):
    return lax.dot_general(a, b, (((0,), (0,)), ((), ())), preferred_element_type=F32)


def dot_nn(a, b):
    return lax.dot_general(a, b, (((1,), (0,)), ((), ())), preferred_element_type=F32)


def rms_recip(values):
    return lax.rsqrt(jnp.mean(values * values, axis=-1, keepdims=True) + EPSILON)


def rms_scale(values, gain):
    return values * rms_recip(values) * gain


def rms_back(values, gain, upstream):
    r = rms_recip(values)
    scaled = upstream * gain
    inner = jnp.mean(scaled * values, axis=-1, keepdims=True)
    grad_values = r * scaled - values * (r * r * r) * inner
    return grad_values, upstream * values * r


def rotate(values, cosine, sine):
    half = values.shape[-1] // 2
    a = values[..., :half]
    b = values[..., half:]
    return jnp.concatenate([a * cosine - b * sine, b * cosine + a * sine], axis=-1)


def layout(doc_row):
    length = doc_row.shape[0]
    indices = jnp.arange(length, dtype=jnp.int32)
    same_doc = doc_row[:, None] == doc_row[None, :]
    earlier = indices[None, :] < indices[:, None]
    position = jnp.sum(jnp.where(same_doc & earlier, 1, 0), axis=1).astype(jnp.int32)
    blocks = position // BLOCK
    allowed = same_doc & (blocks[None, :] <= blocks[:, None])
    return position, allowed


def rotary(position, head_size):
    half = head_size // 2
    frequency = jnp.exp(-jnp.log(ROPE_BASE) * jnp.arange(half, dtype=F32) * 2.0 / head_size)
    angles = position.astype(F32)[:, None] * frequency[None, :]
    return jnp.cos(angles), jnp.sin(angles)


MESH = pl.DeviceIdType.MESH
ANY = pl.BlockSpec(memory_space=pl.ANY)
VMEM = pl.BlockSpec(memory_space=pltpu.VMEM)
NX, NYH, NZ, NC = 4, 2, 4, 2
RING = 4


def cost(microseconds):
    return pl.CostEstimate(flops=0, transcendentals=0, bytes_accessed=int(microseconds * 3.6e6))


class Place:
    def __init__(self):
        dp = lax.axis_index("dp")
        self.t = lax.axis_index("tensor")
        self.c = lax.rem(dp, NC)
        self.z = lax.rem(dp // NC, NZ)
        self.yh = lax.rem(dp // (NC * NZ), NYH)
        self.x = dp // (NC * NZ * NYH)
        self.y = self.yh * 2 + self.t

    def device(self, x=None, yh=None, z=None, c=None, t=None):
        pick = lambda given, own: own if given is None else given
        x, yh, z, c = pick(x, self.x), pick(yh, self.yh), pick(z, self.z), pick(c, self.c)
        return (((x * NYH + yh) * NZ + z) * NC + c, pick(t, self.t))

    def at_y(self, y):
        return self.device(yh=y // 2, t=lax.rem(y, 2))


def after(i):
    return lax.rem(i + 1, RING)


def before(i):
    return lax.rem(i + RING - 1, RING)


def across(i):
    return lax.rem(i + 2, RING)


def greet(peers):
    barrier = pltpu.get_barrier_semaphore()
    for peer in peers:
        pl.semaphore_signal(barrier, inc=1, device_id=peer, device_id_type=MESH)
    pl.semaphore_wait(barrier, len(peers))


class Copies:
    def __init__(self, send, recv, local):
        self.send, self.recv, self.local = send, recv, local
        self.n = self.m = 0
        self.sent = []

    def put(self, src, dst, peer):
        copy = pltpu.make_async_remote_copy(
            src_ref=src,
            dst_ref=dst,
            send_sem=self.send.at[self.n],
            recv_sem=self.recv.at[self.n],
            device_id=peer,
            device_id_type=MESH,
        )
        self.n += 1
        copy.start()
        self.sent.append(copy)
        return copy

    def keep(self, src, dst):
        copy = pltpu.make_async_copy(src, dst, self.local.at[self.m])
        self.m += 1
        copy.start()
        return copy

    def finish(self):
        for copy in self.sent:
            copy.wait_send()


def gather_kernel(q, k, v, o, tok, doc, wa, wb, toks, docs, send, recv, local):
    me = Place()
    x, yh, z, c, p = me.x, me.yh, me.z, me.c, me.y
    sibling = me.device(c=1 - c)
    pair = me.device(yh=1 - yh)
    ring_x = (me.device(x=after(x)), me.device(x=before(x)))
    ring_z = (me.device(z=after(z)), me.device(z=before(z)))
    ring_y = (me.at_y(after(p)), me.at_y(before(p)))
    greet([sibling, pair, *ring_x, *ring_z, *ring_y])
    go = Copies(send, recv, local)

    shards, start = [], 0
    for ref, w in ((q, wa), (k, wa), (v, wa), (o, wb)):
        cols = ref.shape[1] // NYH
        to = w.at[x, yh, z, c, :, pl.ds(0 if w is wb else start, cols)]
        shards.append((ref, cols, to))
        start += cols

    def part(ref, cols, head):
        return ref.at[:, pl.ds(pl.multiple_of(head * cols, cols), cols)]

    pairs = [go.put(part(ref, cols, 1 - yh), to, pair) for ref, cols, to in shards]
    kept = [go.keep(part(ref, cols, yh), to) for ref, cols, to in shards]
    for copy in kept:
        copy.wait()
    for copy in pairs:
        copy.wait_recv()

    ways = (
        (x, z, ring_x, ring_z, lambda i, j: wa.at[i, :, j, c], lambda j: wa.at[:, :, j, c]),
        (z, x, ring_z, ring_x, lambda i, j: wb.at[j, :, i, c], lambda j: wb.at[j, :, :, c]),
    )

    def both(ref, peers):
        return [go.put(ref, ref, peer) for peer in peers]

    def relay(low, high, copies, peers):
        copies[0].wait_recv()
        up = go.put(low.at[0], low.at[0], peers[0])
        copies[1].wait_recv()
        return [up, go.put(high.at[1], high.at[1], peers[1])]

    def arrived(copies):
        for copy in copies:
            copy.wait_recv()

    near = [both(unit(i, j), one) for i, j, one, two, unit, slab in ways]
    own = [both(unit(i, j), two) for i, j, one, two, unit, slab in ways]
    rows = [go.put(tok, toks.at[p], peer) for peer in ring_y]
    rest = [go.keep(tok, toks.at[p]), go.keep(doc, docs.at[yh])]
    tail = [go.put(doc, docs.at[yh], pair)]
    far = [
        relay(unit(before(i), j), unit(after(i), j), copies, one)
        for (i, j, one, two, unit, slab), copies in zip(ways, near)
    ]
    low = [both(unit(before(i), j), two) for i, j, one, two, unit, slab in ways]
    high = [both(unit(after(i), j), two) for i, j, one, two, unit, slab in ways]
    last = []
    for (i, j, one, two, unit, slab), copies in zip(ways, far):
        arrived(copies)
        last.append(both(unit(across(i), j), two))
        tail.append(go.put(slab(j), slab(j), sibling))
    half = tok.shape[0] // 2
    rows[0].wait_recv()
    piece = toks.at[before(p), pl.ds(0, half)]
    tail.append(go.put(piece, piece, ring_y[0]))
    rows[1].wait_recv()
    piece = toks.at[after(p), pl.ds(half, half)]
    tail.append(go.put(piece, piece, ring_y[1]))
    ends = [[], []]
    for place, copies in ((lambda i: i, own), (before, low), (after, high), (across, last)):
        for n, (i, j, one, two, unit, slab) in enumerate(ways):
            u = place(i)
            ends[n] += relay(unit(u, before(j)), unit(u, after(j)), copies[n], two)
    for i, j, one, two, unit, slab in ways:
        tail.append(go.put(slab(before(j)), slab(before(j)), sibling))
        tail.append(go.put(slab(after(j)), slab(after(j)), sibling))
    for (i, j, one, two, unit, slab), copies in zip(ways, ends):
        arrived(copies)
        tail.append(go.put(slab(across(j)), slab(across(j)), sibling))
    arrived(tail)
    for copy in rest:
        copy.wait()
    go.finish()


def gather(query, key, value, out, tokens, docs):
    rows = query.shape[0]
    width_a = (query.shape[1] + key.shape[1] + value.shape[1]) // NYH
    width_b = out.shape[1] // NYH
    lead = (NX, NYH, NZ, NC, rows)
    wa, wb, toks, docs = pl.pallas_call(
        gather_kernel,
        name="gather_weights",
        cost_estimate=cost(60),
        out_shape=(
            jax.ShapeDtypeStruct((*lead, width_a), BF16),
            jax.ShapeDtypeStruct((*lead, width_b), BF16),
            jax.ShapeDtypeStruct((RING, *tokens.shape), BF16),
            jax.ShapeDtypeStruct((NYH, *docs.shape), docs.dtype),
        ),
        in_specs=[ANY] * 6,
        out_specs=(ANY,) * 4,
        scratch_shapes=[
            pltpu.SemaphoreType.DMA((57,)),
            pltpu.SemaphoreType.DMA((57,)),
            pltpu.SemaphoreType.DMA((6,)),
        ],
        compiler_params=pltpu.CompilerParams(collective_id=1, has_side_effects=True),
    )(query, key, value, out, tokens, docs)
    depth = NX * NYH * NZ * NC * rows
    return (
        wa.reshape(depth, width_a),
        wb.reshape(depth, width_b),
        toks.reshape(RING * tokens.shape[0], tokens.shape[1]),
        docs,
    )


def share_kernel(tok, toks, send, recv, local):
    me = Place()
    p = me.y
    ring = (me.at_y(after(p)), me.at_y(before(p)))
    greet(ring)
    go = Copies(send, recv, local)
    half = tok.shape[0] // 2
    direct = [go.put(tok, toks.at[p], peer) for peer in ring]
    kept = go.keep(tok, toks.at[p])
    relays = []
    for h, owner in enumerate((before(p), after(p))):
        direct[h].wait_recv()
        piece = toks.at[owner, pl.ds(h * half, half)]
        relays.append(go.put(piece, piece, ring[h]))
    for copy in relays:
        copy.wait_recv()
    kept.wait()
    go.finish()


def share(tokens, ident):
    toks = pl.pallas_call(
        share_kernel,
        name=f"share_rows_{ident}",
        cost_estimate=cost(13),
        out_shape=jax.ShapeDtypeStruct((RING, *tokens.shape), tokens.dtype),
        in_specs=[ANY],
        out_specs=ANY,
        scratch_shapes=[
            pltpu.SemaphoreType.DMA((4,)),
            pltpu.SemaphoreType.DMA((4,)),
            pltpu.SemaphoreType.DMA((1,)),
        ],
        compiler_params=pltpu.CompilerParams(collective_id=ident, has_side_effects=True),
    )(tokens)
    return toks.reshape(RING * tokens.shape[0], tokens.shape[1])


def reduce_kernel(part, out, held, own, got, send, recv, local):
    me = Place()
    p = me.y
    ring = (me.at_y(after(p)), me.at_y(before(p)))
    greet(ring)
    go = Copies(send, recv, local)
    half = out.shape[0] // 2
    halves = [pl.ds(h * half, half) for h in range(2)]
    near = (after(p), before(p))
    cross = [go.put(part.at[across(p), halves[h]], got.at[h], ring[h]) for h in range(2)]
    kept = [go.keep(part.at[near[h], halves[h]], held.at[h]) for h in range(2)]
    straight = [go.put(part.at[near[h], halves[1 - h]], got.at[2 + h], ring[h]) for h in range(2)]
    mine = go.keep(part.at[p], own)
    sums = []
    for h in range(2):
        kept[h].wait()
        cross[h].wait_recv()
        held[h] = (held[h].astype(F32) + got[h].astype(F32)).astype(BF16)
        sums.append(go.put(held.at[h], got.at[4 + h], ring[h]))
    mine.wait()
    for copy in straight:
        copy.wait_recv()
    for h in range(2):
        sums[h].wait_recv()
        out[halves[h]] = (
            own[halves[h]].astype(F32) + got[4 + h].astype(F32) + got[3 - h].astype(F32)
        )
    go.finish()


def reduce(part, ident):
    rows, width = part.shape[0] // RING, part.shape[1]
    half = rows // 2
    return pl.pallas_call(
        reduce_kernel,
        name=f"reduce_rows_{ident}",
        cost_estimate=cost(15),
        out_shape=jax.ShapeDtypeStruct((rows, width), F32),
        in_specs=[ANY],
        out_specs=VMEM,
        scratch_shapes=[
            pltpu.VMEM((2, half, width), BF16),
            pltpu.VMEM((rows, width), BF16),
            pltpu.VMEM((6, half, width), BF16),
            pltpu.SemaphoreType.DMA((6,)),
            pltpu.SemaphoreType.DMA((6,)),
            pltpu.SemaphoreType.DMA((3,)),
        ],
        compiler_params=pltpu.CompilerParams(
            collective_id=ident, has_side_effects=True, vmem_limit_bytes=24 << 20
        ),
    )(part.reshape(RING, rows, width))


def scatter_kernel(
    ga, gb, gains, piece, oq, ok, ov, oo, og, op, ka, kb, da, db, ra, rb, qa, qb, sa, sb, ta, tb, ua, ub, ma, mb,
    ring_gains, sum_gains, pair_gains, send, recv, local
):
    me = Place()
    x, yh, z, c, t = me.x, me.yh, me.z, me.c, me.t
    sibling = me.device(c=1 - c)
    pair = me.device(yh=1 - yh)
    partner = me.device(t=1 - t)
    ring_x = (me.device(x=after(x)), me.device(x=before(x)))
    ring_z = (me.device(z=after(z)), me.device(z=before(z)))
    round_x = (*ring_x, me.device(x=across(x)))
    round_z = (*ring_z, me.device(z=across(z)))
    greet([sibling, pair, partner, *round_x, *round_z])
    go = Copies(send, recv, local)

    def around(n, term, own, peers):
        ring_gains[n, own] = term
        return [go.put(ring_gains.at[n, own], ring_gains.at[n, own], peer) for peer in peers]

    def ring_sum(n, copies):
        for copy in copies:
            copy.wait_recv()
        return (ring_gains[n, 0] + ring_gains[n, 1]) + (ring_gains[n, 2] + ring_gains[n, 3])

    def swap(n, term, peer):
        sum_gains[n] = term
        return go.put(sum_gains.at[n], pair_gains.at[n], peer)

    def swapped(n, copy):
        copy.wait_recv()
        return sum_gains[n] + pair_gains[n]


    ways = (
        (lambda i, h, n: ga.at[i, h, :, n], x, z, ring_x, ring_z, ka, da, ra, qa, sa, ta),
        (lambda i, h, n: gb.at[:, h, i, n], z, x, ring_z, ring_x, kb, db, rb, qb, sb, tb),
    )
    places = (across, after, before, lambda i: i)

    def spread(ref, peers):
        return [go.put(ref, ref, peer) for peer in peers]

    def arrived(copies):
        for copy in copies:
            copy.wait_recv()

    given, held = [[], []], [[], []]
    for n, place in enumerate(places):
        for w, (slab, i, j, one, two, k, d, r, q, s, u) in enumerate(ways):
            given[w].append([go.put(slab(place(i), h, 1 - c), d.at[n, h], sibling) for h in range(2)])
            held[w].append([go.keep(slab(place(i), h, c), k.at[n, h]) for h in range(2)])

    def ready(w, n, h):
        given[w][n][h].wait_recv()
        held[w][n][h].wait()

    def total(w, n, h, extra):
        slab, i, j, one, two, k, d, r, q, s, u = ways[w]

        def step(m, _):
            value = k[n, h, m].astype(F32) + d[n, h, m].astype(F32)
            for e in extra:
                value += r[e, m].astype(F32)
            k[n, h, m] = value.astype(BF16)
            return 0

        lax.fori_loop(0, k.shape[2], step, 0)

    terms = around(0, gains[...], x, round_x)
    mine = op.at[x, yh, z, c, t]
    held_piece = go.keep(piece, mine)
    pieces = [go.put(piece, mine, sibling)]
    cross, straight, sums = [[], []], [[], []], [[], []]
    for w, (slab, i, j, one, two, k, d, r, q, s, u) in enumerate(ways):
        for h in range(2):
            ready(w, 0, h)
            total(w, 0, h, ())
            cross[w].append(go.put(k.at[0, h], r.at[h], one[h]))
    for w, (slab, i, j, one, two, k, d, r, q, s, u) in enumerate(ways):
        for h in range(2):
            ready(w, 1 + h, 1 - h)
            total(w, 1 + h, 1 - h, ())
            straight[w].append(go.put(k.at[1 + h, 1 - h], r.at[2 + h], one[h]))
    terms = around(1, ring_sum(0, terms), z, round_z)
    arrived(pieces)
    held_piece.wait()
    pieces = spread(op.at[x, yh, z, :, t], [partner])
    for w, (slab, i, j, one, two, k, d, r, q, s, u) in enumerate(ways):
        for h in range(2):
            ready(w, 1 + h, h)
            cross[w][h].wait_recv()
            total(w, 1 + h, h, (h,))
            sums[w].append(go.put(k.at[1 + h, h], r.at[4 + h], one[h]))
    arrived(pieces)
    pieces = spread(op.at[x, yh, z], [pair])
    terms = swap(0, ring_sum(1, terms), pair)
    for w in range(2):
        for h in range(2):
            ready(w, 3, h)
            straight[w][1 - h].wait_recv()
            total(w, 3, h, (3 - h,))
    arrived(pieces)
    pieces = spread(op.at[x, :, z], round_x)
    terms = swap(1, swapped(0, terms), partner)
    over, direct, final = [[], []], [[], []], [[], []]
    for w, (slab, i, j, one, two, k, d, r, q, s, u) in enumerate(ways):
        near = (after(j), before(j))
        for h in range(2):
            sums[w][h].wait_recv()

            def step(m, _, k=k, r=r, h=h):
                k[3, h, m] = (k[3, h, m].astype(F32) + r[4 + h, m].astype(F32)).astype(BF16)
                return 0

            lax.fori_loop(0, k.shape[2], step, 0)
            over[w].append(go.put(k.at[3, h, across(j)], q.at[h], two[h]))
        for h in range(2):
            direct[w].append(go.put(k.at[3, 1 - h, near[h]], q.at[2 + h], two[h]))
    arrived(pieces)
    pieces = spread(op.at[:, :, z], round_z)
    terms = swap(2, swapped(1, terms), sibling)
    for w, (slab, i, j, one, two, k, d, r, q, s, u) in enumerate(ways):
        near = (after(j), before(j))
        for h in range(2):
            over[w][h].wait_recv()
            s[h] = (k[3, h, near[h]].astype(F32) + q[h].astype(F32)).astype(BF16)
            final[w].append(go.put(s.at[h], q.at[4 + h], two[h]))
    last = []
    for w, ((slab, i, j, one, two, k, d, r, q, s, u), v, m) in enumerate(zip(ways, (ua, ub), (ma, mb))):
        arrived(direct[w])
        arrived(final[w])
        for h in range(2):
            u[h] = k[3, h, j].astype(F32) + q[4 + h].astype(F32) + q[3 - h].astype(F32)
        v[...] = u[1 - yh].astype(BF16)
        last.append(go.put(v, m, pair))
    og[...] = swapped(2, terms)

    def write(head, a, b):
        start = 0
        for out, block in ((oq, a), (ok, a), (ov, a), (oo, b)):
            cols = out.shape[1] // NYH
            at = 0 if block is b else start
            out[:, pl.ds(pl.multiple_of(head * cols, cols), cols)] = block[:, at : at + cols]
            start += cols

    write(yh, ta[yh], tb[yh])
    arrived(last)
    write(1 - yh, ma[...].astype(F32), mb[...].astype(F32))
    arrived(pieces)
    go.finish()


def scatter(grad_a, grad_b, gains, piece, columns):
    rows = grad_a.shape[0] // (NX * NYH * NZ * NC)
    lead = (NX, NYH, NZ, NC, rows)
    widths = (grad_a.shape[1], grad_b.shape[1])

    def each(shape, dtype):
        return [pltpu.VMEM((*shape, rows, w), dtype) for w in widths]

    return pl.pallas_call(
        scatter_kernel,
        name="scatter_weights",
        cost_estimate=cost(80),
        out_shape=(
            *(jax.ShapeDtypeStruct((rows, w), F32) for w in columns),
            jax.ShapeDtypeStruct(gains.shape, F32),
            jax.ShapeDtypeStruct((NX, NYH, NZ, NC, 2, *piece.shape), piece.dtype),
        ),
        in_specs=[ANY, ANY, VMEM, ANY],
        out_specs=(*(VMEM,) * 5, ANY),
        scratch_shapes=[
            *each((4, 2, RING), BF16),
            *each((4, 2, RING), BF16),
            *each((6, RING), BF16),
            *each((6,), BF16),
            *each((2,), BF16),
            *each((2,), F32),
            *each((), BF16),
            *each((), BF16),
            pltpu.VMEM((2, RING, *gains.shape), F32),
            pltpu.VMEM((3, *gains.shape), F32),
            pltpu.VMEM((3, *gains.shape), F32),
            pltpu.SemaphoreType.DMA((60,)),
            pltpu.SemaphoreType.DMA((60,)),
            pltpu.SemaphoreType.DMA((17,)),
        ],
        compiler_params=pltpu.CompilerParams(
            collective_id=5, has_side_effects=True, vmem_limit_bytes=40 << 20
        ),
    )(grad_a.reshape(*lead, widths[0]), grad_b.reshape(*lead, widths[1]), gains, piece)


def unit_rows(values):
    return lax.rsqrt(jnp.mean(values * values, axis=-1, keepdims=True) + EPSILON)


def turn(values, cosine, signed):
    return values * cosine + pltpu.roll(values, values.shape[-1] // 2, 1) * signed


def attend_kernel(scale, raw, bias, cosine, signed, qgain, kgain, query, kv, weights, mixed):
    heads = query.shape[1] // cosine.shape[1]
    hd = cosine.shape[1]
    cos, sig = cosine[...], signed[...]
    key_raw = raw[:, heads * hd : (heads + 1) * hd]
    key = turn(key_raw * unit_rows(key_raw) * kgain[...], cos, sig).astype(BF16)
    value = raw[:, (heads + 1) * hd :].astype(BF16)
    kv[:, :hd] = key
    kv[:, hd:] = value
    for h in range(heads):
        at = slice(h * hd, (h + 1) * hd)
        head = raw[:, at]
        rows = turn(head * unit_rows(head) * qgain[...], cos, sig).astype(BF16)
        query[:, at] = rows
        scores = dot_nt(rows, key) * scale + bias[0]
        peak = jnp.max(scores, axis=-1, keepdims=True)
        weight = jnp.exp(scores - peak)
        weight = weight * (1.0 / jnp.sum(weight, axis=-1, keepdims=True))
        weights[0, h] = weight
        mixed[:, at] = dot_nn(weight.astype(BF16), value).astype(BF16)


def attend(raw, bias, cosine, signed, query_gain, key_gain, scale):
    groups, tokens = bias.shape[0], bias.shape[1]
    hd = cosine.shape[1]
    heads = raw.shape[1] // hd - 2
    rows = groups * tokens

    def block(cols):
        return pl.BlockSpec((tokens, cols), lambda g: (g, 0))

    gain = pl.BlockSpec((1, hd), lambda g: (0, 0))
    square = pl.BlockSpec((1, tokens, tokens), lambda g: (g, 0, 0))
    return pl.pallas_call(
        functools.partial(attend_kernel, scale),
        name="attend",
        cost_estimate=cost(8),
        grid=(groups,),
        out_shape=(
            jax.ShapeDtypeStruct((rows, heads * hd), BF16),
            jax.ShapeDtypeStruct((rows, 2 * hd), BF16),
            jax.ShapeDtypeStruct((groups, heads, tokens, tokens), F32),
            jax.ShapeDtypeStruct((rows, heads * hd), BF16),
        ),
        in_specs=[block((heads + 2) * hd), square, block(hd), block(hd), gain, gain],
        out_specs=(
            block(heads * hd),
            block(2 * hd),
            pl.BlockSpec((1, heads, tokens, tokens), lambda g: (g, 0, 0, 0)),
            block(heads * hd),
        ),
        compiler_params=pltpu.CompilerParams(vmem_limit_bytes=40 << 20),
    )(raw, bias, cosine, signed, query_gain.reshape(1, hd), key_gain.reshape(1, hd))


def norm_back(values, gain, upstream):
    r = unit_rows(values)
    scaled = upstream * gain
    inner = jnp.mean(scaled * values, axis=-1, keepdims=True)
    grad = r * scaled - values * (r * r * r * inner)
    return grad, jnp.sum(upstream * values * r, axis=0, keepdims=True)


def attend_back_kernel(
    scale, raw, cosine, signed, qgain, kgain, query, kv, weights, grad_mixed, grad_raw, grad_gains
):
    hd = cosine.shape[1]
    heads = query.shape[1] // hd
    cos, sig = cosine[...], -signed[...]
    key, value = kv[:, :hd], kv[:, hd:]
    grad_key = jnp.zeros(key.shape, F32)
    grad_value = jnp.zeros(key.shape, F32)
    query_gains = jnp.zeros((1, hd), F32)
    for h in range(heads):
        at = slice(h * hd, (h + 1) * hd)
        weight = weights[0, h]
        grad_head = grad_mixed[:, at]
        grad_value += dot_tn(weight.astype(BF16), grad_head)
        grad_soft = dot_nt(grad_head, value)
        delta = jnp.sum(weight * grad_soft, axis=-1, keepdims=True)
        grad_scores = (weight * (grad_soft - delta)).astype(BF16)
        grad_key += dot_tn(grad_scores, query[:, at])
        turned = turn(dot_nn(grad_scores, key) * scale, cos, sig)
        grad, gains = norm_back(raw[:, at], qgain[...], turned)
        grad_raw[:, at] = grad.astype(BF16)
        query_gains += gains
    at = slice(heads * hd, (heads + 1) * hd)
    grad, key_gains = norm_back(raw[:, at], kgain[...], turn(grad_key * scale, cos, sig))
    grad_raw[:, at] = grad.astype(BF16)
    grad_raw[:, (heads + 1) * hd :] = grad_value.astype(BF16)
    gains = jnp.concatenate([query_gains, key_gains], axis=0)

    @pl.when(pl.program_id(0) == 0)
    def _():
        grad_gains[...] = gains

    @pl.when(pl.program_id(0) > 0)
    def _():
        grad_gains[...] += gains


def attend_back(raw, cosine, signed, query_gain, key_gain, query, kv, weights, grad_mixed, scale):
    groups, heads, tokens, _ = weights.shape
    hd = cosine.shape[1]
    rows = groups * tokens

    def block(cols):
        return pl.BlockSpec((tokens, cols), lambda g: (g, 0))

    gain = pl.BlockSpec((1, hd), lambda g: (0, 0))
    return pl.pallas_call(
        functools.partial(attend_back_kernel, scale),
        name="attend_back",
        cost_estimate=cost(14),
        grid=(groups,),
        out_shape=(
            jax.ShapeDtypeStruct((rows, (heads + 2) * hd), BF16),
            jax.ShapeDtypeStruct((2, hd), F32),
        ),
        in_specs=[
            block((heads + 2) * hd),
            block(hd),
            block(hd),
            gain,
            gain,
            block(heads * hd),
            block(2 * hd),
            pl.BlockSpec((1, heads, tokens, tokens), lambda g: (g, 0, 0, 0)),
            block(heads * hd),
        ],
        out_specs=(block((heads + 2) * hd), pl.BlockSpec((2, hd), lambda g: (0, 0))),
        compiler_params=pltpu.CompilerParams(vmem_limit_bytes=40 << 20),
    )(raw, cosine, signed, query_gain.reshape(1, hd), key_gain.reshape(1, hd), query, kv, weights, grad_mixed)


DIMS = (NX, NYH, NZ, NC, 2)
CHUNKS = (256, 256, 256, 256, 256, 256, 256, 128, 128)
TURNS = ("xzy", "zyx", "yxz")


class Route:
    def __init__(self, me, go):
        x, yh, z, c, t = me.x, me.yh, me.z, me.c, me.t
        steps = (1, 3, 2)
        turn = lambda i, d: lax.rem(i + d, RING)
        self.go = go
        self.own = {"x": (x, c), "z": (z,), "y": (yh, t)}
        self.peers = {
            "x": [((x, 1 - c), me.device(c=1 - c))]
            + [
                ((turn(x, d), e), me.device(x=turn(x, d), c=e))
                for d in steps
                for e in (c, 1 - c)
            ],
            "z": [((turn(z, d),), me.device(z=turn(z, d))) for d in steps],
            "y": [
                ((turn(me.y, d) // 2, lax.rem(turn(me.y, d), 2)), me.at_y(turn(me.y, d)))
                for d in steps
            ],
        }

    def everyone(self):
        return [peer for axis in "xzy" for _, peer in self.peers[axis]]

    @staticmethod
    def view(ref, axis, at):
        if axis == "x":
            return ref.at[at[0], :, :, at[1]]
        if axis == "z":
            return ref.at[:, :, at[0]]
        return ref.at[:, at[0], :, :, at[1]]

    def send(self, axis, src, dst):
        own = self.own[axis]
        kept = self.go.keep(self.view(src, axis, own), self.view(dst, axis, own))
        copies = [
            self.go.put(self.view(src, axis, at), self.view(dst, axis, own), peer)
            for at, peer in self.peers[axis]
        ]
        return kept, copies

    @staticmethod
    def wait(sent):
        kept, copies = sent
        for copy in copies:
            copy.wait_recv()
        kept.wait()


def columns(ref, start, size):
    return ref.at[:, :, :, :, :, :, pl.ds(start, size)]


ORDER = ((0, 0), (1, 0), (0, 1), (2, 0), (1, 1), (0, 2), (2, 1), (1, 2), (2, 2))


def enter_kernel(
    sent, told, gate, up, down, router, rows, gate_pre, up_pre, logits, inner_up,
    *rest,
):
    chunks = len(CHUNKS)
    mids = rest[: 2 * chunks]
    held = rest[2 * chunks : 3 * chunks]
    told_v, gate_v, up_v, down_v, router_v, send, recv, local, loads = rest[3 * chunks :]
    me = Place()
    go = Copies(send, recv, local)
    route = Route(me, go)
    pulls = [
        pltpu.make_async_copy(a, b, loads.at[n])
        for n, (a, b) in enumerate(
            ((told, told_v), (down, down_v), (gate, gate_v), (up, up_v), (router, router_v))
        )
    ]
    for pull in pulls:
        pull.start()
    greet(route.everyone())
    starts = [sum(CHUNKS[:n]) for n in range(chunks)]
    sent_on = [None] * chunks
    width = sent.shape[-1]
    total = told_v.shape[0]
    block = 256

    def cotangent_block(n):
        at = pl.ds(n * block, block)
        inner_up[at] = dot_nt(told_v[at, :width], down_v[...])

    def multiply(n, first):
        cols = pl.ds(starts[n], CHUNKS[n])
        flat = held[n].reshape(total, CHUNKS[n])

        def step(m, _):
            at = pl.ds(pl.multiple_of(m * block, block), block)
            part = flat[at]
            for out, weight in ((gate_pre, gate_v), (up_pre, up_v), (logits, router_v)):
                term = dot_nn(part, weight[cols])
                out[at] = term if first else out[at] + term
            return 0

        lax.fori_loop(0, total // block, step, 0)

    outs = []
    pending = list(range(total // block))
    done = False
    first = True
    for triple, crossing in ORDER:
        for n in range(3 * triple, 3 * triple + 3):
            axis = TURNS[n % 3][crossing]
            src = columns(sent, starts[n], CHUNKS[n]) if crossing == 0 else mids[2 * n + crossing - 1]
            dst = held[n] if crossing == 2 else mids[2 * n + crossing]
            if crossing > 0:
                route.wait(sent_on[n])
            sent_on[n] = route.send(axis, src, dst)
        if (triple, crossing) == (1, 0):
            for pull in pulls[:2]:
                pull.wait()
        if pending and (triple, crossing) not in ((0, 0),):
            cotangent_block(pending.pop(0))
        if (triple, crossing) == (2, 1):
            while pending:
                cotangent_block(pending.pop(0))
            for pull in pulls[2:]:
                pull.wait()
        if (triple, crossing) in ((1, 2), (2, 2)):
            ready = triple - 1
            for n in range(3 * ready, 3 * ready + 3):
                route.wait(sent_on[n])
                outs.append(go.keep(held[n], columns(rows, starts[n], CHUNKS[n])))
                multiply(n, first)
                first = False
    for n in range(chunks - 3, chunks):
        route.wait(sent_on[n])
        outs.append(go.keep(held[n], columns(rows, starts[n], CHUNKS[n])))
        multiply(n, first)
    for out in outs:
        out.wait()
    go.finish()


def enter(sent, told, gate, up, down, router):
    slots, width = sent.shape
    hidden, experts = gate.shape[1], router.shape[1]
    cap = slots // math.prod(DIMS)
    lead = (*DIMS, cap)
    chunks = len(CHUNKS)
    rows, gate_pre, up_pre, logits, inner_up = pl.pallas_call(
        enter_kernel,
        name="enter_experts",
        cost_estimate=cost(60),
        out_shape=(
            jax.ShapeDtypeStruct((*lead, width), BF16),
            jax.ShapeDtypeStruct((slots, hidden), F32),
            jax.ShapeDtypeStruct((slots, hidden), F32),
            jax.ShapeDtypeStruct((slots, experts), F32),
            jax.ShapeDtypeStruct((slots, hidden), F32),
        ),
        in_specs=[ANY] * 6,
        out_specs=(ANY, VMEM, VMEM, VMEM, VMEM),
        scratch_shapes=[
            *(pltpu.VMEM((*lead, w), BF16) for w in CHUNKS for _ in range(2)),
            *(pltpu.VMEM((*lead, w), BF16) for w in CHUNKS),
            pltpu.VMEM(told.shape, BF16),
            pltpu.VMEM(gate.shape, BF16),
            pltpu.VMEM(up.shape, BF16),
            pltpu.VMEM(down.shape, BF16),
            pltpu.VMEM(router.shape, BF16),
            pltpu.SemaphoreType.DMA((13 * chunks,)),
            pltpu.SemaphoreType.DMA((13 * chunks,)),
            pltpu.SemaphoreType.DMA((4 * chunks,)),
            pltpu.SemaphoreType.DMA((5,)),
        ],
        compiler_params=pltpu.CompilerParams(
            collective_id=6, has_side_effects=True, vmem_limit_bytes=58 << 20
        ),
    )(sent.reshape(*lead, width), told, gate, up, down, router)
    return rows.reshape(slots, width), gate_pre, up_pre, logits, inner_up


def on_device(
    hidden_in,
    doc_ids,
    expert_ids,
    attn_gain,
    query_weight,
    key_weight,
    value_weight,
    output_weight,
    query_gain,
    key_gain,
    moe_gain,
    router_weight,
    gate_weight,
    up_weight,
    down_weight,
    cotangent,
):
    both = ("dp", "tensor")
    tok, width = hidden_in.shape
    hd = query_gain.shape[0]
    nkv = key_weight.shape[1] // hd
    nq = query_weight.shape[1] // hd
    group = nq // nkv
    experts = router_weight.shape[1]
    routes = expert_ids.shape[1]
    cap = tok * routes // experts
    slots = experts * cap
    scale = 1.0 / math.sqrt(hd)
    tokens = doc_ids.shape[1]
    me = lax.axis_index(both)

    lane = lax.broadcasted_iota(jnp.int32, (1, 1, experts), 2)
    chosen = jnp.sum((expert_ids[:, :, None] == lane).astype(F32), axis=1)
    below = (
        lax.broadcasted_iota(jnp.int32, (tok, tok), 1)
        < lax.broadcasted_iota(jnp.int32, (tok, tok), 0)
    ).astype(BF16)
    rank = dot_nn(below, chosen.astype(BF16))
    place = jnp.where(chosen > 0, rank, -1.0).T
    spread = (
        place[:, None, :] == lax.broadcasted_iota(jnp.int32, (1, cap, 1), 1).astype(F32)
    ).astype(BF16).reshape(slots, tok)

    hidden = hidden_in.astype(F32)
    normed_local = rms_scale(hidden, attn_gain).astype(BF16)

    in_weights, out_weights, normed, docs = gather(
        query_weight,
        key_weight,
        value_weight,
        output_weight.T,
        normed_local,
        jnp.broadcast_to(doc_ids, (8, tokens)).astype(F32),
    )

    spread_late, docs = lax.optimization_barrier((spread, docs))
    cot_out = dot_nn(spread_late, jnp.concatenate([cotangent, chosen.astype(BF16)], axis=1)).astype(BF16)
    cot_in = lax.all_to_all(
        cot_out.reshape(experts, cap, width + experts), both, split_axis=0, concat_axis=0, tiled=True
    ).reshape(slots, width + experts)

    position, allowed = jax.vmap(layout)(docs[:, 0])
    cosine, sine = rotary(position.reshape(-1), hd)
    cosine = jnp.concatenate([cosine, cosine], axis=1)
    signed = jnp.concatenate([-sine, sine], axis=1)
    bias = jnp.where(allowed, 0.0, MASKED).astype(F32)
    raw = dot_nn(normed, in_weights)
    heads = group * hd
    query, kv, attention, mixed = attend(raw, bias, cosine, signed, query_gain, key_gain, scale)
    attn_out = reduce(dot_nt(mixed, out_weights).astype(BF16), 2)

    residual = hidden + attn_out
    moe_input = rms_scale(residual, moe_gain).astype(BF16)
    moe_input, cot_in = lax.optimization_barrier((moe_input, cot_in))
    sent = dot_nn(spread, moe_input).astype(BF16)
    gate_mat, up_mat, down_mat = gate_weight[0], up_weight[0], down_weight[0]
    rows, gate_pre, up_pre, row_logits, inner_up = enter(
        sent, cot_in, gate_mat, up_mat, down_mat, router_weight
    )
    logits = dot_nn(moe_input, router_weight)
    masked = jnp.where(chosen > 0, logits, MASKED)
    probs = jnp.exp(masked - jnp.max(masked, axis=-1, keepdims=True))
    probs = probs / jnp.sum(probs, axis=-1, keepdims=True)

    cot_rows = cot_in[:, :width]
    row_logits = jnp.where(cot_in[:, width:] > 0, row_logits, MASKED)
    row_probs = jnp.exp(row_logits - jnp.max(row_logits, axis=-1, keepdims=True))
    mine = lax.broadcasted_iota(jnp.int32, (1, experts), 1) == me
    prob = jnp.sum(jnp.where(mine, row_probs, 0.0), axis=-1, keepdims=True) / jnp.sum(
        row_probs, axis=-1, keepdims=True
    )
    sigmoid = jax.nn.sigmoid(gate_pre)
    silu = gate_pre * sigmoid
    inner = silu * up_pre
    gate_up = jnp.sum(inner * inner_up, axis=-1, keepdims=True)
    inner_low = (prob * inner).astype(BF16)
    grad_inner = prob * inner_up
    grad_gate = (grad_inner * up_pre * sigmoid * (1.0 + gate_pre * (1.0 - sigmoid))).astype(BF16)
    grad_up = (grad_inner * silu).astype(BF16)
    grad_rows = (dot_nt(grad_gate, gate_mat) + dot_nt(grad_up, up_mat)).astype(BF16)
    gate_up_high = gate_up.astype(BF16)
    gate_up_rest = (gate_up - gate_up_high.astype(F32)).astype(BF16)
    none = jnp.zeros((), BF16)
    home_out = jnp.concatenate(
        [grad_rows, jnp.where(mine, gate_up_high, none), jnp.where(mine, gate_up_rest, none)], axis=1
    )
    home = lax.all_to_all(
        home_out.reshape(experts, cap, width + 2 * experts), both, split_axis=0, concat_axis=0, tiled=True
    ).reshape(slots, width + 2 * experts)
    expert_out = dot_nn(inner_low, down_mat).astype(BF16)
    down_grad = dot_tn(inner_low, cot_rows)
    gate_grad = dot_tn(rows, grad_gate)
    up_grad = dot_tn(rows, grad_up)
    home, down_grad, gate_grad, up_grad = lax.optimization_barrier(
        (home, down_grad, gate_grad, up_grad)
    )

    upstream = cotangent.astype(F32)
    summed = dot_tn(spread, home)
    gate_upstream = summed[:, width : width + experts] + summed[:, width + experts :]
    grad_chosen = probs * (gate_upstream - jnp.sum(probs * gate_upstream, axis=-1, keepdims=True))
    grad_logits = grad_chosen.astype(BF16)
    grad_moe_input = summed[:, :width] + dot_nt(grad_logits, router_weight)
    router_part = dot_tn(moe_input, grad_logits)
    grad_norm, moegain_rows = rms_back(residual, moe_gain, grad_moe_input)
    moegain_part = jnp.sum(moegain_rows, axis=0)
    grad_residual = upstream + grad_norm
    grad_attn = share(grad_residual.astype(BF16), 3)
    pieces = router_part.astype(BF16).reshape(experts, width // experts, experts)
    piece = jnp.sum(lax.all_to_all(pieces, both, 0, 0, tiled=True).astype(F32), axis=0)
    expert_out, grad_attn, piece = lax.optimization_barrier((expert_out, grad_attn, piece))
    returned = lax.all_to_all(
        expert_out.reshape(experts, cap, width), both, split_axis=0, concat_axis=0, tiled=True
    ).reshape(slots, width)

    grad_mixed = dot_nn(grad_attn, out_weights).astype(BF16)
    grad_raw, head_gains = attend_back(
        raw, cosine, signed, query_gain, key_gain, query, kv, attention, grad_mixed, scale
    )
    grad_normed = reduce(dot_nt(grad_raw, in_weights).astype(BF16), 4)
    grad_hidden, attngain_rows = rms_back(hidden, attn_gain, grad_normed)
    input_grad = grad_residual + grad_hidden

    gains = jnp.concatenate([jnp.sum(attngain_rows, axis=0), moegain_part]).reshape(-1, hd)
    gains = jnp.concatenate([gains, head_gains, jnp.zeros((6, hd), F32)], axis=0)

    layer_out = (residual + dot_tn(spread, returned)).astype(BF16)
    query_grad, key_grad, value_grad, out_grad, gains, router_grad = scatter(
        dot_tn(normed, grad_raw).astype(BF16),
        dot_tn(grad_attn, mixed).astype(BF16),
        gains,
        piece.astype(BF16),
        (nq * hd, nkv * hd, nkv * hd, nq * hd),
    )
    at = width // hd
    return (
        layer_out,
        input_grad,
        gains[:at].reshape(-1),
        query_grad,
        key_grad,
        value_grad,
        out_grad.T,
        gains[2 * at],
        gains[2 * at + 1],
        gains[at : 2 * at].reshape(-1),
        router_grad.reshape(width, experts).astype(F32),
        gate_grad[None],
        up_grad[None],
        down_grad[None],
    )


def solution(mesh):
    both = ("dp", "tensor")
    in_specs = (
        P(both, None),
        P("dp", None),
        P(both, None),
        P(),
        P("dp", "tensor"),
        P("dp", "tensor"),
        P("dp", "tensor"),
        P("tensor", "dp"),
        P(),
        P(),
        P(),
        P(),
        P(both, None, None),
        P(both, None, None),
        P(both, None, None),
        P(both, None),
    )
    out_specs = (
        P(both, None),
        P(both, None),
        P(),
        P("dp", "tensor"),
        P("dp", "tensor"),
        P("dp", "tensor"),
        P("tensor", "dp"),
        P(),
        P(),
        P(),
        P(),
        P(both, None, None),
        P(both, None, None),
        P(both, None, None),
    )
    return jax.shard_map(
        on_device, mesh=mesh, in_specs=in_specs, out_specs=out_specs, check_vma=False
    )
```

```python
import functools
import math

import jax
import jax.numpy as jnp
from jax import lax
from jax.experimental import pallas as pl
from jax.experimental.pallas import tpu as pltpu
from jax.sharding import PartitionSpec as P

BLOCK = 128
EPSILON = 1e-06
ROPE_BASE = 1000000.0
MASKED = -1e30
F32 = jnp.float32
BF16 = jnp.bfloat16


def dot_nt(a, b):
    return lax.dot_general(a, b, (((1,), (1,)), ((), ())), preferred_element_type=F32)


def dot_tn(a, b):
    return lax.dot_general(a, b, (((0,), (0,)), ((), ())), preferred_element_type=F32)


def dot_nn(a, b):
    return lax.dot_general(a, b, (((1,), (0,)), ((), ())), preferred_element_type=F32)


def rms_recip(values):
    return lax.rsqrt(jnp.mean(values * values, axis=-1, keepdims=True) + EPSILON)


def rms_scale(values, gain):
    return values * rms_recip(values) * gain


def rms_back(values, gain, upstream):
    r = rms_recip(values)
    scaled = upstream * gain
    inner = jnp.mean(scaled * values, axis=-1, keepdims=True)
    grad_values = r * scaled - values * (r * r * r) * inner
    return grad_values, upstream * values * r


def rotate(values, cosine, sine):
    half = values.shape[-1] // 2
    a = values[..., :half]
    b = values[..., half:]
    return jnp.concatenate([a * cosine - b * sine, b * cosine + a * sine], axis=-1)


def layout(doc_row):
    length = doc_row.shape[0]
    indices = jnp.arange(length, dtype=jnp.int32)
    same_doc = doc_row[:, None] == doc_row[None, :]
    earlier = indices[None, :] < indices[:, None]
    position = jnp.sum(jnp.where(same_doc & earlier, 1, 0), axis=1).astype(jnp.int32)
    blocks = position // BLOCK
    allowed = same_doc & (blocks[None, :] <= blocks[:, None])
    return position, allowed


def rotary(position, head_size):
    half = head_size // 2
    frequency = jnp.exp(-jnp.log(ROPE_BASE) * jnp.arange(half, dtype=F32) * 2.0 / head_size)
    angles = position.astype(F32)[:, None] * frequency[None, :]
    return jnp.cos(angles), jnp.sin(angles)


MESH = pl.DeviceIdType.MESH
ANY = pl.BlockSpec(memory_space=pl.ANY)
VMEM = pl.BlockSpec(memory_space=pltpu.VMEM)
NX, NYH, NZ, NC = 4, 2, 4, 2
RING = 4


def cost(microseconds):
    return pl.CostEstimate(flops=0, transcendentals=0, bytes_accessed=int(microseconds * 3.6e6))


class Place:
    def __init__(self):
        dp = lax.axis_index("dp")
        self.t = lax.axis_index("tensor")
        self.c = lax.rem(dp, NC)
        self.z = lax.rem(dp // NC, NZ)
        self.yh = lax.rem(dp // (NC * NZ), NYH)
        self.x = dp // (NC * NZ * NYH)
        self.y = self.yh * 2 + self.t

    def device(self, x=None, yh=None, z=None, c=None, t=None):
        pick = lambda given, own: own if given is None else given
        x, yh, z, c = pick(x, self.x), pick(yh, self.yh), pick(z, self.z), pick(c, self.c)
        return (((x * NYH + yh) * NZ + z) * NC + c, pick(t, self.t))

    def expert(self):
        return ((((self.x * NYH + self.yh) * NZ + self.z) * NC) + self.c) * 2 + self.t

    def at_y(self, y):
        return self.device(yh=y // 2, t=lax.rem(y, 2))


def after(i):
    return lax.rem(i + 1, RING)


def before(i):
    return lax.rem(i + RING - 1, RING)


def across(i):
    return lax.rem(i + 2, RING)


def greet(peers):
    barrier = pltpu.get_barrier_semaphore()
    for peer in peers:
        pl.semaphore_signal(barrier, inc=1, device_id=peer, device_id_type=MESH)
    pl.semaphore_wait(barrier, len(peers))


class Copies:
    def __init__(self, send, recv, local):
        self.send, self.recv, self.local = send, recv, local
        self.n = self.m = 0
        self.sent = []

    def put(self, src, dst, peer):
        copy = pltpu.make_async_remote_copy(
            src_ref=src,
            dst_ref=dst,
            send_sem=self.send.at[self.n],
            recv_sem=self.recv.at[self.n],
            device_id=peer,
            device_id_type=MESH,
        )
        self.n += 1
        copy.start()
        self.sent.append(copy)
        return copy

    def keep(self, src, dst):
        copy = pltpu.make_async_copy(src, dst, self.local.at[self.m])
        self.m += 1
        copy.start()
        return copy

    def finish(self):
        for copy in self.sent:
            copy.wait_send()


def gather_kernel(q, k, v, o, tok, doc, wa, wb, toks, docs, send, recv, local):
    me = Place()
    x, yh, z, c, p = me.x, me.yh, me.z, me.c, me.y
    sibling = me.device(c=1 - c)
    pair = me.device(yh=1 - yh)
    ring_x = (me.device(x=after(x)), me.device(x=before(x)))
    ring_z = (me.device(z=after(z)), me.device(z=before(z)))
    ring_y = (me.at_y(after(p)), me.at_y(before(p)))
    greet([sibling, pair, *ring_x, *ring_z, *ring_y])
    go = Copies(send, recv, local)

    shards, start = [], 0
    for ref, w in ((q, wa), (k, wa), (v, wa), (o, wb)):
        cols = ref.shape[1] // NYH
        to = w.at[x, yh, z, c, :, pl.ds(0 if w is wb else start, cols)]
        shards.append((ref, cols, to))
        start += cols

    def part(ref, cols, head):
        return ref.at[:, pl.ds(pl.multiple_of(head * cols, cols), cols)]

    pairs = [go.put(part(ref, cols, 1 - yh), to, pair) for ref, cols, to in shards]
    kept = [go.keep(part(ref, cols, yh), to) for ref, cols, to in shards]
    for copy in kept:
        copy.wait()
    for copy in pairs:
        copy.wait_recv()

    ways = (
        (x, z, ring_x, ring_z, lambda i, j: wa.at[i, :, j, c], lambda j: wa.at[:, :, j, c]),
        (z, x, ring_z, ring_x, lambda i, j: wb.at[j, :, i, c], lambda j: wb.at[j, :, :, c]),
    )

    def both(ref, peers):
        return [go.put(ref, ref, peer) for peer in peers]

    def relay(low, high, copies, peers):
        copies[0].wait_recv()
        up = go.put(low.at[0], low.at[0], peers[0])
        copies[1].wait_recv()
        return [up, go.put(high.at[1], high.at[1], peers[1])]

    def arrived(copies):
        for copy in copies:
            copy.wait_recv()

    near = [both(unit(i, j), one) for i, j, one, two, unit, slab in ways]
    own = [both(unit(i, j), two) for i, j, one, two, unit, slab in ways]
    rows = [go.put(tok, toks.at[p], peer) for peer in ring_y]
    rest = [go.keep(tok, toks.at[p]), go.keep(doc, docs.at[yh])]
    tail = [go.put(doc, docs.at[yh], pair)]
    far = [
        relay(unit(before(i), j), unit(after(i), j), copies, one)
        for (i, j, one, two, unit, slab), copies in zip(ways, near)
    ]
    low = [both(unit(before(i), j), two) for i, j, one, two, unit, slab in ways]
    high = [both(unit(after(i), j), two) for i, j, one, two, unit, slab in ways]
    last = []
    for (i, j, one, two, unit, slab), copies in zip(ways, far):
        arrived(copies)
        last.append(both(unit(across(i), j), two))
        tail.append(go.put(slab(j), slab(j), sibling))
    half = tok.shape[0] // 2
    rows[0].wait_recv()
    piece = toks.at[before(p), pl.ds(0, half)]
    tail.append(go.put(piece, piece, ring_y[0]))
    rows[1].wait_recv()
    piece = toks.at[after(p), pl.ds(half, half)]
    tail.append(go.put(piece, piece, ring_y[1]))
    ends = [[], []]
    for place, copies in ((lambda i: i, own), (before, low), (after, high), (across, last)):
        for n, (i, j, one, two, unit, slab) in enumerate(ways):
            u = place(i)
            ends[n] += relay(unit(u, before(j)), unit(u, after(j)), copies[n], two)
    for i, j, one, two, unit, slab in ways:
        tail.append(go.put(slab(before(j)), slab(before(j)), sibling))
        tail.append(go.put(slab(after(j)), slab(after(j)), sibling))
    for (i, j, one, two, unit, slab), copies in zip(ways, ends):
        arrived(copies)
        tail.append(go.put(slab(across(j)), slab(across(j)), sibling))
    arrived(tail)
    for copy in rest:
        copy.wait()
    go.finish()


def gather(query, key, value, out, tokens, docs):
    rows = query.shape[0]
    width_a = (query.shape[1] + key.shape[1] + value.shape[1]) // NYH
    width_b = out.shape[1] // NYH
    lead = (NX, NYH, NZ, NC, rows)
    wa, wb, toks, docs = pl.pallas_call(
        gather_kernel,
        name="gather_weights",
        cost_estimate=cost(60),
        out_shape=(
            jax.ShapeDtypeStruct((*lead, width_a), BF16),
            jax.ShapeDtypeStruct((*lead, width_b), BF16),
            jax.ShapeDtypeStruct((RING, *tokens.shape), BF16),
            jax.ShapeDtypeStruct((NYH, *docs.shape), docs.dtype),
        ),
        in_specs=[ANY] * 6,
        out_specs=(ANY,) * 4,
        scratch_shapes=[
            pltpu.SemaphoreType.DMA((57,)),
            pltpu.SemaphoreType.DMA((57,)),
            pltpu.SemaphoreType.DMA((6,)),
        ],
        compiler_params=pltpu.CompilerParams(collective_id=1, has_side_effects=True),
    )(query, key, value, out, tokens, docs)
    depth = NX * NYH * NZ * NC * rows
    return (
        wa.reshape(depth, width_a),
        wb.reshape(depth, width_b),
        toks.reshape(RING * tokens.shape[0], tokens.shape[1]),
        docs,
    )


def share_kernel(tok, toks, send, recv, local):
    me = Place()
    p = me.y
    ring = (me.at_y(after(p)), me.at_y(before(p)))
    greet(ring)
    go = Copies(send, recv, local)
    half = tok.shape[0] // 2
    direct = [go.put(tok, toks.at[p], peer) for peer in ring]
    kept = go.keep(tok, toks.at[p])
    relays = []
    for h, owner in enumerate((before(p), after(p))):
        direct[h].wait_recv()
        piece = toks.at[owner, pl.ds(h * half, half)]
        relays.append(go.put(piece, piece, ring[h]))
    for copy in relays:
        copy.wait_recv()
    kept.wait()
    go.finish()


def share(tokens, ident):
    toks = pl.pallas_call(
        share_kernel,
        name=f"share_rows_{ident}",
        cost_estimate=cost(13),
        out_shape=jax.ShapeDtypeStruct((RING, *tokens.shape), tokens.dtype),
        in_specs=[ANY],
        out_specs=ANY,
        scratch_shapes=[
            pltpu.SemaphoreType.DMA((4,)),
            pltpu.SemaphoreType.DMA((4,)),
            pltpu.SemaphoreType.DMA((1,)),
        ],
        compiler_params=pltpu.CompilerParams(collective_id=ident, has_side_effects=True),
    )(tokens)
    return toks.reshape(RING * tokens.shape[0], tokens.shape[1])


def reduce_kernel(part, out, held, own, got, send, recv, local):
    me = Place()
    p = me.y
    ring = (me.at_y(after(p)), me.at_y(before(p)))
    greet(ring)
    go = Copies(send, recv, local)
    half = out.shape[0] // 2
    halves = [pl.ds(h * half, half) for h in range(2)]
    near = (after(p), before(p))
    cross = [go.put(part.at[across(p), halves[h]], got.at[h], ring[h]) for h in range(2)]
    kept = [go.keep(part.at[near[h], halves[h]], held.at[h]) for h in range(2)]
    straight = [go.put(part.at[near[h], halves[1 - h]], got.at[2 + h], ring[h]) for h in range(2)]
    mine = go.keep(part.at[p], own)
    sums = []
    for h in range(2):
        kept[h].wait()
        cross[h].wait_recv()
        held[h] = (held[h].astype(F32) + got[h].astype(F32)).astype(BF16)
        sums.append(go.put(held.at[h], got.at[4 + h], ring[h]))
    mine.wait()
    for copy in straight:
        copy.wait_recv()
    for h in range(2):
        sums[h].wait_recv()
        out[halves[h]] = (
            own[halves[h]].astype(F32) + got[4 + h].astype(F32) + got[3 - h].astype(F32)
        )
    go.finish()


def reduce(part, ident):
    rows, width = part.shape[0] // RING, part.shape[1]
    half = rows // 2
    return pl.pallas_call(
        reduce_kernel,
        name=f"reduce_rows_{ident}",
        cost_estimate=cost(15),
        out_shape=jax.ShapeDtypeStruct((rows, width), F32),
        in_specs=[ANY],
        out_specs=VMEM,
        scratch_shapes=[
            pltpu.VMEM((2, half, width), BF16),
            pltpu.VMEM((rows, width), BF16),
            pltpu.VMEM((6, half, width), BF16),
            pltpu.SemaphoreType.DMA((6,)),
            pltpu.SemaphoreType.DMA((6,)),
            pltpu.SemaphoreType.DMA((3,)),
        ],
        compiler_params=pltpu.CompilerParams(
            collective_id=ident, has_side_effects=True, vmem_limit_bytes=24 << 20
        ),
    )(part.reshape(RING, rows, width))


def scatter_kernel(
    ga, gb, gains, piece, oq, ok, ov, oo, og, op, ka, kb, da, db, ra, rb, qa, qb, sa, sb, ta, tb, ua, ub, ma, mb,
    ring_gains, sum_gains, pair_gains, send, recv, local
):
    me = Place()
    x, yh, z, c, t = me.x, me.yh, me.z, me.c, me.t
    sibling = me.device(c=1 - c)
    pair = me.device(yh=1 - yh)
    partner = me.device(t=1 - t)
    ring_x = (me.device(x=after(x)), me.device(x=before(x)))
    ring_z = (me.device(z=after(z)), me.device(z=before(z)))
    round_x = (*ring_x, me.device(x=across(x)))
    round_z = (*ring_z, me.device(z=across(z)))
    greet([sibling, pair, partner, *round_x, *round_z])
    go = Copies(send, recv, local)

    def around(n, term, own, peers):
        ring_gains[n, own] = term
        return [go.put(ring_gains.at[n, own], ring_gains.at[n, own], peer) for peer in peers]

    def ring_sum(n, copies):
        for copy in copies:
            copy.wait_recv()
        return (ring_gains[n, 0] + ring_gains[n, 1]) + (ring_gains[n, 2] + ring_gains[n, 3])

    def swap(n, term, peer):
        sum_gains[n] = term
        return go.put(sum_gains.at[n], pair_gains.at[n], peer)

    def swapped(n, copy):
        copy.wait_recv()
        return sum_gains[n] + pair_gains[n]


    ways = (
        (lambda i, h, n: ga.at[i, h, :, n], x, z, ring_x, ring_z, ka, da, ra, qa, sa, ta),
        (lambda i, h, n: gb.at[:, h, i, n], z, x, ring_z, ring_x, kb, db, rb, qb, sb, tb),
    )
    places = (across, after, before, lambda i: i)

    def spread(ref, peers):
        return [go.put(ref, ref, peer) for peer in peers]

    def arrived(copies):
        for copy in copies:
            copy.wait_recv()

    given, held = [[], []], [[], []]
    for n, place in enumerate(places):
        for w, (slab, i, j, one, two, k, d, r, q, s, u) in enumerate(ways):
            given[w].append([go.put(slab(place(i), h, 1 - c), d.at[n, h], sibling) for h in range(2)])
            held[w].append([go.keep(slab(place(i), h, c), k.at[n, h]) for h in range(2)])

    def ready(w, n, h):
        given[w][n][h].wait_recv()
        held[w][n][h].wait()

    def total(w, n, h, extra):
        slab, i, j, one, two, k, d, r, q, s, u = ways[w]

        def step(m, _):
            value = k[n, h, m].astype(F32) + d[n, h, m].astype(F32)
            for e in extra:
                value += r[e, m].astype(F32)
            k[n, h, m] = value.astype(BF16)
            return 0

        lax.fori_loop(0, k.shape[2], step, 0)

    terms = around(0, gains[...], x, round_x)
    mine = op.at[x, yh, z, c, t]
    held_piece = go.keep(piece, mine)
    pieces = [go.put(piece, mine, sibling)]
    cross, straight, sums = [[], []], [[], []], [[], []]
    for w, (slab, i, j, one, two, k, d, r, q, s, u) in enumerate(ways):
        for h in range(2):
            ready(w, 0, h)
            total(w, 0, h, ())
            cross[w].append(go.put(k.at[0, h], r.at[h], one[h]))
    for w, (slab, i, j, one, two, k, d, r, q, s, u) in enumerate(ways):
        for h in range(2):
            ready(w, 1 + h, 1 - h)
            total(w, 1 + h, 1 - h, ())
            straight[w].append(go.put(k.at[1 + h, 1 - h], r.at[2 + h], one[h]))
    terms = around(1, ring_sum(0, terms), z, round_z)
    arrived(pieces)
    held_piece.wait()
    pieces = spread(op.at[x, yh, z, :, t], [partner])
    for w, (slab, i, j, one, two, k, d, r, q, s, u) in enumerate(ways):
        for h in range(2):
            ready(w, 1 + h, h)
            cross[w][h].wait_recv()
            total(w, 1 + h, h, (h,))
            sums[w].append(go.put(k.at[1 + h, h], r.at[4 + h], one[h]))
    arrived(pieces)
    pieces = spread(op.at[x, yh, z], [pair])
    terms = swap(0, ring_sum(1, terms), pair)
    for w in range(2):
        for h in range(2):
            ready(w, 3, h)
            straight[w][1 - h].wait_recv()
            total(w, 3, h, (3 - h,))
    arrived(pieces)
    pieces = spread(op.at[x, :, z], round_x)
    terms = swap(1, swapped(0, terms), partner)
    over, direct, final = [[], []], [[], []], [[], []]
    for w, (slab, i, j, one, two, k, d, r, q, s, u) in enumerate(ways):
        near = (after(j), before(j))
        for h in range(2):
            sums[w][h].wait_recv()

            def step(m, _, k=k, r=r, h=h):
                k[3, h, m] = (k[3, h, m].astype(F32) + r[4 + h, m].astype(F32)).astype(BF16)
                return 0

            lax.fori_loop(0, k.shape[2], step, 0)
            over[w].append(go.put(k.at[3, h, across(j)], q.at[h], two[h]))
        for h in range(2):
            direct[w].append(go.put(k.at[3, 1 - h, near[h]], q.at[2 + h], two[h]))
    arrived(pieces)
    pieces = spread(op.at[:, :, z], round_z)
    terms = swap(2, swapped(1, terms), sibling)
    for w, (slab, i, j, one, two, k, d, r, q, s, u) in enumerate(ways):
        near = (after(j), before(j))
        for h in range(2):
            over[w][h].wait_recv()
            s[h] = (k[3, h, near[h]].astype(F32) + q[h].astype(F32)).astype(BF16)
            final[w].append(go.put(s.at[h], q.at[4 + h], two[h]))
    last = []
    for w, ((slab, i, j, one, two, k, d, r, q, s, u), v, m) in enumerate(zip(ways, (ua, ub), (ma, mb))):
        arrived(direct[w])
        arrived(final[w])
        for h in range(2):
            u[h] = k[3, h, j].astype(F32) + q[4 + h].astype(F32) + q[3 - h].astype(F32)
        v[...] = u[1 - yh].astype(BF16)
        last.append(go.put(v, m, pair))
    og[...] = swapped(2, terms)

    def write(head, a, b):
        start = 0
        for out, block in ((oq, a), (ok, a), (ov, a), (oo, b)):
            cols = out.shape[1] // NYH
            at = 0 if block is b else start
            out[:, pl.ds(pl.multiple_of(head * cols, cols), cols)] = block[:, at : at + cols]
            start += cols

    write(yh, ta[yh], tb[yh])
    arrived(last)
    write(1 - yh, ma[...].astype(F32), mb[...].astype(F32))
    arrived(pieces)
    go.finish()


def scatter(grad_a, grad_b, gains, piece, columns):
    rows = grad_a.shape[0] // (NX * NYH * NZ * NC)
    lead = (NX, NYH, NZ, NC, rows)
    widths = (grad_a.shape[1], grad_b.shape[1])

    def each(shape, dtype):
        return [pltpu.VMEM((*shape, rows, w), dtype) for w in widths]

    return pl.pallas_call(
        scatter_kernel,
        name="scatter_weights",
        cost_estimate=cost(80),
        out_shape=(
            *(jax.ShapeDtypeStruct((rows, w), F32) for w in columns),
            jax.ShapeDtypeStruct(gains.shape, F32),
            jax.ShapeDtypeStruct((NX, NYH, NZ, NC, 2, *piece.shape), piece.dtype),
        ),
        in_specs=[ANY, ANY, VMEM, ANY],
        out_specs=(*(VMEM,) * 5, ANY),
        scratch_shapes=[
            *each((4, 2, RING), BF16),
            *each((4, 2, RING), BF16),
            *each((6, RING), BF16),
            *each((6,), BF16),
            *each((2,), BF16),
            *each((2,), F32),
            *each((), BF16),
            *each((), BF16),
            pltpu.VMEM((2, RING, *gains.shape), F32),
            pltpu.VMEM((3, *gains.shape), F32),
            pltpu.VMEM((3, *gains.shape), F32),
            pltpu.SemaphoreType.DMA((60,)),
            pltpu.SemaphoreType.DMA((60,)),
            pltpu.SemaphoreType.DMA((17,)),
        ],
        compiler_params=pltpu.CompilerParams(
            collective_id=5, has_side_effects=True, vmem_limit_bytes=40 << 20
        ),
    )(grad_a.reshape(*lead, widths[0]), grad_b.reshape(*lead, widths[1]), gains, piece)


def unit_rows(values):
    return lax.rsqrt(jnp.mean(values * values, axis=-1, keepdims=True) + EPSILON)


def turn(values, cosine, signed):
    return values * cosine + pltpu.roll(values, values.shape[-1] // 2, 1) * signed


def attend_kernel(scale, raw, bias, cosine, signed, qgain, kgain, query, kv, weights, mixed):
    heads = query.shape[1] // cosine.shape[1]
    hd = cosine.shape[1]
    cos, sig = cosine[...], signed[...]
    key_raw = raw[:, heads * hd : (heads + 1) * hd]
    key = turn(key_raw * unit_rows(key_raw) * kgain[...], cos, sig).astype(BF16)
    value = raw[:, (heads + 1) * hd :].astype(BF16)
    kv[:, :hd] = key
    kv[:, hd:] = value
    for h in range(heads):
        at = slice(h * hd, (h + 1) * hd)
        head = raw[:, at]
        rows = turn(head * unit_rows(head) * qgain[...], cos, sig).astype(BF16)
        query[:, at] = rows
        scores = dot_nt(rows, key) * scale + bias[0]
        peak = jnp.max(scores, axis=-1, keepdims=True)
        weight = jnp.exp(scores - peak)
        weight = weight * (1.0 / jnp.sum(weight, axis=-1, keepdims=True))
        weights[0, h] = weight
        mixed[:, at] = dot_nn(weight.astype(BF16), value).astype(BF16)


def attend(raw, bias, cosine, signed, query_gain, key_gain, scale):
    groups, tokens = bias.shape[0], bias.shape[1]
    hd = cosine.shape[1]
    heads = raw.shape[1] // hd - 2
    rows = groups * tokens

    def block(cols):
        return pl.BlockSpec((tokens, cols), lambda g: (g, 0))

    gain = pl.BlockSpec((1, hd), lambda g: (0, 0))
    square = pl.BlockSpec((1, tokens, tokens), lambda g: (g, 0, 0))
    return pl.pallas_call(
        functools.partial(attend_kernel, scale),
        name="attend",
        cost_estimate=cost(8),
        grid=(groups,),
        out_shape=(
            jax.ShapeDtypeStruct((rows, heads * hd), BF16),
            jax.ShapeDtypeStruct((rows, 2 * hd), BF16),
            jax.ShapeDtypeStruct((groups, heads, tokens, tokens), F32),
            jax.ShapeDtypeStruct((rows, heads * hd), BF16),
        ),
        in_specs=[block((heads + 2) * hd), square, block(hd), block(hd), gain, gain],
        out_specs=(
            block(heads * hd),
            block(2 * hd),
            pl.BlockSpec((1, heads, tokens, tokens), lambda g: (g, 0, 0, 0)),
            block(heads * hd),
        ),
        compiler_params=pltpu.CompilerParams(vmem_limit_bytes=40 << 20),
    )(raw, bias, cosine, signed, query_gain.reshape(1, hd), key_gain.reshape(1, hd))


def norm_back(values, gain, upstream):
    r = unit_rows(values)
    scaled = upstream * gain
    inner = jnp.mean(scaled * values, axis=-1, keepdims=True)
    grad = r * scaled - values * (r * r * r * inner)
    return grad, jnp.sum(upstream * values * r, axis=0, keepdims=True)


def attend_back_kernel(
    scale, raw, cosine, signed, qgain, kgain, query, kv, weights, grad_mixed, grad_raw, grad_gains
):
    hd = cosine.shape[1]
    heads = query.shape[1] // hd
    cos, sig = cosine[...], -signed[...]
    key, value = kv[:, :hd], kv[:, hd:]
    grad_key = jnp.zeros(key.shape, F32)
    grad_value = jnp.zeros(key.shape, F32)
    query_gains = jnp.zeros((1, hd), F32)
    for h in range(heads):
        at = slice(h * hd, (h + 1) * hd)
        weight = weights[0, h]
        grad_head = grad_mixed[:, at]
        grad_value += dot_tn(weight.astype(BF16), grad_head)
        grad_soft = dot_nt(grad_head, value)
        delta = jnp.sum(weight * grad_soft, axis=-1, keepdims=True)
        grad_scores = (weight * (grad_soft - delta)).astype(BF16)
        grad_key += dot_tn(grad_scores, query[:, at])
        turned = turn(dot_nn(grad_scores, key) * scale, cos, sig)
        grad, gains = norm_back(raw[:, at], qgain[...], turned)
        grad_raw[:, at] = grad.astype(BF16)
        query_gains += gains
    at = slice(heads * hd, (heads + 1) * hd)
    grad, key_gains = norm_back(raw[:, at], kgain[...], turn(grad_key * scale, cos, sig))
    grad_raw[:, at] = grad.astype(BF16)
    grad_raw[:, (heads + 1) * hd :] = grad_value.astype(BF16)
    gains = jnp.concatenate([query_gains, key_gains], axis=0)

    @pl.when(pl.program_id(0) == 0)
    def _():
        grad_gains[...] = gains

    @pl.when(pl.program_id(0) > 0)
    def _():
        grad_gains[...] += gains


def attend_back(raw, cosine, signed, query_gain, key_gain, query, kv, weights, grad_mixed, scale):
    groups, heads, tokens, _ = weights.shape
    hd = cosine.shape[1]
    rows = groups * tokens

    def block(cols):
        return pl.BlockSpec((tokens, cols), lambda g: (g, 0))

    gain = pl.BlockSpec((1, hd), lambda g: (0, 0))
    return pl.pallas_call(
        functools.partial(attend_back_kernel, scale),
        name="attend_back",
        cost_estimate=cost(14),
        grid=(groups,),
        out_shape=(
            jax.ShapeDtypeStruct((rows, (heads + 2) * hd), BF16),
            jax.ShapeDtypeStruct((2, hd), F32),
        ),
        in_specs=[
            block((heads + 2) * hd),
            block(hd),
            block(hd),
            gain,
            gain,
            block(heads * hd),
            block(2 * hd),
            pl.BlockSpec((1, heads, tokens, tokens), lambda g: (g, 0, 0, 0)),
            block(heads * hd),
        ],
        out_specs=(block((heads + 2) * hd), pl.BlockSpec((2, hd), lambda g: (0, 0))),
        compiler_params=pltpu.CompilerParams(vmem_limit_bytes=40 << 20),
    )(raw, cosine, signed, query_gain.reshape(1, hd), key_gain.reshape(1, hd), query, kv, weights, grad_mixed)


DIMS = (NX, NYH, NZ, NC, 2)
CHUNKS = (256, 256, 256, 256, 256, 256, 256, 128, 128)
BACK = (256,) * 9
TURNS = ("xzy", "zyx", "yxz")


class Route:
    def __init__(self, me, go):
        x, yh, z, c, t = me.x, me.yh, me.z, me.c, me.t
        steps = (1, 3, 2)
        turn = lambda i, d: lax.rem(i + d, RING)
        self.go = go
        self.own = {"x": (x, c), "z": (z,), "y": (yh, t)}
        self.peers = {
            "x": [((x, 1 - c), me.device(c=1 - c))]
            + [
                ((turn(x, d), e), me.device(x=turn(x, d), c=e))
                for d in steps
                for e in (c, 1 - c)
            ],
            "z": [((turn(z, d),), me.device(z=turn(z, d))) for d in steps],
            "y": [
                ((turn(me.y, d) // 2, lax.rem(turn(me.y, d), 2)), me.at_y(turn(me.y, d)))
                for d in steps
            ],
        }

    def everyone(self):
        return [peer for axis in "xzy" for _, peer in self.peers[axis]]

    @staticmethod
    def view(ref, axis, at):
        if axis == "x":
            return ref.at[at[0], :, :, at[1]]
        if axis == "z":
            return ref.at[:, :, at[0]]
        return ref.at[:, at[0], :, :, at[1]]

    def send(self, axis, src, dst):
        own = self.own[axis]
        kept = self.go.keep(self.view(src, axis, own), self.view(dst, axis, own))
        copies = [
            self.go.put(self.view(src, axis, at), self.view(dst, axis, own), peer)
            for at, peer in self.peers[axis]
        ]
        return kept, copies

    @staticmethod
    def wait(sent):
        kept, copies = sent
        for copy in copies:
            copy.wait_recv()
        kept.wait()


def columns(ref, start, size):
    return ref.at[:, :, :, :, :, :, pl.ds(start, size)]


ORDER = ((0, 0), (1, 0), (0, 1), (2, 0), (1, 1), (0, 2), (2, 1), (1, 2), (2, 2))


def enter_kernel(
    sent, told, gate, up, down, router, rows, inner_low, grad_gate, grad_up, extra, *rest
):
    chunks = len(CHUNKS)
    mids = rest[: 2 * chunks]
    held = rest[2 * chunks : 3 * chunks]
    (
        told_v, gate_v, up_v, down_v, router_v, gate_pre, up_pre, logits, inner_up, send, recv, local, loads,
    ) = rest[3 * chunks :]
    me = Place()
    go = Copies(send, recv, local)
    route = Route(me, go)
    pulls = [
        pltpu.make_async_copy(a, b, loads.at[n])
        for n, (a, b) in enumerate(
            ((told, told_v), (down, down_v), (gate, gate_v), (up, up_v), (router, router_v))
        )
    ]
    greet(route.everyone())
    starts = [sum(CHUNKS[:n]) for n in range(chunks)]
    sent_on = [None] * chunks
    outs = []
    width = sent.shape[-1]
    total = told_v.shape[0]
    experts = router.shape[1]
    index = me.expert()
    block = 256

    def cotangent(n):
        at = pl.ds(n * block, block)
        inner_up[at] = dot_nt(told_v[at, :width], down_v[...])

    def multiply(n, close=False):
        route.wait(sent_on[n])
        outs.append(go.keep(held[n], columns(rows, starts[n], CHUNKS[n])))
        cols = pl.ds(starts[n], CHUNKS[n])
        flat = held[n].reshape(total, CHUNKS[n])

        def step(m, _):
            at = pl.ds(pl.multiple_of(m * block, block), block)
            part = flat[at]
            terms = []
            for out, weight in ((gate_pre, gate_v), (up_pre, up_v), (logits, router_v)):
                term = dot_nn(part, weight[cols])
                if n > 0:
                    term = out[at] + term
                if not close:
                    out[at] = term
                terms.append(term)
            if close:
                finish(at, *terms)
            return 0

        lax.fori_loop(0, total // block, step, 0)

    def finish(at, before_gate, before_up, row_logits):
        row_logits = jnp.where(told_v[at, width:] > 0, row_logits, MASKED)
        powers = jnp.exp(row_logits - jnp.max(row_logits, axis=-1, keepdims=True))
        lane = lax.broadcasted_iota(jnp.int32, (1, experts), 1) == index
        prob = jnp.sum(jnp.where(lane, powers, 0.0), axis=-1, keepdims=True) / jnp.sum(
            powers, axis=-1, keepdims=True
        )
        back = inner_up[at]
        sigmoid = 1.0 / (1.0 + jnp.exp(-before_gate))
        silu = before_gate * sigmoid
        inner = silu * before_up
        gate_up = jnp.sum(inner * back, axis=-1, keepdims=True)
        inner_low[at] = (prob * inner).astype(BF16)
        back = prob * back
        grad_gate[at] = (back * before_up * sigmoid * (1.0 + before_gate * (1.0 - sigmoid))).astype(BF16)
        grad_up[at] = (back * silu).astype(BF16)
        high = gate_up.astype(BF16).astype(F32)
        extra[at, :experts] = jnp.where(lane, high, 0.0).astype(BF16)
        extra[at, experts:] = jnp.where(lane, gate_up - high, 0.0).astype(BF16)

    blocks = list(range(total // block))
    for triple, crossing in ORDER:
        for n in range(3 * triple, 3 * triple + 3):
            src = columns(sent, starts[n], CHUNKS[n]) if crossing == 0 else mids[2 * n + crossing - 1]
            dst = held[n] if crossing == 2 else mids[2 * n + crossing]
            if crossing > 0:
                route.wait(sent_on[n])
            sent_on[n] = route.send(TURNS[n % 3][crossing], src, dst)
            if crossing == 2 and triple > 0:
                multiply(n - 3)
            elif blocks and triple + crossing > 1:
                cotangent(blocks.pop(0))
        if (triple, crossing) == (1, 0):
            for pull in pulls:
                pull.start()
            for pull in pulls[:2]:
                pull.wait()
        if (triple, crossing) == (2, 1):
            for pull in pulls[2:]:
                pull.wait()
    for n in range(chunks - 3, chunks):
        multiply(n, close=n == chunks - 1)
    for out in outs:
        out.wait()
    go.finish()


def enter(sent, told, gate, up, down, router):
    slots, width = sent.shape
    hidden, experts = gate.shape[1], router.shape[1]
    cap = slots // math.prod(DIMS)
    lead = (*DIMS, cap)
    chunks = len(CHUNKS)
    low = jax.ShapeDtypeStruct((slots, hidden), BF16)
    rows, *rest = pl.pallas_call(
        enter_kernel,
        name="enter_experts",
        cost_estimate=cost(60),
        out_shape=(
            jax.ShapeDtypeStruct((*lead, width), BF16),
            low,
            low,
            low,
            jax.ShapeDtypeStruct((slots, 2 * experts), BF16),
        ),
        in_specs=[ANY] * 6,
        out_specs=(ANY, VMEM, VMEM, VMEM, VMEM),
        scratch_shapes=[
            *(pltpu.VMEM((*lead, w), BF16) for w in CHUNKS for _ in range(2)),
            *(pltpu.VMEM((*lead, w), BF16) for w in CHUNKS),
            pltpu.VMEM(told.shape, BF16),
            pltpu.VMEM(gate.shape, BF16),
            pltpu.VMEM(up.shape, BF16),
            pltpu.VMEM(down.shape, BF16),
            pltpu.VMEM(router.shape, BF16),
            pltpu.VMEM((slots, hidden), F32),
            pltpu.VMEM((slots, hidden), F32),
            pltpu.VMEM((slots, experts), F32),
            pltpu.VMEM((slots, hidden), F32),
            pltpu.SemaphoreType.DMA((13 * chunks,)),
            pltpu.SemaphoreType.DMA((13 * chunks,)),
            pltpu.SemaphoreType.DMA((4 * chunks,)),
            pltpu.SemaphoreType.DMA((5,)),
        ],
        compiler_params=pltpu.CompilerParams(
            collective_id=6, has_side_effects=True, vmem_limit_bytes=58 << 20
        ),
    )(sent.reshape(*lead, width), told, gate, up, down, router)
    return rows.reshape(slots, width), *rest


def leave_kernel(
    grad_gate, grad_up, extra, inner_low, spread, gate, up, down, summed, expert_out, *rest
):
    chunks = len(BACK)
    source = rest[: chunks - 1]
    mids = rest[chunks - 1 : 3 * chunks - 1]
    held = rest[3 * chunks - 1 : 4 * chunks - 1]
    gate_g, up_g, inner_v, spread_v, gate_v, up_v, down_v, out_v, send, recv, local, loads, puts = rest[4 * chunks - 1 :]
    me = Place()
    go = Copies(send, recv, local)
    route = Route(me, go)
    starts = [sum(BACK[:n]) for n in range(chunks)]
    total = gate_g.shape[0]
    block = 256
    pulls = {}
    count = 0
    for name, a, b in (("gg", grad_gate, gate_g), ("gu", grad_up, up_g)):
        pulls[name] = pltpu.make_async_copy(a, b, loads.at[count])
        count += 1
    for n in range(chunks - 1):
        cols = pl.ds(starts[n], BACK[n])
        for name, a, b in ((("g", n), gate, gate_v), (("u", n), up, up_v)):
            pulls[name] = pltpu.make_async_copy(a.at[cols], b.at[cols], loads.at[count])
            count += 1
    for name, a, b in (("inner", inner_low, inner_v), ("spread", spread, spread_v), ("down", down, down_v)):
        pulls[name] = pltpu.make_async_copy(a, b, loads.at[count])
        count += 1
    late = ("inner", "spread", "down")
    for name, pull in pulls.items():
        if name not in late:
            pull.start()
    greet(route.everyone())
    sent_on = [None] * chunks
    pushes = []

    def gradient(n):
        cols = pl.ds(starts[n], BACK[n])
        for name in (("g", n), ("u", n)):
            pulls[name].wait()
        flat = source[n].reshape(total, BACK[n])

        def step(m, _):
            at = pl.ds(pl.multiple_of(m * block, block), block)
            flat[at] = (dot_nt(gate_g[at], gate_v[cols]) + dot_nt(up_g[at], up_v[cols])).astype(BF16)
            return 0

        lax.fori_loop(0, total // block, step, 0)

    def result(m):
        if m == 0:
            pulls["inner"].wait()
            pulls["down"].wait()
        at = pl.ds(m * block, block)
        out_v[at] = dot_nn(inner_v[at], down_v[...]).astype(BF16)
        push = pltpu.make_async_copy(out_v.at[at], expert_out.at[at], puts.at[m])
        push.start()
        pushes.append(push)

    def combine(n):
        route.wait(sent_on[n])
        summed[:, starts[n] : starts[n] + BACK[n]] = dot_tn(spread_v[...], held[n].reshape(total, BACK[n])[...])

    results = list(range(total // block))
    for triple, crossing in ORDER:
        for n in range(3 * triple, 3 * triple + 3):
            dst = held[n] if crossing == 2 else mids[2 * n + crossing]
            if crossing > 0:
                route.wait(sent_on[n])
                src = mids[2 * n + crossing - 1]
            elif n == chunks - 1:
                src = extra
            else:
                if n == 0:
                    pulls["gg"].wait()
                    pulls["gu"].wait()
                gradient(n)
                src = source[n]
            sent_on[n] = route.send(TURNS[n % 3][crossing], src, dst)
            if crossing == 2 and triple > 0:
                if n == 3:
                    pulls["spread"].wait()
                combine(n - 3)
            elif results and triple + crossing > 1 and crossing > 0:
                result(results.pop(0))
        if (triple, crossing) == (1, 0):
            for name in late:
                pulls[name].start()
    for n in range(chunks - 3, chunks):
        combine(n)
    for push in pushes:
        push.wait()
    go.finish()


def leave(grad_gate, grad_up, extra, inner_low, spread, gate, up, down):
    slots, hidden = grad_gate.shape
    width, tok = gate.shape[0], spread.shape[1]
    cap = slots // math.prod(DIMS)
    lead = (*DIMS, cap)
    chunks = len(BACK)
    return pl.pallas_call(
        leave_kernel,
        name="leave_experts",
        cost_estimate=cost(60),
        out_shape=(
            jax.ShapeDtypeStruct((tok, sum(BACK)), F32),
            jax.ShapeDtypeStruct((slots, width), BF16),
        ),
        in_specs=[ANY] * 8,
        out_specs=(VMEM, ANY),
        scratch_shapes=[
            *(pltpu.VMEM((*lead, w), BF16) for w in BACK[:-1]),
            *(pltpu.VMEM((*lead, w), BF16) for w in BACK for _ in range(2)),
            *(pltpu.VMEM((*lead, w), BF16) for w in BACK),
            pltpu.VMEM(grad_gate.shape, BF16),
            pltpu.VMEM(grad_up.shape, BF16),
            pltpu.VMEM(inner_low.shape, BF16),
            pltpu.VMEM(spread.shape, BF16),
            pltpu.VMEM(gate.shape, BF16),
            pltpu.VMEM(up.shape, BF16),
            pltpu.VMEM(down.shape, BF16),
            pltpu.VMEM((slots, width), BF16),
            pltpu.SemaphoreType.DMA((13 * chunks,)),
            pltpu.SemaphoreType.DMA((13 * chunks,)),
            pltpu.SemaphoreType.DMA((3 * chunks,)),
            pltpu.SemaphoreType.DMA((2 * chunks + 3,)),
            pltpu.SemaphoreType.DMA((4,)),
        ],
        compiler_params=pltpu.CompilerParams(
            collective_id=7, has_side_effects=True, vmem_limit_bytes=58 << 20
        ),
    )(grad_gate, grad_up, extra.reshape(*lead, extra.shape[1]), inner_low, spread, gate, up, down)


def on_device(
    hidden_in,
    doc_ids,
    expert_ids,
    attn_gain,
    query_weight,
    key_weight,
    value_weight,
    output_weight,
    query_gain,
    key_gain,
    moe_gain,
    router_weight,
    gate_weight,
    up_weight,
    down_weight,
    cotangent,
):
    both = ("dp", "tensor")
    tok, width = hidden_in.shape
    hd = query_gain.shape[0]
    nkv = key_weight.shape[1] // hd
    nq = query_weight.shape[1] // hd
    group = nq // nkv
    experts = router_weight.shape[1]
    routes = expert_ids.shape[1]
    cap = tok * routes // experts
    slots = experts * cap
    scale = 1.0 / math.sqrt(hd)
    tokens = doc_ids.shape[1]

    lane = lax.broadcasted_iota(jnp.int32, (1, 1, experts), 2)
    chosen = jnp.sum((expert_ids[:, :, None] == lane).astype(F32), axis=1)
    below = (
        lax.broadcasted_iota(jnp.int32, (tok, tok), 1)
        < lax.broadcasted_iota(jnp.int32, (tok, tok), 0)
    ).astype(BF16)
    rank = dot_nn(below, chosen.astype(BF16))
    place = jnp.where(chosen > 0, rank, -1.0).T
    spread = (
        place[:, None, :] == lax.broadcasted_iota(jnp.int32, (1, cap, 1), 1).astype(F32)
    ).astype(BF16).reshape(slots, tok)

    hidden = hidden_in.astype(F32)
    normed_local = rms_scale(hidden, attn_gain).astype(BF16)

    in_weights, out_weights, normed, docs = gather(
        query_weight,
        key_weight,
        value_weight,
        output_weight.T,
        normed_local,
        jnp.broadcast_to(doc_ids, (8, tokens)).astype(F32),
    )

    spread_late, docs = lax.optimization_barrier((spread, docs))
    cot_out = dot_nn(spread_late, jnp.concatenate([cotangent, chosen.astype(BF16)], axis=1)).astype(BF16)
    cot_in = lax.all_to_all(
        cot_out.reshape(experts, cap, width + experts), both, split_axis=0, concat_axis=0, tiled=True
    ).reshape(slots, width + experts)

    position, allowed = jax.vmap(layout)(docs[:, 0])
    cosine, sine = rotary(position.reshape(-1), hd)
    cosine = jnp.concatenate([cosine, cosine], axis=1)
    signed = jnp.concatenate([-sine, sine], axis=1)
    bias = jnp.where(allowed, 0.0, MASKED).astype(F32)
    raw = dot_nn(normed, in_weights)
    heads = group * hd
    query, kv, attention, mixed = attend(raw, bias, cosine, signed, query_gain, key_gain, scale)
    attn_out = reduce(dot_nt(mixed, out_weights).astype(BF16), 2)

    residual = hidden + attn_out
    moe_input = rms_scale(residual, moe_gain).astype(BF16)
    moe_input, cot_in = lax.optimization_barrier((moe_input, cot_in))
    sent = dot_nn(spread, moe_input).astype(BF16)
    gate_mat, up_mat, down_mat = gate_weight[0], up_weight[0], down_weight[0]
    rows, inner_low, grad_gate, grad_up, extra = enter(
        sent, cot_in, gate_mat, up_mat, down_mat, router_weight
    )
    summed, expert_out = leave(
        grad_gate, grad_up, extra, inner_low, spread, gate_mat, up_mat, down_mat
    )
    logits = dot_nn(moe_input, router_weight)
    masked = jnp.where(chosen > 0, logits, MASKED)
    probs = jnp.exp(masked - jnp.max(masked, axis=-1, keepdims=True))
    probs = probs / jnp.sum(probs, axis=-1, keepdims=True)

    upstream = cotangent.astype(F32)
    gate_upstream = summed[:, width : width + experts] + summed[:, width + experts :]
    grad_chosen = probs * (gate_upstream - jnp.sum(probs * gate_upstream, axis=-1, keepdims=True))
    grad_logits = grad_chosen.astype(BF16)
    grad_moe_input = summed[:, :width] + dot_nt(grad_logits, router_weight)
    router_part = dot_tn(moe_input, grad_logits)
    grad_norm, moegain_rows = rms_back(residual, moe_gain, grad_moe_input)
    moegain_part = jnp.sum(moegain_rows, axis=0)
    grad_residual = upstream + grad_norm
    grad_attn = share(grad_residual.astype(BF16), 3)
    pieces = router_part.astype(BF16).reshape(experts, width // experts, experts)
    piece = jnp.sum(lax.all_to_all(pieces, both, 0, 0, tiled=True).astype(F32), axis=0)
    expert_out, grad_attn, piece = lax.optimization_barrier((expert_out, grad_attn, piece))
    returned = lax.all_to_all(
        expert_out.reshape(experts, cap, width), both, split_axis=0, concat_axis=0, tiled=True
    ).reshape(slots, width)

    cot_rows = cot_in[:, :width]
    down_grad = dot_tn(inner_low, cot_rows)
    gate_grad = dot_tn(rows, grad_gate)
    up_grad = dot_tn(rows, grad_up)

    grad_mixed = dot_nn(grad_attn, out_weights).astype(BF16)
    grad_raw, head_gains = attend_back(
        raw, cosine, signed, query_gain, key_gain, query, kv, attention, grad_mixed, scale
    )
    grad_normed = reduce(dot_nt(grad_raw, in_weights).astype(BF16), 4)
    grad_hidden, attngain_rows = rms_back(hidden, attn_gain, grad_normed)
    input_grad = grad_residual + grad_hidden

    gains = jnp.concatenate([jnp.sum(attngain_rows, axis=0), moegain_part]).reshape(-1, hd)
    gains = jnp.concatenate([gains, head_gains, jnp.zeros((6, hd), F32)], axis=0)

    layer_out = (residual + dot_tn(spread, returned)).astype(BF16)
    query_grad, key_grad, value_grad, out_grad, gains, router_grad = scatter(
        dot_tn(normed, grad_raw).astype(BF16),
        dot_tn(grad_attn, mixed).astype(BF16),
        gains,
        piece.astype(BF16),
        (nq * hd, nkv * hd, nkv * hd, nq * hd),
    )
    at = width // hd
    return (
        layer_out,
        input_grad,
        gains[:at].reshape(-1),
        query_grad,
        key_grad,
        value_grad,
        out_grad.T,
        gains[2 * at],
        gains[2 * at + 1],
        gains[at : 2 * at].reshape(-1),
        router_grad.reshape(width, experts).astype(F32),
        gate_grad[None],
        up_grad[None],
        down_grad[None],
    )


def solution(mesh):
    both = ("dp", "tensor")
    in_specs = (
        P(both, None),
        P("dp", None),
        P(both, None),
        P(),
        P("dp", "tensor"),
        P("dp", "tensor"),
        P("dp", "tensor"),
        P("tensor", "dp"),
        P(),
        P(),
        P(),
        P(),
        P(both, None, None),
        P(both, None, None),
        P(both, None, None),
        P(both, None),
    )
    out_specs = (
        P(both, None),
        P(both, None),
        P(),
        P("dp", "tensor"),
        P("dp", "tensor"),
        P("dp", "tensor"),
        P("tensor", "dp"),
        P(),
        P(),
        P(),
        P(),
        P(both, None, None),
        P(both, None, None),
        P(both, None, None),
    )
    return jax.shard_map(
        on_device, mesh=mesh, in_specs=in_specs, out_specs=out_specs, check_vma=False
    )
```

```python
import functools
import math

import jax
import jax.numpy as jnp
from jax import lax
from jax.experimental import pallas as pl
from jax.experimental.pallas import tpu as pltpu
from jax.sharding import PartitionSpec as P

BLOCK = 128
EPSILON = 1e-06
ROPE_BASE = 1000000.0
MASKED = -1e30
F32 = jnp.float32
BF16 = jnp.bfloat16


def dot_nt(a, b):
    return lax.dot_general(a, b, (((1,), (1,)), ((), ())), preferred_element_type=F32)


def dot_tn(a, b):
    return lax.dot_general(a, b, (((0,), (0,)), ((), ())), preferred_element_type=F32)


def dot_nn(a, b):
    return lax.dot_general(a, b, (((1,), (0,)), ((), ())), preferred_element_type=F32)


def rms_recip(values):
    return lax.rsqrt(jnp.mean(values * values, axis=-1, keepdims=True) + EPSILON)


def rms_scale(values, gain):
    return values * rms_recip(values) * gain


def rms_back(values, gain, upstream):
    r = rms_recip(values)
    scaled = upstream * gain
    inner = jnp.mean(scaled * values, axis=-1, keepdims=True)
    grad_values = r * scaled - values * (r * r * r) * inner
    return grad_values, upstream * values * r


def rotate(values, cosine, sine):
    half = values.shape[-1] // 2
    a = values[..., :half]
    b = values[..., half:]
    return jnp.concatenate([a * cosine - b * sine, b * cosine + a * sine], axis=-1)


def layout(doc_row):
    length = doc_row.shape[0]
    indices = jnp.arange(length, dtype=jnp.int32)
    same_doc = doc_row[:, None] == doc_row[None, :]
    earlier = indices[None, :] < indices[:, None]
    position = jnp.sum(jnp.where(same_doc & earlier, 1, 0), axis=1).astype(jnp.int32)
    blocks = position // BLOCK
    allowed = same_doc & (blocks[None, :] <= blocks[:, None])
    return position, allowed


def rotary(position, head_size):
    half = head_size // 2
    frequency = jnp.exp(-jnp.log(ROPE_BASE) * jnp.arange(half, dtype=F32) * 2.0 / head_size)
    angles = position.astype(F32)[:, None] * frequency[None, :]
    return jnp.cos(angles), jnp.sin(angles)


MESH = pl.DeviceIdType.MESH
ANY = pl.BlockSpec(memory_space=pl.ANY)
VMEM = pl.BlockSpec(memory_space=pltpu.VMEM)
NX, NYH, NZ, NC = 4, 2, 4, 2
RING = 4


def cost(microseconds):
    return pl.CostEstimate(flops=0, transcendentals=0, bytes_accessed=int(microseconds * 3.6e6))


class Place:
    def __init__(self):
        dp = lax.axis_index("dp")
        self.t = lax.axis_index("tensor")
        self.c = lax.rem(dp, NC)
        self.z = lax.rem(dp // NC, NZ)
        self.yh = lax.rem(dp // (NC * NZ), NYH)
        self.x = dp // (NC * NZ * NYH)
        self.y = self.yh * 2 + self.t

    def device(self, x=None, yh=None, z=None, c=None, t=None):
        pick = lambda given, own: own if given is None else given
        x, yh, z, c = pick(x, self.x), pick(yh, self.yh), pick(z, self.z), pick(c, self.c)
        return (((x * NYH + yh) * NZ + z) * NC + c, pick(t, self.t))

    def expert(self):
        return ((((self.x * NYH + self.yh) * NZ + self.z) * NC) + self.c) * 2 + self.t

    def at_y(self, y):
        return self.device(yh=y // 2, t=lax.rem(y, 2))


def after(i):
    return lax.rem(i + 1, RING)


def before(i):
    return lax.rem(i + RING - 1, RING)


def across(i):
    return lax.rem(i + 2, RING)


def greet(peers):
    barrier = pltpu.get_barrier_semaphore()
    for peer in peers:
        pl.semaphore_signal(barrier, inc=1, device_id=peer, device_id_type=MESH)
    pl.semaphore_wait(barrier, len(peers))


class Copies:
    def __init__(self, send, recv, local):
        self.send, self.recv, self.local = send, recv, local
        self.n = self.m = 0
        self.sent = []

    def put(self, src, dst, peer):
        copy = pltpu.make_async_remote_copy(
            src_ref=src,
            dst_ref=dst,
            send_sem=self.send.at[self.n],
            recv_sem=self.recv.at[self.n],
            device_id=peer,
            device_id_type=MESH,
        )
        self.n += 1
        copy.start()
        self.sent.append(copy)
        return copy

    def keep(self, src, dst):
        copy = pltpu.make_async_copy(src, dst, self.local.at[self.m])
        self.m += 1
        copy.start()
        return copy

    def finish(self):
        for copy in self.sent:
            copy.wait_send()


def gather_kernel(q, k, v, o, tok, doc, wa, wb, toks, docs, send, recv, local):
    me = Place()
    x, yh, z, c, p = me.x, me.yh, me.z, me.c, me.y
    sibling = me.device(c=1 - c)
    pair = me.device(yh=1 - yh)
    ring_x = (me.device(x=after(x)), me.device(x=before(x)))
    ring_z = (me.device(z=after(z)), me.device(z=before(z)))
    ring_y = (me.at_y(after(p)), me.at_y(before(p)))
    greet([sibling, pair, *ring_x, *ring_z, *ring_y])
    go = Copies(send, recv, local)

    shards, start = [], 0
    for ref, w in ((q, wa), (k, wa), (v, wa), (o, wb)):
        cols = ref.shape[1] // NYH
        to = w.at[x, yh, z, c, :, pl.ds(0 if w is wb else start, cols)]
        shards.append((ref, cols, to))
        start += cols

    def part(ref, cols, head):
        return ref.at[:, pl.ds(pl.multiple_of(head * cols, cols), cols)]

    pairs = [go.put(part(ref, cols, 1 - yh), to, pair) for ref, cols, to in shards]
    kept = [go.keep(part(ref, cols, yh), to) for ref, cols, to in shards]
    for copy in kept:
        copy.wait()
    for copy in pairs:
        copy.wait_recv()

    ways = (
        (x, z, ring_x, ring_z, lambda i, j: wa.at[i, :, j, c], lambda j: wa.at[:, :, j, c]),
        (z, x, ring_z, ring_x, lambda i, j: wb.at[j, :, i, c], lambda j: wb.at[j, :, :, c]),
    )

    def both(ref, peers):
        return [go.put(ref, ref, peer) for peer in peers]

    def relay(low, high, copies, peers):
        copies[0].wait_recv()
        up = go.put(low.at[0], low.at[0], peers[0])
        copies[1].wait_recv()
        return [up, go.put(high.at[1], high.at[1], peers[1])]

    def arrived(copies):
        for copy in copies:
            copy.wait_recv()

    near = [both(unit(i, j), one) for i, j, one, two, unit, slab in ways]
    own = [both(unit(i, j), two) for i, j, one, two, unit, slab in ways]
    rows = [go.put(tok, toks.at[p], peer) for peer in ring_y]
    rest = [go.keep(tok, toks.at[p]), go.keep(doc, docs.at[yh])]
    tail = [go.put(doc, docs.at[yh], pair)]
    far = [
        relay(unit(before(i), j), unit(after(i), j), copies, one)
        for (i, j, one, two, unit, slab), copies in zip(ways, near)
    ]
    low = [both(unit(before(i), j), two) for i, j, one, two, unit, slab in ways]
    high = [both(unit(after(i), j), two) for i, j, one, two, unit, slab in ways]
    last = []
    for (i, j, one, two, unit, slab), copies in zip(ways, far):
        arrived(copies)
        last.append(both(unit(across(i), j), two))
        tail.append(go.put(slab(j), slab(j), sibling))
    half = tok.shape[0] // 2
    rows[0].wait_recv()
    piece = toks.at[before(p), pl.ds(0, half)]
    tail.append(go.put(piece, piece, ring_y[0]))
    rows[1].wait_recv()
    piece = toks.at[after(p), pl.ds(half, half)]
    tail.append(go.put(piece, piece, ring_y[1]))
    ends = [[], []]
    for place, copies in ((lambda i: i, own), (before, low), (after, high), (across, last)):
        for n, (i, j, one, two, unit, slab) in enumerate(ways):
            u = place(i)
            ends[n] += relay(unit(u, before(j)), unit(u, after(j)), copies[n], two)
    for i, j, one, two, unit, slab in ways:
        tail.append(go.put(slab(before(j)), slab(before(j)), sibling))
        tail.append(go.put(slab(after(j)), slab(after(j)), sibling))
    for (i, j, one, two, unit, slab), copies in zip(ways, ends):
        arrived(copies)
        tail.append(go.put(slab(across(j)), slab(across(j)), sibling))
    arrived(tail)
    for copy in rest:
        copy.wait()
    go.finish()


def gather(query, key, value, out, tokens, docs):
    rows = query.shape[0]
    width_a = (query.shape[1] + key.shape[1] + value.shape[1]) // NYH
    width_b = out.shape[1] // NYH
    lead = (NX, NYH, NZ, NC, rows)
    wa, wb, toks, docs = pl.pallas_call(
        gather_kernel,
        name="gather_weights",
        cost_estimate=cost(60),
        out_shape=(
            jax.ShapeDtypeStruct((*lead, width_a), BF16),
            jax.ShapeDtypeStruct((*lead, width_b), BF16),
            jax.ShapeDtypeStruct((RING, *tokens.shape), BF16),
            jax.ShapeDtypeStruct((NYH, *docs.shape), docs.dtype),
        ),
        in_specs=[ANY] * 6,
        out_specs=(ANY,) * 4,
        scratch_shapes=[
            pltpu.SemaphoreType.DMA((57,)),
            pltpu.SemaphoreType.DMA((57,)),
            pltpu.SemaphoreType.DMA((6,)),
        ],
        compiler_params=pltpu.CompilerParams(collective_id=1, has_side_effects=True),
    )(query, key, value, out, tokens, docs)
    depth = NX * NYH * NZ * NC * rows
    return (
        wa.reshape(depth, width_a),
        wb.reshape(depth, width_b),
        toks.reshape(RING * tokens.shape[0], tokens.shape[1]),
        docs,
    )


def share_kernel(tok, part, toks, piece, got_x, sum_x, got_z, sum_z, got_y, send, recv, local):
    me = Place()
    x, yh, z, c, p = me.x, me.yh, me.z, me.c, me.y
    ring = (me.at_y(after(p)), me.at_y(before(p)))
    go = Copies(send, recv, local)
    route = Route(me, go)
    greet(route.everyone())
    half = tok.shape[0] // 2
    direct = [go.put(tok, toks.at[p], peer) for peer in ring]
    kept = go.keep(tok, toks.at[p])
    own = go.keep(part.at[x, :, :, c], got_x.at[x * NC + c])
    terms = [
        go.put(part.at[at[0], :, :, at[1]], got_x.at[x * NC + c], peer)
        for at, peer in route.peers["x"]
    ]

    def arrived(copies):
        for copy in copies:
            copy.wait_recv()

    def added(got):
        value = got[0].astype(F32)
        for n in range(1, got.shape[0]):
            value += got[n].astype(F32)
        return value

    own.wait()
    arrived(terms)
    sum_x[...] = added(got_x)
    got_z[z] = sum_x[:, z]
    terms = [go.put(sum_x.at[:, at[0]], got_z.at[z], peer) for at, peer in route.peers["z"]]
    relays = []
    for h, owner in enumerate((before(p), after(p))):
        direct[h].wait_recv()
        rows = toks.at[owner, pl.ds(h * half, half)]
        relays.append(go.put(rows, rows, ring[h]))
    arrived(terms)
    sum_z[...] = added(got_z)
    got_y[p] = sum_z[yh, me.t]
    terms = [go.put(sum_z.at[at[0], at[1]], got_y.at[p], peer) for at, peer in route.peers["y"]]
    arrived(terms)
    piece[...] = added(got_y).astype(piece.dtype)
    arrived(relays)
    kept.wait()
    go.finish()


def share(tokens, part, ident):
    rows, lanes = part.shape[0] // math.prod(DIMS), part.shape[1]
    toks, piece = pl.pallas_call(
        share_kernel,
        name=f"share_rows_{ident}",
        cost_estimate=cost(20),
        out_shape=(
            jax.ShapeDtypeStruct((RING, *tokens.shape), tokens.dtype),
            jax.ShapeDtypeStruct((rows, lanes), BF16),
        ),
        in_specs=[ANY, ANY],
        out_specs=(ANY, VMEM),
        scratch_shapes=[
            pltpu.VMEM((NX * NC, NYH, NZ, 2, rows, lanes), BF16),
            pltpu.VMEM((NYH, NZ, 2, rows, lanes), F32),
            pltpu.VMEM((NZ, NYH, 2, rows, lanes), F32),
            pltpu.VMEM((NYH, 2, rows, lanes), F32),
            pltpu.VMEM((RING, rows, lanes), F32),
            pltpu.SemaphoreType.DMA((17,)),
            pltpu.SemaphoreType.DMA((17,)),
            pltpu.SemaphoreType.DMA((2,)),
        ],
        compiler_params=pltpu.CompilerParams(collective_id=ident, has_side_effects=True),
    )(tokens, part.reshape(*DIMS, rows, lanes))
    return toks.reshape(RING * tokens.shape[0], tokens.shape[1]), piece


def reduce_kernel(part, out, held, own, got, send, recv, local):
    me = Place()
    p = me.y
    ring = (me.at_y(after(p)), me.at_y(before(p)))
    greet(ring)
    go = Copies(send, recv, local)
    half = out.shape[0] // 2
    halves = [pl.ds(h * half, half) for h in range(2)]
    near = (after(p), before(p))
    cross = [go.put(part.at[across(p), halves[h]], got.at[h], ring[h]) for h in range(2)]
    kept = [go.keep(part.at[near[h], halves[h]], held.at[h]) for h in range(2)]
    straight = [go.put(part.at[near[h], halves[1 - h]], got.at[2 + h], ring[h]) for h in range(2)]
    mine = go.keep(part.at[p], own)
    sums = []
    for h in range(2):
        kept[h].wait()
        cross[h].wait_recv()
        held[h] = (held[h].astype(F32) + got[h].astype(F32)).astype(BF16)
        sums.append(go.put(held.at[h], got.at[4 + h], ring[h]))
    mine.wait()
    for copy in straight:
        copy.wait_recv()
    for h in range(2):
        sums[h].wait_recv()
        out[halves[h]] = (
            own[halves[h]].astype(F32) + got[4 + h].astype(F32) + got[3 - h].astype(F32)
        )
    go.finish()


def reduce(part, ident):
    rows, width = part.shape[0] // RING, part.shape[1]
    half = rows // 2
    return pl.pallas_call(
        reduce_kernel,
        name=f"reduce_rows_{ident}",
        cost_estimate=cost(1),
        out_shape=jax.ShapeDtypeStruct((rows, width), F32),
        in_specs=[ANY],
        out_specs=VMEM,
        scratch_shapes=[
            pltpu.VMEM((2, half, width), BF16),
            pltpu.VMEM((rows, width), BF16),
            pltpu.VMEM((6, half, width), BF16),
            pltpu.SemaphoreType.DMA((6,)),
            pltpu.SemaphoreType.DMA((6,)),
            pltpu.SemaphoreType.DMA((3,)),
        ],
        compiler_params=pltpu.CompilerParams(
            collective_id=ident, has_side_effects=True, vmem_limit_bytes=24 << 20
        ),
    )(part.reshape(RING, rows, width))


def scatter_kernel(
    ga, gb, gains, piece, returned, slots, residual, oq, ok, ov, oo, og, op, layer, back_v, slots_v, ka, kb, da, db, ra, rb, qa, qb, sa, sb, ta, tb, ua, ub, ma, mb,
    ring_gains, sum_gains, pair_gains, send, recv, local
):
    me = Place()
    x, yh, z, c, t = me.x, me.yh, me.z, me.c, me.t
    sibling = me.device(c=1 - c)
    pair = me.device(yh=1 - yh)
    partner = me.device(t=1 - t)
    ring_x = (me.device(x=after(x)), me.device(x=before(x)))
    ring_z = (me.device(z=after(z)), me.device(z=before(z)))
    round_x = (*ring_x, me.device(x=across(x)))
    round_z = (*ring_z, me.device(z=across(z)))
    greet([sibling, pair, partner, *round_x, *round_z])
    go = Copies(send, recv, local)

    def around(n, term, own, peers):
        ring_gains[n, own] = term
        return [go.put(ring_gains.at[n, own], ring_gains.at[n, own], peer) for peer in peers]

    def ring_sum(n, copies):
        for copy in copies:
            copy.wait_recv()
        return (ring_gains[n, 0] + ring_gains[n, 1]) + (ring_gains[n, 2] + ring_gains[n, 3])

    def swap(n, term, peer):
        sum_gains[n] = term
        return go.put(sum_gains.at[n], pair_gains.at[n], peer)

    def swapped(n, copy):
        copy.wait_recv()
        return sum_gains[n] + pair_gains[n]


    ways = (
        (lambda i, h, n: ga.at[i, h, :, n], x, z, ring_x, ring_z, ka, da, ra, qa, sa, ta),
        (lambda i, h, n: gb.at[:, h, i, n], z, x, ring_z, ring_x, kb, db, rb, qb, sb, tb),
    )
    places = (across, after, before, lambda i: i)

    def spread(ref, peers):
        return [go.put(ref, ref, peer) for peer in peers]

    def arrived(copies):
        for copy in copies:
            copy.wait_recv()

    given, held = [[], []], [[], []]
    for n, place in enumerate(places):
        for w, (slab, i, j, one, two, k, d, r, q, s, u) in enumerate(ways):
            given[w].append([go.put(slab(place(i), h, 1 - c), d.at[n, h], sibling) for h in range(2)])
            held[w].append([go.keep(slab(place(i), h, c), k.at[n, h]) for h in range(2)])

    def ready(w, n, h):
        given[w][n][h].wait_recv()
        held[w][n][h].wait()

    def total(w, n, h, extra):
        slab, i, j, one, two, k, d, r, q, s, u = ways[w]

        def step(m, _):
            value = k[n, h, m].astype(F32) + d[n, h, m].astype(F32)
            for e in extra:
                value += r[e, m].astype(F32)
            k[n, h, m] = value.astype(BF16)
            return 0

        lax.fori_loop(0, k.shape[2], step, 0)

    terms = around(0, gains[...], x, round_x)
    mine = op.at[x, yh, z, c, t]
    held_piece = go.keep(piece, mine)
    pieces = [go.put(piece, mine, sibling)]
    pulls = [go.keep(returned, back_v), go.keep(slots, slots_v)]
    cross, straight, sums = [[], []], [[], []], [[], []]
    for w, (slab, i, j, one, two, k, d, r, q, s, u) in enumerate(ways):
        for h in range(2):
            ready(w, 0, h)
            total(w, 0, h, ())
            cross[w].append(go.put(k.at[0, h], r.at[h], one[h]))
    for w, (slab, i, j, one, two, k, d, r, q, s, u) in enumerate(ways):
        for h in range(2):
            ready(w, 1 + h, 1 - h)
            total(w, 1 + h, 1 - h, ())
            straight[w].append(go.put(k.at[1 + h, 1 - h], r.at[2 + h], one[h]))
    for pull in pulls:
        pull.wait()
    for m in range(4):
        cols = pl.ds(m * layer.shape[1] // 4, layer.shape[1] // 4)
        layer[:, cols] = (residual[:, cols] + dot_tn(slots_v[...], back_v[:, cols])).astype(layer.dtype)
    terms = around(1, ring_sum(0, terms), z, round_z)
    arrived(pieces)
    held_piece.wait()
    pieces = spread(op.at[x, yh, z, :, t], [partner])
    for w, (slab, i, j, one, two, k, d, r, q, s, u) in enumerate(ways):
        for h in range(2):
            ready(w, 1 + h, h)
            cross[w][h].wait_recv()
            total(w, 1 + h, h, (h,))
            sums[w].append(go.put(k.at[1 + h, h], r.at[4 + h], one[h]))
    arrived(pieces)
    pieces = spread(op.at[x, yh, z], [pair])
    terms = swap(0, ring_sum(1, terms), pair)
    for w in range(2):
        for h in range(2):
            ready(w, 3, h)
            straight[w][1 - h].wait_recv()
            total(w, 3, h, (3 - h,))
    arrived(pieces)
    pieces = spread(op.at[x, :, z], round_x)
    terms = swap(1, swapped(0, terms), partner)
    over, direct, final = [[], []], [[], []], [[], []]
    for w, (slab, i, j, one, two, k, d, r, q, s, u) in enumerate(ways):
        near = (after(j), before(j))
        for h in range(2):
            sums[w][h].wait_recv()

            def step(m, _, k=k, r=r, h=h):
                k[3, h, m] = (k[3, h, m].astype(F32) + r[4 + h, m].astype(F32)).astype(BF16)
                return 0

            lax.fori_loop(0, k.shape[2], step, 0)
            over[w].append(go.put(k.at[3, h, across(j)], q.at[h], two[h]))
        for h in range(2):
            direct[w].append(go.put(k.at[3, 1 - h, near[h]], q.at[2 + h], two[h]))
    arrived(pieces)
    pieces = spread(op.at[:, :, z], round_z)
    terms = swap(2, swapped(1, terms), sibling)
    for w, (slab, i, j, one, two, k, d, r, q, s, u) in enumerate(ways):
        near = (after(j), before(j))
        for h in range(2):
            over[w][h].wait_recv()
            s[h] = (k[3, h, near[h]].astype(F32) + q[h].astype(F32)).astype(BF16)
            final[w].append(go.put(s.at[h], q.at[4 + h], two[h]))
    last = []
    for w, ((slab, i, j, one, two, k, d, r, q, s, u), v, m) in enumerate(zip(ways, (ua, ub), (ma, mb))):
        arrived(direct[w])
        arrived(final[w])
        for h in range(2):
            u[h] = k[3, h, j].astype(F32) + q[4 + h].astype(F32) + q[3 - h].astype(F32)
        v[...] = u[1 - yh].astype(BF16)
        last.append(go.put(v, m, pair))
    og[...] = swapped(2, terms)

    def write(head, a, b):
        start = 0
        for out, block in ((oq, a), (ok, a), (ov, a), (oo, b)):
            cols = out.shape[1] // NYH
            at = 0 if block is b else start
            out[:, pl.ds(pl.multiple_of(head * cols, cols), cols)] = block[:, at : at + cols]
            start += cols

    write(yh, ta[yh], tb[yh])
    arrived(last)
    write(1 - yh, ma[...].astype(F32), mb[...].astype(F32))
    arrived(pieces)
    go.finish()


def scatter(grad_a, grad_b, gains, piece, returned, slots, residual, columns):
    rows = grad_a.shape[0] // (NX * NYH * NZ * NC)
    lead = (NX, NYH, NZ, NC, rows)
    widths = (grad_a.shape[1], grad_b.shape[1])

    def each(shape, dtype):
        return [pltpu.VMEM((*shape, rows, w), dtype) for w in widths]

    return pl.pallas_call(
        scatter_kernel,
        name="scatter_weights",
        cost_estimate=cost(80),
        out_shape=(
            *(jax.ShapeDtypeStruct((rows, w), F32) for w in columns),
            jax.ShapeDtypeStruct(gains.shape, F32),
            jax.ShapeDtypeStruct((NX, NYH, NZ, NC, 2, *piece.shape), piece.dtype),
            jax.ShapeDtypeStruct(residual.shape, BF16),
        ),
        in_specs=[ANY, ANY, VMEM, ANY, ANY, ANY, VMEM],
        out_specs=(*(VMEM,) * 5, ANY, VMEM),
        scratch_shapes=[
            pltpu.VMEM(returned.shape, BF16),
            pltpu.VMEM(slots.shape, BF16),
            *each((4, 2, RING), BF16),
            *each((4, 2, RING), BF16),
            *each((6, RING), BF16),
            *each((6,), BF16),
            *each((2,), BF16),
            *each((2,), F32),
            *each((), BF16),
            *each((), BF16),
            pltpu.VMEM((2, RING, *gains.shape), F32),
            pltpu.VMEM((3, *gains.shape), F32),
            pltpu.VMEM((3, *gains.shape), F32),
            pltpu.SemaphoreType.DMA((60,)),
            pltpu.SemaphoreType.DMA((60,)),
            pltpu.SemaphoreType.DMA((19,)),
        ],
        compiler_params=pltpu.CompilerParams(
            collective_id=5, has_side_effects=True, vmem_limit_bytes=48 << 20
        ),
    )(grad_a.reshape(*lead, widths[0]), grad_b.reshape(*lead, widths[1]), gains, piece, returned, slots, residual)


def unit_rows(values):
    return lax.rsqrt(jnp.mean(values * values, axis=-1, keepdims=True) + EPSILON)


def turn(values, cosine, signed):
    return values * cosine + pltpu.roll(values, values.shape[-1] // 2, 1) * signed


def attend_kernel(scale, raw, bias, cosine, signed, qgain, kgain, query, kv, weights, mixed):
    heads = query.shape[1] // cosine.shape[1]
    hd = cosine.shape[1]
    cos, sig = cosine[...], signed[...]
    key_raw = raw[:, heads * hd : (heads + 1) * hd]
    key = turn(key_raw * unit_rows(key_raw) * kgain[...], cos, sig).astype(BF16)
    value = raw[:, (heads + 1) * hd :].astype(BF16)
    kv[:, :hd] = key
    kv[:, hd:] = value
    for h in range(heads):
        at = slice(h * hd, (h + 1) * hd)
        head = raw[:, at]
        rows = turn(head * unit_rows(head) * qgain[...], cos, sig).astype(BF16)
        query[:, at] = rows
        scores = dot_nt(rows, key) * scale + bias[0]
        peak = jnp.max(scores, axis=-1, keepdims=True)
        weight = jnp.exp(scores - peak)
        weight = weight * (1.0 / jnp.sum(weight, axis=-1, keepdims=True))
        weights[0, h] = weight
        mixed[:, at] = dot_nn(weight.astype(BF16), value).astype(BF16)


def attend(raw, bias, cosine, signed, query_gain, key_gain, scale):
    groups, tokens = bias.shape[0], bias.shape[1]
    hd = cosine.shape[1]
    heads = raw.shape[1] // hd - 2
    rows = groups * tokens

    def block(cols):
        return pl.BlockSpec((tokens, cols), lambda g: (g, 0))

    gain = pl.BlockSpec((1, hd), lambda g: (0, 0))
    square = pl.BlockSpec((1, tokens, tokens), lambda g: (g, 0, 0))
    return pl.pallas_call(
        functools.partial(attend_kernel, scale),
        name="attend",
        cost_estimate=cost(8),
        grid=(groups,),
        out_shape=(
            jax.ShapeDtypeStruct((rows, heads * hd), BF16),
            jax.ShapeDtypeStruct((rows, 2 * hd), BF16),
            jax.ShapeDtypeStruct((groups, heads, tokens, tokens), F32),
            jax.ShapeDtypeStruct((rows, heads * hd), BF16),
        ),
        in_specs=[block((heads + 2) * hd), square, block(hd), block(hd), gain, gain],
        out_specs=(
            block(heads * hd),
            block(2 * hd),
            pl.BlockSpec((1, heads, tokens, tokens), lambda g: (g, 0, 0, 0)),
            block(heads * hd),
        ),
        compiler_params=pltpu.CompilerParams(vmem_limit_bytes=40 << 20),
    )(raw, bias, cosine, signed, query_gain.reshape(1, hd), key_gain.reshape(1, hd))


def norm_back(values, gain, upstream):
    r = unit_rows(values)
    scaled = upstream * gain
    inner = jnp.mean(scaled * values, axis=-1, keepdims=True)
    grad = r * scaled - values * (r * r * r * inner)
    return grad, jnp.sum(upstream * values * r, axis=0, keepdims=True)


def attend_back_kernel(
    scale, raw, cosine, signed, qgain, kgain, query, kv, weights, grad_mixed, grad_raw, grad_gains
):
    hd = cosine.shape[1]
    heads = query.shape[1] // hd
    cos, sig = cosine[...], -signed[...]
    key, value = kv[:, :hd], kv[:, hd:]
    grad_key = jnp.zeros(key.shape, F32)
    grad_value = jnp.zeros(key.shape, F32)
    query_gains = jnp.zeros((1, hd), F32)
    for h in range(heads):
        at = slice(h * hd, (h + 1) * hd)
        weight = weights[0, h]
        grad_head = grad_mixed[:, at]
        grad_value += dot_tn(weight.astype(BF16), grad_head)
        grad_soft = dot_nt(grad_head, value)
        delta = jnp.sum(weight * grad_soft, axis=-1, keepdims=True)
        grad_scores = (weight * (grad_soft - delta)).astype(BF16)
        grad_key += dot_tn(grad_scores, query[:, at])
        turned = turn(dot_nn(grad_scores, key) * scale, cos, sig)
        grad, gains = norm_back(raw[:, at], qgain[...], turned)
        grad_raw[:, at] = grad.astype(BF16)
        query_gains += gains
    at = slice(heads * hd, (heads + 1) * hd)
    grad, key_gains = norm_back(raw[:, at], kgain[...], turn(grad_key * scale, cos, sig))
    grad_raw[:, at] = grad.astype(BF16)
    grad_raw[:, (heads + 1) * hd :] = grad_value.astype(BF16)
    gains = jnp.concatenate([query_gains, key_gains], axis=0)

    @pl.when(pl.program_id(0) == 0)
    def _():
        grad_gains[...] = gains

    @pl.when(pl.program_id(0) > 0)
    def _():
        grad_gains[...] += gains


def attend_back(raw, cosine, signed, query_gain, key_gain, query, kv, weights, grad_mixed, scale):
    groups, heads, tokens, _ = weights.shape
    hd = cosine.shape[1]
    rows = groups * tokens

    def block(cols):
        return pl.BlockSpec((tokens, cols), lambda g: (g, 0))

    gain = pl.BlockSpec((1, hd), lambda g: (0, 0))
    return pl.pallas_call(
        functools.partial(attend_back_kernel, scale),
        name="attend_back",
        cost_estimate=cost(1),
        grid=(groups,),
        out_shape=(
            jax.ShapeDtypeStruct((rows, (heads + 2) * hd), BF16),
            jax.ShapeDtypeStruct((2, hd), F32),
        ),
        in_specs=[
            block((heads + 2) * hd),
            block(hd),
            block(hd),
            gain,
            gain,
            block(heads * hd),
            block(2 * hd),
            pl.BlockSpec((1, heads, tokens, tokens), lambda g: (g, 0, 0, 0)),
            block(heads * hd),
        ],
        out_specs=(block((heads + 2) * hd), pl.BlockSpec((2, hd), lambda g: (0, 0))),
        compiler_params=pltpu.CompilerParams(vmem_limit_bytes=40 << 20),
    )(raw, cosine, signed, query_gain.reshape(1, hd), key_gain.reshape(1, hd), query, kv, weights, grad_mixed)


DIMS = (NX, NYH, NZ, NC, 2)
CHUNKS = (256, 256, 256, 256, 256, 256, 256, 128, 128)
BACK = (256,) * 9
TURNS = ("xzy", "zyx", "yxz")


class Route:
    def __init__(self, me, go):
        x, yh, z, c, t = me.x, me.yh, me.z, me.c, me.t
        steps = (1, 3, 2)
        turn = lambda i, d: lax.rem(i + d, RING)
        self.go = go
        self.own = {"x": (x, c), "z": (z,), "y": (yh, t)}
        self.peers = {
            "x": [((x, 1 - c), me.device(c=1 - c))]
            + [
                ((turn(x, d), e), me.device(x=turn(x, d), c=e))
                for d in steps
                for e in (c, 1 - c)
            ],
            "z": [((turn(z, d),), me.device(z=turn(z, d))) for d in steps],
            "y": [
                ((turn(me.y, d) // 2, lax.rem(turn(me.y, d), 2)), me.at_y(turn(me.y, d)))
                for d in steps
            ],
        }

    def everyone(self):
        return [peer for axis in "xzy" for _, peer in self.peers[axis]]

    @staticmethod
    def view(ref, axis, at):
        if axis == "x":
            return ref.at[at[0], :, :, at[1]]
        if axis == "z":
            return ref.at[:, :, at[0]]
        return ref.at[:, at[0], :, :, at[1]]

    def send(self, axis, src, dst):
        own = self.own[axis]
        kept = self.go.keep(self.view(src, axis, own), self.view(dst, axis, own))
        copies = [
            self.go.put(self.view(src, axis, at), self.view(dst, axis, own), peer)
            for at, peer in self.peers[axis]
        ]
        return kept, copies

    @staticmethod
    def wait(sent):
        kept, copies = sent
        for copy in copies:
            copy.wait_recv()
        kept.wait()


def columns(ref, start, size):
    return ref.at[:, :, :, :, :, :, pl.ds(start, size)]


ORDER = ((0, 0), (1, 0), (0, 1), (2, 0), (1, 1), (0, 2), (2, 1), (1, 2), (2, 2))


def enter_kernel(
    sent, told, gate, up, down, router, rows, inner_low, grad_gate, grad_up, extra, *rest
):
    chunks = len(CHUNKS)
    mids = rest[: 2 * chunks]
    held = rest[2 * chunks : 3 * chunks]
    (
        told_v, gate_v, up_v, down_v, router_v, gate_pre, up_pre, logits, inner_up, send, recv, local, loads,
    ) = rest[3 * chunks :]
    me = Place()
    go = Copies(send, recv, local)
    route = Route(me, go)
    pulls = [
        pltpu.make_async_copy(a, b, loads.at[n])
        for n, (a, b) in enumerate(
            ((told, told_v), (down, down_v), (gate, gate_v), (up, up_v), (router, router_v))
        )
    ]
    greet(route.everyone())
    starts = [sum(CHUNKS[:n]) for n in range(chunks)]
    sent_on = [None] * chunks
    outs = []
    width = sent.shape[-1]
    total = told_v.shape[0]
    experts = router.shape[1]
    index = me.expert()
    block = 256

    def cotangent(n):
        at = pl.ds(n * block, block)
        inner_up[at] = dot_nt(told_v[at, :width], down_v[...])

    def multiply(n, close=False):
        route.wait(sent_on[n])
        outs.append(go.keep(held[n], columns(rows, starts[n], CHUNKS[n])))
        cols = pl.ds(starts[n], CHUNKS[n])
        flat = held[n].reshape(total, CHUNKS[n])

        def step(m, _):
            at = pl.ds(pl.multiple_of(m * block, block), block)
            part = flat[at]
            terms = []
            for out, weight in ((gate_pre, gate_v), (up_pre, up_v), (logits, router_v)):
                term = dot_nn(part, weight[cols])
                if n > 0:
                    term = out[at] + term
                if not close:
                    out[at] = term
                terms.append(term)
            if close:
                finish(at, *terms)
            return 0

        lax.fori_loop(0, total // block, step, 0)

    def finish(at, before_gate, before_up, row_logits):
        row_logits = jnp.where(told_v[at, width:] > 0, row_logits, MASKED)
        powers = jnp.exp(row_logits - jnp.max(row_logits, axis=-1, keepdims=True))
        lane = lax.broadcasted_iota(jnp.int32, (1, experts), 1) == index
        prob = jnp.sum(jnp.where(lane, powers, 0.0), axis=-1, keepdims=True) / jnp.sum(
            powers, axis=-1, keepdims=True
        )
        back = inner_up[at]
        sigmoid = 1.0 / (1.0 + jnp.exp(-before_gate))
        silu = before_gate * sigmoid
        inner = silu * before_up
        gate_up = jnp.sum(inner * back, axis=-1, keepdims=True)
        inner_low[at] = (prob * inner).astype(BF16)
        back = prob * back
        grad_gate[at] = (back * before_up * sigmoid * (1.0 + before_gate * (1.0 - sigmoid))).astype(BF16)
        grad_up[at] = (back * silu).astype(BF16)
        high = gate_up.astype(BF16).astype(F32)
        extra[at, :experts] = jnp.where(lane, high, 0.0).astype(BF16)
        extra[at, experts:] = jnp.where(lane, gate_up - high, 0.0).astype(BF16)

    blocks = list(range(total // block))
    for triple, crossing in ORDER:
        for n in range(3 * triple, 3 * triple + 3):
            src = columns(sent, starts[n], CHUNKS[n]) if crossing == 0 else mids[2 * n + crossing - 1]
            dst = held[n] if crossing == 2 else mids[2 * n + crossing]
            if crossing > 0:
                route.wait(sent_on[n])
            sent_on[n] = route.send(TURNS[n % 3][crossing], src, dst)
            if crossing == 2 and triple > 0:
                multiply(n - 3)
            elif blocks and triple + crossing > 1:
                cotangent(blocks.pop(0))
        if (triple, crossing) == (1, 0):
            for pull in pulls:
                pull.start()
            for pull in pulls[:2]:
                pull.wait()
        if (triple, crossing) == (2, 1):
            for pull in pulls[2:]:
                pull.wait()
    for n in range(chunks - 3, chunks):
        multiply(n, close=n == chunks - 1)
    for out in outs:
        out.wait()
    go.finish()


def enter(sent, told, gate, up, down, router):
    slots, width = sent.shape
    hidden, experts = gate.shape[1], router.shape[1]
    cap = slots // math.prod(DIMS)
    lead = (*DIMS, cap)
    chunks = len(CHUNKS)
    low = jax.ShapeDtypeStruct((slots, hidden), BF16)
    rows, *rest = pl.pallas_call(
        enter_kernel,
        name="enter_experts",
        cost_estimate=cost(60),
        out_shape=(
            jax.ShapeDtypeStruct((*lead, width), BF16),
            low,
            low,
            low,
            jax.ShapeDtypeStruct((slots, 2 * experts), BF16),
        ),
        in_specs=[ANY] * 6,
        out_specs=(ANY, VMEM, VMEM, VMEM, VMEM),
        scratch_shapes=[
            *(pltpu.VMEM((*lead, w), BF16) for w in CHUNKS for _ in range(2)),
            *(pltpu.VMEM((*lead, w), BF16) for w in CHUNKS),
            pltpu.VMEM(told.shape, BF16),
            pltpu.VMEM(gate.shape, BF16),
            pltpu.VMEM(up.shape, BF16),
            pltpu.VMEM(down.shape, BF16),
            pltpu.VMEM(router.shape, BF16),
            pltpu.VMEM((slots, hidden), F32),
            pltpu.VMEM((slots, hidden), F32),
            pltpu.VMEM((slots, experts), F32),
            pltpu.VMEM((slots, hidden), F32),
            pltpu.SemaphoreType.DMA((13 * chunks,)),
            pltpu.SemaphoreType.DMA((13 * chunks,)),
            pltpu.SemaphoreType.DMA((4 * chunks,)),
            pltpu.SemaphoreType.DMA((5,)),
        ],
        compiler_params=pltpu.CompilerParams(
            collective_id=6, has_side_effects=True, vmem_limit_bytes=58 << 20
        ),
    )(sent.reshape(*lead, width), told, gate, up, down, router)
    return rows.reshape(slots, width), *rest


def leave_kernel(
    grad_gate, grad_up, extra, inner_low, spread, gate, up, down, summed, expert_out, *rest
):
    chunks = len(BACK)
    source = rest[: chunks - 1]
    mids = rest[chunks - 1 : 3 * chunks - 1]
    held = rest[3 * chunks - 1 : 4 * chunks - 1]
    gate_g, up_g, inner_v, spread_v, gate_v, up_v, down_v, out_v, send, recv, local, loads, puts = rest[4 * chunks - 1 :]
    me = Place()
    go = Copies(send, recv, local)
    route = Route(me, go)
    starts = [sum(BACK[:n]) for n in range(chunks)]
    total = gate_g.shape[0]
    block = 256
    pulls = {}
    count = 0
    for name, a, b in (("gg", grad_gate, gate_g), ("gu", grad_up, up_g)):
        pulls[name] = pltpu.make_async_copy(a, b, loads.at[count])
        count += 1
    for n in range(chunks - 1):
        cols = pl.ds(starts[n], BACK[n])
        for name, a, b in ((("g", n), gate, gate_v), (("u", n), up, up_v)):
            pulls[name] = pltpu.make_async_copy(a.at[cols], b.at[cols], loads.at[count])
            count += 1
    for name, a, b in (("inner", inner_low, inner_v), ("spread", spread, spread_v), ("down", down, down_v)):
        pulls[name] = pltpu.make_async_copy(a, b, loads.at[count])
        count += 1
    late = ("inner", "spread", "down")
    for name, pull in pulls.items():
        if name not in late:
            pull.start()
    greet(route.everyone())
    sent_on = [None] * chunks
    pushes = []

    def gradient(n):
        cols = pl.ds(starts[n], BACK[n])
        for name in (("g", n), ("u", n)):
            pulls[name].wait()
        flat = source[n].reshape(total, BACK[n])

        def step(m, _):
            at = pl.ds(pl.multiple_of(m * block, block), block)
            flat[at] = (dot_nt(gate_g[at], gate_v[cols]) + dot_nt(up_g[at], up_v[cols])).astype(BF16)
            return 0

        lax.fori_loop(0, total // block, step, 0)

    def result(m):
        if m == 0:
            pulls["inner"].wait()
            pulls["down"].wait()
        at = pl.ds(m * block, block)
        out_v[at] = dot_nn(inner_v[at], down_v[...]).astype(BF16)
        push = pltpu.make_async_copy(out_v.at[at], expert_out.at[at], puts.at[m])
        push.start()
        pushes.append(push)

    def combine(n):
        route.wait(sent_on[n])
        summed[:, starts[n] : starts[n] + BACK[n]] = dot_tn(spread_v[...], held[n].reshape(total, BACK[n])[...])

    results = list(range(total // block))
    for triple, crossing in ORDER:
        for n in range(3 * triple, 3 * triple + 3):
            dst = held[n] if crossing == 2 else mids[2 * n + crossing]
            if crossing > 0:
                route.wait(sent_on[n])
                src = mids[2 * n + crossing - 1]
            elif n == chunks - 1:
                src = extra
            else:
                if n == 0:
                    pulls["gg"].wait()
                    pulls["gu"].wait()
                gradient(n)
                src = source[n]
            sent_on[n] = route.send(TURNS[n % 3][crossing], src, dst)
            if crossing == 2 and triple > 0:
                if n == 3:
                    pulls["spread"].wait()
                combine(n - 3)
            elif results and triple + crossing > 1 and crossing > 0:
                result(results.pop(0))
        if (triple, crossing) == (1, 0):
            for name in late:
                pulls[name].start()
    for n in range(chunks - 3, chunks):
        combine(n)
    for push in pushes:
        push.wait()
    go.finish()


def leave(grad_gate, grad_up, extra, inner_low, spread, gate, up, down):
    slots, hidden = grad_gate.shape
    width, tok = gate.shape[0], spread.shape[1]
    cap = slots // math.prod(DIMS)
    lead = (*DIMS, cap)
    chunks = len(BACK)
    return pl.pallas_call(
        leave_kernel,
        name="leave_experts",
        cost_estimate=cost(60),
        out_shape=(
            jax.ShapeDtypeStruct((tok, sum(BACK)), F32),
            jax.ShapeDtypeStruct((slots, width), BF16),
        ),
        in_specs=[ANY] * 8,
        out_specs=(VMEM, ANY),
        scratch_shapes=[
            *(pltpu.VMEM((*lead, w), BF16) for w in BACK[:-1]),
            *(pltpu.VMEM((*lead, w), BF16) for w in BACK for _ in range(2)),
            *(pltpu.VMEM((*lead, w), BF16) for w in BACK),
            pltpu.VMEM(grad_gate.shape, BF16),
            pltpu.VMEM(grad_up.shape, BF16),
            pltpu.VMEM(inner_low.shape, BF16),
            pltpu.VMEM(spread.shape, BF16),
            pltpu.VMEM(gate.shape, BF16),
            pltpu.VMEM(up.shape, BF16),
            pltpu.VMEM(down.shape, BF16),
            pltpu.VMEM((slots, width), BF16),
            pltpu.SemaphoreType.DMA((13 * chunks,)),
            pltpu.SemaphoreType.DMA((13 * chunks,)),
            pltpu.SemaphoreType.DMA((3 * chunks,)),
            pltpu.SemaphoreType.DMA((2 * chunks + 3,)),
            pltpu.SemaphoreType.DMA((4,)),
        ],
        compiler_params=pltpu.CompilerParams(
            collective_id=7, has_side_effects=True, vmem_limit_bytes=58 << 20
        ),
    )(grad_gate, grad_up, extra.reshape(*lead, extra.shape[1]), inner_low, spread, gate, up, down)


def on_device(
    hidden_in,
    doc_ids,
    expert_ids,
    attn_gain,
    query_weight,
    key_weight,
    value_weight,
    output_weight,
    query_gain,
    key_gain,
    moe_gain,
    router_weight,
    gate_weight,
    up_weight,
    down_weight,
    cotangent,
):
    both = ("dp", "tensor")
    tok, width = hidden_in.shape
    hd = query_gain.shape[0]
    nkv = key_weight.shape[1] // hd
    nq = query_weight.shape[1] // hd
    group = nq // nkv
    experts = router_weight.shape[1]
    routes = expert_ids.shape[1]
    cap = tok * routes // experts
    slots = experts * cap
    scale = 1.0 / math.sqrt(hd)
    tokens = doc_ids.shape[1]

    lane = lax.broadcasted_iota(jnp.int32, (1, 1, experts), 2)
    chosen = jnp.sum((expert_ids[:, :, None] == lane).astype(F32), axis=1)
    below = (
        lax.broadcasted_iota(jnp.int32, (tok, tok), 1)
        < lax.broadcasted_iota(jnp.int32, (tok, tok), 0)
    ).astype(BF16)
    rank = dot_nn(below, chosen.astype(BF16))
    place = jnp.where(chosen > 0, rank, -1.0).T
    spread = (
        place[:, None, :] == lax.broadcasted_iota(jnp.int32, (1, cap, 1), 1).astype(F32)
    ).astype(BF16).reshape(slots, tok)

    hidden = hidden_in.astype(F32)
    normed_local = rms_scale(hidden, attn_gain).astype(BF16)

    in_weights, out_weights, normed, docs = gather(
        query_weight,
        key_weight,
        value_weight,
        output_weight.T,
        normed_local,
        jnp.broadcast_to(doc_ids, (8, tokens)).astype(F32),
    )

    spread_late, docs = lax.optimization_barrier((spread, docs))
    cot_out = dot_nn(spread_late, jnp.concatenate([cotangent, chosen.astype(BF16)], axis=1)).astype(BF16)
    cot_in = lax.all_to_all(
        cot_out.reshape(experts, cap, width + experts), both, split_axis=0, concat_axis=0, tiled=True
    ).reshape(slots, width + experts)

    position, allowed = jax.vmap(layout)(docs[:, 0])
    cosine, sine = rotary(position.reshape(-1), hd)
    cosine = jnp.concatenate([cosine, cosine], axis=1)
    signed = jnp.concatenate([-sine, sine], axis=1)
    bias = jnp.where(allowed, 0.0, MASKED).astype(F32)
    raw = dot_nn(normed, in_weights)
    heads = group * hd
    query, kv, attention, mixed = attend(raw, bias, cosine, signed, query_gain, key_gain, scale)
    attn_out = reduce(dot_nt(mixed, out_weights).astype(BF16), 2)

    residual = hidden + attn_out
    moe_input = rms_scale(residual, moe_gain).astype(BF16)
    moe_input, cot_in = lax.optimization_barrier((moe_input, cot_in))
    sent = dot_nn(spread, moe_input).astype(BF16)
    gate_mat, up_mat, down_mat = gate_weight[0], up_weight[0], down_weight[0]
    rows, inner_low, grad_gate, grad_up, extra = enter(
        sent, cot_in, gate_mat, up_mat, down_mat, router_weight
    )
    summed, expert_out = leave(
        grad_gate, grad_up, extra, inner_low, spread, gate_mat, up_mat, down_mat
    )
    logits = dot_nn(moe_input, router_weight)
    masked = jnp.where(chosen > 0, logits, MASKED)
    probs = jnp.exp(masked - jnp.max(masked, axis=-1, keepdims=True))
    probs = probs / jnp.sum(probs, axis=-1, keepdims=True)

    upstream = cotangent.astype(F32)
    gate_upstream = summed[:, width : width + experts] + summed[:, width + experts :]
    grad_chosen = probs * (gate_upstream - jnp.sum(probs * gate_upstream, axis=-1, keepdims=True))
    grad_logits = grad_chosen.astype(BF16)
    grad_moe_input = summed[:, :width] + dot_nt(grad_logits, router_weight)
    router_part = dot_tn(moe_input, grad_logits)
    grad_norm, moegain_rows = rms_back(residual, moe_gain, grad_moe_input)
    moegain_part = jnp.sum(moegain_rows, axis=0)
    grad_residual = upstream + grad_norm
    grad_attn, piece = share(grad_residual.astype(BF16), router_part.astype(BF16), 3)
    expert_out, grad_attn = lax.optimization_barrier((expert_out, grad_attn))
    returned = lax.all_to_all(
        expert_out.reshape(experts, cap, width), both, split_axis=0, concat_axis=0, tiled=True
    ).reshape(slots, width)

    grad_mixed = dot_nn(grad_attn, out_weights).astype(BF16)
    grad_raw, head_gains = attend_back(
        raw, cosine, signed, query_gain, key_gain, query, kv, attention, grad_mixed, scale
    )
    inner_low, rows, cot_in, grad_raw = lax.optimization_barrier(
        (inner_low, rows, cot_in, grad_raw)
    )
    down_grad = dot_tn(inner_low, cot_in[:, :width])
    gate_grad = dot_tn(rows, grad_gate)
    up_grad = dot_tn(rows, grad_up)
    normed_part, down_grad, gate_grad, up_grad = lax.optimization_barrier(
        (dot_nt(grad_raw, in_weights).astype(BF16), down_grad, gate_grad, up_grad)
    )
    grad_normed = reduce(normed_part, 4)
    grad_normed, returned = lax.optimization_barrier((grad_normed, returned))
    grad_hidden, attngain_rows = rms_back(hidden, attn_gain, grad_normed)
    input_grad = grad_residual + grad_hidden

    gains = jnp.concatenate([jnp.sum(attngain_rows, axis=0), moegain_part]).reshape(-1, hd)
    gains = jnp.concatenate([gains, head_gains, jnp.zeros((6, hd), F32)], axis=0)

    query_grad, key_grad, value_grad, out_grad, gains, router_grad, layer_out = scatter(
        dot_tn(normed, grad_raw).astype(BF16),
        dot_tn(grad_attn, mixed).astype(BF16),
        gains,
        piece,
        returned,
        spread,
        residual,
        (nq * hd, nkv * hd, nkv * hd, nq * hd),
    )
    at = width // hd
    return (
        layer_out,
        input_grad,
        gains[:at].reshape(-1),
        query_grad,
        key_grad,
        value_grad,
        out_grad.T,
        gains[2 * at],
        gains[2 * at + 1],
        gains[at : 2 * at].reshape(-1),
        router_grad.reshape(width, experts).astype(F32),
        gate_grad[None],
        up_grad[None],
        down_grad[None],
    )


def solution(mesh):
    both = ("dp", "tensor")
    in_specs = (
        P(both, None),
        P("dp", None),
        P(both, None),
        P(),
        P("dp", "tensor"),
        P("dp", "tensor"),
        P("dp", "tensor"),
        P("tensor", "dp"),
        P(),
        P(),
        P(),
        P(),
        P(both, None, None),
        P(both, None, None),
        P(both, None, None),
        P(both, None),
    )
    out_specs = (
        P(both, None),
        P(both, None),
        P(),
        P("dp", "tensor"),
        P("dp", "tensor"),
        P("dp", "tensor"),
        P("tensor", "dp"),
        P(),
        P(),
        P(),
        P(),
        P(both, None, None),
        P(both, None, None),
        P(both, None, None),
    )
    return jax.shard_map(
        on_device, mesh=mesh, in_specs=in_specs, out_specs=out_specs, check_vma=False
    )
```

```python
import functools
import math

import jax
import jax.numpy as jnp
from jax import lax
from jax.experimental import pallas as pl
from jax.experimental.pallas import tpu as pltpu
from jax.sharding import PartitionSpec as P

BLOCK = 128
EPSILON = 1e-06
ROPE_BASE = 1000000.0
MASKED = -1e30
F32 = jnp.float32
BF16 = jnp.bfloat16


def dot_nt(a, b):
    return lax.dot_general(a, b, (((1,), (1,)), ((), ())), preferred_element_type=F32)


def dot_tn(a, b):
    return lax.dot_general(a, b, (((0,), (0,)), ((), ())), preferred_element_type=F32)


def dot_nn(a, b):
    return lax.dot_general(a, b, (((1,), (0,)), ((), ())), preferred_element_type=F32)


def rms_recip(values):
    return lax.rsqrt(jnp.mean(values * values, axis=-1, keepdims=True) + EPSILON)


def rms_scale(values, gain):
    return values * rms_recip(values) * gain


def rms_back(values, gain, upstream):
    r = rms_recip(values)
    scaled = upstream * gain
    inner = jnp.mean(scaled * values, axis=-1, keepdims=True)
    grad_values = r * scaled - values * (r * r * r) * inner
    return grad_values, upstream * values * r


def rotate(values, cosine, sine):
    half = values.shape[-1] // 2
    a = values[..., :half]
    b = values[..., half:]
    return jnp.concatenate([a * cosine - b * sine, b * cosine + a * sine], axis=-1)


def layout(doc_row):
    length = doc_row.shape[0]
    indices = jnp.arange(length, dtype=jnp.int32)
    same_doc = doc_row[:, None] == doc_row[None, :]
    earlier = indices[None, :] < indices[:, None]
    position = jnp.sum(jnp.where(same_doc & earlier, 1, 0), axis=1).astype(jnp.int32)
    blocks = position // BLOCK
    allowed = same_doc & (blocks[None, :] <= blocks[:, None])
    return position, allowed


def rotary(position, head_size):
    half = head_size // 2
    frequency = jnp.exp(-jnp.log(ROPE_BASE) * jnp.arange(half, dtype=F32) * 2.0 / head_size)
    angles = position.astype(F32)[:, None] * frequency[None, :]
    return jnp.cos(angles), jnp.sin(angles)


MESH = pl.DeviceIdType.MESH
ANY = pl.BlockSpec(memory_space=pl.ANY)
VMEM = pl.BlockSpec(memory_space=pltpu.VMEM)
NX, NYH, NZ, NC = 4, 2, 4, 2
RING = 4


def cost(microseconds):
    return pl.CostEstimate(flops=0, transcendentals=0, bytes_accessed=int(microseconds * 3.6e6))


class Place:
    def __init__(self):
        dp = lax.axis_index("dp")
        self.t = lax.axis_index("tensor")
        self.c = lax.rem(dp, NC)
        self.z = lax.rem(dp // NC, NZ)
        self.yh = lax.rem(dp // (NC * NZ), NYH)
        self.x = dp // (NC * NZ * NYH)
        self.y = self.yh * 2 + self.t

    def device(self, x=None, yh=None, z=None, c=None, t=None):
        pick = lambda given, own: own if given is None else given
        x, yh, z, c = pick(x, self.x), pick(yh, self.yh), pick(z, self.z), pick(c, self.c)
        return (((x * NYH + yh) * NZ + z) * NC + c, pick(t, self.t))

    def expert(self):
        return ((((self.x * NYH + self.yh) * NZ + self.z) * NC) + self.c) * 2 + self.t

    def at_y(self, y):
        return self.device(yh=y // 2, t=lax.rem(y, 2))


def after(i):
    return lax.rem(i + 1, RING)


def before(i):
    return lax.rem(i + RING - 1, RING)


def across(i):
    return lax.rem(i + 2, RING)


def greet(peers):
    barrier = pltpu.get_barrier_semaphore()
    for peer in peers:
        pl.semaphore_signal(barrier, inc=1, device_id=peer, device_id_type=MESH)
    pl.semaphore_wait(barrier, len(peers))


class Copies:
    def __init__(self, send, recv, local):
        self.send, self.recv, self.local = send, recv, local
        self.n = self.m = 0
        self.sent = []
        self.waited = set()

    def put(self, src, dst, peer):
        copy = pltpu.make_async_remote_copy(
            src_ref=src,
            dst_ref=dst,
            send_sem=self.send.at[self.n],
            recv_sem=self.recv.at[self.n],
            device_id=peer,
            device_id_type=MESH,
        )
        self.n += 1
        copy.start()
        self.sent.append(copy)
        return copy

    def keep(self, src, dst):
        copy = pltpu.make_async_copy(src, dst, self.local.at[self.m])
        self.m += 1
        copy.start()
        return copy

    def release(self, copies):
        for copy in copies:
            copy.wait_send()
            self.waited.add(id(copy))

    def finish(self):
        for copy in self.sent:
            if id(copy) not in self.waited:
                copy.wait_send()


def gather_kernel(q, k, v, o, tok, doc, wa, wb, toks, docs, send, recv, local):
    me = Place()
    x, yh, z, c, p = me.x, me.yh, me.z, me.c, me.y
    sibling = me.device(c=1 - c)
    pair = me.device(yh=1 - yh)
    ring_x = (me.device(x=after(x)), me.device(x=before(x)))
    ring_z = (me.device(z=after(z)), me.device(z=before(z)))
    ring_y = (me.at_y(after(p)), me.at_y(before(p)))
    greet([sibling, pair, *ring_x, *ring_z, *ring_y])
    go = Copies(send, recv, local)

    shards, start = [], 0
    for ref, w in ((q, wa), (k, wa), (v, wa), (o, wb)):
        cols = ref.shape[1] // NYH
        to = w.at[x, yh, z, c, :, pl.ds(0 if w is wb else start, cols)]
        shards.append((ref, cols, to))
        start += cols

    def part(ref, cols, head):
        return ref.at[:, pl.ds(pl.multiple_of(head * cols, cols), cols)]

    pairs = [go.put(part(ref, cols, 1 - yh), to, pair) for ref, cols, to in shards]
    kept = [go.keep(part(ref, cols, yh), to) for ref, cols, to in shards]
    for copy in kept:
        copy.wait()
    for copy in pairs:
        copy.wait_recv()

    ways = (
        (x, z, ring_x, ring_z, lambda i, j: wa.at[i, :, j, c], lambda j: wa.at[:, :, j, c]),
        (z, x, ring_z, ring_x, lambda i, j: wb.at[j, :, i, c], lambda j: wb.at[j, :, :, c]),
    )

    def both(ref, peers):
        return [go.put(ref, ref, peer) for peer in peers]

    def relay(low, high, copies, peers):
        copies[0].wait_recv()
        up = go.put(low.at[0], low.at[0], peers[0])
        copies[1].wait_recv()
        return [up, go.put(high.at[1], high.at[1], peers[1])]

    def arrived(copies):
        for copy in copies:
            copy.wait_recv()

    near = [both(unit(i, j), one) for i, j, one, two, unit, slab in ways]
    own = [both(unit(i, j), two) for i, j, one, two, unit, slab in ways]
    rows = [go.put(tok, toks.at[p], peer) for peer in ring_y]
    rest = [go.keep(tok, toks.at[p]), go.keep(doc, docs.at[yh])]
    tail = [go.put(doc, docs.at[yh], pair)]
    far = [
        relay(unit(before(i), j), unit(after(i), j), copies, one)
        for (i, j, one, two, unit, slab), copies in zip(ways, near)
    ]
    low = [both(unit(before(i), j), two) for i, j, one, two, unit, slab in ways]
    high = [both(unit(after(i), j), two) for i, j, one, two, unit, slab in ways]
    last = []
    for (i, j, one, two, unit, slab), copies in zip(ways, far):
        arrived(copies)
        last.append(both(unit(across(i), j), two))
        tail.append(go.put(slab(j), slab(j), sibling))
    half = tok.shape[0] // 2
    rows[0].wait_recv()
    piece = toks.at[before(p), pl.ds(0, half)]
    tail.append(go.put(piece, piece, ring_y[0]))
    rows[1].wait_recv()
    piece = toks.at[after(p), pl.ds(half, half)]
    tail.append(go.put(piece, piece, ring_y[1]))
    ends = [[], []]
    for place, copies in ((lambda i: i, own), (before, low), (after, high), (across, last)):
        for n, (i, j, one, two, unit, slab) in enumerate(ways):
            u = place(i)
            ends[n] += relay(unit(u, before(j)), unit(u, after(j)), copies[n], two)
    for i, j, one, two, unit, slab in ways:
        tail.append(go.put(slab(before(j)), slab(before(j)), sibling))
        tail.append(go.put(slab(after(j)), slab(after(j)), sibling))
    for (i, j, one, two, unit, slab), copies in zip(ways, ends):
        arrived(copies)
        tail.append(go.put(slab(across(j)), slab(across(j)), sibling))
    arrived(tail)
    for copy in rest:
        copy.wait()
    go.finish()


def gather(query, key, value, out, tokens, docs):
    rows = query.shape[0]
    width_a = (query.shape[1] + key.shape[1] + value.shape[1]) // NYH
    width_b = out.shape[1] // NYH
    lead = (NX, NYH, NZ, NC, rows)
    wa, wb, toks, docs = pl.pallas_call(
        gather_kernel,
        name="gather_weights",
        cost_estimate=cost(60),
        out_shape=(
            jax.ShapeDtypeStruct((*lead, width_a), BF16),
            jax.ShapeDtypeStruct((*lead, width_b), BF16),
            jax.ShapeDtypeStruct((RING, *tokens.shape), BF16),
            jax.ShapeDtypeStruct((NYH, *docs.shape), docs.dtype),
        ),
        in_specs=[ANY] * 6,
        out_specs=(ANY,) * 4,
        scratch_shapes=[
            pltpu.SemaphoreType.DMA((57,)),
            pltpu.SemaphoreType.DMA((57,)),
            pltpu.SemaphoreType.DMA((6,)),
        ],
        compiler_params=pltpu.CompilerParams(collective_id=1, has_side_effects=True),
    )(query, key, value, out, tokens, docs)
    depth = NX * NYH * NZ * NC * rows
    return (
        wa.reshape(depth, width_a),
        wb.reshape(depth, width_b),
        toks.reshape(RING * tokens.shape[0], tokens.shape[1]),
        docs,
    )


def share_kernel(tok, part, toks, piece, got_x, sum_x, got_z, sum_z, got_y, send, recv, local):
    me = Place()
    x, yh, z, c, p = me.x, me.yh, me.z, me.c, me.y
    ring = (me.at_y(after(p)), me.at_y(before(p)))
    go = Copies(send, recv, local)
    route = Route(me, go)
    greet(route.everyone())
    half = tok.shape[0] // 2
    direct = [go.put(tok, toks.at[p], peer) for peer in ring]
    kept = go.keep(tok, toks.at[p])
    own = go.keep(part.at[x, :, :, c], got_x.at[x * NC + c])
    terms = [
        go.put(part.at[at[0], :, :, at[1]], got_x.at[x * NC + c], peer)
        for at, peer in route.peers["x"]
    ]

    def arrived(copies):
        for copy in copies:
            copy.wait_recv()

    def added(got):
        value = got[0].astype(F32)
        for n in range(1, got.shape[0]):
            value += got[n].astype(F32)
        return value

    own.wait()
    arrived(terms)
    sum_x[...] = added(got_x)
    got_z[z] = sum_x[:, z]
    terms = [go.put(sum_x.at[:, at[0]], got_z.at[z], peer) for at, peer in route.peers["z"]]
    relays = []
    for h, owner in enumerate((before(p), after(p))):
        direct[h].wait_recv()
        rows = toks.at[owner, pl.ds(h * half, half)]
        relays.append(go.put(rows, rows, ring[h]))
    arrived(terms)
    sum_z[...] = added(got_z)
    got_y[p] = sum_z[yh, me.t]
    terms = [go.put(sum_z.at[at[0], at[1]], got_y.at[p], peer) for at, peer in route.peers["y"]]
    arrived(terms)
    piece[...] = added(got_y).astype(piece.dtype)
    arrived(relays)
    kept.wait()
    go.finish()


def share(tokens, part, ident):
    rows, lanes = part.shape[0] // math.prod(DIMS), part.shape[1]
    toks, piece = pl.pallas_call(
        share_kernel,
        name=f"share_rows_{ident}",
        cost_estimate=cost(20),
        out_shape=(
            jax.ShapeDtypeStruct((RING, *tokens.shape), tokens.dtype),
            jax.ShapeDtypeStruct((rows, lanes), BF16),
        ),
        in_specs=[ANY, ANY],
        out_specs=(ANY, VMEM),
        scratch_shapes=[
            pltpu.VMEM((NX * NC, NYH, NZ, 2, rows, lanes), BF16),
            pltpu.VMEM((NYH, NZ, 2, rows, lanes), F32),
            pltpu.VMEM((NZ, NYH, 2, rows, lanes), F32),
            pltpu.VMEM((NYH, 2, rows, lanes), F32),
            pltpu.VMEM((RING, rows, lanes), F32),
            pltpu.SemaphoreType.DMA((17,)),
            pltpu.SemaphoreType.DMA((17,)),
            pltpu.SemaphoreType.DMA((2,)),
        ],
        compiler_params=pltpu.CompilerParams(collective_id=ident, has_side_effects=True),
    )(tokens, part.reshape(*DIMS, rows, lanes))
    return toks.reshape(RING * tokens.shape[0], tokens.shape[1]), piece


def reduce_kernel(part, out, held, own, got, send, recv, local):
    me = Place()
    p = me.y
    ring = (me.at_y(after(p)), me.at_y(before(p)))
    greet(ring)
    go = Copies(send, recv, local)
    half = out.shape[0] // 2
    halves = [pl.ds(h * half, half) for h in range(2)]
    near = (after(p), before(p))
    cross = [go.put(part.at[across(p), halves[h]], got.at[h], ring[h]) for h in range(2)]
    kept = [go.keep(part.at[near[h], halves[h]], held.at[h]) for h in range(2)]
    straight = [go.put(part.at[near[h], halves[1 - h]], got.at[2 + h], ring[h]) for h in range(2)]
    mine = go.keep(part.at[p], own)
    sums = []
    for h in range(2):
        kept[h].wait()
        cross[h].wait_recv()
        held[h] = (held[h].astype(F32) + got[h].astype(F32)).astype(BF16)
        sums.append(go.put(held.at[h], got.at[4 + h], ring[h]))
    mine.wait()
    for copy in straight:
        copy.wait_recv()
    for h in range(2):
        sums[h].wait_recv()
        out[halves[h]] = (
            own[halves[h]].astype(F32) + got[4 + h].astype(F32) + got[3 - h].astype(F32)
        )
    go.finish()


def reduce(part, ident):
    rows, width = part.shape[0] // RING, part.shape[1]
    half = rows // 2
    return pl.pallas_call(
        reduce_kernel,
        name=f"reduce_rows_{ident}",
        cost_estimate=cost(1),
        out_shape=jax.ShapeDtypeStruct((rows, width), F32),
        in_specs=[ANY],
        out_specs=VMEM,
        scratch_shapes=[
            pltpu.VMEM((2, half, width), BF16),
            pltpu.VMEM((rows, width), BF16),
            pltpu.VMEM((6, half, width), BF16),
            pltpu.SemaphoreType.DMA((6,)),
            pltpu.SemaphoreType.DMA((6,)),
            pltpu.SemaphoreType.DMA((3,)),
        ],
        compiler_params=pltpu.CompilerParams(
            collective_id=ident, has_side_effects=True, vmem_limit_bytes=24 << 20
        ),
    )(part.reshape(RING, rows, width))


def scatter_kernel(
    ga, gb, gains, piece, returned, slots, residual, oq, ok, ov, oo, og, op, layer, back_v, slots_v, ka, kb, da, db, ra, rb, qa, qb, sa, sb, ta, tb, ua, ub, ma, mb,
    ring_gains, sum_gains, pair_gains, send, recv, local
):
    me = Place()
    x, yh, z, c, t = me.x, me.yh, me.z, me.c, me.t
    sibling = me.device(c=1 - c)
    pair = me.device(yh=1 - yh)
    partner = me.device(t=1 - t)
    ring_x = (me.device(x=after(x)), me.device(x=before(x)))
    ring_z = (me.device(z=after(z)), me.device(z=before(z)))
    round_x = (*ring_x, me.device(x=across(x)))
    round_z = (*ring_z, me.device(z=across(z)))
    greet([sibling, pair, partner, *round_x, *round_z])
    go = Copies(send, recv, local)

    def around(n, term, own, peers):
        ring_gains[n, own] = term
        return [go.put(ring_gains.at[n, own], ring_gains.at[n, own], peer) for peer in peers]

    def ring_sum(n, copies):
        for copy in copies:
            copy.wait_recv()
        return (ring_gains[n, 0] + ring_gains[n, 1]) + (ring_gains[n, 2] + ring_gains[n, 3])

    def swap(n, term, peer):
        sum_gains[n] = term
        return go.put(sum_gains.at[n], pair_gains.at[n], peer)

    def swapped(n, copy):
        copy.wait_recv()
        return sum_gains[n] + pair_gains[n]


    ways = (
        (lambda i, h, n: ga.at[i, h, :, n], x, z, ring_x, ring_z, ka, da, ra, qa, sa, ta),
        (lambda i, h, n: gb.at[:, h, i, n], z, x, ring_z, ring_x, kb, db, rb, qb, sb, tb),
    )
    places = (across, after, before, lambda i: i)

    def spread(ref, peers):
        return [go.put(ref, ref, peer) for peer in peers]

    def arrived(copies):
        for copy in copies:
            copy.wait_recv()

    given, held = [[], []], [[], []]
    for n, place in enumerate(places):
        for w, (slab, i, j, one, two, k, d, r, q, s, u) in enumerate(ways):
            given[w].append([go.put(slab(place(i), h, 1 - c), d.at[n, h], sibling) for h in range(2)])
            held[w].append([go.keep(slab(place(i), h, c), k.at[n, h]) for h in range(2)])

    def ready(w, n, h):
        given[w][n][h].wait_recv()
        held[w][n][h].wait()

    def total(w, n, h, extra):
        slab, i, j, one, two, k, d, r, q, s, u = ways[w]

        def step(m, _):
            value = k[n, h, m].astype(F32) + d[n, h, m].astype(F32)
            for e in extra:
                value += r[e, m].astype(F32)
            k[n, h, m] = value.astype(BF16)
            return 0

        lax.fori_loop(0, k.shape[2], step, 0)

    terms = around(0, gains[...], x, round_x)
    mine = op.at[x, yh, z, c, t]
    held_piece = go.keep(piece, mine)
    pieces = [go.put(piece, mine, sibling)]
    pulls = [go.keep(returned, back_v), go.keep(slots, slots_v)]
    cross, straight, sums = [[], []], [[], []], [[], []]
    for w, (slab, i, j, one, two, k, d, r, q, s, u) in enumerate(ways):
        for h in range(2):
            ready(w, 0, h)
            total(w, 0, h, ())
            cross[w].append(go.put(k.at[0, h], r.at[h], one[h]))
    for w, (slab, i, j, one, two, k, d, r, q, s, u) in enumerate(ways):
        for h in range(2):
            ready(w, 1 + h, 1 - h)
            total(w, 1 + h, 1 - h, ())
            straight[w].append(go.put(k.at[1 + h, 1 - h], r.at[2 + h], one[h]))
    for pull in pulls:
        pull.wait()
    for m in range(4):
        cols = pl.ds(m * layer.shape[1] // 4, layer.shape[1] // 4)
        layer[:, cols] = (residual[:, cols] + dot_tn(slots_v[...], back_v[:, cols])).astype(layer.dtype)
    terms = around(1, ring_sum(0, terms), z, round_z)
    arrived(pieces)
    held_piece.wait()
    pieces = spread(op.at[x, yh, z, :, t], [partner])
    for w, (slab, i, j, one, two, k, d, r, q, s, u) in enumerate(ways):
        for h in range(2):
            ready(w, 1 + h, h)
            cross[w][h].wait_recv()
            total(w, 1 + h, h, (h,))
            sums[w].append(go.put(k.at[1 + h, h], r.at[4 + h], one[h]))
    arrived(pieces)
    pieces = spread(op.at[x, yh, z], [pair])
    terms = swap(0, ring_sum(1, terms), pair)
    for w in range(2):
        for h in range(2):
            ready(w, 3, h)
            straight[w][1 - h].wait_recv()
            total(w, 3, h, (3 - h,))
    arrived(pieces)
    pieces = spread(op.at[x, :, z], round_x)
    terms = swap(1, swapped(0, terms), partner)
    over, direct, final = [[], []], [[], []], [[], []]
    for w, (slab, i, j, one, two, k, d, r, q, s, u) in enumerate(ways):
        near = (after(j), before(j))
        for h in range(2):
            sums[w][h].wait_recv()

            def step(m, _, k=k, r=r, h=h):
                k[3, h, m] = (k[3, h, m].astype(F32) + r[4 + h, m].astype(F32)).astype(BF16)
                return 0

            lax.fori_loop(0, k.shape[2], step, 0)
            over[w].append(go.put(k.at[3, h, across(j)], q.at[h], two[h]))
        for h in range(2):
            direct[w].append(go.put(k.at[3, 1 - h, near[h]], q.at[2 + h], two[h]))
    arrived(pieces)
    pieces = spread(op.at[:, :, z], round_z)
    terms = swap(2, swapped(1, terms), sibling)
    for w, (slab, i, j, one, two, k, d, r, q, s, u) in enumerate(ways):
        near = (after(j), before(j))
        for h in range(2):
            over[w][h].wait_recv()
            s[h] = (k[3, h, near[h]].astype(F32) + q[h].astype(F32)).astype(BF16)
            final[w].append(go.put(s.at[h], q.at[4 + h], two[h]))
    last = []
    for w, ((slab, i, j, one, two, k, d, r, q, s, u), v, m) in enumerate(zip(ways, (ua, ub), (ma, mb))):
        arrived(direct[w])
        arrived(final[w])
        for h in range(2):
            u[h] = k[3, h, j].astype(F32) + q[4 + h].astype(F32) + q[3 - h].astype(F32)
        v[...] = u[1 - yh].astype(BF16)
        last.append(go.put(v, m, pair))
    og[...] = swapped(2, terms)

    def write(head, a, b):
        start = 0
        for out, block in ((oq, a), (ok, a), (ov, a), (oo, b)):
            cols = out.shape[1] // NYH
            at = 0 if block is b else start
            out[:, pl.ds(pl.multiple_of(head * cols, cols), cols)] = block[:, at : at + cols]
            start += cols

    write(yh, ta[yh], tb[yh])
    arrived(last)
    write(1 - yh, ma[...].astype(F32), mb[...].astype(F32))
    arrived(pieces)
    go.finish()


def scatter(grad_a, grad_b, gains, piece, returned, slots, residual, columns):
    rows = grad_a.shape[0] // (NX * NYH * NZ * NC)
    lead = (NX, NYH, NZ, NC, rows)
    widths = (grad_a.shape[1], grad_b.shape[1])

    def each(shape, dtype):
        return [pltpu.VMEM((*shape, rows, w), dtype) for w in widths]

    return pl.pallas_call(
        scatter_kernel,
        name="scatter_weights",
        cost_estimate=cost(80),
        out_shape=(
            *(jax.ShapeDtypeStruct((rows, w), F32) for w in columns),
            jax.ShapeDtypeStruct(gains.shape, F32),
            jax.ShapeDtypeStruct((NX, NYH, NZ, NC, 2, *piece.shape), piece.dtype),
            jax.ShapeDtypeStruct(residual.shape, BF16),
        ),
        in_specs=[ANY, ANY, VMEM, ANY, ANY, ANY, VMEM],
        out_specs=(*(VMEM,) * 5, ANY, VMEM),
        scratch_shapes=[
            pltpu.VMEM(returned.shape, BF16),
            pltpu.VMEM(slots.shape, BF16),
            *each((4, 2, RING), BF16),
            *each((4, 2, RING), BF16),
            *each((6, RING), BF16),
            *each((6,), BF16),
            *each((2,), BF16),
            *each((2,), F32),
            *each((), BF16),
            *each((), BF16),
            pltpu.VMEM((2, RING, *gains.shape), F32),
            pltpu.VMEM((3, *gains.shape), F32),
            pltpu.VMEM((3, *gains.shape), F32),
            pltpu.SemaphoreType.DMA((60,)),
            pltpu.SemaphoreType.DMA((60,)),
            pltpu.SemaphoreType.DMA((19,)),
        ],
        compiler_params=pltpu.CompilerParams(
            collective_id=5, has_side_effects=True, vmem_limit_bytes=48 << 20
        ),
    )(grad_a.reshape(*lead, widths[0]), grad_b.reshape(*lead, widths[1]), gains, piece, returned, slots, residual)


def unit_rows(values):
    return lax.rsqrt(jnp.mean(values * values, axis=-1, keepdims=True) + EPSILON)


def turn(values, cosine, signed):
    return values * cosine + pltpu.roll(values, values.shape[-1] // 2, 1) * signed


def attend_kernel(scale, raw, bias, cosine, signed, qgain, kgain, query, kv, weights, mixed):
    heads = query.shape[1] // cosine.shape[1]
    hd = cosine.shape[1]
    cos, sig = cosine[...], signed[...]
    key_raw = raw[:, heads * hd : (heads + 1) * hd]
    key = turn(key_raw * unit_rows(key_raw) * kgain[...], cos, sig).astype(BF16)
    value = raw[:, (heads + 1) * hd :].astype(BF16)
    kv[:, :hd] = key
    kv[:, hd:] = value
    for h in range(heads):
        at = slice(h * hd, (h + 1) * hd)
        head = raw[:, at]
        rows = turn(head * unit_rows(head) * qgain[...], cos, sig).astype(BF16)
        query[:, at] = rows
        scores = dot_nt(rows, key) * scale + bias[0]
        peak = jnp.max(scores, axis=-1, keepdims=True)
        weight = jnp.exp(scores - peak)
        weight = weight * (1.0 / jnp.sum(weight, axis=-1, keepdims=True))
        weights[0, h] = weight
        mixed[:, at] = dot_nn(weight.astype(BF16), value).astype(BF16)


def attend(raw, bias, cosine, signed, query_gain, key_gain, scale):
    groups, tokens = bias.shape[0], bias.shape[1]
    hd = cosine.shape[1]
    heads = raw.shape[1] // hd - 2
    rows = groups * tokens

    def block(cols):
        return pl.BlockSpec((tokens, cols), lambda g: (g, 0))

    gain = pl.BlockSpec((1, hd), lambda g: (0, 0))
    square = pl.BlockSpec((1, tokens, tokens), lambda g: (g, 0, 0))
    return pl.pallas_call(
        functools.partial(attend_kernel, scale),
        name="attend",
        cost_estimate=cost(8),
        grid=(groups,),
        out_shape=(
            jax.ShapeDtypeStruct((rows, heads * hd), BF16),
            jax.ShapeDtypeStruct((rows, 2 * hd), BF16),
            jax.ShapeDtypeStruct((groups, heads, tokens, tokens), F32),
            jax.ShapeDtypeStruct((rows, heads * hd), BF16),
        ),
        in_specs=[block((heads + 2) * hd), square, block(hd), block(hd), gain, gain],
        out_specs=(
            block(heads * hd),
            block(2 * hd),
            pl.BlockSpec((1, heads, tokens, tokens), lambda g: (g, 0, 0, 0)),
            block(heads * hd),
        ),
        compiler_params=pltpu.CompilerParams(vmem_limit_bytes=40 << 20),
    )(raw, bias, cosine, signed, query_gain.reshape(1, hd), key_gain.reshape(1, hd))


def norm_back(values, gain, upstream):
    r = unit_rows(values)
    scaled = upstream * gain
    inner = jnp.mean(scaled * values, axis=-1, keepdims=True)
    grad = r * scaled - values * (r * r * r * inner)
    return grad, jnp.sum(upstream * values * r, axis=0, keepdims=True)


def attend_back_kernel(
    scale, raw, cosine, signed, qgain, kgain, query, kv, weights, grad_mixed, grad_raw, grad_gains
):
    hd = cosine.shape[1]
    heads = query.shape[1] // hd
    cos, sig = cosine[...], -signed[...]
    key, value = kv[:, :hd], kv[:, hd:]
    grad_key = jnp.zeros(key.shape, F32)
    grad_value = jnp.zeros(key.shape, F32)
    query_gains = jnp.zeros((1, hd), F32)
    for h in range(heads):
        at = slice(h * hd, (h + 1) * hd)
        weight = weights[0, h]
        grad_head = grad_mixed[:, at]
        grad_value += dot_tn(weight.astype(BF16), grad_head)
        grad_soft = dot_nt(grad_head, value)
        delta = jnp.sum(weight * grad_soft, axis=-1, keepdims=True)
        grad_scores = (weight * (grad_soft - delta)).astype(BF16)
        grad_key += dot_tn(grad_scores, query[:, at])
        turned = turn(dot_nn(grad_scores, key) * scale, cos, sig)
        grad, gains = norm_back(raw[:, at], qgain[...], turned)
        grad_raw[:, at] = grad.astype(BF16)
        query_gains += gains
    at = slice(heads * hd, (heads + 1) * hd)
    grad, key_gains = norm_back(raw[:, at], kgain[...], turn(grad_key * scale, cos, sig))
    grad_raw[:, at] = grad.astype(BF16)
    grad_raw[:, (heads + 1) * hd :] = grad_value.astype(BF16)
    gains = jnp.concatenate([query_gains, key_gains], axis=0)

    @pl.when(pl.program_id(0) == 0)
    def _():
        grad_gains[...] = gains

    @pl.when(pl.program_id(0) > 0)
    def _():
        grad_gains[...] += gains


def attend_back(raw, cosine, signed, query_gain, key_gain, query, kv, weights, grad_mixed, scale):
    groups, heads, tokens, _ = weights.shape
    hd = cosine.shape[1]
    rows = groups * tokens

    def block(cols):
        return pl.BlockSpec((tokens, cols), lambda g: (g, 0))

    gain = pl.BlockSpec((1, hd), lambda g: (0, 0))
    return pl.pallas_call(
        functools.partial(attend_back_kernel, scale),
        name="attend_back",
        cost_estimate=cost(1),
        grid=(groups,),
        out_shape=(
            jax.ShapeDtypeStruct((rows, (heads + 2) * hd), BF16),
            jax.ShapeDtypeStruct((2, hd), F32),
        ),
        in_specs=[
            block((heads + 2) * hd),
            block(hd),
            block(hd),
            gain,
            gain,
            block(heads * hd),
            block(2 * hd),
            pl.BlockSpec((1, heads, tokens, tokens), lambda g: (g, 0, 0, 0)),
            block(heads * hd),
        ],
        out_specs=(block((heads + 2) * hd), pl.BlockSpec((2, hd), lambda g: (0, 0))),
        compiler_params=pltpu.CompilerParams(vmem_limit_bytes=40 << 20),
    )(raw, cosine, signed, query_gain.reshape(1, hd), key_gain.reshape(1, hd), query, kv, weights, grad_mixed)


DIMS = (NX, NYH, NZ, NC, 2)
CHUNKS = (256, 256, 256, 256, 256, 256, 256, 128, 128)
BACK = (256,) * 9
TURNS = ("xzy", "zyx", "yxz")


class Route:
    def __init__(self, me, go):
        x, yh, z, c, t = me.x, me.yh, me.z, me.c, me.t
        steps = (1, 3, 2)
        turn = lambda i, d: lax.rem(i + d, RING)
        self.go = go
        self.own = {"x": (x, c), "z": (z,), "y": (yh, t)}
        self.peers = {
            "x": [((x, 1 - c), me.device(c=1 - c))]
            + [
                ((turn(x, d), e), me.device(x=turn(x, d), c=e))
                for d in steps
                for e in (c, 1 - c)
            ],
            "z": [((turn(z, d),), me.device(z=turn(z, d))) for d in steps],
            "y": [
                ((turn(me.y, d) // 2, lax.rem(turn(me.y, d), 2)), me.at_y(turn(me.y, d)))
                for d in steps
            ],
        }

    def everyone(self):
        return [peer for axis in "xzy" for _, peer in self.peers[axis]]

    @staticmethod
    def view(ref, axis, at):
        if axis == "x":
            return ref.at[at[0], :, :, at[1]]
        if axis == "z":
            return ref.at[:, :, at[0]]
        return ref.at[:, at[0], :, :, at[1]]

    def send(self, axis, src, dst):
        own = self.own[axis]
        kept = self.go.keep(self.view(src, axis, own), self.view(dst, axis, own))
        copies = [
            self.go.put(self.view(src, axis, at), self.view(dst, axis, own), peer)
            for at, peer in self.peers[axis]
        ]
        return kept, copies

    @staticmethod
    def wait(sent):
        kept, copies = sent
        for copy in copies:
            copy.wait_recv()
        kept.wait()


def columns(ref, start, size):
    return ref.at[:, :, :, :, :, :, pl.ds(start, size)]


ORDER = ((0, 0), (1, 0), (0, 1), (2, 0), (1, 1), (0, 2), (2, 1), (1, 2), (2, 2))


def experts_kernel(
    tokens, spread, told, gate, up, down, router, rows, inner_low, grad_gate, grad_up, summed, expert_out, *rest
):
    chunks = len(CHUNKS)
    taken = iter(rest)
    take = lambda count: [next(taken) for _ in range(count)]
    first = take(4)
    mids_in, held_in = take(2 * chunks), take(chunks)
    mids_out, held_out = take(2 * chunks), take(chunks)
    last_source, extra = take(2)
    first += [extra, last_source]
    tokens_v, spread_v, asked_v, blocks_v, gate_v, up_v, down_v, router_v = take(8)
    gate_pre, up_pre, logits, inner_up, inner_v, gate_g, up_g = take(7)
    send, recv, local, back_send, back_recv, back_local, loads, told_sem, puts = take(9)
    me = Place()
    go, back = Copies(send, recv, local), Copies(back_send, back_recv, back_local)
    way_in, way_out = Route(me, go), Route(me, back)
    width = tokens.shape[1]
    slots, lanes = spread.shape[0], router.shape[1]
    block = 256
    index = me.expert()
    starts = [sum(CHUNKS[:n]) for n in range(chunks)]
    blocks = list(range(slots // block))

    early = [pltpu.make_async_copy(a, b, loads.at[n]) for n, (a, b) in enumerate(((tokens, tokens_v), (spread, spread_v)))]
    late = [
        pltpu.make_async_copy(a, b, loads.at[2 + n])
        for n, (a, b) in enumerate(
            ((down, down_v), (gate, gate_v), (up, up_v), (router, router_v), (told.at[:, pl.ds(width, lanes)], asked_v))
        )
    ]
    for pull in early:
        pull.start()
    greet(way_in.everyone())
    for pull in early:
        pull.wait()

    def load(m):
        at = pl.ds(m * block, block)
        return pltpu.make_async_copy(told.at[at, pl.ds(0, width)], blocks_v.at[m % 2], told_sem.at[m % 2])

    def each_block(step):
        def run(m, _):
            step(pl.ds(pl.multiple_of(m * block, block), block))
            return 0

        lax.fori_loop(0, slots // block, run, 0)

    sent_on, started = [None] * chunks, [None] * chunks
    outs = []

    def dispatch(n):
        buffer = first[n % 6]
        if n >= 6:
            go.release(started[n - 6][1])
        cols = pl.ds(starts[n], CHUNKS[n])
        flat = buffer.reshape(slots, buffer.shape[-1])

        def step(at):
            flat[at, : CHUNKS[n]] = dot_nn(spread_v[at], tokens_v[:, cols]).astype(BF16)

        each_block(step)
        return columns(buffer, 0, CHUNKS[n])

    def cotangent(m):
        load(m).wait()
        at = pl.ds(m * block, block)
        inner_up[at] = dot_nt(blocks_v[m % 2], down_v[...])
        if m + 2 < len(blocks):
            load(m + 2).start()

    def multiply(n, close=False):
        way_in.wait(sent_on[n])
        outs.append(go.keep(held_in[n], columns(rows, starts[n], CHUNKS[n])))
        cols = pl.ds(starts[n], CHUNKS[n])
        flat = held_in[n].reshape(slots, CHUNKS[n])

        def step(at):
            part = flat[at]
            terms = []
            for out, weight in ((gate_pre, gate_v), (up_pre, up_v), (logits, router_v)):
                term = dot_nn(part, weight[cols])
                if n > 0:
                    term = out[at] + term
                if not close:
                    out[at] = term
                terms.append(term)
            if close:
                finish(at, *terms)

        each_block(step)

    def finish(at, before_gate, before_up, row_logits):
        row_logits = jnp.where(asked_v[at] > 0, row_logits, MASKED)
        powers = jnp.exp(row_logits - jnp.max(row_logits, axis=-1, keepdims=True))
        lane = lax.broadcasted_iota(jnp.int32, (1, lanes), 1) == index
        prob = jnp.sum(jnp.where(lane, powers, 0.0), axis=-1, keepdims=True) / jnp.sum(
            powers, axis=-1, keepdims=True
        )
        after_inner = inner_up[at]
        sigmoid = 1.0 / (1.0 + jnp.exp(-before_gate))
        silu = before_gate * sigmoid
        inner = silu * before_up
        gate_up = jnp.sum(inner * after_inner, axis=-1, keepdims=True)
        inner_v[at] = (prob * inner).astype(BF16)
        after_inner = prob * after_inner
        gate_g[at] = (after_inner * before_up * sigmoid * (1.0 + before_gate * (1.0 - sigmoid))).astype(BF16)
        up_g[at] = (after_inner * silu).astype(BF16)
        high = gate_up.astype(BF16).astype(F32)
        flat = extra.reshape(slots, 2 * lanes)
        flat[at, :lanes] = jnp.where(lane, high, 0.0).astype(BF16)
        flat[at, lanes:] = jnp.where(lane, gate_up - high, 0.0).astype(BF16)

    todo = list(blocks)
    for triple, crossing in ORDER:
        for n in range(3 * triple, 3 * triple + 3):
            if n >= 6 and crossing == 2:
                go.release(started[n - 2][1] if n < 8 else [])
            if crossing == 0:
                src = dispatch(n)
            else:
                way_in.wait(sent_on[n])
                src = mids_in[2 * n + crossing - 1]
            dst = held_in[n] if crossing == 2 else mids_in[2 * n + crossing]
            sent_on[n] = way_in.send(TURNS[n % 3][crossing], src, dst)
            if crossing == 0:
                started[n] = sent_on[n]
            if crossing == 2 and triple > 0:
                multiply(n - 3)
            elif todo and triple + crossing > 1 and crossing > 0:
                cotangent(todo.pop(0))
        if (triple, crossing) == (1, 0):
            load(0).start()
            load(1).start()
            for pull in late:
                pull.start()
            late[0].wait()
        if (triple, crossing) == (2, 1):
            while todo:
                cotangent(todo.pop(0))
            for pull in late[1:]:
                pull.wait()
    for n in range(chunks - 3, chunks):
        multiply(n, close=n == chunks - 1)
    results = [
        pltpu.make_async_copy(a, b, puts.at[n])
        for n, (a, b) in enumerate(((inner_v, inner_low), (gate_g, grad_gate), (up_g, grad_up)))
    ]
    for result in results:
        result.start()
    for out in outs:
        out.wait()

    begins = [sum(BACK[:n]) for n in range(chunks)]
    sources = [*held_in[: chunks - 2], last_source]
    sent_back = [None] * chunks
    pushes = [None] * len(blocks)

    def gradient(n):
        cols = pl.ds(begins[n], BACK[n])
        flat = sources[n].reshape(slots, BACK[n])

        def step(at):
            flat[at] = (dot_nt(gate_g[at], gate_v[cols]) + dot_nt(up_g[at], up_v[cols])).astype(BF16)

        each_block(step)

    def outcome(m):
        if m >= 2:
            pushes[m - 2].wait()
        at = pl.ds(m * block, block)
        blocks_v[m % 2] = dot_nn(inner_v[at], down_v[...]).astype(BF16)
        pushes[m] = pltpu.make_async_copy(blocks_v.at[m % 2], expert_out.at[at], puts.at[3 + m])
        pushes[m].start()

    def combine(n):
        way_out.wait(sent_back[n])
        summed[:, begins[n] : begins[n] + BACK[n]] = dot_tn(
            spread_v[...], held_out[n].reshape(slots, BACK[n])[...]
        )

    todo = list(blocks)
    for triple, crossing in ORDER:
        for n in range(3 * triple, 3 * triple + 3):
            dst = held_out[n] if crossing == 2 else mids_out[2 * n + crossing]
            if crossing > 0:
                way_out.wait(sent_back[n])
                src = mids_out[2 * n + crossing - 1]
            elif n == chunks - 1:
                src = extra
            else:
                gradient(n)
                src = sources[n]
            sent_back[n] = way_out.send(TURNS[n % 3][crossing], src, dst)
            if crossing == 2 and triple > 0:
                combine(n - 3)
            elif todo and triple + crossing > 1 and crossing > 0:
                outcome(todo.pop(0))
    for n in range(chunks - 3, chunks):
        combine(n)
    for copy in (*results, *pushes[-2:]):
        copy.wait()
    go.finish()
    back.finish()


def experts(tokens, spread, told, gate, up, down, router):
    tok, width = tokens.shape
    slots = spread.shape[0]
    hidden, lanes = gate.shape[1], router.shape[1]
    lead = (*DIMS, slots // math.prod(DIMS))
    chunks = len(CHUNKS)
    low = jax.ShapeDtypeStruct((slots, hidden), BF16)

    def held(widths):
        return [pltpu.VMEM((*lead, w), BF16) for w in widths]

    twice = lambda widths: [w for w in widths for _ in range(2)]
    rows, *others = pl.pallas_call(
        experts_kernel,
        name="experts",
        cost_estimate=cost(120),
        out_shape=(
            jax.ShapeDtypeStruct((*lead, width), BF16),
            low,
            low,
            low,
            jax.ShapeDtypeStruct((tok, sum(BACK)), F32),
            jax.ShapeDtypeStruct((slots, width), BF16),
        ),
        in_specs=[ANY] * 7,
        out_specs=(ANY, ANY, ANY, ANY, VMEM, ANY),
        scratch_shapes=[
            *held(CHUNKS[:4]),
            *held(twice(CHUNKS)),
            *held(CHUNKS),
            *held(twice(BACK)),
            *held(BACK),
            *held((BACK[-2], BACK[-1])),
            pltpu.VMEM(tokens.shape, BF16),
            pltpu.VMEM(spread.shape, BF16),
            pltpu.VMEM((slots, lanes), BF16),
            pltpu.VMEM((2, 256, width), BF16),
            pltpu.VMEM(gate.shape, BF16),
            pltpu.VMEM(up.shape, BF16),
            pltpu.VMEM(down.shape, BF16),
            pltpu.VMEM(router.shape, BF16),
            pltpu.VMEM((slots, hidden), F32),
            pltpu.VMEM((slots, hidden), F32),
            pltpu.VMEM((slots, lanes), F32),
            pltpu.VMEM((slots, hidden), F32),
            *(pltpu.VMEM((slots, hidden), BF16) for _ in range(3)),
            pltpu.SemaphoreType.DMA((13 * chunks,)),
            pltpu.SemaphoreType.DMA((13 * chunks,)),
            pltpu.SemaphoreType.DMA((4 * chunks,)),
            pltpu.SemaphoreType.DMA((13 * chunks,)),
            pltpu.SemaphoreType.DMA((13 * chunks,)),
            pltpu.SemaphoreType.DMA((3 * chunks,)),
            pltpu.SemaphoreType.DMA((7,)),
            pltpu.SemaphoreType.DMA((2,)),
            pltpu.SemaphoreType.DMA((7,)),
        ],
        compiler_params=pltpu.CompilerParams(
            collective_id=6, has_side_effects=True, vmem_limit_bytes=61 << 20
        ),
    )(tokens, spread, told, gate, up, down, router)
    return rows.reshape(slots, width), *others


def on_device(
    hidden_in,
    doc_ids,
    expert_ids,
    attn_gain,
    query_weight,
    key_weight,
    value_weight,
    output_weight,
    query_gain,
    key_gain,
    moe_gain,
    router_weight,
    gate_weight,
    up_weight,
    down_weight,
    cotangent,
):
    both = ("dp", "tensor")
    tok, width = hidden_in.shape
    hd = query_gain.shape[0]
    nkv = key_weight.shape[1] // hd
    nq = query_weight.shape[1] // hd
    group = nq // nkv
    count = router_weight.shape[1]
    routes = expert_ids.shape[1]
    cap = tok * routes // count
    slots = count * cap
    scale = 1.0 / math.sqrt(hd)
    tokens = doc_ids.shape[1]

    lane = lax.broadcasted_iota(jnp.int32, (1, 1, count), 2)
    chosen = jnp.sum((expert_ids[:, :, None] == lane).astype(F32), axis=1)
    below = (
        lax.broadcasted_iota(jnp.int32, (tok, tok), 1)
        < lax.broadcasted_iota(jnp.int32, (tok, tok), 0)
    ).astype(BF16)
    rank = dot_nn(below, chosen.astype(BF16))
    place = jnp.where(chosen > 0, rank, -1.0).T
    spread = (
        place[:, None, :] == lax.broadcasted_iota(jnp.int32, (1, cap, 1), 1).astype(F32)
    ).astype(BF16).reshape(slots, tok)

    hidden = hidden_in.astype(F32)
    normed_local = rms_scale(hidden, attn_gain).astype(BF16)

    in_weights, out_weights, normed, docs = gather(
        query_weight,
        key_weight,
        value_weight,
        output_weight.T,
        normed_local,
        jnp.broadcast_to(doc_ids, (8, tokens)).astype(F32),
    )

    spread_late, docs = lax.optimization_barrier((spread, docs))
    cot_out = dot_nn(spread_late, jnp.concatenate([cotangent, chosen.astype(BF16)], axis=1)).astype(BF16)
    cot_in = lax.all_to_all(
        cot_out.reshape(count, cap, width + count), both, split_axis=0, concat_axis=0, tiled=True
    ).reshape(slots, width + count)

    position, allowed = jax.vmap(layout)(docs[:, 0])
    cosine, sine = rotary(position.reshape(-1), hd)
    cosine = jnp.concatenate([cosine, cosine], axis=1)
    signed = jnp.concatenate([-sine, sine], axis=1)
    bias = jnp.where(allowed, 0.0, MASKED).astype(F32)
    raw = dot_nn(normed, in_weights)
    heads = group * hd
    query, kv, attention, mixed = attend(raw, bias, cosine, signed, query_gain, key_gain, scale)
    attn_out = reduce(dot_nt(mixed, out_weights).astype(BF16), 2)

    residual = hidden + attn_out
    moe_input = rms_scale(residual, moe_gain).astype(BF16)
    moe_input, cot_in = lax.optimization_barrier((moe_input, cot_in))
    gate_mat, up_mat, down_mat = gate_weight[0], up_weight[0], down_weight[0]
    rows, inner_low, grad_gate, grad_up, summed, expert_out = experts(
        moe_input, spread, cot_in, gate_mat, up_mat, down_mat, router_weight
    )
    logits = dot_nn(moe_input, router_weight)
    masked = jnp.where(chosen > 0, logits, MASKED)
    probs = jnp.exp(masked - jnp.max(masked, axis=-1, keepdims=True))
    probs = probs / jnp.sum(probs, axis=-1, keepdims=True)

    upstream = cotangent.astype(F32)
    gate_upstream = summed[:, width : width + count] + summed[:, width + count :]
    grad_chosen = probs * (gate_upstream - jnp.sum(probs * gate_upstream, axis=-1, keepdims=True))
    grad_logits = grad_chosen.astype(BF16)
    grad_moe_input = summed[:, :width] + dot_nt(grad_logits, router_weight)
    router_part = dot_tn(moe_input, grad_logits)
    grad_norm, moegain_rows = rms_back(residual, moe_gain, grad_moe_input)
    moegain_part = jnp.sum(moegain_rows, axis=0)
    grad_residual = upstream + grad_norm
    grad_attn, piece = share(grad_residual.astype(BF16), router_part.astype(BF16), 3)
    expert_out, grad_attn = lax.optimization_barrier((expert_out, grad_attn))
    returned = lax.all_to_all(
        expert_out.reshape(count, cap, width), both, split_axis=0, concat_axis=0, tiled=True
    ).reshape(slots, width)

    grad_mixed = dot_nn(grad_attn, out_weights).astype(BF16)
    grad_raw, head_gains = attend_back(
        raw, cosine, signed, query_gain, key_gain, query, kv, attention, grad_mixed, scale
    )
    inner_low, rows, cot_in, grad_raw = lax.optimization_barrier(
        (inner_low, rows, cot_in, grad_raw)
    )
    down_grad = dot_tn(inner_low, cot_in[:, :width])
    gate_grad = dot_tn(rows, grad_gate)
    up_grad = dot_tn(rows, grad_up)
    normed_part, down_grad, gate_grad, up_grad = lax.optimization_barrier(
        (dot_nt(grad_raw, in_weights).astype(BF16), down_grad, gate_grad, up_grad)
    )
    grad_normed = reduce(normed_part, 4)
    grad_normed, returned = lax.optimization_barrier((grad_normed, returned))
    grad_hidden, attngain_rows = rms_back(hidden, attn_gain, grad_normed)
    input_grad = grad_residual + grad_hidden

    gains = jnp.concatenate([jnp.sum(attngain_rows, axis=0), moegain_part]).reshape(-1, hd)
    gains = jnp.concatenate([gains, head_gains, jnp.zeros((6, hd), F32)], axis=0)

    query_grad, key_grad, value_grad, out_grad, gains, router_grad, layer_out = scatter(
        dot_tn(normed, grad_raw).astype(BF16),
        dot_tn(grad_attn, mixed).astype(BF16),
        gains,
        piece,
        returned,
        spread,
        residual,
        (nq * hd, nkv * hd, nkv * hd, nq * hd),
    )
    at = width // hd
    return (
        layer_out,
        input_grad,
        gains[:at].reshape(-1),
        query_grad,
        key_grad,
        value_grad,
        out_grad.T,
        gains[2 * at],
        gains[2 * at + 1],
        gains[at : 2 * at].reshape(-1),
        router_grad.reshape(width, count).astype(F32),
        gate_grad[None],
        up_grad[None],
        down_grad[None],
    )


def solution(mesh):
    both = ("dp", "tensor")
    in_specs = (
        P(both, None),
        P("dp", None),
        P(both, None),
        P(),
        P("dp", "tensor"),
        P("dp", "tensor"),
        P("dp", "tensor"),
        P("tensor", "dp"),
        P(),
        P(),
        P(),
        P(),
        P(both, None, None),
        P(both, None, None),
        P(both, None, None),
        P(both, None),
    )
    out_specs = (
        P(both, None),
        P(both, None),
        P(),
        P("dp", "tensor"),
        P("dp", "tensor"),
        P("dp", "tensor"),
        P("tensor", "dp"),
        P(),
        P(),
        P(),
        P(),
        P(both, None, None),
        P(both, None, None),
        P(both, None, None),
    )
    return jax.shard_map(
        on_device, mesh=mesh, in_specs=in_specs, out_specs=out_specs, check_vma=False
    )
```

```python
import functools
import math

import jax
import jax.numpy as jnp
from jax import lax
from jax.experimental import pallas as pl
from jax.experimental.pallas import tpu as pltpu
from jax.sharding import PartitionSpec as P

BLOCK = 128
EPSILON = 1e-06
ROPE_BASE = 1000000.0
MASKED = -1e30
F32 = jnp.float32
BF16 = jnp.bfloat16


def dot_nt(a, b):
    return lax.dot_general(a, b, (((1,), (1,)), ((), ())), preferred_element_type=F32)


def dot_tn(a, b):
    return lax.dot_general(a, b, (((0,), (0,)), ((), ())), preferred_element_type=F32)


def dot_nn(a, b):
    return lax.dot_general(a, b, (((1,), (0,)), ((), ())), preferred_element_type=F32)


def rms_recip(values):
    return lax.rsqrt(jnp.mean(values * values, axis=-1, keepdims=True) + EPSILON)


def rms_scale(values, gain):
    return values * rms_recip(values) * gain


def rms_back(values, gain, upstream):
    r = rms_recip(values)
    scaled = upstream * gain
    inner = jnp.mean(scaled * values, axis=-1, keepdims=True)
    grad_values = r * scaled - values * (r * r * r) * inner
    return grad_values, upstream * values * r


def rotate(values, cosine, sine):
    half = values.shape[-1] // 2
    a = values[..., :half]
    b = values[..., half:]
    return jnp.concatenate([a * cosine - b * sine, b * cosine + a * sine], axis=-1)


def layout(doc_row):
    length = doc_row.shape[0]
    indices = jnp.arange(length, dtype=jnp.int32)
    same_doc = doc_row[:, None] == doc_row[None, :]
    earlier = indices[None, :] < indices[:, None]
    position = jnp.sum(jnp.where(same_doc & earlier, 1, 0), axis=1).astype(jnp.int32)
    blocks = position // BLOCK
    allowed = same_doc & (blocks[None, :] <= blocks[:, None])
    return position, allowed


def rotary(position, head_size):
    half = head_size // 2
    frequency = jnp.exp(-jnp.log(ROPE_BASE) * jnp.arange(half, dtype=F32) * 2.0 / head_size)
    angles = position.astype(F32)[:, None] * frequency[None, :]
    return jnp.cos(angles), jnp.sin(angles)


MESH = pl.DeviceIdType.MESH
ANY = pl.BlockSpec(memory_space=pl.ANY)
VMEM = pl.BlockSpec(memory_space=pltpu.VMEM)
NX, NYH, NZ, NC = 4, 2, 4, 2
RING = 4
EARLY = 256


def cost(microseconds):
    return pl.CostEstimate(flops=0, transcendentals=0, bytes_accessed=int(microseconds * 3.6e6))


class Place:
    def __init__(self):
        dp = lax.axis_index("dp")
        self.t = lax.axis_index("tensor")
        self.c = lax.rem(dp, NC)
        self.z = lax.rem(dp // NC, NZ)
        self.yh = lax.rem(dp // (NC * NZ), NYH)
        self.x = dp // (NC * NZ * NYH)
        self.y = self.yh * 2 + self.t

    def device(self, x=None, yh=None, z=None, c=None, t=None):
        pick = lambda given, own: own if given is None else given
        x, yh, z, c = pick(x, self.x), pick(yh, self.yh), pick(z, self.z), pick(c, self.c)
        return (((x * NYH + yh) * NZ + z) * NC + c, pick(t, self.t))

    def expert(self):
        return ((((self.x * NYH + self.yh) * NZ + self.z) * NC) + self.c) * 2 + self.t

    def at_y(self, y):
        return self.device(yh=y // 2, t=lax.rem(y, 2))


def after(i):
    return lax.rem(i + 1, RING)


def before(i):
    return lax.rem(i + RING - 1, RING)


def across(i):
    return lax.rem(i + 2, RING)


def greet(peers):
    barrier = pltpu.get_barrier_semaphore()
    for peer in peers:
        pl.semaphore_signal(barrier, inc=1, device_id=peer, device_id_type=MESH)
    pl.semaphore_wait(barrier, len(peers))


class Copies:
    def __init__(self, send, recv, local):
        self.send, self.recv, self.local = send, recv, local
        self.n = self.m = 0
        self.sent = []
        self.waited = set()

    def put(self, src, dst, peer):
        copy = pltpu.make_async_remote_copy(
            src_ref=src,
            dst_ref=dst,
            send_sem=self.send.at[self.n],
            recv_sem=self.recv.at[self.n],
            device_id=peer,
            device_id_type=MESH,
        )
        self.n += 1
        copy.start()
        self.sent.append(copy)
        return copy

    def keep(self, src, dst):
        copy = pltpu.make_async_copy(src, dst, self.local.at[self.m])
        self.m += 1
        copy.start()
        return copy

    def release(self, copies):
        for copy in copies:
            copy.wait_send()
            self.waited.add(id(copy))

    def finish(self):
        for copy in self.sent:
            if id(copy) not in self.waited:
                copy.wait_send()


def gather_kernel(
    q, k, v, o, hidden, gain, doc, spread, cot, chosen, wa, wb, toks, docs, told, later, *rest
):
    sources, mids = rest[:3], rest[3:9]
    tok, stage, send, recv, local = rest[9:]
    me = Place()
    x, yh, z, c, p = me.x, me.yh, me.z, me.c, me.y
    sibling = me.device(c=1 - c)
    pair = me.device(yh=1 - yh)
    ring_x = (me.device(x=after(x)), me.device(x=before(x)))
    ring_z = (me.device(z=after(z)), me.device(z=before(z)))
    ring_y = (me.at_y(after(p)), me.at_y(before(p)))
    go = Copies(send, recv, local)
    route = Route(me, go)
    greet(route.everyone())
    slots, block = spread.shape[0], 256

    def dispatch(n):
        cols = pl.ds(n * EARLY, EARLY)
        flat = sources[n].reshape(slots, EARLY)

        def step(m, _):
            at = pl.ds(pl.multiple_of(m * block, block), block)
            flat[at] = dot_nn(spread[at], cot[:, cols]).astype(BF16)
            return 0

        lax.fori_loop(0, slots // block, step, 0)
        return sources[n]

    pushes = [None] * (slots // block)

    def layout_later(m):
        if m >= 2:
            pushes[m - 2].wait()
        at = pl.ds(m * block, block)
        cut = cot.shape[1] - 3 * EARLY
        stage[m % 2, :, :cut] = dot_nn(spread[at], cot[:, 3 * EARLY :]).astype(BF16)
        stage[m % 2, :, cut:] = dot_nn(spread[at], chosen[...]).astype(BF16)
        pushes[m] = go.keep(stage.at[m % 2], later.at[at])

    crossed = [None] * 3

    def cross(step):
        for n in range(3):
            if step > 0:
                route.wait(crossed[n])
            src = dispatch(n) if step == 0 else mids[2 * n + step - 1]
            dst = columns(told, n * EARLY, EARLY) if step == 2 else mids[2 * n + step]
            crossed[n] = route.send(TURNS[n][step], src, dst)

    shards, start = [], 0
    for ref, w in ((q, wa), (k, wa), (v, wa), (o, wb)):
        cols = ref.shape[1] // NYH
        to = w.at[x, yh, z, c, :, pl.ds(0 if w is wb else start, cols)]
        shards.append((ref, cols, to))
        start += cols

    def part(ref, cols, head):
        return ref.at[:, pl.ds(pl.multiple_of(head * cols, cols), cols)]

    pairs = [go.put(part(ref, cols, 1 - yh), to, pair) for ref, cols, to in shards]
    kept = [go.keep(part(ref, cols, yh), to) for ref, cols, to in shards]
    rows = hidden[...].astype(F32)
    tok[...] = (rows * unit_rows(rows) * gain[...]).astype(BF16)
    for copy in kept:
        copy.wait()
    for copy in pairs:
        copy.wait_recv()

    ways = (
        (x, z, ring_x, ring_z, lambda i, j: wa.at[i, :, j, c], lambda j: wa.at[:, :, j, c]),
        (z, x, ring_z, ring_x, lambda i, j: wb.at[j, :, i, c], lambda j: wb.at[j, :, :, c]),
    )

    def both(ref, peers):
        return [go.put(ref, ref, peer) for peer in peers]

    def relay(low, high, copies, peers):
        copies[0].wait_recv()
        up = go.put(low.at[0], low.at[0], peers[0])
        copies[1].wait_recv()
        return [up, go.put(high.at[1], high.at[1], peers[1])]

    def arrived(copies):
        for copy in copies:
            copy.wait_recv()

    near = [both(unit(i, j), one) for i, j, one, two, unit, slab in ways]
    own = [both(unit(i, j), two) for i, j, one, two, unit, slab in ways]
    rows = [go.put(tok, toks.at[p], peer) for peer in ring_y]
    kept_rows = [go.keep(tok, toks.at[p]), go.keep(doc, docs.at[yh])]
    tail = [go.put(doc, docs.at[yh], pair)]
    cross(0)
    far = [
        relay(unit(before(i), j), unit(after(i), j), copies, one)
        for (i, j, one, two, unit, slab), copies in zip(ways, near)
    ]
    low = [both(unit(before(i), j), two) for i, j, one, two, unit, slab in ways]
    high = [both(unit(after(i), j), two) for i, j, one, two, unit, slab in ways]
    layout_later(0)
    last = []
    for (i, j, one, two, unit, slab), copies in zip(ways, far):
        arrived(copies)
        last.append(both(unit(across(i), j), two))
        tail.append(go.put(slab(j), slab(j), sibling))
    cross(1)
    layout_later(1)
    half = tok.shape[0] // 2
    rows[0].wait_recv()
    piece = toks.at[before(p), pl.ds(0, half)]
    tail.append(go.put(piece, piece, ring_y[0]))
    rows[1].wait_recv()
    piece = toks.at[after(p), pl.ds(half, half)]
    tail.append(go.put(piece, piece, ring_y[1]))
    ends = [[], []]
    for place, copies in ((lambda i: i, own), (before, low), (after, high), (across, last)):
        for n, (i, j, one, two, unit, slab) in enumerate(ways):
            u = place(i)
            ends[n] += relay(unit(u, before(j)), unit(u, after(j)), copies[n], two)
        if copies is high:
            cross(2)
            layout_later(2)
            layout_later(3)
    for i, j, one, two, unit, slab in ways:
        tail.append(go.put(slab(before(j)), slab(before(j)), sibling))
        tail.append(go.put(slab(after(j)), slab(after(j)), sibling))
    for (i, j, one, two, unit, slab), copies in zip(ways, ends):
        arrived(copies)
        tail.append(go.put(slab(across(j)), slab(across(j)), sibling))
    arrived(tail)
    for copy in (*kept_rows, *pushes[-2:]):
        copy.wait()
    for sent in crossed:
        route.wait(sent)
    go.finish()


def gather(query, key, value, out, hidden, gain, docs, spread, cot, chosen):
    rows = query.shape[0]
    width_a = (query.shape[1] + key.shape[1] + value.shape[1]) // NYH
    width_b = out.shape[1] // NYH
    lead = (NX, NYH, NZ, NC, rows)
    slots, width = spread.shape[0], cot.shape[1]
    blocks = (*DIMS, slots // math.prod(DIMS))
    left = width - 3 * EARLY + chosen.shape[1]
    wa, wb, toks, docs, told, later = pl.pallas_call(
        gather_kernel,
        name="gather_weights",
        cost_estimate=cost(60),
        out_shape=(
            jax.ShapeDtypeStruct((*lead, width_a), BF16),
            jax.ShapeDtypeStruct((*lead, width_b), BF16),
            jax.ShapeDtypeStruct((RING, *hidden.shape), BF16),
            jax.ShapeDtypeStruct((NYH, *docs.shape), docs.dtype),
            jax.ShapeDtypeStruct((*blocks, 3 * EARLY), BF16),
            jax.ShapeDtypeStruct((slots, left), BF16),
        ),
        in_specs=[*(ANY,) * 4, VMEM, VMEM, ANY, VMEM, VMEM, VMEM],
        out_specs=(ANY,) * 6,
        scratch_shapes=[
            *(pltpu.VMEM((*blocks, EARLY), BF16) for _ in range(9)),
            pltpu.VMEM(hidden.shape, BF16),
            pltpu.VMEM((2, 256, left), BF16),
            pltpu.SemaphoreType.DMA((96,)),
            pltpu.SemaphoreType.DMA((96,)),
            pltpu.SemaphoreType.DMA((19,)),
        ],
        compiler_params=pltpu.CompilerParams(
            collective_id=1, has_side_effects=True, vmem_limit_bytes=24 << 20
        ),
    )(query, key, value, out, hidden, gain.reshape(1, -1), docs, spread, cot, chosen)
    depth = NX * NYH * NZ * NC * rows
    return (
        wa.reshape(depth, width_a),
        wb.reshape(depth, width_b),
        toks.reshape(RING * hidden.shape[0], hidden.shape[1]),
        docs,
        told.reshape(slots, 3 * EARLY),
        later,
    )


def share_kernel(tok, part, toks, piece, got_x, sum_x, got_z, sum_z, got_y, send, recv, local):
    me = Place()
    x, yh, z, c, p = me.x, me.yh, me.z, me.c, me.y
    ring = (me.at_y(after(p)), me.at_y(before(p)))
    go = Copies(send, recv, local)
    route = Route(me, go)
    greet(route.everyone())
    half = tok.shape[0] // 2
    direct = [go.put(tok, toks.at[p], peer) for peer in ring]
    kept = go.keep(tok, toks.at[p])
    own = go.keep(part.at[x, :, :, c], got_x.at[x * NC + c])
    terms = [
        go.put(part.at[at[0], :, :, at[1]], got_x.at[x * NC + c], peer)
        for at, peer in route.peers["x"]
    ]

    def arrived(copies):
        for copy in copies:
            copy.wait_recv()

    def added(got):
        value = got[0].astype(F32)
        for n in range(1, got.shape[0]):
            value += got[n].astype(F32)
        return value

    own.wait()
    arrived(terms)
    sum_x[...] = added(got_x)
    got_z[z] = sum_x[:, z]
    terms = [go.put(sum_x.at[:, at[0]], got_z.at[z], peer) for at, peer in route.peers["z"]]
    relays = []
    for h, owner in enumerate((before(p), after(p))):
        direct[h].wait_recv()
        rows = toks.at[owner, pl.ds(h * half, half)]
        relays.append(go.put(rows, rows, ring[h]))
    arrived(terms)
    sum_z[...] = added(got_z)
    got_y[p] = sum_z[yh, me.t]
    terms = [go.put(sum_z.at[at[0], at[1]], got_y.at[p], peer) for at, peer in route.peers["y"]]
    arrived(terms)
    piece[...] = added(got_y).astype(piece.dtype)
    arrived(relays)
    kept.wait()
    go.finish()


def share(tokens, part, ident):
    rows, lanes = part.shape[0] // math.prod(DIMS), part.shape[1]
    toks, piece = pl.pallas_call(
        share_kernel,
        name=f"share_rows_{ident}",
        cost_estimate=cost(20),
        out_shape=(
            jax.ShapeDtypeStruct((RING, *tokens.shape), tokens.dtype),
            jax.ShapeDtypeStruct((rows, lanes), BF16),
        ),
        in_specs=[ANY, ANY],
        out_specs=(ANY, VMEM),
        scratch_shapes=[
            pltpu.VMEM((NX * NC, NYH, NZ, 2, rows, lanes), BF16),
            pltpu.VMEM((NYH, NZ, 2, rows, lanes), F32),
            pltpu.VMEM((NZ, NYH, 2, rows, lanes), F32),
            pltpu.VMEM((NYH, 2, rows, lanes), F32),
            pltpu.VMEM((RING, rows, lanes), F32),
            pltpu.SemaphoreType.DMA((17,)),
            pltpu.SemaphoreType.DMA((17,)),
            pltpu.SemaphoreType.DMA((2,)),
        ],
        compiler_params=pltpu.CompilerParams(collective_id=ident, has_side_effects=True),
    )(tokens, part.reshape(*DIMS, rows, lanes))
    return toks.reshape(RING * tokens.shape[0], tokens.shape[1]), piece


def reduce_kernel(part, out, held, own, got, send, recv, local):
    me = Place()
    p = me.y
    ring = (me.at_y(after(p)), me.at_y(before(p)))
    greet(ring)
    go = Copies(send, recv, local)
    half = out.shape[0] // 2
    halves = [pl.ds(h * half, half) for h in range(2)]
    near = (after(p), before(p))
    cross = [go.put(part.at[across(p), halves[h]], got.at[h], ring[h]) for h in range(2)]
    kept = [go.keep(part.at[near[h], halves[h]], held.at[h]) for h in range(2)]
    straight = [go.put(part.at[near[h], halves[1 - h]], got.at[2 + h], ring[h]) for h in range(2)]
    mine = go.keep(part.at[p], own)
    sums = []
    for h in range(2):
        kept[h].wait()
        cross[h].wait_recv()
        held[h] = (held[h].astype(F32) + got[h].astype(F32)).astype(BF16)
        sums.append(go.put(held.at[h], got.at[4 + h], ring[h]))
    mine.wait()
    for copy in straight:
        copy.wait_recv()
    for h in range(2):
        sums[h].wait_recv()
        out[halves[h]] = (
            own[halves[h]].astype(F32) + got[4 + h].astype(F32) + got[3 - h].astype(F32)
        )
    go.finish()


def reduce(part, ident):
    rows, width = part.shape[0] // RING, part.shape[1]
    half = rows // 2
    return pl.pallas_call(
        reduce_kernel,
        name=f"reduce_rows_{ident}",
        cost_estimate=cost(1),
        out_shape=jax.ShapeDtypeStruct((rows, width), F32),
        in_specs=[ANY],
        out_specs=VMEM,
        scratch_shapes=[
            pltpu.VMEM((2, half, width), BF16),
            pltpu.VMEM((rows, width), BF16),
            pltpu.VMEM((6, half, width), BF16),
            pltpu.SemaphoreType.DMA((6,)),
            pltpu.SemaphoreType.DMA((6,)),
            pltpu.SemaphoreType.DMA((3,)),
        ],
        compiler_params=pltpu.CompilerParams(
            collective_id=ident, has_side_effects=True, vmem_limit_bytes=24 << 20
        ),
    )(part.reshape(RING, rows, width))


def scatter_kernel(
    ga, gb, gains, piece, returned, slots, residual, oq, ok, ov, oo, og, op, layer, back_v, slots_v, ka, kb, da, db, ra, rb, qa, qb, sa, sb, ta, tb, ua, ub, ma, mb,
    ring_gains, sum_gains, pair_gains, send, recv, local
):
    me = Place()
    x, yh, z, c, t = me.x, me.yh, me.z, me.c, me.t
    sibling = me.device(c=1 - c)
    pair = me.device(yh=1 - yh)
    partner = me.device(t=1 - t)
    ring_x = (me.device(x=after(x)), me.device(x=before(x)))
    ring_z = (me.device(z=after(z)), me.device(z=before(z)))
    round_x = (*ring_x, me.device(x=across(x)))
    round_z = (*ring_z, me.device(z=across(z)))
    greet([sibling, pair, partner, *round_x, *round_z])
    go = Copies(send, recv, local)

    def around(n, term, own, peers):
        ring_gains[n, own] = term
        return [go.put(ring_gains.at[n, own], ring_gains.at[n, own], peer) for peer in peers]

    def ring_sum(n, copies):
        for copy in copies:
            copy.wait_recv()
        return (ring_gains[n, 0] + ring_gains[n, 1]) + (ring_gains[n, 2] + ring_gains[n, 3])

    def swap(n, term, peer):
        sum_gains[n] = term
        return go.put(sum_gains.at[n], pair_gains.at[n], peer)

    def swapped(n, copy):
        copy.wait_recv()
        return sum_gains[n] + pair_gains[n]


    ways = (
        (lambda i, h, n: ga.at[i, h, :, n], x, z, ring_x, ring_z, ka, da, ra, qa, sa, ta),
        (lambda i, h, n: gb.at[:, h, i, n], z, x, ring_z, ring_x, kb, db, rb, qb, sb, tb),
    )
    places = (across, after, before, lambda i: i)

    def spread(ref, peers):
        return [go.put(ref, ref, peer) for peer in peers]

    def arrived(copies):
        for copy in copies:
            copy.wait_recv()

    given, held = [[], []], [[], []]
    for n, place in enumerate(places):
        for w, (slab, i, j, one, two, k, d, r, q, s, u) in enumerate(ways):
            given[w].append([go.put(slab(place(i), h, 1 - c), d.at[n, h], sibling) for h in range(2)])
            held[w].append([go.keep(slab(place(i), h, c), k.at[n, h]) for h in range(2)])

    def ready(w, n, h):
        given[w][n][h].wait_recv()
        held[w][n][h].wait()

    def total(w, n, h, extra):
        slab, i, j, one, two, k, d, r, q, s, u = ways[w]

        def step(m, _):
            value = k[n, h, m].astype(F32) + d[n, h, m].astype(F32)
            for e in extra:
                value += r[e, m].astype(F32)
            k[n, h, m] = value.astype(BF16)
            return 0

        lax.fori_loop(0, k.shape[2], step, 0)

    terms = around(0, gains[...], x, round_x)
    mine = op.at[x, yh, z, c, t]
    held_piece = go.keep(piece, mine)
    pieces = [go.put(piece, mine, sibling)]
    pulls = [go.keep(returned, back_v), go.keep(slots, slots_v)]
    cross, straight, sums = [[], []], [[], []], [[], []]
    for w, (slab, i, j, one, two, k, d, r, q, s, u) in enumerate(ways):
        for h in range(2):
            ready(w, 0, h)
            total(w, 0, h, ())
            cross[w].append(go.put(k.at[0, h], r.at[h], one[h]))
    for w, (slab, i, j, one, two, k, d, r, q, s, u) in enumerate(ways):
        for h in range(2):
            ready(w, 1 + h, 1 - h)
            total(w, 1 + h, 1 - h, ())
            straight[w].append(go.put(k.at[1 + h, 1 - h], r.at[2 + h], one[h]))
    for pull in pulls:
        pull.wait()
    for m in range(4):
        cols = pl.ds(m * layer.shape[1] // 4, layer.shape[1] // 4)
        layer[:, cols] = (residual[:, cols] + dot_tn(slots_v[...], back_v[:, cols])).astype(layer.dtype)
    terms = around(1, ring_sum(0, terms), z, round_z)
    arrived(pieces)
    held_piece.wait()
    pieces = spread(op.at[x, yh, z, :, t], [partner])
    for w, (slab, i, j, one, two, k, d, r, q, s, u) in enumerate(ways):
        for h in range(2):
            ready(w, 1 + h, h)
            cross[w][h].wait_recv()
            total(w, 1 + h, h, (h,))
            sums[w].append(go.put(k.at[1 + h, h], r.at[4 + h], one[h]))
    arrived(pieces)
    pieces = spread(op.at[x, yh, z], [pair])
    terms = swap(0, ring_sum(1, terms), pair)
    for w in range(2):
        for h in range(2):
            ready(w, 3, h)
            straight[w][1 - h].wait_recv()
            total(w, 3, h, (3 - h,))
    arrived(pieces)
    pieces = spread(op.at[x, :, z], round_x)
    terms = swap(1, swapped(0, terms), partner)
    over, direct, final = [[], []], [[], []], [[], []]
    for w, (slab, i, j, one, two, k, d, r, q, s, u) in enumerate(ways):
        near = (after(j), before(j))
        for h in range(2):
            sums[w][h].wait_recv()

            def step(m, _, k=k, r=r, h=h):
                k[3, h, m] = (k[3, h, m].astype(F32) + r[4 + h, m].astype(F32)).astype(BF16)
                return 0

            lax.fori_loop(0, k.shape[2], step, 0)
            over[w].append(go.put(k.at[3, h, across(j)], q.at[h], two[h]))
        for h in range(2):
            direct[w].append(go.put(k.at[3, 1 - h, near[h]], q.at[2 + h], two[h]))
    arrived(pieces)
    pieces = spread(op.at[:, :, z], round_z)
    terms = swap(2, swapped(1, terms), sibling)
    for w, (slab, i, j, one, two, k, d, r, q, s, u) in enumerate(ways):
        near = (after(j), before(j))
        for h in range(2):
            over[w][h].wait_recv()
            s[h] = (k[3, h, near[h]].astype(F32) + q[h].astype(F32)).astype(BF16)
            final[w].append(go.put(s.at[h], q.at[4 + h], two[h]))
    last = []
    for w, ((slab, i, j, one, two, k, d, r, q, s, u), v, m) in enumerate(zip(ways, (ua, ub), (ma, mb))):
        arrived(direct[w])
        arrived(final[w])
        for h in range(2):
            u[h] = k[3, h, j].astype(F32) + q[4 + h].astype(F32) + q[3 - h].astype(F32)
        v[...] = u[1 - yh].astype(BF16)
        last.append(go.put(v, m, pair))
    og[...] = swapped(2, terms)

    def write(head, a, b):
        start = 0
        for out, block in ((oq, a), (ok, a), (ov, a), (oo, b)):
            cols = out.shape[1] // NYH
            at = 0 if block is b else start
            out[:, pl.ds(pl.multiple_of(head * cols, cols), cols)] = block[:, at : at + cols]
            start += cols

    write(yh, ta[yh], tb[yh])
    arrived(last)
    write(1 - yh, ma[...].astype(F32), mb[...].astype(F32))
    arrived(pieces)
    go.finish()


def scatter(grad_a, grad_b, gains, piece, returned, slots, residual, columns):
    rows = grad_a.shape[0] // (NX * NYH * NZ * NC)
    lead = (NX, NYH, NZ, NC, rows)
    widths = (grad_a.shape[1], grad_b.shape[1])

    def each(shape, dtype):
        return [pltpu.VMEM((*shape, rows, w), dtype) for w in widths]

    return pl.pallas_call(
        scatter_kernel,
        name="scatter_weights",
        cost_estimate=cost(80),
        out_shape=(
            *(jax.ShapeDtypeStruct((rows, w), F32) for w in columns),
            jax.ShapeDtypeStruct(gains.shape, F32),
            jax.ShapeDtypeStruct((NX, NYH, NZ, NC, 2, *piece.shape), piece.dtype),
            jax.ShapeDtypeStruct(residual.shape, BF16),
        ),
        in_specs=[ANY, ANY, VMEM, ANY, ANY, ANY, VMEM],
        out_specs=(*(VMEM,) * 5, ANY, VMEM),
        scratch_shapes=[
            pltpu.VMEM(returned.shape, BF16),
            pltpu.VMEM(slots.shape, BF16),
            *each((4, 2, RING), BF16),
            *each((4, 2, RING), BF16),
            *each((6, RING), BF16),
            *each((6,), BF16),
            *each((2,), BF16),
            *each((2,), F32),
            *each((), BF16),
            *each((), BF16),
            pltpu.VMEM((2, RING, *gains.shape), F32),
            pltpu.VMEM((3, *gains.shape), F32),
            pltpu.VMEM((3, *gains.shape), F32),
            pltpu.SemaphoreType.DMA((60,)),
            pltpu.SemaphoreType.DMA((60,)),
            pltpu.SemaphoreType.DMA((19,)),
        ],
        compiler_params=pltpu.CompilerParams(
            collective_id=5, has_side_effects=True, vmem_limit_bytes=48 << 20
        ),
    )(grad_a.reshape(*lead, widths[0]), grad_b.reshape(*lead, widths[1]), gains, piece, returned, slots, residual)


def unit_rows(values):
    return lax.rsqrt(jnp.mean(values * values, axis=-1, keepdims=True) + EPSILON)


def turn(values, cosine, signed):
    return values * cosine + pltpu.roll(values, values.shape[-1] // 2, 1) * signed


def attend_kernel(scale, raw, bias, cosine, signed, qgain, kgain, query, kv, weights, mixed):
    heads = query.shape[1] // cosine.shape[1]
    hd = cosine.shape[1]
    cos, sig = cosine[...], signed[...]
    key_raw = raw[:, heads * hd : (heads + 1) * hd]
    key = turn(key_raw * unit_rows(key_raw) * kgain[...], cos, sig).astype(BF16)
    value = raw[:, (heads + 1) * hd :].astype(BF16)
    kv[:, :hd] = key
    kv[:, hd:] = value
    for h in range(heads):
        at = slice(h * hd, (h + 1) * hd)
        head = raw[:, at]
        rows = turn(head * unit_rows(head) * qgain[...], cos, sig).astype(BF16)
        query[:, at] = rows
        scores = dot_nt(rows, key) * scale + bias[0]
        peak = jnp.max(scores, axis=-1, keepdims=True)
        weight = jnp.exp(scores - peak)
        weight = weight * (1.0 / jnp.sum(weight, axis=-1, keepdims=True))
        weights[0, h] = weight
        mixed[:, at] = dot_nn(weight.astype(BF16), value).astype(BF16)


def attend(raw, bias, cosine, signed, query_gain, key_gain, scale):
    groups, tokens = bias.shape[0], bias.shape[1]
    hd = cosine.shape[1]
    heads = raw.shape[1] // hd - 2
    rows = groups * tokens

    def block(cols):
        return pl.BlockSpec((tokens, cols), lambda g: (g, 0))

    gain = pl.BlockSpec((1, hd), lambda g: (0, 0))
    square = pl.BlockSpec((1, tokens, tokens), lambda g: (g, 0, 0))
    return pl.pallas_call(
        functools.partial(attend_kernel, scale),
        name="attend",
        cost_estimate=cost(8),
        grid=(groups,),
        out_shape=(
            jax.ShapeDtypeStruct((rows, heads * hd), BF16),
            jax.ShapeDtypeStruct((rows, 2 * hd), BF16),
            jax.ShapeDtypeStruct((groups, heads, tokens, tokens), F32),
            jax.ShapeDtypeStruct((rows, heads * hd), BF16),
        ),
        in_specs=[block((heads + 2) * hd), square, block(hd), block(hd), gain, gain],
        out_specs=(
            block(heads * hd),
            block(2 * hd),
            pl.BlockSpec((1, heads, tokens, tokens), lambda g: (g, 0, 0, 0)),
            block(heads * hd),
        ),
        compiler_params=pltpu.CompilerParams(vmem_limit_bytes=40 << 20),
    )(raw, bias, cosine, signed, query_gain.reshape(1, hd), key_gain.reshape(1, hd))


def norm_back(values, gain, upstream):
    r = unit_rows(values)
    scaled = upstream * gain
    inner = jnp.mean(scaled * values, axis=-1, keepdims=True)
    grad = r * scaled - values * (r * r * r * inner)
    return grad, jnp.sum(upstream * values * r, axis=0, keepdims=True)


def attend_back_kernel(
    scale, raw, cosine, signed, qgain, kgain, query, kv, weights, grad_mixed, grad_raw, grad_gains
):
    hd = cosine.shape[1]
    heads = query.shape[1] // hd
    cos, sig = cosine[...], -signed[...]
    key, value = kv[:, :hd], kv[:, hd:]
    grad_key = jnp.zeros(key.shape, F32)
    grad_value = jnp.zeros(key.shape, F32)
    query_gains = jnp.zeros((1, hd), F32)
    for h in range(heads):
        at = slice(h * hd, (h + 1) * hd)
        weight = weights[0, h]
        grad_head = grad_mixed[:, at]
        grad_value += dot_tn(weight.astype(BF16), grad_head)
        grad_soft = dot_nt(grad_head, value)
        delta = jnp.sum(weight * grad_soft, axis=-1, keepdims=True)
        grad_scores = (weight * (grad_soft - delta)).astype(BF16)
        grad_key += dot_tn(grad_scores, query[:, at])
        turned = turn(dot_nn(grad_scores, key) * scale, cos, sig)
        grad, gains = norm_back(raw[:, at], qgain[...], turned)
        grad_raw[:, at] = grad.astype(BF16)
        query_gains += gains
    at = slice(heads * hd, (heads + 1) * hd)
    grad, key_gains = norm_back(raw[:, at], kgain[...], turn(grad_key * scale, cos, sig))
    grad_raw[:, at] = grad.astype(BF16)
    grad_raw[:, (heads + 1) * hd :] = grad_value.astype(BF16)
    gains = jnp.concatenate([query_gains, key_gains], axis=0)

    @pl.when(pl.program_id(0) == 0)
    def _():
        grad_gains[...] = gains

    @pl.when(pl.program_id(0) > 0)
    def _():
        grad_gains[...] += gains


def attend_back(raw, cosine, signed, query_gain, key_gain, query, kv, weights, grad_mixed, scale):
    groups, heads, tokens, _ = weights.shape
    hd = cosine.shape[1]
    rows = groups * tokens

    def block(cols):
        return pl.BlockSpec((tokens, cols), lambda g: (g, 0))

    gain = pl.BlockSpec((1, hd), lambda g: (0, 0))
    return pl.pallas_call(
        functools.partial(attend_back_kernel, scale),
        name="attend_back",
        cost_estimate=cost(1),
        grid=(groups,),
        out_shape=(
            jax.ShapeDtypeStruct((rows, (heads + 2) * hd), BF16),
            jax.ShapeDtypeStruct((2, hd), F32),
        ),
        in_specs=[
            block((heads + 2) * hd),
            block(hd),
            block(hd),
            gain,
            gain,
            block(heads * hd),
            block(2 * hd),
            pl.BlockSpec((1, heads, tokens, tokens), lambda g: (g, 0, 0, 0)),
            block(heads * hd),
        ],
        out_specs=(block((heads + 2) * hd), pl.BlockSpec((2, hd), lambda g: (0, 0))),
        compiler_params=pltpu.CompilerParams(vmem_limit_bytes=40 << 20),
    )(raw, cosine, signed, query_gain.reshape(1, hd), key_gain.reshape(1, hd), query, kv, weights, grad_mixed)


DIMS = (NX, NYH, NZ, NC, 2)
CHUNKS = (256, 256, 256, 256, 256, 256, 256, 128, 128)
BACK = (256,) * 9
TURNS = ("xzy", "zyx", "yxz")


class Route:
    def __init__(self, me, go):
        x, yh, z, c, t = me.x, me.yh, me.z, me.c, me.t
        steps = (1, 3, 2)
        turn = lambda i, d: lax.rem(i + d, RING)
        self.go = go
        self.own = {"x": (x, c), "z": (z,), "y": (yh, t)}
        self.peers = {
            "x": [((x, 1 - c), me.device(c=1 - c))]
            + [
                ((turn(x, d), e), me.device(x=turn(x, d), c=e))
                for d in steps
                for e in (c, 1 - c)
            ],
            "z": [((turn(z, d),), me.device(z=turn(z, d))) for d in steps],
            "y": [
                ((turn(me.y, d) // 2, lax.rem(turn(me.y, d), 2)), me.at_y(turn(me.y, d)))
                for d in steps
            ],
        }

    def everyone(self):
        return [peer for axis in "xzy" for _, peer in self.peers[axis]]

    @staticmethod
    def view(ref, axis, at):
        if axis == "x":
            return ref.at[at[0], :, :, at[1]]
        if axis == "z":
            return ref.at[:, :, at[0]]
        return ref.at[:, at[0], :, :, at[1]]

    def send(self, axis, src, dst):
        own = self.own[axis]
        kept = self.go.keep(self.view(src, axis, own), self.view(dst, axis, own))
        copies = [
            self.go.put(self.view(src, axis, at), self.view(dst, axis, own), peer)
            for at, peer in self.peers[axis]
        ]
        return kept, copies

    @staticmethod
    def wait(sent):
        kept, copies = sent
        for copy in copies:
            copy.wait_recv()
        kept.wait()


def columns(ref, start, size):
    return ref.at[:, :, :, :, :, :, pl.ds(start, size)]


ORDER = ((0, 0), (1, 0), (0, 1), (2, 0), (1, 1), (0, 2), (2, 1), (1, 2), (2, 2))


def experts_kernel(
    tokens, spread, told, later, gate, up, down, router, rows, inner_low, grad_gate, grad_up, summed, expert_out, *rest
):
    chunks = len(CHUNKS)
    taken = iter(rest)
    take = lambda count: [next(taken) for _ in range(count)]
    first = take(4)
    mids_in, held_in = take(2 * chunks), take(chunks)
    mids_out, held_out = take(2 * chunks), take(chunks)
    last_source, extra = take(2)
    first += [extra, last_source]
    tokens_v, spread_v, asked_v, blocks_v, gate_v, up_v, down_v, router_v = take(8)
    gate_pre, up_pre, logits, inner_up, inner_v, gate_g, up_g = take(7)
    send, recv, local, back_send, back_recv, back_local, loads, told_sem, puts = take(9)
    me = Place()
    go, back = Copies(send, recv, local), Copies(back_send, back_recv, back_local)
    way_in, way_out = Route(me, go), Route(me, back)
    width = tokens.shape[1]
    slots, lanes = spread.shape[0], router.shape[1]
    block = 256
    index = me.expert()
    starts = [sum(CHUNKS[:n]) for n in range(chunks)]
    blocks = list(range(slots // block))

    early = [pltpu.make_async_copy(a, b, loads.at[n]) for n, (a, b) in enumerate(((tokens, tokens_v), (spread, spread_v)))]
    late = [
        pltpu.make_async_copy(a, b, loads.at[2 + n])
        for n, (a, b) in enumerate(
            ((down, down_v), (gate, gate_v), (up, up_v), (router, router_v), (later.at[:, pl.ds(width - told.shape[1], lanes)], asked_v))
        )
    ]
    for pull in early:
        pull.start()
    greet(way_in.everyone())
    for pull in early:
        pull.wait()

    def load(m):
        at, cut = pl.ds(m * block, block), told.shape[1]
        return [
            pltpu.make_async_copy(told.at[at], blocks_v.at[m % 2, :, pl.ds(0, cut)], told_sem.at[0, m % 2]),
            pltpu.make_async_copy(
                later.at[at, pl.ds(0, width - cut)], blocks_v.at[m % 2, :, pl.ds(cut, width - cut)], told_sem.at[1, m % 2]
            ),
        ]

    def each_block(step):
        def run(m, _):
            step(pl.ds(pl.multiple_of(m * block, block), block))
            return 0

        lax.fori_loop(0, slots // block, run, 0)

    sent_on, started = [None] * chunks, [None] * chunks
    outs = []

    def dispatch(n):
        buffer = first[n % 6]
        if n >= 6:
            go.release(started[n - 6][1])
        cols = pl.ds(starts[n], CHUNKS[n])
        flat = buffer.reshape(slots, buffer.shape[-1])

        def step(at):
            flat[at, : CHUNKS[n]] = dot_nn(spread_v[at], tokens_v[:, cols]).astype(BF16)

        each_block(step)
        return columns(buffer, 0, CHUNKS[n])

    def cotangent(m):
        for pull in load(m):
            pull.wait()
        at = pl.ds(m * block, block)
        inner_up[at] = dot_nt(blocks_v[m % 2], down_v[...])
        if m + 2 < len(blocks):
            for pull in load(m + 2):
                pull.start()

    def multiply(n, close=False):
        way_in.wait(sent_on[n])
        outs.append(go.keep(held_in[n], columns(rows, starts[n], CHUNKS[n])))
        cols = pl.ds(starts[n], CHUNKS[n])
        flat = held_in[n].reshape(slots, CHUNKS[n])

        def step(at):
            part = flat[at]
            terms = []
            for out, weight in ((gate_pre, gate_v), (up_pre, up_v), (logits, router_v)):
                term = dot_nn(part, weight[cols])
                if n > 0:
                    term = out[at] + term
                if not close:
                    out[at] = term
                terms.append(term)
            if close:
                finish(at, *terms)

        each_block(step)

    def finish(at, before_gate, before_up, row_logits):
        row_logits = jnp.where(asked_v[at] > 0, row_logits, MASKED)
        powers = jnp.exp(row_logits - jnp.max(row_logits, axis=-1, keepdims=True))
        lane = lax.broadcasted_iota(jnp.int32, (1, lanes), 1) == index
        prob = jnp.sum(jnp.where(lane, powers, 0.0), axis=-1, keepdims=True) / jnp.sum(
            powers, axis=-1, keepdims=True
        )
        after_inner = inner_up[at]
        sigmoid = 1.0 / (1.0 + jnp.exp(-before_gate))
        silu = before_gate * sigmoid
        inner = silu * before_up
        gate_up = jnp.sum(inner * after_inner, axis=-1, keepdims=True)
        inner_v[at] = (prob * inner).astype(BF16)
        after_inner = prob * after_inner
        gate_g[at] = (after_inner * before_up * sigmoid * (1.0 + before_gate * (1.0 - sigmoid))).astype(BF16)
        up_g[at] = (after_inner * silu).astype(BF16)
        high = gate_up.astype(BF16).astype(F32)
        flat = extra.reshape(slots, 2 * lanes)
        flat[at, :lanes] = jnp.where(lane, high, 0.0).astype(BF16)
        flat[at, lanes:] = jnp.where(lane, gate_up - high, 0.0).astype(BF16)

    todo = list(blocks)
    for triple, crossing in ORDER:
        for n in range(3 * triple, 3 * triple + 3):
            if n >= 6 and crossing == 2:
                go.release(started[n - 2][1] if n < 8 else [])
            if crossing == 0:
                src = dispatch(n)
            else:
                way_in.wait(sent_on[n])
                src = mids_in[2 * n + crossing - 1]
            dst = held_in[n] if crossing == 2 else mids_in[2 * n + crossing]
            sent_on[n] = way_in.send(TURNS[n % 3][crossing], src, dst)
            if crossing == 0:
                started[n] = sent_on[n]
            if crossing == 2 and triple > 0:
                multiply(n - 3)
            elif todo and triple + crossing > 1 and crossing > 0:
                cotangent(todo.pop(0))
        if (triple, crossing) == (1, 0):
            for pull in (*load(0), *load(1), *late):
                pull.start()
            late[0].wait()
        if (triple, crossing) == (2, 1):
            while todo:
                cotangent(todo.pop(0))
            for pull in late[1:]:
                pull.wait()
    for n in range(chunks - 3, chunks):
        multiply(n, close=n == chunks - 1)
    results = [
        pltpu.make_async_copy(a, b, puts.at[n])
        for n, (a, b) in enumerate(((inner_v, inner_low), (gate_g, grad_gate), (up_g, grad_up)))
    ]
    for result in results:
        result.start()
    for out in outs:
        out.wait()

    begins = [sum(BACK[:n]) for n in range(chunks)]
    sources = [*held_in[: chunks - 2], last_source]
    sent_back = [None] * chunks
    pushes = [None] * len(blocks)

    def gradient(n):
        cols = pl.ds(begins[n], BACK[n])
        flat = sources[n].reshape(slots, BACK[n])

        def step(at):
            flat[at] = (dot_nt(gate_g[at], gate_v[cols]) + dot_nt(up_g[at], up_v[cols])).astype(BF16)

        each_block(step)

    def outcome(m):
        if m >= 2:
            pushes[m - 2].wait()
        at = pl.ds(m * block, block)
        blocks_v[m % 2] = dot_nn(inner_v[at], down_v[...]).astype(BF16)
        pushes[m] = pltpu.make_async_copy(blocks_v.at[m % 2], expert_out.at[at], puts.at[3 + m])
        pushes[m].start()

    def combine(n):
        way_out.wait(sent_back[n])
        summed[:, begins[n] : begins[n] + BACK[n]] = dot_tn(
            spread_v[...], held_out[n].reshape(slots, BACK[n])[...]
        )

    todo = list(blocks)
    for triple, crossing in ORDER:
        for n in range(3 * triple, 3 * triple + 3):
            dst = held_out[n] if crossing == 2 else mids_out[2 * n + crossing]
            if crossing > 0:
                way_out.wait(sent_back[n])
                src = mids_out[2 * n + crossing - 1]
            elif n == chunks - 1:
                src = extra
            else:
                gradient(n)
                src = sources[n]
            sent_back[n] = way_out.send(TURNS[n % 3][crossing], src, dst)
            if crossing == 2 and triple > 0:
                combine(n - 3)
            elif todo and triple + crossing > 1 and crossing > 0:
                outcome(todo.pop(0))
    for n in range(chunks - 3, chunks):
        combine(n)
    for copy in (*results, *pushes[-2:]):
        copy.wait()
    go.finish()
    back.finish()


def experts(tokens, spread, told, later, gate, up, down, router):
    tok, width = tokens.shape
    slots = spread.shape[0]
    hidden, lanes = gate.shape[1], router.shape[1]
    lead = (*DIMS, slots // math.prod(DIMS))
    chunks = len(CHUNKS)
    low = jax.ShapeDtypeStruct((slots, hidden), BF16)

    def held(widths):
        return [pltpu.VMEM((*lead, w), BF16) for w in widths]

    twice = lambda widths: [w for w in widths for _ in range(2)]
    rows, *others = pl.pallas_call(
        experts_kernel,
        name="experts",
        cost_estimate=cost(120),
        out_shape=(
            jax.ShapeDtypeStruct((*lead, width), BF16),
            low,
            low,
            low,
            jax.ShapeDtypeStruct((tok, sum(BACK)), F32),
            jax.ShapeDtypeStruct((slots, width), BF16),
        ),
        in_specs=[ANY] * 8,
        out_specs=(ANY, ANY, ANY, ANY, VMEM, ANY),
        scratch_shapes=[
            *held(CHUNKS[:4]),
            *held(twice(CHUNKS)),
            *held(CHUNKS),
            *held(twice(BACK)),
            *held(BACK),
            *held((BACK[-2], BACK[-1])),
            pltpu.VMEM(tokens.shape, BF16),
            pltpu.VMEM(spread.shape, BF16),
            pltpu.VMEM((slots, lanes), BF16),
            pltpu.VMEM((2, 256, width), BF16),
            pltpu.VMEM(gate.shape, BF16),
            pltpu.VMEM(up.shape, BF16),
            pltpu.VMEM(down.shape, BF16),
            pltpu.VMEM(router.shape, BF16),
            pltpu.VMEM((slots, hidden), F32),
            pltpu.VMEM((slots, hidden), F32),
            pltpu.VMEM((slots, lanes), F32),
            pltpu.VMEM((slots, hidden), F32),
            *(pltpu.VMEM((slots, hidden), BF16) for _ in range(3)),
            pltpu.SemaphoreType.DMA((13 * chunks,)),
            pltpu.SemaphoreType.DMA((13 * chunks,)),
            pltpu.SemaphoreType.DMA((4 * chunks,)),
            pltpu.SemaphoreType.DMA((13 * chunks,)),
            pltpu.SemaphoreType.DMA((13 * chunks,)),
            pltpu.SemaphoreType.DMA((3 * chunks,)),
            pltpu.SemaphoreType.DMA((7,)),
            pltpu.SemaphoreType.DMA((2, 2)),
            pltpu.SemaphoreType.DMA((7,)),
        ],
        compiler_params=pltpu.CompilerParams(
            collective_id=6, has_side_effects=True, vmem_limit_bytes=61 << 20
        ),
    )(tokens, spread, told, later, gate, up, down, router)
    return rows.reshape(slots, width), *others


def on_device(
    hidden_in,
    doc_ids,
    expert_ids,
    attn_gain,
    query_weight,
    key_weight,
    value_weight,
    output_weight,
    query_gain,
    key_gain,
    moe_gain,
    router_weight,
    gate_weight,
    up_weight,
    down_weight,
    cotangent,
):
    both = ("dp", "tensor")
    tok, width = hidden_in.shape
    hd = query_gain.shape[0]
    nkv = key_weight.shape[1] // hd
    nq = query_weight.shape[1] // hd
    group = nq // nkv
    count = router_weight.shape[1]
    routes = expert_ids.shape[1]
    cap = tok * routes // count
    slots = count * cap
    scale = 1.0 / math.sqrt(hd)
    tokens = doc_ids.shape[1]

    lane = lax.broadcasted_iota(jnp.int32, (1, 1, count), 2)
    chosen = jnp.sum((expert_ids[:, :, None] == lane).astype(F32), axis=1)
    below = (
        lax.broadcasted_iota(jnp.int32, (tok, tok), 1)
        < lax.broadcasted_iota(jnp.int32, (tok, tok), 0)
    ).astype(BF16)
    rank = dot_nn(below, chosen.astype(BF16))
    place = jnp.where(chosen > 0, rank, -1.0).T
    spread = (
        place[:, None, :] == lax.broadcasted_iota(jnp.int32, (1, cap, 1), 1).astype(F32)
    ).astype(BF16).reshape(slots, tok)

    hidden = hidden_in.astype(F32)

    in_weights, out_weights, normed, docs, told, later = gather(
        query_weight,
        key_weight,
        value_weight,
        output_weight.T,
        hidden_in,
        attn_gain,
        jnp.broadcast_to(doc_ids, (8, tokens)).astype(F32),
        spread,
        cotangent,
        chosen.astype(BF16),
    )
    later = lax.all_to_all(
        later.reshape(count, cap, later.shape[1]), both, split_axis=0, concat_axis=0, tiled=True
    ).reshape(slots, later.shape[1])

    position, allowed = jax.vmap(layout)(docs[:, 0])
    cosine, sine = rotary(position.reshape(-1), hd)
    cosine = jnp.concatenate([cosine, cosine], axis=1)
    signed = jnp.concatenate([-sine, sine], axis=1)
    bias = jnp.where(allowed, 0.0, MASKED).astype(F32)
    raw = dot_nn(normed, in_weights)
    heads = group * hd
    query, kv, attention, mixed = attend(raw, bias, cosine, signed, query_gain, key_gain, scale)
    attn_out = reduce(dot_nt(mixed, out_weights).astype(BF16), 2)

    residual = hidden + attn_out
    moe_input = rms_scale(residual, moe_gain).astype(BF16)
    moe_input, later = lax.optimization_barrier((moe_input, later))
    gate_mat, up_mat, down_mat = gate_weight[0], up_weight[0], down_weight[0]
    rows, inner_low, grad_gate, grad_up, summed, expert_out = experts(
        moe_input, spread, told, later, gate_mat, up_mat, down_mat, router_weight
    )
    logits = dot_nn(moe_input, router_weight)
    masked = jnp.where(chosen > 0, logits, MASKED)
    probs = jnp.exp(masked - jnp.max(masked, axis=-1, keepdims=True))
    probs = probs / jnp.sum(probs, axis=-1, keepdims=True)

    upstream = cotangent.astype(F32)
    gate_upstream = summed[:, width : width + count] + summed[:, width + count :]
    grad_chosen = probs * (gate_upstream - jnp.sum(probs * gate_upstream, axis=-1, keepdims=True))
    grad_logits = grad_chosen.astype(BF16)
    grad_moe_input = summed[:, :width] + dot_nt(grad_logits, router_weight)
    router_part = dot_tn(moe_input, grad_logits)
    grad_norm, moegain_rows = rms_back(residual, moe_gain, grad_moe_input)
    moegain_part = jnp.sum(moegain_rows, axis=0)
    grad_residual = upstream + grad_norm
    grad_attn, piece = share(grad_residual.astype(BF16), router_part.astype(BF16), 3)
    expert_out, grad_attn = lax.optimization_barrier((expert_out, grad_attn))
    returned = lax.all_to_all(
        expert_out.reshape(count, cap, width), both, split_axis=0, concat_axis=0, tiled=True
    ).reshape(slots, width)

    grad_mixed = dot_nn(grad_attn, out_weights).astype(BF16)
    grad_raw, head_gains = attend_back(
        raw, cosine, signed, query_gain, key_gain, query, kv, attention, grad_mixed, scale
    )
    inner_low, rows, told, later, grad_raw = lax.optimization_barrier(
        (inner_low, rows, told, later, grad_raw)
    )
    cot_rows = jnp.concatenate([told, later[:, : width - told.shape[1]]], axis=1)
    down_grad = dot_tn(inner_low, cot_rows)
    gate_grad = dot_tn(rows, grad_gate)
    up_grad = dot_tn(rows, grad_up)
    normed_part, down_grad, gate_grad, up_grad = lax.optimization_barrier(
        (dot_nt(grad_raw, in_weights).astype(BF16), down_grad, gate_grad, up_grad)
    )
    grad_normed = reduce(normed_part, 4)
    grad_normed, returned = lax.optimization_barrier((grad_normed, returned))
    grad_hidden, attngain_rows = rms_back(hidden, attn_gain, grad_normed)
    input_grad = grad_residual + grad_hidden

    gains = jnp.concatenate([jnp.sum(attngain_rows, axis=0), moegain_part]).reshape(-1, hd)
    gains = jnp.concatenate([gains, head_gains, jnp.zeros((6, hd), F32)], axis=0)

    query_grad, key_grad, value_grad, out_grad, gains, router_grad, layer_out = scatter(
        dot_tn(normed, grad_raw).astype(BF16),
        dot_tn(grad_attn, mixed).astype(BF16),
        gains,
        piece,
        returned,
        spread,
        residual,
        (nq * hd, nkv * hd, nkv * hd, nq * hd),
    )
    at = width // hd
    return (
        layer_out,
        input_grad,
        gains[:at].reshape(-1),
        query_grad,
        key_grad,
        value_grad,
        out_grad.T,
        gains[2 * at],
        gains[2 * at + 1],
        gains[at : 2 * at].reshape(-1),
        router_grad.reshape(width, count).astype(F32),
        gate_grad[None],
        up_grad[None],
        down_grad[None],
    )


def solution(mesh):
    both = ("dp", "tensor")
    in_specs = (
        P(both, None),
        P("dp", None),
        P(both, None),
        P(),
        P("dp", "tensor"),
        P("dp", "tensor"),
        P("dp", "tensor"),
        P("tensor", "dp"),
        P(),
        P(),
        P(),
        P(),
        P(both, None, None),
        P(both, None, None),
        P(both, None, None),
        P(both, None),
    )
    out_specs = (
        P(both, None),
        P(both, None),
        P(),
        P("dp", "tensor"),
        P("dp", "tensor"),
        P("dp", "tensor"),
        P("tensor", "dp"),
        P(),
        P(),
        P(),
        P(),
        P(both, None, None),
        P(both, None, None),
        P(both, None, None),
    )
    return jax.shard_map(
        on_device, mesh=mesh, in_specs=in_specs, out_specs=out_specs, check_vma=False
    )
```

```python
import functools
import math

import jax
import jax.numpy as jnp
from jax import lax
from jax.experimental import pallas as pl
from jax.experimental.pallas import tpu as pltpu
from jax.sharding import PartitionSpec as P

BLOCK = 128
EPSILON = 1e-06
ROPE_BASE = 1000000.0
MASKED = -1e30
F32 = jnp.float32
BF16 = jnp.bfloat16


def dot_nt(a, b):
    return lax.dot_general(a, b, (((1,), (1,)), ((), ())), preferred_element_type=F32)


def dot_tn(a, b):
    return lax.dot_general(a, b, (((0,), (0,)), ((), ())), preferred_element_type=F32)


def dot_nn(a, b):
    return lax.dot_general(a, b, (((1,), (0,)), ((), ())), preferred_element_type=F32)


def rms_recip(values):
    return lax.rsqrt(jnp.mean(values * values, axis=-1, keepdims=True) + EPSILON)


def rms_scale(values, gain):
    return values * rms_recip(values) * gain


def rms_back(values, gain, upstream):
    r = rms_recip(values)
    scaled = upstream * gain
    inner = jnp.mean(scaled * values, axis=-1, keepdims=True)
    grad_values = r * scaled - values * (r * r * r) * inner
    return grad_values, upstream * values * r


def rotate(values, cosine, sine):
    half = values.shape[-1] // 2
    a = values[..., :half]
    b = values[..., half:]
    return jnp.concatenate([a * cosine - b * sine, b * cosine + a * sine], axis=-1)


def layout(doc_row):
    length = doc_row.shape[0]
    indices = jnp.arange(length, dtype=jnp.int32)
    same_doc = doc_row[:, None] == doc_row[None, :]
    earlier = indices[None, :] < indices[:, None]
    position = jnp.sum(jnp.where(same_doc & earlier, 1, 0), axis=1).astype(jnp.int32)
    blocks = position // BLOCK
    allowed = same_doc & (blocks[None, :] <= blocks[:, None])
    return position, allowed


def rotary(position, head_size):
    half = head_size // 2
    frequency = jnp.exp(-jnp.log(ROPE_BASE) * jnp.arange(half, dtype=F32) * 2.0 / head_size)
    angles = position.astype(F32)[:, None] * frequency[None, :]
    return jnp.cos(angles), jnp.sin(angles)


MESH = pl.DeviceIdType.MESH
ANY = pl.BlockSpec(memory_space=pl.ANY)
VMEM = pl.BlockSpec(memory_space=pltpu.VMEM)
NX, NYH, NZ, NC = 4, 2, 4, 2
RING = 4
EARLY = 256


def cost(microseconds):
    return pl.CostEstimate(flops=0, transcendentals=0, bytes_accessed=int(microseconds * 3.6e6))


class Place:
    def __init__(self):
        dp = lax.axis_index("dp")
        self.t = lax.axis_index("tensor")
        self.c = lax.rem(dp, NC)
        self.z = lax.rem(dp // NC, NZ)
        self.yh = lax.rem(dp // (NC * NZ), NYH)
        self.x = dp // (NC * NZ * NYH)
        self.y = self.yh * 2 + self.t

    def device(self, x=None, yh=None, z=None, c=None, t=None):
        pick = lambda given, own: own if given is None else given
        x, yh, z, c = pick(x, self.x), pick(yh, self.yh), pick(z, self.z), pick(c, self.c)
        return (((x * NYH + yh) * NZ + z) * NC + c, pick(t, self.t))

    def expert(self):
        return ((((self.x * NYH + self.yh) * NZ + self.z) * NC) + self.c) * 2 + self.t

    def at_y(self, y):
        return self.device(yh=y // 2, t=lax.rem(y, 2))


def after(i):
    return lax.rem(i + 1, RING)


def before(i):
    return lax.rem(i + RING - 1, RING)


def across(i):
    return lax.rem(i + 2, RING)


def greet(peers):
    barrier = pltpu.get_barrier_semaphore()
    for peer in peers:
        pl.semaphore_signal(barrier, inc=1, device_id=peer, device_id_type=MESH)
    pl.semaphore_wait(barrier, len(peers))


class Copies:
    def __init__(self, send, recv, local):
        self.send, self.recv, self.local = send, recv, local
        self.n = self.m = 0
        self.sent = []
        self.waited = set()

    def put(self, src, dst, peer):
        copy = pltpu.make_async_remote_copy(
            src_ref=src,
            dst_ref=dst,
            send_sem=self.send.at[self.n],
            recv_sem=self.recv.at[self.n],
            device_id=peer,
            device_id_type=MESH,
        )
        self.n += 1
        copy.start()
        self.sent.append(copy)
        return copy

    def keep(self, src, dst):
        copy = pltpu.make_async_copy(src, dst, self.local.at[self.m])
        self.m += 1
        copy.start()
        return copy

    def release(self, copies):
        for copy in copies:
            copy.wait_send()
            self.waited.add(id(copy))

    def finish(self):
        for copy in self.sent:
            if id(copy) not in self.waited:
                copy.wait_send()


def gather_kernel(
    q, k, v, o, hidden_h, gain, doc, spread_h, cot_h, chosen_h, wa, wb, toks, docs, told, later, *rest
):
    sources, mids = rest[:3], rest[3:9]
    hidden, spread, cot, chosen, tok, stage, send, recv, local = rest[9:]
    me = Place()
    x, yh, z, c, p = me.x, me.yh, me.z, me.c, me.y
    sibling = me.device(c=1 - c)
    pair = me.device(yh=1 - yh)
    ring_x = (me.device(x=after(x)), me.device(x=before(x)))
    ring_z = (me.device(z=after(z)), me.device(z=before(z)))
    ring_y = (me.at_y(after(p)), me.at_y(before(p)))
    go = Copies(send, recv, local)
    route = Route(me, go)
    pulls = [go.keep(a, b) for a, b in ((hidden_h, hidden), (spread_h, spread), (cot_h, cot), (chosen_h, chosen))]
    greet(route.everyone())
    slots, block = spread.shape[0], 256

    def dispatch(n):
        cols = pl.ds(n * EARLY, EARLY)
        flat = sources[n].reshape(slots, EARLY)

        def step(m, _):
            at = pl.ds(pl.multiple_of(m * block, block), block)
            flat[at] = dot_nn(spread[at], cot[:, cols]).astype(BF16)
            return 0

        lax.fori_loop(0, slots // block, step, 0)
        return sources[n]

    pushes = [None] * (slots // block)

    def layout_later(m):
        if m >= 2:
            pushes[m - 2].wait()
        at = pl.ds(m * block, block)
        cut = cot.shape[1] - 3 * EARLY
        stage[m % 2, :, :cut] = dot_nn(spread[at], cot[:, 3 * EARLY :]).astype(BF16)
        stage[m % 2, :, cut:] = dot_nn(spread[at], chosen[...]).astype(BF16)
        pushes[m] = go.keep(stage.at[m % 2], later.at[at])

    crossed = [None] * 3

    def cross(step):
        for n in range(3):
            if step > 0:
                route.wait(crossed[n])
            src = dispatch(n) if step == 0 else mids[2 * n + step - 1]
            dst = columns(told, n * EARLY, EARLY) if step == 2 else mids[2 * n + step]
            crossed[n] = route.send(TURNS[n][step], src, dst)

    shards, start = [], 0
    for ref, w in ((q, wa), (k, wa), (v, wa), (o, wb)):
        cols = ref.shape[1] // NYH
        to = w.at[x, yh, z, c, :, pl.ds(0 if w is wb else start, cols)]
        shards.append((ref, cols, to))
        start += cols

    def part(ref, cols, head):
        return ref.at[:, pl.ds(pl.multiple_of(head * cols, cols), cols)]

    pairs = [go.put(part(ref, cols, 1 - yh), to, pair) for ref, cols, to in shards]
    kept = [go.keep(part(ref, cols, yh), to) for ref, cols, to in shards]
    for pull in pulls:
        pull.wait()
    rows = hidden[...].astype(F32)
    tok[...] = (rows * unit_rows(rows) * gain[...]).astype(BF16)
    for copy in kept:
        copy.wait()
    for copy in pairs:
        copy.wait_recv()

    ways = (
        (x, z, ring_x, ring_z, lambda i, j: wa.at[i, :, j, c], lambda j: wa.at[:, :, j, c]),
        (z, x, ring_z, ring_x, lambda i, j: wb.at[j, :, i, c], lambda j: wb.at[j, :, :, c]),
    )

    def both(ref, peers):
        return [go.put(ref, ref, peer) for peer in peers]

    def relay(low, high, copies, peers):
        copies[0].wait_recv()
        up = go.put(low.at[0], low.at[0], peers[0])
        copies[1].wait_recv()
        return [up, go.put(high.at[1], high.at[1], peers[1])]

    def arrived(copies):
        for copy in copies:
            copy.wait_recv()

    near = [both(unit(i, j), one) for i, j, one, two, unit, slab in ways]
    own = [both(unit(i, j), two) for i, j, one, two, unit, slab in ways]
    rows = [go.put(tok, toks.at[p], peer) for peer in ring_y]
    kept_rows = [go.keep(tok, toks.at[p]), go.keep(doc, docs.at[yh])]
    tail = [go.put(doc, docs.at[yh], pair)]
    cross(0)
    far = [
        relay(unit(before(i), j), unit(after(i), j), copies, one)
        for (i, j, one, two, unit, slab), copies in zip(ways, near)
    ]
    low = [both(unit(before(i), j), two) for i, j, one, two, unit, slab in ways]
    high = [both(unit(after(i), j), two) for i, j, one, two, unit, slab in ways]
    layout_later(0)
    last = []
    for (i, j, one, two, unit, slab), copies in zip(ways, far):
        arrived(copies)
        last.append(both(unit(across(i), j), two))
        tail.append(go.put(slab(j), slab(j), sibling))
    cross(1)
    layout_later(1)
    half = tok.shape[0] // 2
    rows[0].wait_recv()
    piece = toks.at[before(p), pl.ds(0, half)]
    tail.append(go.put(piece, piece, ring_y[0]))
    rows[1].wait_recv()
    piece = toks.at[after(p), pl.ds(half, half)]
    tail.append(go.put(piece, piece, ring_y[1]))
    ends = [[], []]
    for place, copies in ((lambda i: i, own), (before, low), (after, high), (across, last)):
        for n, (i, j, one, two, unit, slab) in enumerate(ways):
            u = place(i)
            ends[n] += relay(unit(u, before(j)), unit(u, after(j)), copies[n], two)
        if copies is high:
            cross(2)
            layout_later(2)
            layout_later(3)
    for i, j, one, two, unit, slab in ways:
        tail.append(go.put(slab(before(j)), slab(before(j)), sibling))
        tail.append(go.put(slab(after(j)), slab(after(j)), sibling))
    for (i, j, one, two, unit, slab), copies in zip(ways, ends):
        arrived(copies)
        tail.append(go.put(slab(across(j)), slab(across(j)), sibling))
    arrived(tail)
    for copy in (*kept_rows, *pushes[-2:]):
        copy.wait()
    for sent in crossed:
        route.wait(sent)
    go.finish()


def gather(query, key, value, out, hidden, gain, docs, spread, cot, chosen):
    rows = query.shape[0]
    width_a = (query.shape[1] + key.shape[1] + value.shape[1]) // NYH
    width_b = out.shape[1] // NYH
    lead = (NX, NYH, NZ, NC, rows)
    slots, width = spread.shape[0], cot.shape[1]
    blocks = (*DIMS, slots // math.prod(DIMS))
    left = width - 3 * EARLY + chosen.shape[1]
    wa, wb, toks, docs, told, later = pl.pallas_call(
        gather_kernel,
        name="gather_weights",
        cost_estimate=cost(60),
        out_shape=(
            jax.ShapeDtypeStruct((*lead, width_a), BF16),
            jax.ShapeDtypeStruct((*lead, width_b), BF16),
            jax.ShapeDtypeStruct((RING, *hidden.shape), BF16),
            jax.ShapeDtypeStruct((NYH, *docs.shape), docs.dtype),
            jax.ShapeDtypeStruct((*blocks, 3 * EARLY), BF16),
            jax.ShapeDtypeStruct((slots, left), BF16),
        ),
        in_specs=[*(ANY,) * 5, VMEM, *(ANY,) * 4],
        out_specs=(ANY,) * 6,
        scratch_shapes=[
            *(pltpu.VMEM((*blocks, EARLY), BF16) for _ in range(9)),
            *(pltpu.VMEM(a.shape, BF16) for a in (hidden, spread, cot, chosen, hidden)),
            pltpu.VMEM((2, 256, left), BF16),
            pltpu.SemaphoreType.DMA((96,)),
            pltpu.SemaphoreType.DMA((96,)),
            pltpu.SemaphoreType.DMA((23,)),
        ],
        compiler_params=pltpu.CompilerParams(
            collective_id=1, has_side_effects=True, vmem_limit_bytes=60 << 20
        ),
    )(query, key, value, out, hidden, gain.reshape(1, -1), docs, spread, cot, chosen)
    depth = NX * NYH * NZ * NC * rows
    return (
        wa.reshape(depth, width_a),
        wb.reshape(depth, width_b),
        toks.reshape(RING * hidden.shape[0], hidden.shape[1]),
        docs,
        told.reshape(slots, 3 * EARLY),
        later,
    )


def share_kernel(tok, part, toks, piece, got_x, sum_x, got_z, sum_z, got_y, send, recv, local):
    me = Place()
    x, yh, z, c, p = me.x, me.yh, me.z, me.c, me.y
    ring = (me.at_y(after(p)), me.at_y(before(p)))
    go = Copies(send, recv, local)
    route = Route(me, go)
    greet(route.everyone())
    half = tok.shape[0] // 2
    direct = [go.put(tok, toks.at[p], peer) for peer in ring]
    kept = go.keep(tok, toks.at[p])
    own = go.keep(part.at[x, :, :, c], got_x.at[x * NC + c])
    terms = [
        go.put(part.at[at[0], :, :, at[1]], got_x.at[x * NC + c], peer)
        for at, peer in route.peers["x"]
    ]

    def arrived(copies):
        for copy in copies:
            copy.wait_recv()

    def added(got):
        value = got[0].astype(F32)
        for n in range(1, got.shape[0]):
            value += got[n].astype(F32)
        return value

    own.wait()
    arrived(terms)
    sum_x[...] = added(got_x)
    got_z[z] = sum_x[:, z]
    terms = [go.put(sum_x.at[:, at[0]], got_z.at[z], peer) for at, peer in route.peers["z"]]
    relays = []
    for h, owner in enumerate((before(p), after(p))):
        direct[h].wait_recv()
        rows = toks.at[owner, pl.ds(h * half, half)]
        relays.append(go.put(rows, rows, ring[h]))
    arrived(terms)
    sum_z[...] = added(got_z)
    got_y[p] = sum_z[yh, me.t]
    terms = [go.put(sum_z.at[at[0], at[1]], got_y.at[p], peer) for at, peer in route.peers["y"]]
    arrived(terms)
    piece[...] = added(got_y).astype(piece.dtype)
    arrived(relays)
    kept.wait()
    go.finish()


def share(tokens, part, ident):
    rows, lanes = part.shape[0] // math.prod(DIMS), part.shape[1]
    toks, piece = pl.pallas_call(
        share_kernel,
        name=f"share_rows_{ident}",
        cost_estimate=cost(20),
        out_shape=(
            jax.ShapeDtypeStruct((RING, *tokens.shape), tokens.dtype),
            jax.ShapeDtypeStruct((rows, lanes), BF16),
        ),
        in_specs=[ANY, ANY],
        out_specs=(ANY, VMEM),
        scratch_shapes=[
            pltpu.VMEM((NX * NC, NYH, NZ, 2, rows, lanes), BF16),
            pltpu.VMEM((NYH, NZ, 2, rows, lanes), F32),
            pltpu.VMEM((NZ, NYH, 2, rows, lanes), F32),
            pltpu.VMEM((NYH, 2, rows, lanes), F32),
            pltpu.VMEM((RING, rows, lanes), F32),
            pltpu.SemaphoreType.DMA((17,)),
            pltpu.SemaphoreType.DMA((17,)),
            pltpu.SemaphoreType.DMA((2,)),
        ],
        compiler_params=pltpu.CompilerParams(collective_id=ident, has_side_effects=True),
    )(tokens, part.reshape(*DIMS, rows, lanes))
    return toks.reshape(RING * tokens.shape[0], tokens.shape[1]), piece


def reduce_kernel(part, out, held, own, got, send, recv, local):
    me = Place()
    p = me.y
    ring = (me.at_y(after(p)), me.at_y(before(p)))
    greet(ring)
    go = Copies(send, recv, local)
    half = out.shape[0] // 2
    halves = [pl.ds(h * half, half) for h in range(2)]
    near = (after(p), before(p))
    cross = [go.put(part.at[across(p), halves[h]], got.at[h], ring[h]) for h in range(2)]
    kept = [go.keep(part.at[near[h], halves[h]], held.at[h]) for h in range(2)]
    straight = [go.put(part.at[near[h], halves[1 - h]], got.at[2 + h], ring[h]) for h in range(2)]
    mine = go.keep(part.at[p], own)
    sums = []
    for h in range(2):
        kept[h].wait()
        cross[h].wait_recv()
        held[h] = (held[h].astype(F32) + got[h].astype(F32)).astype(BF16)
        sums.append(go.put(held.at[h], got.at[4 + h], ring[h]))
    mine.wait()
    for copy in straight:
        copy.wait_recv()
    for h in range(2):
        sums[h].wait_recv()
        out[halves[h]] = (
            own[halves[h]].astype(F32) + got[4 + h].astype(F32) + got[3 - h].astype(F32)
        )
    go.finish()


def reduce(part, ident):
    rows, width = part.shape[0] // RING, part.shape[1]
    half = rows // 2
    return pl.pallas_call(
        reduce_kernel,
        name=f"reduce_rows_{ident}",
        cost_estimate=cost(1),
        out_shape=jax.ShapeDtypeStruct((rows, width), F32),
        in_specs=[ANY],
        out_specs=VMEM,
        scratch_shapes=[
            pltpu.VMEM((2, half, width), BF16),
            pltpu.VMEM((rows, width), BF16),
            pltpu.VMEM((6, half, width), BF16),
            pltpu.SemaphoreType.DMA((6,)),
            pltpu.SemaphoreType.DMA((6,)),
            pltpu.SemaphoreType.DMA((3,)),
        ],
        compiler_params=pltpu.CompilerParams(
            collective_id=ident, has_side_effects=True, vmem_limit_bytes=24 << 20
        ),
    )(part.reshape(RING, rows, width))


def scatter_kernel(
    ga, gb, gains, piece, returned, slots, residual, oq, ok, ov, oo, og, op, layer, back_v, slots_v, ka, kb, da, db, ra, rb, qa, qb, sa, sb, ta, tb, ua, ub, ma, mb,
    ring_gains, sum_gains, pair_gains, send, recv, local
):
    me = Place()
    x, yh, z, c, t = me.x, me.yh, me.z, me.c, me.t
    sibling = me.device(c=1 - c)
    pair = me.device(yh=1 - yh)
    partner = me.device(t=1 - t)
    ring_x = (me.device(x=after(x)), me.device(x=before(x)))
    ring_z = (me.device(z=after(z)), me.device(z=before(z)))
    round_x = (*ring_x, me.device(x=across(x)))
    round_z = (*ring_z, me.device(z=across(z)))
    greet([sibling, pair, partner, *round_x, *round_z])
    go = Copies(send, recv, local)

    def around(n, term, own, peers):
        ring_gains[n, own] = term
        return [go.put(ring_gains.at[n, own], ring_gains.at[n, own], peer) for peer in peers]

    def ring_sum(n, copies):
        for copy in copies:
            copy.wait_recv()
        return (ring_gains[n, 0] + ring_gains[n, 1]) + (ring_gains[n, 2] + ring_gains[n, 3])

    def swap(n, term, peer):
        sum_gains[n] = term
        return go.put(sum_gains.at[n], pair_gains.at[n], peer)

    def swapped(n, copy):
        copy.wait_recv()
        return sum_gains[n] + pair_gains[n]


    ways = (
        (lambda i, h, n: ga.at[i, h, :, n], x, z, ring_x, ring_z, ka, da, ra, qa, sa, ta),
        (lambda i, h, n: gb.at[:, h, i, n], z, x, ring_z, ring_x, kb, db, rb, qb, sb, tb),
    )
    places = (across, after, before, lambda i: i)

    def spread(ref, peers):
        return [go.put(ref, ref, peer) for peer in peers]

    def arrived(copies):
        for copy in copies:
            copy.wait_recv()

    given, held = [[], []], [[], []]
    for n, place in enumerate(places):
        for w, (slab, i, j, one, two, k, d, r, q, s, u) in enumerate(ways):
            given[w].append([go.put(slab(place(i), h, 1 - c), d.at[n, h], sibling) for h in range(2)])
            held[w].append([go.keep(slab(place(i), h, c), k.at[n, h]) for h in range(2)])

    def ready(w, n, h):
        given[w][n][h].wait_recv()
        held[w][n][h].wait()

    def total(w, n, h, extra):
        slab, i, j, one, two, k, d, r, q, s, u = ways[w]

        def step(m, _):
            value = k[n, h, m].astype(F32) + d[n, h, m].astype(F32)
            for e in extra:
                value += r[e, m].astype(F32)
            k[n, h, m] = value.astype(BF16)
            return 0

        lax.fori_loop(0, k.shape[2], step, 0)

    terms = around(0, gains[...], x, round_x)
    mine = op.at[x, yh, z, c, t]
    held_piece = go.keep(piece, mine)
    pieces = [go.put(piece, mine, sibling)]
    pulls = [go.keep(returned, back_v), go.keep(slots, slots_v)]
    cross, straight, sums = [[], []], [[], []], [[], []]
    for w, (slab, i, j, one, two, k, d, r, q, s, u) in enumerate(ways):
        for h in range(2):
            ready(w, 0, h)
            total(w, 0, h, ())
            cross[w].append(go.put(k.at[0, h], r.at[h], one[h]))
    for w, (slab, i, j, one, two, k, d, r, q, s, u) in enumerate(ways):
        for h in range(2):
            ready(w, 1 + h, 1 - h)
            total(w, 1 + h, 1 - h, ())
            straight[w].append(go.put(k.at[1 + h, 1 - h], r.at[2 + h], one[h]))
    for pull in pulls:
        pull.wait()
    for m in range(4):
        cols = pl.ds(m * layer.shape[1] // 4, layer.shape[1] // 4)
        layer[:, cols] = (residual[:, cols] + dot_tn(slots_v[...], back_v[:, cols])).astype(layer.dtype)
    terms = around(1, ring_sum(0, terms), z, round_z)
    arrived(pieces)
    held_piece.wait()
    pieces = spread(op.at[x, yh, z, :, t], [partner])
    for w, (slab, i, j, one, two, k, d, r, q, s, u) in enumerate(ways):
        for h in range(2):
            ready(w, 1 + h, h)
            cross[w][h].wait_recv()
            total(w, 1 + h, h, (h,))
            sums[w].append(go.put(k.at[1 + h, h], r.at[4 + h], one[h]))
    arrived(pieces)
    pieces = spread(op.at[x, yh, z], [pair])
    terms = swap(0, ring_sum(1, terms), pair)
    for w in range(2):
        for h in range(2):
            ready(w, 3, h)
            straight[w][1 - h].wait_recv()
            total(w, 3, h, (3 - h,))
    arrived(pieces)
    pieces = spread(op.at[x, :, z], round_x)
    terms = swap(1, swapped(0, terms), partner)
    over, direct, final = [[], []], [[], []], [[], []]
    for w, (slab, i, j, one, two, k, d, r, q, s, u) in enumerate(ways):
        near = (after(j), before(j))
        for h in range(2):
            sums[w][h].wait_recv()

            def step(m, _, k=k, r=r, h=h):
                k[3, h, m] = (k[3, h, m].astype(F32) + r[4 + h, m].astype(F32)).astype(BF16)
                return 0

            lax.fori_loop(0, k.shape[2], step, 0)
            over[w].append(go.put(k.at[3, h, across(j)], q.at[h], two[h]))
        for h in range(2):
            direct[w].append(go.put(k.at[3, 1 - h, near[h]], q.at[2 + h], two[h]))
    arrived(pieces)
    pieces = spread(op.at[:, :, z], round_z)
    terms = swap(2, swapped(1, terms), sibling)
    for w, (slab, i, j, one, two, k, d, r, q, s, u) in enumerate(ways):
        near = (after(j), before(j))
        for h in range(2):
            over[w][h].wait_recv()
            s[h] = (k[3, h, near[h]].astype(F32) + q[h].astype(F32)).astype(BF16)
            final[w].append(go.put(s.at[h], q.at[4 + h], two[h]))
    last = []
    for w, ((slab, i, j, one, two, k, d, r, q, s, u), v, m) in enumerate(zip(ways, (ua, ub), (ma, mb))):
        arrived(direct[w])
        arrived(final[w])
        for h in range(2):
            u[h] = k[3, h, j].astype(F32) + q[4 + h].astype(F32) + q[3 - h].astype(F32)
        v[...] = u[1 - yh].astype(BF16)
        last.append(go.put(v, m, pair))
    og[...] = swapped(2, terms)

    def write(head, a, b):
        start = 0
        for out, block in ((oq, a), (ok, a), (ov, a), (oo, b)):
            cols = out.shape[1] // NYH
            at = 0 if block is b else start
            out[:, pl.ds(pl.multiple_of(head * cols, cols), cols)] = block[:, at : at + cols]
            start += cols

    write(yh, ta[yh], tb[yh])
    arrived(last)
    write(1 - yh, ma[...].astype(F32), mb[...].astype(F32))
    arrived(pieces)
    go.finish()


def scatter(grad_a, grad_b, gains, piece, returned, slots, residual, columns):
    rows = grad_a.shape[0] // (NX * NYH * NZ * NC)
    lead = (NX, NYH, NZ, NC, rows)
    widths = (grad_a.shape[1], grad_b.shape[1])

    def each(shape, dtype):
        return [pltpu.VMEM((*shape, rows, w), dtype) for w in widths]

    return pl.pallas_call(
        scatter_kernel,
        name="scatter_weights",
        cost_estimate=cost(80),
        out_shape=(
            *(jax.ShapeDtypeStruct((rows, w), F32) for w in columns),
            jax.ShapeDtypeStruct(gains.shape, F32),
            jax.ShapeDtypeStruct((NX, NYH, NZ, NC, 2, *piece.shape), piece.dtype),
            jax.ShapeDtypeStruct(residual.shape, BF16),
        ),
        in_specs=[ANY, ANY, VMEM, ANY, ANY, ANY, VMEM],
        out_specs=(*(VMEM,) * 5, ANY, VMEM),
        scratch_shapes=[
            pltpu.VMEM(returned.shape, BF16),
            pltpu.VMEM(slots.shape, BF16),
            *each((4, 2, RING), BF16),
            *each((4, 2, RING), BF16),
            *each((6, RING), BF16),
            *each((6,), BF16),
            *each((2,), BF16),
            *each((2,), F32),
            *each((), BF16),
            *each((), BF16),
            pltpu.VMEM((2, RING, *gains.shape), F32),
            pltpu.VMEM((3, *gains.shape), F32),
            pltpu.VMEM((3, *gains.shape), F32),
            pltpu.SemaphoreType.DMA((60,)),
            pltpu.SemaphoreType.DMA((60,)),
            pltpu.SemaphoreType.DMA((19,)),
        ],
        compiler_params=pltpu.CompilerParams(
            collective_id=5, has_side_effects=True, vmem_limit_bytes=48 << 20
        ),
    )(grad_a.reshape(*lead, widths[0]), grad_b.reshape(*lead, widths[1]), gains, piece, returned, slots, residual)


def unit_rows(values):
    return lax.rsqrt(jnp.mean(values * values, axis=-1, keepdims=True) + EPSILON)


def turn(values, cosine, signed):
    return values * cosine + pltpu.roll(values, values.shape[-1] // 2, 1) * signed


def attend_kernel(scale, raw, bias, cosine, signed, qgain, kgain, query, kv, weights, mixed):
    heads = query.shape[1] // cosine.shape[1]
    hd = cosine.shape[1]
    cos, sig = cosine[...], signed[...]
    key_raw = raw[:, heads * hd : (heads + 1) * hd]
    key = turn(key_raw * unit_rows(key_raw) * kgain[...], cos, sig).astype(BF16)
    value = raw[:, (heads + 1) * hd :].astype(BF16)
    kv[:, :hd] = key
    kv[:, hd:] = value
    for h in range(heads):
        at = slice(h * hd, (h + 1) * hd)
        head = raw[:, at]
        rows = turn(head * unit_rows(head) * qgain[...], cos, sig).astype(BF16)
        query[:, at] = rows
        scores = dot_nt(rows, key) * scale + bias[0]
        peak = jnp.max(scores, axis=-1, keepdims=True)
        weight = jnp.exp(scores - peak)
        weight = weight * (1.0 / jnp.sum(weight, axis=-1, keepdims=True))
        weights[0, h] = weight
        mixed[:, at] = dot_nn(weight.astype(BF16), value).astype(BF16)


def attend(raw, bias, cosine, signed, query_gain, key_gain, scale):
    groups, tokens = bias.shape[0], bias.shape[1]
    hd = cosine.shape[1]
    heads = raw.shape[1] // hd - 2
    rows = groups * tokens

    def block(cols):
        return pl.BlockSpec((tokens, cols), lambda g: (g, 0))

    gain = pl.BlockSpec((1, hd), lambda g: (0, 0))
    square = pl.BlockSpec((1, tokens, tokens), lambda g: (g, 0, 0))
    return pl.pallas_call(
        functools.partial(attend_kernel, scale),
        name="attend",
        cost_estimate=cost(8),
        grid=(groups,),
        out_shape=(
            jax.ShapeDtypeStruct((rows, heads * hd), BF16),
            jax.ShapeDtypeStruct((rows, 2 * hd), BF16),
            jax.ShapeDtypeStruct((groups, heads, tokens, tokens), F32),
            jax.ShapeDtypeStruct((rows, heads * hd), BF16),
        ),
        in_specs=[block((heads + 2) * hd), square, block(hd), block(hd), gain, gain],
        out_specs=(
            block(heads * hd),
            block(2 * hd),
            pl.BlockSpec((1, heads, tokens, tokens), lambda g: (g, 0, 0, 0)),
            block(heads * hd),
        ),
        compiler_params=pltpu.CompilerParams(vmem_limit_bytes=40 << 20),
    )(raw, bias, cosine, signed, query_gain.reshape(1, hd), key_gain.reshape(1, hd))


def norm_back(values, gain, upstream):
    r = unit_rows(values)
    scaled = upstream * gain
    inner = jnp.mean(scaled * values, axis=-1, keepdims=True)
    grad = r * scaled - values * (r * r * r * inner)
    return grad, jnp.sum(upstream * values * r, axis=0, keepdims=True)


def attend_back_kernel(
    scale, raw, cosine, signed, qgain, kgain, query, kv, weights, grad_mixed, grad_raw, grad_gains
):
    hd = cosine.shape[1]
    heads = query.shape[1] // hd
    cos, sig = cosine[...], -signed[...]
    key, value = kv[:, :hd], kv[:, hd:]
    grad_key = jnp.zeros(key.shape, F32)
    grad_value = jnp.zeros(key.shape, F32)
    query_gains = jnp.zeros((1, hd), F32)
    for h in range(heads):
        at = slice(h * hd, (h + 1) * hd)
        weight = weights[0, h]
        grad_head = grad_mixed[:, at]
        grad_value += dot_tn(weight.astype(BF16), grad_head)
        grad_soft = dot_nt(grad_head, value)
        delta = jnp.sum(weight * grad_soft, axis=-1, keepdims=True)
        grad_scores = (weight * (grad_soft - delta)).astype(BF16)
        grad_key += dot_tn(grad_scores, query[:, at])
        turned = turn(dot_nn(grad_scores, key) * scale, cos, sig)
        grad, gains = norm_back(raw[:, at], qgain[...], turned)
        grad_raw[:, at] = grad.astype(BF16)
        query_gains += gains
    at = slice(heads * hd, (heads + 1) * hd)
    grad, key_gains = norm_back(raw[:, at], kgain[...], turn(grad_key * scale, cos, sig))
    grad_raw[:, at] = grad.astype(BF16)
    grad_raw[:, (heads + 1) * hd :] = grad_value.astype(BF16)
    gains = jnp.concatenate([query_gains, key_gains], axis=0)

    @pl.when(pl.program_id(0) == 0)
    def _():
        grad_gains[...] = gains

    @pl.when(pl.program_id(0) > 0)
    def _():
        grad_gains[...] += gains


def attend_back(raw, cosine, signed, query_gain, key_gain, query, kv, weights, grad_mixed, scale):
    groups, heads, tokens, _ = weights.shape
    hd = cosine.shape[1]
    rows = groups * tokens

    def block(cols):
        return pl.BlockSpec((tokens, cols), lambda g: (g, 0))

    gain = pl.BlockSpec((1, hd), lambda g: (0, 0))
    return pl.pallas_call(
        functools.partial(attend_back_kernel, scale),
        name="attend_back",
        cost_estimate=cost(1),
        grid=(groups,),
        out_shape=(
            jax.ShapeDtypeStruct((rows, (heads + 2) * hd), BF16),
            jax.ShapeDtypeStruct((2, hd), F32),
        ),
        in_specs=[
            block((heads + 2) * hd),
            block(hd),
            block(hd),
            gain,
            gain,
            block(heads * hd),
            block(2 * hd),
            pl.BlockSpec((1, heads, tokens, tokens), lambda g: (g, 0, 0, 0)),
            block(heads * hd),
        ],
        out_specs=(block((heads + 2) * hd), pl.BlockSpec((2, hd), lambda g: (0, 0))),
        compiler_params=pltpu.CompilerParams(vmem_limit_bytes=40 << 20),
    )(raw, cosine, signed, query_gain.reshape(1, hd), key_gain.reshape(1, hd), query, kv, weights, grad_mixed)


DIMS = (NX, NYH, NZ, NC, 2)
CHUNKS = (256, 256, 256, 256, 256, 256, 256, 128, 128)
BACK = (256,) * 9
TURNS = ("xzy", "zyx", "yxz")


class Route:
    def __init__(self, me, go):
        x, yh, z, c, t = me.x, me.yh, me.z, me.c, me.t
        steps = (1, 3, 2)
        turn = lambda i, d: lax.rem(i + d, RING)
        self.go = go
        self.own = {"x": (x, c), "z": (z,), "y": (yh, t)}
        self.peers = {
            "x": [((x, 1 - c), me.device(c=1 - c))]
            + [
                ((turn(x, d), e), me.device(x=turn(x, d), c=e))
                for d in steps
                for e in (c, 1 - c)
            ],
            "z": [((turn(z, d),), me.device(z=turn(z, d))) for d in steps],
            "y": [
                ((turn(me.y, d) // 2, lax.rem(turn(me.y, d), 2)), me.at_y(turn(me.y, d)))
                for d in steps
            ],
        }

    def everyone(self):
        return [peer for axis in "xzy" for _, peer in self.peers[axis]]

    @staticmethod
    def view(ref, axis, at):
        if axis == "x":
            return ref.at[at[0], :, :, at[1]]
        if axis == "z":
            return ref.at[:, :, at[0]]
        return ref.at[:, at[0], :, :, at[1]]

    def send(self, axis, src, dst):
        own = self.own[axis]
        kept = self.go.keep(self.view(src, axis, own), self.view(dst, axis, own))
        copies = [
            self.go.put(self.view(src, axis, at), self.view(dst, axis, own), peer)
            for at, peer in self.peers[axis]
        ]
        return kept, copies

    @staticmethod
    def wait(sent):
        kept, copies = sent
        for copy in copies:
            copy.wait_recv()
        kept.wait()


def columns(ref, start, size):
    return ref.at[:, :, :, :, :, :, pl.ds(start, size)]


ORDER = ((0, 0), (1, 0), (0, 1), (2, 0), (1, 1), (0, 2), (2, 1), (1, 2), (2, 2))


def experts_kernel(
    tokens, spread, told, later, gate, up, down, router, rows, inner_low, grad_gate, grad_up, summed, expert_out, *rest
):
    chunks = len(CHUNKS)
    taken = iter(rest)
    take = lambda count: [next(taken) for _ in range(count)]
    first = take(4)
    mids_in, held_in = take(2 * chunks), take(chunks)
    mids_out, held_out = take(2 * chunks), take(chunks)
    last_source, extra = take(2)
    first += [extra, last_source]
    tokens_v, spread_v, asked_v, blocks_v, gate_v, up_v, down_v, router_v = take(8)
    gate_pre, up_pre, logits, inner_up, inner_v, gate_g, up_g = take(7)
    send, recv, local, back_send, back_recv, back_local, loads, told_sem, puts = take(9)
    me = Place()
    go, back = Copies(send, recv, local), Copies(back_send, back_recv, back_local)
    way_in, way_out = Route(me, go), Route(me, back)
    width = tokens.shape[1]
    slots, lanes = spread.shape[0], router.shape[1]
    block = 256
    index = me.expert()
    starts = [sum(CHUNKS[:n]) for n in range(chunks)]
    blocks = list(range(slots // block))

    early = [pltpu.make_async_copy(a, b, loads.at[n]) for n, (a, b) in enumerate(((tokens, tokens_v), (spread, spread_v)))]
    late = [
        pltpu.make_async_copy(a, b, loads.at[2 + n])
        for n, (a, b) in enumerate(
            ((down, down_v), (gate, gate_v), (up, up_v), (router, router_v), (later.at[:, pl.ds(width - told.shape[1], lanes)], asked_v))
        )
    ]
    for pull in early:
        pull.start()
    greet(way_in.everyone())
    for pull in early:
        pull.wait()

    def load(m):
        at, cut = pl.ds(m * block, block), told.shape[1]
        return [
            pltpu.make_async_copy(told.at[at], blocks_v.at[m % 2, :, pl.ds(0, cut)], told_sem.at[0, m % 2]),
            pltpu.make_async_copy(
                later.at[at, pl.ds(0, width - cut)], blocks_v.at[m % 2, :, pl.ds(cut, width - cut)], told_sem.at[1, m % 2]
            ),
        ]

    def each_block(step):
        def run(m, _):
            step(pl.ds(pl.multiple_of(m * block, block), block))
            return 0

        lax.fori_loop(0, slots // block, run, 0)

    sent_on, started = [None] * chunks, [None] * chunks
    outs = []

    def dispatch(n):
        buffer = first[n % 6]
        if n >= 6:
            go.release(started[n - 6][1])
        cols = pl.ds(starts[n], CHUNKS[n])
        flat = buffer.reshape(slots, buffer.shape[-1])

        def step(at):
            flat[at, : CHUNKS[n]] = dot_nn(spread_v[at], tokens_v[:, cols]).astype(BF16)

        each_block(step)
        return columns(buffer, 0, CHUNKS[n])

    def cotangent(m):
        for pull in load(m):
            pull.wait()
        at = pl.ds(m * block, block)
        inner_up[at] = dot_nt(blocks_v[m % 2], down_v[...])
        if m + 2 < len(blocks):
            for pull in load(m + 2):
                pull.start()

    def multiply(n, close=False):
        way_in.wait(sent_on[n])
        outs.append(go.keep(held_in[n], columns(rows, starts[n], CHUNKS[n])))
        cols = pl.ds(starts[n], CHUNKS[n])
        flat = held_in[n].reshape(slots, CHUNKS[n])

        def step(at):
            part = flat[at]
            terms = []
            for out, weight in ((gate_pre, gate_v), (up_pre, up_v), (logits, router_v)):
                term = dot_nn(part, weight[cols])
                if n > 0:
                    term = out[at] + term
                if not close:
                    out[at] = term
                terms.append(term)
            if close:
                finish(at, *terms)

        each_block(step)

    def finish(at, before_gate, before_up, row_logits):
        row_logits = jnp.where(asked_v[at] > 0, row_logits, MASKED)
        powers = jnp.exp(row_logits - jnp.max(row_logits, axis=-1, keepdims=True))
        lane = lax.broadcasted_iota(jnp.int32, (1, lanes), 1) == index
        prob = jnp.sum(jnp.where(lane, powers, 0.0), axis=-1, keepdims=True) / jnp.sum(
            powers, axis=-1, keepdims=True
        )
        after_inner = inner_up[at]
        sigmoid = 1.0 / (1.0 + jnp.exp(-before_gate))
        silu = before_gate * sigmoid
        inner = silu * before_up
        gate_up = jnp.sum(inner * after_inner, axis=-1, keepdims=True)
        inner_v[at] = (prob * inner).astype(BF16)
        after_inner = prob * after_inner
        gate_g[at] = (after_inner * before_up * sigmoid * (1.0 + before_gate * (1.0 - sigmoid))).astype(BF16)
        up_g[at] = (after_inner * silu).astype(BF16)
        high = gate_up.astype(BF16).astype(F32)
        flat = extra.reshape(slots, 2 * lanes)
        flat[at, :lanes] = jnp.where(lane, high, 0.0).astype(BF16)
        flat[at, lanes:] = jnp.where(lane, gate_up - high, 0.0).astype(BF16)

    todo = list(blocks)
    for triple, crossing in ORDER:
        for n in range(3 * triple, 3 * triple + 3):
            if n >= 6 and crossing == 2:
                go.release(started[n - 2][1] if n < 8 else [])
            if crossing == 0:
                src = dispatch(n)
            else:
                way_in.wait(sent_on[n])
                src = mids_in[2 * n + crossing - 1]
            dst = held_in[n] if crossing == 2 else mids_in[2 * n + crossing]
            sent_on[n] = way_in.send(TURNS[n % 3][crossing], src, dst)
            if crossing == 0:
                started[n] = sent_on[n]
            if crossing == 2 and triple > 0:
                multiply(n - 3)
            elif todo and triple + crossing > 1 and crossing > 0:
                cotangent(todo.pop(0))
        if (triple, crossing) == (1, 0):
            for pull in (*load(0), *load(1), *late):
                pull.start()
            late[0].wait()
        if (triple, crossing) == (2, 1):
            while todo:
                cotangent(todo.pop(0))
            for pull in late[1:]:
                pull.wait()
    for n in range(chunks - 3, chunks):
        multiply(n, close=n == chunks - 1)
    results = [
        pltpu.make_async_copy(a, b, puts.at[n])
        for n, (a, b) in enumerate(((inner_v, inner_low), (gate_g, grad_gate), (up_g, grad_up)))
    ]
    for result in results:
        result.start()
    for out in outs:
        out.wait()

    begins = [sum(BACK[:n]) for n in range(chunks)]
    sources = [*held_in[: chunks - 2], last_source]
    sent_back = [None] * chunks
    pushes = [None] * len(blocks)

    def gradient(n):
        cols = pl.ds(begins[n], BACK[n])
        flat = sources[n].reshape(slots, BACK[n])

        def step(at):
            flat[at] = (dot_nt(gate_g[at], gate_v[cols]) + dot_nt(up_g[at], up_v[cols])).astype(BF16)

        each_block(step)

    def outcome(m):
        if m >= 2:
            pushes[m - 2].wait()
        at = pl.ds(m * block, block)
        blocks_v[m % 2] = dot_nn(inner_v[at], down_v[...]).astype(BF16)
        pushes[m] = pltpu.make_async_copy(blocks_v.at[m % 2], expert_out.at[at], puts.at[3 + m])
        pushes[m].start()

    def combine(n):
        way_out.wait(sent_back[n])
        summed[:, begins[n] : begins[n] + BACK[n]] = dot_tn(
            spread_v[...], held_out[n].reshape(slots, BACK[n])[...]
        )

    todo = list(blocks)
    for triple, crossing in ORDER:
        for n in range(3 * triple, 3 * triple + 3):
            dst = held_out[n] if crossing == 2 else mids_out[2 * n + crossing]
            if crossing > 0:
                way_out.wait(sent_back[n])
                src = mids_out[2 * n + crossing - 1]
            elif n == chunks - 1:
                src = extra
            else:
                gradient(n)
                src = sources[n]
            sent_back[n] = way_out.send(TURNS[n % 3][crossing], src, dst)
            if crossing == 2 and triple > 0:
                combine(n - 3)
            elif todo and triple + crossing > 1 and crossing > 0:
                outcome(todo.pop(0))
    for n in range(chunks - 3, chunks):
        combine(n)
    for copy in (*results, *pushes[-2:]):
        copy.wait()
    go.finish()
    back.finish()


def experts(tokens, spread, told, later, gate, up, down, router):
    tok, width = tokens.shape
    slots = spread.shape[0]
    hidden, lanes = gate.shape[1], router.shape[1]
    lead = (*DIMS, slots // math.prod(DIMS))
    chunks = len(CHUNKS)
    low = jax.ShapeDtypeStruct((slots, hidden), BF16)

    def held(widths):
        return [pltpu.VMEM((*lead, w), BF16) for w in widths]

    twice = lambda widths: [w for w in widths for _ in range(2)]
    rows, *others = pl.pallas_call(
        experts_kernel,
        name="experts",
        cost_estimate=cost(120),
        out_shape=(
            jax.ShapeDtypeStruct((*lead, width), BF16),
            low,
            low,
            low,
            jax.ShapeDtypeStruct((tok, sum(BACK)), F32),
            jax.ShapeDtypeStruct((slots, width), BF16),
        ),
        in_specs=[ANY] * 8,
        out_specs=(ANY, ANY, ANY, ANY, VMEM, ANY),
        scratch_shapes=[
            *held(CHUNKS[:4]),
            *held(twice(CHUNKS)),
            *held(CHUNKS),
            *held(twice(BACK)),
            *held(BACK),
            *held((BACK[-2], BACK[-1])),
            pltpu.VMEM(tokens.shape, BF16),
            pltpu.VMEM(spread.shape, BF16),
            pltpu.VMEM((slots, lanes), BF16),
            pltpu.VMEM((2, 256, width), BF16),
            pltpu.VMEM(gate.shape, BF16),
            pltpu.VMEM(up.shape, BF16),
            pltpu.VMEM(down.shape, BF16),
            pltpu.VMEM(router.shape, BF16),
            pltpu.VMEM((slots, hidden), F32),
            pltpu.VMEM((slots, hidden), F32),
            pltpu.VMEM((slots, lanes), F32),
            pltpu.VMEM((slots, hidden), F32),
            *(pltpu.VMEM((slots, hidden), BF16) for _ in range(3)),
            pltpu.SemaphoreType.DMA((13 * chunks,)),
            pltpu.SemaphoreType.DMA((13 * chunks,)),
            pltpu.SemaphoreType.DMA((4 * chunks,)),
            pltpu.SemaphoreType.DMA((13 * chunks,)),
            pltpu.SemaphoreType.DMA((13 * chunks,)),
            pltpu.SemaphoreType.DMA((3 * chunks,)),
            pltpu.SemaphoreType.DMA((7,)),
            pltpu.SemaphoreType.DMA((2, 2)),
            pltpu.SemaphoreType.DMA((7,)),
        ],
        compiler_params=pltpu.CompilerParams(
            collective_id=6, has_side_effects=True, vmem_limit_bytes=61 << 20
        ),
    )(tokens, spread, told, later, gate, up, down, router)
    return rows.reshape(slots, width), *others


def on_device(
    hidden_in,
    doc_ids,
    expert_ids,
    attn_gain,
    query_weight,
    key_weight,
    value_weight,
    output_weight,
    query_gain,
    key_gain,
    moe_gain,
    router_weight,
    gate_weight,
    up_weight,
    down_weight,
    cotangent,
):
    both = ("dp", "tensor")
    tok, width = hidden_in.shape
    hd = query_gain.shape[0]
    nkv = key_weight.shape[1] // hd
    nq = query_weight.shape[1] // hd
    group = nq // nkv
    count = router_weight.shape[1]
    routes = expert_ids.shape[1]
    cap = tok * routes // count
    slots = count * cap
    scale = 1.0 / math.sqrt(hd)
    tokens = doc_ids.shape[1]

    lane = lax.broadcasted_iota(jnp.int32, (1, 1, count), 2)
    chosen = jnp.sum((expert_ids[:, :, None] == lane).astype(F32), axis=1)
    below = (
        lax.broadcasted_iota(jnp.int32, (tok, tok), 1)
        < lax.broadcasted_iota(jnp.int32, (tok, tok), 0)
    ).astype(BF16)
    rank = dot_nn(below, chosen.astype(BF16))
    place = jnp.where(chosen > 0, rank, -1.0).T
    spread = (
        place[:, None, :] == lax.broadcasted_iota(jnp.int32, (1, cap, 1), 1).astype(F32)
    ).astype(BF16).reshape(slots, tok)

    hidden = hidden_in.astype(F32)

    in_weights, out_weights, normed, docs, told, later = gather(
        query_weight,
        key_weight,
        value_weight,
        output_weight.T,
        hidden_in,
        attn_gain,
        jnp.broadcast_to(doc_ids, (8, tokens)).astype(F32),
        spread,
        cotangent,
        chosen.astype(BF16),
    )
    later = lax.all_to_all(
        later.reshape(count, cap, later.shape[1]), both, split_axis=0, concat_axis=0, tiled=True
    ).reshape(slots, later.shape[1])

    position, allowed = jax.vmap(layout)(docs[:, 0])
    cosine, sine = rotary(position.reshape(-1), hd)
    cosine = jnp.concatenate([cosine, cosine], axis=1)
    signed = jnp.concatenate([-sine, sine], axis=1)
    bias = jnp.where(allowed, 0.0, MASKED).astype(F32)
    raw = dot_nn(normed, in_weights)
    heads = group * hd
    query, kv, attention, mixed = attend(raw, bias, cosine, signed, query_gain, key_gain, scale)
    attn_out = reduce(dot_nt(mixed, out_weights).astype(BF16), 2)

    residual = hidden + attn_out
    moe_input = rms_scale(residual, moe_gain).astype(BF16)
    moe_input, later = lax.optimization_barrier((moe_input, later))
    gate_mat, up_mat, down_mat = gate_weight[0], up_weight[0], down_weight[0]
    rows, inner_low, grad_gate, grad_up, summed, expert_out = experts(
        moe_input, spread, told, later, gate_mat, up_mat, down_mat, router_weight
    )
    logits = dot_nn(moe_input, router_weight)
    masked = jnp.where(chosen > 0, logits, MASKED)
    probs = jnp.exp(masked - jnp.max(masked, axis=-1, keepdims=True))
    probs = probs / jnp.sum(probs, axis=-1, keepdims=True)

    upstream = cotangent.astype(F32)
    gate_upstream = summed[:, width : width + count] + summed[:, width + count :]
    grad_chosen = probs * (gate_upstream - jnp.sum(probs * gate_upstream, axis=-1, keepdims=True))
    grad_logits = grad_chosen.astype(BF16)
    grad_moe_input = summed[:, :width] + dot_nt(grad_logits, router_weight)
    router_part = dot_tn(moe_input, grad_logits)
    grad_norm, moegain_rows = rms_back(residual, moe_gain, grad_moe_input)
    moegain_part = jnp.sum(moegain_rows, axis=0)
    grad_residual = upstream + grad_norm
    grad_attn, piece = share(grad_residual.astype(BF16), router_part.astype(BF16), 3)
    expert_out, grad_attn = lax.optimization_barrier((expert_out, grad_attn))
    returned = lax.all_to_all(
        expert_out.reshape(count, cap, width), both, split_axis=0, concat_axis=0, tiled=True
    ).reshape(slots, width)

    grad_mixed = dot_nn(grad_attn, out_weights).astype(BF16)
    grad_raw, head_gains = attend_back(
        raw, cosine, signed, query_gain, key_gain, query, kv, attention, grad_mixed, scale
    )
    inner_low, rows, told, later, grad_raw = lax.optimization_barrier(
        (inner_low, rows, told, later, grad_raw)
    )
    cot_rows = jnp.concatenate([told, later[:, : width - told.shape[1]]], axis=1)
    down_grad = dot_tn(inner_low, cot_rows)
    gate_grad = dot_tn(rows, grad_gate)
    up_grad = dot_tn(rows, grad_up)
    normed_part, down_grad, gate_grad, up_grad = lax.optimization_barrier(
        (dot_nt(grad_raw, in_weights).astype(BF16), down_grad, gate_grad, up_grad)
    )
    grad_normed = reduce(normed_part, 4)
    grad_normed, returned = lax.optimization_barrier((grad_normed, returned))
    grad_hidden, attngain_rows = rms_back(hidden, attn_gain, grad_normed)
    input_grad = grad_residual + grad_hidden

    gains = jnp.concatenate([jnp.sum(attngain_rows, axis=0), moegain_part]).reshape(-1, hd)
    gains = jnp.concatenate([gains, head_gains, jnp.zeros((6, hd), F32)], axis=0)

    query_grad, key_grad, value_grad, out_grad, gains, router_grad, layer_out = scatter(
        dot_tn(normed, grad_raw).astype(BF16),
        dot_tn(grad_attn, mixed).astype(BF16),
        gains,
        piece,
        returned,
        spread,
        residual,
        (nq * hd, nkv * hd, nkv * hd, nq * hd),
    )
    at = width // hd
    return (
        layer_out,
        input_grad,
        gains[:at].reshape(-1),
        query_grad,
        key_grad,
        value_grad,
        out_grad.T,
        gains[2 * at],
        gains[2 * at + 1],
        gains[at : 2 * at].reshape(-1),
        router_grad.reshape(width, count).astype(F32),
        gate_grad[None],
        up_grad[None],
        down_grad[None],
    )


def solution(mesh):
    both = ("dp", "tensor")
    in_specs = (
        P(both, None),
        P("dp", None),
        P(both, None),
        P(),
        P("dp", "tensor"),
        P("dp", "tensor"),
        P("dp", "tensor"),
        P("tensor", "dp"),
        P(),
        P(),
        P(),
        P(),
        P(both, None, None),
        P(both, None, None),
        P(both, None, None),
        P(both, None),
    )
    out_specs = (
        P(both, None),
        P(both, None),
        P(),
        P("dp", "tensor"),
        P("dp", "tensor"),
        P("dp", "tensor"),
        P("tensor", "dp"),
        P(),
        P(),
        P(),
        P(),
        P(both, None, None),
        P(both, None, None),
        P(both, None, None),
    )
    return jax.shard_map(
        on_device, mesh=mesh, in_specs=in_specs, out_specs=out_specs, check_vma=False
    )
```

```python
import functools
import math

import jax
import jax.numpy as jnp
from jax import lax
from jax.experimental import pallas as pl
from jax.experimental.pallas import tpu as pltpu
from jax.sharding import PartitionSpec as P

BLOCK = 128
EPSILON = 1e-06
ROPE_BASE = 1000000.0
MASKED = -1e30
F32 = jnp.float32
BF16 = jnp.bfloat16


def dot_nt(a, b):
    return lax.dot_general(a, b, (((1,), (1,)), ((), ())), preferred_element_type=F32)


def dot_tn(a, b):
    return lax.dot_general(a, b, (((0,), (0,)), ((), ())), preferred_element_type=F32)


def dot_nn(a, b):
    return lax.dot_general(a, b, (((1,), (0,)), ((), ())), preferred_element_type=F32)


def rms_recip(values):
    return lax.rsqrt(jnp.mean(values * values, axis=-1, keepdims=True) + EPSILON)


def rms_scale(values, gain):
    return values * rms_recip(values) * gain


def rms_back(values, gain, upstream):
    r = rms_recip(values)
    scaled = upstream * gain
    inner = jnp.mean(scaled * values, axis=-1, keepdims=True)
    grad_values = r * scaled - values * (r * r * r) * inner
    return grad_values, upstream * values * r


def rotate(values, cosine, sine):
    half = values.shape[-1] // 2
    a = values[..., :half]
    b = values[..., half:]
    return jnp.concatenate([a * cosine - b * sine, b * cosine + a * sine], axis=-1)


def layout(doc_row):
    length = doc_row.shape[0]
    indices = jnp.arange(length, dtype=jnp.int32)
    same_doc = doc_row[:, None] == doc_row[None, :]
    earlier = indices[None, :] < indices[:, None]
    position = jnp.sum(jnp.where(same_doc & earlier, 1, 0), axis=1).astype(jnp.int32)
    blocks = position // BLOCK
    allowed = same_doc & (blocks[None, :] <= blocks[:, None])
    return position, allowed


def rotary(position, head_size):
    half = head_size // 2
    frequency = jnp.exp(-jnp.log(ROPE_BASE) * jnp.arange(half, dtype=F32) * 2.0 / head_size)
    angles = position.astype(F32)[:, None] * frequency[None, :]
    return jnp.cos(angles), jnp.sin(angles)


MESH = pl.DeviceIdType.MESH
ANY = pl.BlockSpec(memory_space=pl.ANY)
VMEM = pl.BlockSpec(memory_space=pltpu.VMEM)
NX, NYH, NZ, NC = 4, 2, 4, 2
RING = 4
EARLY = 256


def cost(microseconds):
    return pl.CostEstimate(flops=0, transcendentals=0, bytes_accessed=int(microseconds * 3.6e6))


class Place:
    def __init__(self):
        dp = lax.axis_index("dp")
        self.t = lax.axis_index("tensor")
        self.c = lax.rem(dp, NC)
        self.z = lax.rem(dp // NC, NZ)
        self.yh = lax.rem(dp // (NC * NZ), NYH)
        self.x = dp // (NC * NZ * NYH)
        self.y = self.yh * 2 + self.t

    def device(self, x=None, yh=None, z=None, c=None, t=None):
        pick = lambda given, own: own if given is None else given
        x, yh, z, c = pick(x, self.x), pick(yh, self.yh), pick(z, self.z), pick(c, self.c)
        return (((x * NYH + yh) * NZ + z) * NC + c, pick(t, self.t))

    def expert(self):
        return ((((self.x * NYH + self.yh) * NZ + self.z) * NC) + self.c) * 2 + self.t

    def at_y(self, y):
        return self.device(yh=y // 2, t=lax.rem(y, 2))


def after(i):
    return lax.rem(i + 1, RING)


def before(i):
    return lax.rem(i + RING - 1, RING)


def across(i):
    return lax.rem(i + 2, RING)


def greet(peers):
    barrier = pltpu.get_barrier_semaphore()
    for peer in peers:
        pl.semaphore_signal(barrier, inc=1, device_id=peer, device_id_type=MESH)
    pl.semaphore_wait(barrier, len(peers))


class Copies:
    def __init__(self, send, recv, local):
        self.send, self.recv, self.local = send, recv, local
        self.n = self.m = 0
        self.sent = []
        self.waited = set()

    def put(self, src, dst, peer):
        copy = pltpu.make_async_remote_copy(
            src_ref=src,
            dst_ref=dst,
            send_sem=self.send.at[self.n],
            recv_sem=self.recv.at[self.n],
            device_id=peer,
            device_id_type=MESH,
        )
        self.n += 1
        copy.start()
        self.sent.append(copy)
        return copy

    def keep(self, src, dst):
        copy = pltpu.make_async_copy(src, dst, self.local.at[self.m])
        self.m += 1
        copy.start()
        return copy

    def release(self, copies):
        for copy in copies:
            copy.wait_send()
            self.waited.add(id(copy))

    def finish(self):
        for copy in self.sent:
            if id(copy) not in self.waited:
                copy.wait_send()


def gather_kernel(
    q, k, v, o, hidden_h, gain, doc, spread_h, cot_h, chosen_h, wa, wb, toks, docs, told, later, *rest
):
    sources, mids = rest[:3], rest[3:9]
    hidden, spread, cot, chosen, tok, stage, send, recv, local = rest[9:]
    me = Place()
    x, yh, z, c, p = me.x, me.yh, me.z, me.c, me.y
    sibling = me.device(c=1 - c)
    pair = me.device(yh=1 - yh)
    ring_x = (me.device(x=after(x)), me.device(x=before(x)))
    ring_z = (me.device(z=after(z)), me.device(z=before(z)))
    ring_y = (me.at_y(after(p)), me.at_y(before(p)))
    go = Copies(send, recv, local)
    route = Route(me, go)
    pulls = [go.keep(a, b) for a, b in ((hidden_h, hidden), (spread_h, spread), (cot_h, cot), (chosen_h, chosen))]
    greet(route.everyone())
    slots, block = spread.shape[0], 256

    def dispatch(n):
        cols = pl.ds(n * EARLY, EARLY)
        flat = sources[n].reshape(slots, EARLY)

        def step(m, _):
            at = pl.ds(pl.multiple_of(m * block, block), block)
            flat[at] = dot_nn(spread[at], cot[:, cols]).astype(BF16)
            return 0

        lax.fori_loop(0, slots // block, step, 0)
        return sources[n]

    pushes = [None] * (slots // block)

    def layout_later(m):
        if m >= 2:
            pushes[m - 2].wait()
        at = pl.ds(m * block, block)
        cut = cot.shape[1] - 3 * EARLY
        stage[m % 2, :, :cut] = dot_nn(spread[at], cot[:, 3 * EARLY :]).astype(BF16)
        stage[m % 2, :, cut:] = dot_nn(spread[at], chosen[...]).astype(BF16)
        pushes[m] = go.keep(stage.at[m % 2], later.at[at])

    crossed = [None] * 3

    def cross(step):
        for n in range(3):
            if step > 0:
                route.wait(crossed[n])
            src = dispatch(n) if step == 0 else mids[2 * n + step - 1]
            dst = columns(told, n * EARLY, EARLY) if step == 2 else mids[2 * n + step]
            crossed[n] = route.send(TURNS[n][step], src, dst)

    shards, start = [], 0
    for ref, w in ((q, wa), (k, wa), (v, wa), (o, wb)):
        cols = ref.shape[1] // NYH
        to = w.at[x, yh, z, c, :, pl.ds(0 if w is wb else start, cols)]
        shards.append((ref, cols, to))
        start += cols

    def part(ref, cols, head):
        return ref.at[:, pl.ds(pl.multiple_of(head * cols, cols), cols)]

    pairs = [go.put(part(ref, cols, 1 - yh), to, pair) for ref, cols, to in shards]
    kept = [go.keep(part(ref, cols, yh), to) for ref, cols, to in shards]
    for pull in pulls:
        pull.wait()
    rows = hidden[...].astype(F32)
    tok[...] = (rows * unit_rows(rows) * gain[...]).astype(BF16)
    for copy in kept:
        copy.wait()
    for copy in pairs:
        copy.wait_recv()

    ways = (
        (x, z, ring_x, ring_z, lambda i, j: wa.at[i, :, j, c], lambda j: wa.at[:, :, j, c]),
        (z, x, ring_z, ring_x, lambda i, j: wb.at[j, :, i, c], lambda j: wb.at[j, :, :, c]),
    )

    def both(ref, peers):
        return [go.put(ref, ref, peer) for peer in peers]

    def relay(low, high, copies, peers):
        copies[0].wait_recv()
        up = go.put(low.at[0], low.at[0], peers[0])
        copies[1].wait_recv()
        return [up, go.put(high.at[1], high.at[1], peers[1])]

    def arrived(copies):
        for copy in copies:
            copy.wait_recv()

    near = [both(unit(i, j), one) for i, j, one, two, unit, slab in ways]
    own = [both(unit(i, j), two) for i, j, one, two, unit, slab in ways]
    rows = [go.put(tok, toks.at[p], peer) for peer in ring_y]
    kept_rows = [go.keep(tok, toks.at[p]), go.keep(doc, docs.at[yh])]
    tail = [go.put(doc, docs.at[yh], pair)]
    cross(0)
    far = [
        relay(unit(before(i), j), unit(after(i), j), copies, one)
        for (i, j, one, two, unit, slab), copies in zip(ways, near)
    ]
    low = [both(unit(before(i), j), two) for i, j, one, two, unit, slab in ways]
    high = [both(unit(after(i), j), two) for i, j, one, two, unit, slab in ways]
    last = []
    for (i, j, one, two, unit, slab), copies in zip(ways, far):
        arrived(copies)
        last.append(both(unit(across(i), j), two))
        tail.append(go.put(slab(j), slab(j), sibling))
    layout_later(0)
    cross(1)
    half = tok.shape[0] // 2
    rows[0].wait_recv()
    piece = toks.at[before(p), pl.ds(0, half)]
    tail.append(go.put(piece, piece, ring_y[0]))
    rows[1].wait_recv()
    piece = toks.at[after(p), pl.ds(half, half)]
    tail.append(go.put(piece, piece, ring_y[1]))
    ends = [[], []]
    for place, copies in ((lambda i: i, own), (before, low), (after, high), (across, last)):
        for n, (i, j, one, two, unit, slab) in enumerate(ways):
            u = place(i)
            ends[n] += relay(unit(u, before(j)), unit(u, after(j)), copies[n], two)
        if copies is high:
            cross(2)
    for i, j, one, two, unit, slab in ways:
        tail.append(go.put(slab(before(j)), slab(before(j)), sibling))
        tail.append(go.put(slab(after(j)), slab(after(j)), sibling))
    for m in range(1, slots // block):
        layout_later(m)
    for (i, j, one, two, unit, slab), copies in zip(ways, ends):
        arrived(copies)
        tail.append(go.put(slab(across(j)), slab(across(j)), sibling))
    arrived(tail)
    for copy in (*kept_rows, *pushes[-2:]):
        copy.wait()
    for sent in crossed:
        route.wait(sent)
    go.finish()


def gather(query, key, value, out, hidden, gain, docs, spread, cot, chosen):
    rows = query.shape[0]
    width_a = (query.shape[1] + key.shape[1] + value.shape[1]) // NYH
    width_b = out.shape[1] // NYH
    lead = (NX, NYH, NZ, NC, rows)
    slots, width = spread.shape[0], cot.shape[1]
    blocks = (*DIMS, slots // math.prod(DIMS))
    left = width - 3 * EARLY + chosen.shape[1]
    wa, wb, toks, docs, told, later = pl.pallas_call(
        gather_kernel,
        name="gather_weights",
        cost_estimate=cost(60),
        out_shape=(
            jax.ShapeDtypeStruct((*lead, width_a), BF16),
            jax.ShapeDtypeStruct((*lead, width_b), BF16),
            jax.ShapeDtypeStruct((RING, *hidden.shape), BF16),
            jax.ShapeDtypeStruct((NYH, *docs.shape), docs.dtype),
            jax.ShapeDtypeStruct((*blocks, 3 * EARLY), BF16),
            jax.ShapeDtypeStruct((slots, left), BF16),
        ),
        in_specs=[*(ANY,) * 5, VMEM, *(ANY,) * 4],
        out_specs=(ANY,) * 6,
        scratch_shapes=[
            *(pltpu.VMEM((*blocks, EARLY), BF16) for _ in range(9)),
            *(pltpu.VMEM(a.shape, BF16) for a in (hidden, spread, cot, chosen, hidden)),
            pltpu.VMEM((2, 256, left), BF16),
            pltpu.SemaphoreType.DMA((96,)),
            pltpu.SemaphoreType.DMA((96,)),
            pltpu.SemaphoreType.DMA((23,)),
        ],
        compiler_params=pltpu.CompilerParams(
            collective_id=1, has_side_effects=True, vmem_limit_bytes=60 << 20
        ),
    )(query, key, value, out, hidden, gain.reshape(1, -1), docs, spread, cot, chosen)
    depth = NX * NYH * NZ * NC * rows
    return (
        wa.reshape(depth, width_a),
        wb.reshape(depth, width_b),
        toks.reshape(RING * hidden.shape[0], hidden.shape[1]),
        docs,
        told.reshape(slots, 3 * EARLY),
        later,
    )


def share_kernel(tok, part, toks, piece, got_x, sum_x, got_z, sum_z, got_y, send, recv, local):
    me = Place()
    x, yh, z, c, p = me.x, me.yh, me.z, me.c, me.y
    ring = (me.at_y(after(p)), me.at_y(before(p)))
    go = Copies(send, recv, local)
    route = Route(me, go)
    greet(route.everyone())
    half = tok.shape[0] // 2
    halves = [pl.ds(h * half, half) for h in range(2)]
    direct = [go.put(tok.at[halves[h]], toks.at[p, halves[h]], ring[h]) for h in range(2)]
    others = [go.put(tok.at[halves[1 - h]], toks.at[p, halves[1 - h]], ring[h]) for h in range(2)]
    kept = go.keep(tok, toks.at[p])
    own = go.keep(part.at[x, :, :, c], got_x.at[x * NC + c])
    terms = [
        go.put(part.at[at[0], :, :, at[1]], got_x.at[x * NC + c], peer)
        for at, peer in route.peers["x"]
    ]

    def arrived(copies):
        for copy in copies:
            copy.wait_recv()

    def added(got):
        value = got[0].astype(F32)
        for n in range(1, got.shape[0]):
            value += got[n].astype(F32)
        return value

    own.wait()
    arrived(terms)
    sum_x[...] = added(got_x)
    got_z[z] = sum_x[:, z]
    terms = [go.put(sum_x.at[:, at[0]], got_z.at[z], peer) for at, peer in route.peers["z"]]
    relays = []
    for h, owner in enumerate((before(p), after(p))):
        direct[h].wait_recv()
        rows = toks.at[owner, halves[h]]
        relays.append(go.put(rows, rows, ring[h]))
    arrived(terms)
    sum_z[...] = added(got_z)
    got_y[p] = sum_z[yh, me.t]
    terms = [go.put(sum_z.at[at[0], at[1]], got_y.at[p], peer) for at, peer in route.peers["y"]]
    arrived(terms)
    piece[...] = added(got_y).astype(piece.dtype)
    arrived(others)
    arrived(relays)
    kept.wait()
    go.finish()


def share(tokens, part, ident):
    rows, lanes = part.shape[0] // math.prod(DIMS), part.shape[1]
    toks, piece = pl.pallas_call(
        share_kernel,
        name=f"share_rows_{ident}",
        cost_estimate=cost(20),
        out_shape=(
            jax.ShapeDtypeStruct((RING, *tokens.shape), tokens.dtype),
            jax.ShapeDtypeStruct((rows, lanes), BF16),
        ),
        in_specs=[ANY, ANY],
        out_specs=(ANY, VMEM),
        scratch_shapes=[
            pltpu.VMEM((NX * NC, NYH, NZ, 2, rows, lanes), BF16),
            pltpu.VMEM((NYH, NZ, 2, rows, lanes), F32),
            pltpu.VMEM((NZ, NYH, 2, rows, lanes), F32),
            pltpu.VMEM((NYH, 2, rows, lanes), F32),
            pltpu.VMEM((RING, rows, lanes), F32),
            pltpu.SemaphoreType.DMA((19,)),
            pltpu.SemaphoreType.DMA((19,)),
            pltpu.SemaphoreType.DMA((2,)),
        ],
        compiler_params=pltpu.CompilerParams(collective_id=ident, has_side_effects=True),
    )(tokens, part.reshape(*DIMS, rows, lanes))
    return toks.reshape(RING * tokens.shape[0], tokens.shape[1]), piece


def reduce_kernel(part, out, held, own, got, send, recv, local):
    me = Place()
    p = me.y
    ring = (me.at_y(after(p)), me.at_y(before(p)))
    greet(ring)
    go = Copies(send, recv, local)
    half = out.shape[0] // 2
    halves = [pl.ds(h * half, half) for h in range(2)]
    near = (after(p), before(p))
    cross = [go.put(part.at[across(p), halves[h]], got.at[h], ring[h]) for h in range(2)]
    kept = [go.keep(part.at[near[h], halves[h]], held.at[h]) for h in range(2)]
    straight = [go.put(part.at[near[h], halves[1 - h]], got.at[2 + h], ring[h]) for h in range(2)]
    mine = go.keep(part.at[p], own)
    sums = []
    for h in range(2):
        kept[h].wait()
        cross[h].wait_recv()
        held[h] = (held[h].astype(F32) + got[h].astype(F32)).astype(BF16)
        sums.append(go.put(held.at[h], got.at[4 + h], ring[h]))
    mine.wait()
    for copy in straight:
        copy.wait_recv()
    for h in range(2):
        sums[h].wait_recv()
        out[halves[h]] = (
            own[halves[h]].astype(F32) + got[4 + h].astype(F32) + got[3 - h].astype(F32)
        )
    go.finish()


def reduce(part, ident):
    rows, width = part.shape[0] // RING, part.shape[1]
    half = rows // 2
    return pl.pallas_call(
        reduce_kernel,
        name=f"reduce_rows_{ident}",
        cost_estimate=cost(1),
        out_shape=jax.ShapeDtypeStruct((rows, width), F32),
        in_specs=[ANY],
        out_specs=VMEM,
        scratch_shapes=[
            pltpu.VMEM((2, half, width), BF16),
            pltpu.VMEM((rows, width), BF16),
            pltpu.VMEM((6, half, width), BF16),
            pltpu.SemaphoreType.DMA((6,)),
            pltpu.SemaphoreType.DMA((6,)),
            pltpu.SemaphoreType.DMA((3,)),
        ],
        compiler_params=pltpu.CompilerParams(
            collective_id=ident, has_side_effects=True, vmem_limit_bytes=24 << 20
        ),
    )(part.reshape(RING, rows, width))


def scatter_kernel(
    ga, gb, gains, piece, returned, slots, residual, oq, ok, ov, oo, og, op, layer, back_v, slots_v, ka, kb, da, db, ra, rb, qa, qb, sa, sb, ta, tb, ua, ub, ma, mb,
    ring_gains, sum_gains, pair_gains, send, recv, local
):
    me = Place()
    x, yh, z, c, t = me.x, me.yh, me.z, me.c, me.t
    sibling = me.device(c=1 - c)
    pair = me.device(yh=1 - yh)
    partner = me.device(t=1 - t)
    ring_x = (me.device(x=after(x)), me.device(x=before(x)))
    ring_z = (me.device(z=after(z)), me.device(z=before(z)))
    round_x = (*ring_x, me.device(x=across(x)))
    round_z = (*ring_z, me.device(z=across(z)))
    greet([sibling, pair, partner, *round_x, *round_z])
    go = Copies(send, recv, local)

    def around(n, term, own, peers):
        ring_gains[n, own] = term
        return [go.put(ring_gains.at[n, own], ring_gains.at[n, own], peer) for peer in peers]

    def ring_sum(n, copies):
        for copy in copies:
            copy.wait_recv()
        return (ring_gains[n, 0] + ring_gains[n, 1]) + (ring_gains[n, 2] + ring_gains[n, 3])

    def swap(n, term, peer):
        sum_gains[n] = term
        return go.put(sum_gains.at[n], pair_gains.at[n], peer)

    def swapped(n, copy):
        copy.wait_recv()
        return sum_gains[n] + pair_gains[n]


    ways = (
        (lambda i, h, n: ga.at[i, h, :, n], x, z, ring_x, ring_z, ka, da, ra, qa, sa, ta),
        (lambda i, h, n: gb.at[:, h, i, n], z, x, ring_z, ring_x, kb, db, rb, qb, sb, tb),
    )
    places = (across, after, before, lambda i: i)

    def spread(ref, peers):
        return [go.put(ref, ref, peer) for peer in peers]

    def arrived(copies):
        for copy in copies:
            copy.wait_recv()

    given, held = [[], []], [[], []]
    for n, place in enumerate(places):
        for w, (slab, i, j, one, two, k, d, r, q, s, u) in enumerate(ways):
            given[w].append([go.put(slab(place(i), h, 1 - c), d.at[n, h], sibling) for h in range(2)])
            held[w].append([go.keep(slab(place(i), h, c), k.at[n, h]) for h in range(2)])

    def ready(w, n, h):
        given[w][n][h].wait_recv()
        held[w][n][h].wait()

    def total(w, n, h, extra):
        slab, i, j, one, two, k, d, r, q, s, u = ways[w]

        def step(m, _):
            value = k[n, h, m].astype(F32) + d[n, h, m].astype(F32)
            for e in extra:
                value += r[e, m].astype(F32)
            k[n, h, m] = value.astype(BF16)
            return 0

        lax.fori_loop(0, k.shape[2], step, 0)

    terms = around(0, gains[...], x, round_x)
    mine = op.at[x, yh, z, c, t]
    held_piece = go.keep(piece, mine)
    pieces = [go.put(piece, mine, sibling)]
    pulls = [go.keep(returned, back_v), go.keep(slots, slots_v)]
    cross, straight, sums = [[], []], [[], []], [[], []]
    for w, (slab, i, j, one, two, k, d, r, q, s, u) in enumerate(ways):
        for h in range(2):
            ready(w, 0, h)
            total(w, 0, h, ())
            cross[w].append(go.put(k.at[0, h], r.at[h], one[h]))
    for w, (slab, i, j, one, two, k, d, r, q, s, u) in enumerate(ways):
        for h in range(2):
            ready(w, 1 + h, 1 - h)
            total(w, 1 + h, 1 - h, ())
            straight[w].append(go.put(k.at[1 + h, 1 - h], r.at[2 + h], one[h]))
    for pull in pulls:
        pull.wait()
    for m in range(4):
        cols = pl.ds(m * layer.shape[1] // 4, layer.shape[1] // 4)
        layer[:, cols] = (residual[:, cols] + dot_tn(slots_v[...], back_v[:, cols])).astype(layer.dtype)
    terms = around(1, ring_sum(0, terms), z, round_z)
    arrived(pieces)
    held_piece.wait()
    pieces = spread(op.at[x, yh, z, :, t], [partner])
    for w, (slab, i, j, one, two, k, d, r, q, s, u) in enumerate(ways):
        for h in range(2):
            ready(w, 1 + h, h)
            cross[w][h].wait_recv()
            total(w, 1 + h, h, (h,))
            sums[w].append(go.put(k.at[1 + h, h], r.at[4 + h], one[h]))
    arrived(pieces)
    pieces = spread(op.at[x, yh, z], [pair])
    terms = swap(0, ring_sum(1, terms), pair)
    for w in range(2):
        for h in range(2):
            ready(w, 3, h)
            straight[w][1 - h].wait_recv()
            total(w, 3, h, (3 - h,))
    arrived(pieces)
    pieces = spread(op.at[x, :, z], round_x)
    terms = swap(1, swapped(0, terms), partner)
    over, direct, final = [[], []], [[], []], [[], []]
    for w, (slab, i, j, one, two, k, d, r, q, s, u) in enumerate(ways):
        near = (after(j), before(j))
        for h in range(2):
            sums[w][h].wait_recv()

            def step(m, _, k=k, r=r, h=h):
                k[3, h, m] = (k[3, h, m].astype(F32) + r[4 + h, m].astype(F32)).astype(BF16)
                return 0

            lax.fori_loop(0, k.shape[2], step, 0)
            over[w].append(go.put(k.at[3, h, across(j)], q.at[h], two[h]))
        for h in range(2):
            direct[w].append(go.put(k.at[3, 1 - h, near[h]], q.at[2 + h], two[h]))
    arrived(pieces)
    pieces = spread(op.at[:, :, z], round_z)
    terms = swap(2, swapped(1, terms), sibling)
    for w, (slab, i, j, one, two, k, d, r, q, s, u) in enumerate(ways):
        near = (after(j), before(j))
        for h in range(2):
            over[w][h].wait_recv()
            s[h] = (k[3, h, near[h]].astype(F32) + q[h].astype(F32)).astype(BF16)
            final[w].append(go.put(s.at[h], q.at[4 + h], two[h]))
    last = []
    for w, ((slab, i, j, one, two, k, d, r, q, s, u), v, m) in enumerate(zip(ways, (ua, ub), (ma, mb))):
        arrived(direct[w])
        arrived(final[w])
        for h in range(2):
            u[h] = k[3, h, j].astype(F32) + q[4 + h].astype(F32) + q[3 - h].astype(F32)
        v[...] = u[1 - yh].astype(BF16)
        last.append(go.put(v, m, pair))
    og[...] = swapped(2, terms)

    def write(head, a, b):
        start = 0
        for out, block in ((oq, a), (ok, a), (ov, a), (oo, b)):
            cols = out.shape[1] // NYH
            at = 0 if block is b else start
            out[:, pl.ds(pl.multiple_of(head * cols, cols), cols)] = block[:, at : at + cols]
            start += cols

    write(yh, ta[yh], tb[yh])
    arrived(last)
    write(1 - yh, ma[...].astype(F32), mb[...].astype(F32))
    arrived(pieces)
    go.finish()


def scatter(grad_a, grad_b, gains, piece, returned, slots, residual, columns):
    rows = grad_a.shape[0] // (NX * NYH * NZ * NC)
    lead = (NX, NYH, NZ, NC, rows)
    widths = (grad_a.shape[1], grad_b.shape[1])

    def each(shape, dtype):
        return [pltpu.VMEM((*shape, rows, w), dtype) for w in widths]

    return pl.pallas_call(
        scatter_kernel,
        name="scatter_weights",
        cost_estimate=cost(80),
        out_shape=(
            *(jax.ShapeDtypeStruct((rows, w), F32) for w in columns),
            jax.ShapeDtypeStruct(gains.shape, F32),
            jax.ShapeDtypeStruct((NX, NYH, NZ, NC, 2, *piece.shape), piece.dtype),
            jax.ShapeDtypeStruct(residual.shape, BF16),
        ),
        in_specs=[ANY, ANY, VMEM, ANY, ANY, ANY, VMEM],
        out_specs=(*(VMEM,) * 5, ANY, VMEM),
        scratch_shapes=[
            pltpu.VMEM(returned.shape, BF16),
            pltpu.VMEM(slots.shape, BF16),
            *each((4, 2, RING), BF16),
            *each((4, 2, RING), BF16),
            *each((6, RING), BF16),
            *each((6,), BF16),
            *each((2,), BF16),
            *each((2,), F32),
            *each((), BF16),
            *each((), BF16),
            pltpu.VMEM((2, RING, *gains.shape), F32),
            pltpu.VMEM((3, *gains.shape), F32),
            pltpu.VMEM((3, *gains.shape), F32),
            pltpu.SemaphoreType.DMA((60,)),
            pltpu.SemaphoreType.DMA((60,)),
            pltpu.SemaphoreType.DMA((19,)),
        ],
        compiler_params=pltpu.CompilerParams(
            collective_id=5, has_side_effects=True, vmem_limit_bytes=48 << 20
        ),
    )(grad_a.reshape(*lead, widths[0]), grad_b.reshape(*lead, widths[1]), gains, piece, returned, slots, residual)


def unit_rows(values):
    return lax.rsqrt(jnp.mean(values * values, axis=-1, keepdims=True) + EPSILON)


def turn(values, cosine, signed):
    return values * cosine + pltpu.roll(values, values.shape[-1] // 2, 1) * signed


def attend_kernel(scale, raw, bias, cosine, signed, qgain, kgain, query, kv, weights, mixed):
    heads = query.shape[1] // cosine.shape[1]
    hd = cosine.shape[1]
    cos, sig = cosine[...], signed[...]
    key_raw = raw[:, heads * hd : (heads + 1) * hd]
    key = turn(key_raw * unit_rows(key_raw) * kgain[...], cos, sig).astype(BF16)
    value = raw[:, (heads + 1) * hd :].astype(BF16)
    kv[:, :hd] = key
    kv[:, hd:] = value
    for h in range(heads):
        at = slice(h * hd, (h + 1) * hd)
        head = raw[:, at]
        rows = turn(head * unit_rows(head) * qgain[...], cos, sig).astype(BF16)
        query[:, at] = rows
        scores = dot_nt(rows, key) * scale + bias[0]
        peak = jnp.max(scores, axis=-1, keepdims=True)
        weight = jnp.exp(scores - peak)
        weight = weight * (1.0 / jnp.sum(weight, axis=-1, keepdims=True))
        weights[0, h] = weight
        mixed[:, at] = dot_nn(weight.astype(BF16), value).astype(BF16)


def attend(raw, bias, cosine, signed, query_gain, key_gain, scale):
    groups, tokens = bias.shape[0], bias.shape[1]
    hd = cosine.shape[1]
    heads = raw.shape[1] // hd - 2
    rows = groups * tokens

    def block(cols):
        return pl.BlockSpec((tokens, cols), lambda g: (g, 0))

    gain = pl.BlockSpec((1, hd), lambda g: (0, 0))
    square = pl.BlockSpec((1, tokens, tokens), lambda g: (g, 0, 0))
    return pl.pallas_call(
        functools.partial(attend_kernel, scale),
        name="attend",
        cost_estimate=cost(8),
        grid=(groups,),
        out_shape=(
            jax.ShapeDtypeStruct((rows, heads * hd), BF16),
            jax.ShapeDtypeStruct((rows, 2 * hd), BF16),
            jax.ShapeDtypeStruct((groups, heads, tokens, tokens), F32),
            jax.ShapeDtypeStruct((rows, heads * hd), BF16),
        ),
        in_specs=[block((heads + 2) * hd), square, block(hd), block(hd), gain, gain],
        out_specs=(
            block(heads * hd),
            block(2 * hd),
            pl.BlockSpec((1, heads, tokens, tokens), lambda g: (g, 0, 0, 0)),
            block(heads * hd),
        ),
        compiler_params=pltpu.CompilerParams(vmem_limit_bytes=40 << 20),
    )(raw, bias, cosine, signed, query_gain.reshape(1, hd), key_gain.reshape(1, hd))


def norm_back(values, gain, upstream):
    r = unit_rows(values)
    scaled = upstream * gain
    inner = jnp.mean(scaled * values, axis=-1, keepdims=True)
    grad = r * scaled - values * (r * r * r * inner)
    return grad, jnp.sum(upstream * values * r, axis=0, keepdims=True)


def attend_back_kernel(
    scale, raw, cosine, signed, qgain, kgain, query, kv, weights, grad_mixed, grad_raw, grad_gains
):
    hd = cosine.shape[1]
    heads = query.shape[1] // hd
    cos, sig = cosine[...], -signed[...]
    key, value = kv[:, :hd], kv[:, hd:]
    grad_key = jnp.zeros(key.shape, F32)
    grad_value = jnp.zeros(key.shape, F32)
    query_gains = jnp.zeros((1, hd), F32)
    for h in range(heads):
        at = slice(h * hd, (h + 1) * hd)
        weight = weights[0, h]
        grad_head = grad_mixed[:, at]
        grad_value += dot_tn(weight.astype(BF16), grad_head)
        grad_soft = dot_nt(grad_head, value)
        delta = jnp.sum(weight * grad_soft, axis=-1, keepdims=True)
        grad_scores = (weight * (grad_soft - delta)).astype(BF16)
        grad_key += dot_tn(grad_scores, query[:, at])
        turned = turn(dot_nn(grad_scores, key) * scale, cos, sig)
        grad, gains = norm_back(raw[:, at], qgain[...], turned)
        grad_raw[:, at] = grad.astype(BF16)
        query_gains += gains
    at = slice(heads * hd, (heads + 1) * hd)
    grad, key_gains = norm_back(raw[:, at], kgain[...], turn(grad_key * scale, cos, sig))
    grad_raw[:, at] = grad.astype(BF16)
    grad_raw[:, (heads + 1) * hd :] = grad_value.astype(BF16)
    gains = jnp.concatenate([query_gains, key_gains], axis=0)

    @pl.when(pl.program_id(0) == 0)
    def _():
        grad_gains[...] = gains

    @pl.when(pl.program_id(0) > 0)
    def _():
        grad_gains[...] += gains


def attend_back(raw, cosine, signed, query_gain, key_gain, query, kv, weights, grad_mixed, scale):
    groups, heads, tokens, _ = weights.shape
    hd = cosine.shape[1]
    rows = groups * tokens

    def block(cols):
        return pl.BlockSpec((tokens, cols), lambda g: (g, 0))

    gain = pl.BlockSpec((1, hd), lambda g: (0, 0))
    return pl.pallas_call(
        functools.partial(attend_back_kernel, scale),
        name="attend_back",
        cost_estimate=cost(1),
        grid=(groups,),
        out_shape=(
            jax.ShapeDtypeStruct((rows, (heads + 2) * hd), BF16),
            jax.ShapeDtypeStruct((2, hd), F32),
        ),
        in_specs=[
            block((heads + 2) * hd),
            block(hd),
            block(hd),
            gain,
            gain,
            block(heads * hd),
            block(2 * hd),
            pl.BlockSpec((1, heads, tokens, tokens), lambda g: (g, 0, 0, 0)),
            block(heads * hd),
        ],
        out_specs=(block((heads + 2) * hd), pl.BlockSpec((2, hd), lambda g: (0, 0))),
        compiler_params=pltpu.CompilerParams(vmem_limit_bytes=40 << 20),
    )(raw, cosine, signed, query_gain.reshape(1, hd), key_gain.reshape(1, hd), query, kv, weights, grad_mixed)


DIMS = (NX, NYH, NZ, NC, 2)
CHUNKS = (256, 256, 256, 256, 256, 256, 256, 128, 128)
BACK = (256,) * 9
TURNS = ("xzy", "zyx", "yxz")


class Route:
    def __init__(self, me, go):
        x, yh, z, c, t = me.x, me.yh, me.z, me.c, me.t
        steps = (1, 3, 2)
        turn = lambda i, d: lax.rem(i + d, RING)
        self.go = go
        self.own = {"x": (x, c), "z": (z,), "y": (yh, t)}
        self.peers = {
            "x": [((x, 1 - c), me.device(c=1 - c))]
            + [
                ((turn(x, d), e), me.device(x=turn(x, d), c=e))
                for d in steps
                for e in (c, 1 - c)
            ],
            "z": [((turn(z, d),), me.device(z=turn(z, d))) for d in steps],
            "y": [
                ((turn(me.y, d) // 2, lax.rem(turn(me.y, d), 2)), me.at_y(turn(me.y, d)))
                for d in steps
            ],
        }

    def everyone(self):
        return [peer for axis in "xzy" for _, peer in self.peers[axis]]

    @staticmethod
    def view(ref, axis, at):
        if axis == "x":
            return ref.at[at[0], :, :, at[1]]
        if axis == "z":
            return ref.at[:, :, at[0]]
        return ref.at[:, at[0], :, :, at[1]]

    def send(self, axis, src, dst):
        own = self.own[axis]
        kept = self.go.keep(self.view(src, axis, own), self.view(dst, axis, own))
        copies = [
            self.go.put(self.view(src, axis, at), self.view(dst, axis, own), peer)
            for at, peer in self.peers[axis]
        ]
        return kept, copies

    @staticmethod
    def wait(sent):
        kept, copies = sent
        for copy in copies:
            copy.wait_recv()
        kept.wait()


def columns(ref, start, size):
    return ref.at[:, :, :, :, :, :, pl.ds(start, size)]


ORDER = ((0, 0), (1, 0), (0, 1), (2, 0), (1, 1), (0, 2), (2, 1), (1, 2), (2, 2))


def experts_kernel(
    tokens, spread, told, later, gate, up, down, router, rows, inner_low, grad_gate, grad_up, summed, expert_out, *rest
):
    chunks = len(CHUNKS)
    taken = iter(rest)
    take = lambda count: [next(taken) for _ in range(count)]
    first = take(4)
    mids_in, held_in = take(2 * chunks), take(chunks)
    mids_out, held_out = take(2 * chunks), take(chunks)
    last_source, extra = take(2)
    first += [extra, last_source]
    tokens_v, spread_v, asked_v, blocks_v, gate_v, up_v, down_v, router_v = take(8)
    gate_pre, up_pre, logits, inner_up, inner_v, gate_g, up_g = take(7)
    send, recv, local, back_send, back_recv, back_local, loads, told_sem, puts = take(9)
    me = Place()
    go, back = Copies(send, recv, local), Copies(back_send, back_recv, back_local)
    way_in, way_out = Route(me, go), Route(me, back)
    width = tokens.shape[1]
    slots, lanes = spread.shape[0], router.shape[1]
    block = 256
    index = me.expert()
    starts = [sum(CHUNKS[:n]) for n in range(chunks)]
    blocks = list(range(slots // block))

    early = [pltpu.make_async_copy(a, b, loads.at[n]) for n, (a, b) in enumerate(((tokens, tokens_v), (spread, spread_v)))]
    late = [
        pltpu.make_async_copy(a, b, loads.at[2 + n])
        for n, (a, b) in enumerate(
            ((down, down_v), (gate, gate_v), (up, up_v), (router, router_v), (later.at[:, pl.ds(width - told.shape[1], lanes)], asked_v))
        )
    ]
    for pull in early:
        pull.start()
    greet(way_in.everyone())
    for pull in early:
        pull.wait()

    def load(m):
        at, cut = pl.ds(m * block, block), told.shape[1]
        return [
            pltpu.make_async_copy(told.at[at], blocks_v.at[m % 2, :, pl.ds(0, cut)], told_sem.at[0, m % 2]),
            pltpu.make_async_copy(
                later.at[at, pl.ds(0, width - cut)], blocks_v.at[m % 2, :, pl.ds(cut, width - cut)], told_sem.at[1, m % 2]
            ),
        ]

    def each_block(step):
        def run(m, _):
            step(pl.ds(pl.multiple_of(m * block, block), block))
            return 0

        lax.fori_loop(0, slots // block, run, 0)

    sent_on, started = [None] * chunks, [None] * chunks
    outs = []

    def dispatch(n):
        buffer = first[n % 6]
        if n >= 6:
            go.release(started[n - 6][1])
        cols = pl.ds(starts[n], CHUNKS[n])
        flat = buffer.reshape(slots, buffer.shape[-1])

        def step(at):
            flat[at, : CHUNKS[n]] = dot_nn(spread_v[at], tokens_v[:, cols]).astype(BF16)

        each_block(step)
        return columns(buffer, 0, CHUNKS[n])

    def cotangent(m):
        for pull in load(m):
            pull.wait()
        at = pl.ds(m * block, block)
        inner_up[at] = dot_nt(blocks_v[m % 2], down_v[...])
        if m + 2 < len(blocks):
            for pull in load(m + 2):
                pull.start()

    def multiply(n, close=False):
        way_in.wait(sent_on[n])
        outs.append(go.keep(held_in[n], columns(rows, starts[n], CHUNKS[n])))
        cols = pl.ds(starts[n], CHUNKS[n])
        flat = held_in[n].reshape(slots, CHUNKS[n])

        def step(at):
            part = flat[at]
            terms = []
            for out, weight in ((gate_pre, gate_v), (up_pre, up_v), (logits, router_v)):
                term = dot_nn(part, weight[cols])
                if n > 0:
                    term = out[at] + term
                if not close:
                    out[at] = term
                terms.append(term)
            if close:
                finish(at, *terms)

        each_block(step)

    def finish(at, before_gate, before_up, row_logits):
        row_logits = jnp.where(asked_v[at] > 0, row_logits, MASKED)
        powers = jnp.exp(row_logits - jnp.max(row_logits, axis=-1, keepdims=True))
        lane = lax.broadcasted_iota(jnp.int32, (1, lanes), 1) == index
        prob = jnp.sum(jnp.where(lane, powers, 0.0), axis=-1, keepdims=True) / jnp.sum(
            powers, axis=-1, keepdims=True
        )
        after_inner = inner_up[at]
        sigmoid = 1.0 / (1.0 + jnp.exp(-before_gate))
        silu = before_gate * sigmoid
        inner = silu * before_up
        gate_up = jnp.sum(inner * after_inner, axis=-1, keepdims=True)
        inner_v[at] = (prob * inner).astype(BF16)
        after_inner = prob * after_inner
        gate_g[at] = (after_inner * before_up * sigmoid * (1.0 + before_gate * (1.0 - sigmoid))).astype(BF16)
        up_g[at] = (after_inner * silu).astype(BF16)
        high = gate_up.astype(BF16).astype(F32)
        flat = extra.reshape(slots, 2 * lanes)
        flat[at, :lanes] = jnp.where(lane, high, 0.0).astype(BF16)
        flat[at, lanes:] = jnp.where(lane, gate_up - high, 0.0).astype(BF16)

    todo = list(blocks)
    for triple, crossing in ORDER:
        for n in range(3 * triple, 3 * triple + 3):
            if n >= 6 and crossing == 2:
                go.release(started[n - 2][1] if n < 8 else [])
            if crossing == 0:
                src = dispatch(n)
            else:
                way_in.wait(sent_on[n])
                src = mids_in[2 * n + crossing - 1]
            dst = held_in[n] if crossing == 2 else mids_in[2 * n + crossing]
            sent_on[n] = way_in.send(TURNS[n % 3][crossing], src, dst)
            if crossing == 0:
                started[n] = sent_on[n]
            if crossing == 2 and triple > 0:
                multiply(n - 3)
            elif todo and triple + crossing > 1 and crossing > 0:
                cotangent(todo.pop(0))
        if (triple, crossing) == (1, 0):
            for pull in (*load(0), *load(1), *late):
                pull.start()
            late[0].wait()
        if (triple, crossing) == (2, 1):
            while todo:
                cotangent(todo.pop(0))
            for pull in late[1:]:
                pull.wait()
    for n in range(chunks - 3, chunks):
        multiply(n, close=n == chunks - 1)
    results = [
        pltpu.make_async_copy(a, b, puts.at[n])
        for n, (a, b) in enumerate(((inner_v, inner_low), (gate_g, grad_gate), (up_g, grad_up)))
    ]
    for out in outs:
        out.wait()

    begins = [sum(BACK[:n]) for n in range(chunks)]
    sources = [*held_in[: chunks - 2], last_source]
    sent_back = [None] * chunks
    pushes = [None] * len(blocks)

    def gradient(n):
        cols = pl.ds(begins[n], BACK[n])
        flat = sources[n].reshape(slots, BACK[n])

        def step(at):
            flat[at] = (dot_nt(gate_g[at], gate_v[cols]) + dot_nt(up_g[at], up_v[cols])).astype(BF16)

        each_block(step)

    def outcome(m):
        if m >= 2:
            pushes[m - 2].wait()
        at = pl.ds(m * block, block)
        blocks_v[m % 2] = dot_nn(inner_v[at], down_v[...]).astype(BF16)
        pushes[m] = pltpu.make_async_copy(blocks_v.at[m % 2], expert_out.at[at], puts.at[3 + m])
        pushes[m].start()

    def combine(n):
        way_out.wait(sent_back[n])
        summed[:, begins[n] : begins[n] + BACK[n]] = dot_tn(
            spread_v[...], held_out[n].reshape(slots, BACK[n])[...]
        )

    todo = list(blocks)
    for triple, crossing in ORDER:
        for n in range(3 * triple, 3 * triple + 3):
            dst = held_out[n] if crossing == 2 else mids_out[2 * n + crossing]
            if crossing > 0:
                way_out.wait(sent_back[n])
                src = mids_out[2 * n + crossing - 1]
            elif n == chunks - 1:
                src = extra
            else:
                gradient(n)
                src = sources[n]
            sent_back[n] = way_out.send(TURNS[n % 3][crossing], src, dst)
            if crossing == 2 and triple > 0:
                combine(n - 3)
            elif todo and triple + crossing > 1 and crossing > 0:
                outcome(todo.pop(0))
        if (triple, crossing) == (1, 0):
            for result in results:
                result.start()
    for n in range(chunks - 3, chunks):
        combine(n)
    for copy in (*results, *pushes[-2:]):
        copy.wait()
    go.finish()
    back.finish()


def experts(tokens, spread, told, later, gate, up, down, router):
    tok, width = tokens.shape
    slots = spread.shape[0]
    hidden, lanes = gate.shape[1], router.shape[1]
    lead = (*DIMS, slots // math.prod(DIMS))
    chunks = len(CHUNKS)
    low = jax.ShapeDtypeStruct((slots, hidden), BF16)

    def held(widths):
        return [pltpu.VMEM((*lead, w), BF16) for w in widths]

    twice = lambda widths: [w for w in widths for _ in range(2)]
    rows, *others = pl.pallas_call(
        experts_kernel,
        name="experts",
        cost_estimate=cost(120),
        out_shape=(
            jax.ShapeDtypeStruct((*lead, width), BF16),
            low,
            low,
            low,
            jax.ShapeDtypeStruct((tok, sum(BACK)), F32),
            jax.ShapeDtypeStruct((slots, width), BF16),
        ),
        in_specs=[ANY] * 8,
        out_specs=(ANY, ANY, ANY, ANY, VMEM, ANY),
        scratch_shapes=[
            *held(CHUNKS[:4]),
            *held(twice(CHUNKS)),
            *held(CHUNKS),
            *held(twice(BACK)),
            *held(BACK),
            *held((BACK[-2], BACK[-1])),
            pltpu.VMEM(tokens.shape, BF16),
            pltpu.VMEM(spread.shape, BF16),
            pltpu.VMEM((slots, lanes), BF16),
            pltpu.VMEM((2, 256, width), BF16),
            pltpu.VMEM(gate.shape, BF16),
            pltpu.VMEM(up.shape, BF16),
            pltpu.VMEM(down.shape, BF16),
            pltpu.VMEM(router.shape, BF16),
            pltpu.VMEM((slots, hidden), F32),
            pltpu.VMEM((slots, hidden), F32),
            pltpu.VMEM((slots, lanes), F32),
            pltpu.VMEM((slots, hidden), F32),
            *(pltpu.VMEM((slots, hidden), BF16) for _ in range(3)),
            pltpu.SemaphoreType.DMA((13 * chunks,)),
            pltpu.SemaphoreType.DMA((13 * chunks,)),
            pltpu.SemaphoreType.DMA((4 * chunks,)),
            pltpu.SemaphoreType.DMA((13 * chunks,)),
            pltpu.SemaphoreType.DMA((13 * chunks,)),
            pltpu.SemaphoreType.DMA((3 * chunks,)),
            pltpu.SemaphoreType.DMA((7,)),
            pltpu.SemaphoreType.DMA((2, 2)),
            pltpu.SemaphoreType.DMA((7,)),
        ],
        compiler_params=pltpu.CompilerParams(
            collective_id=6, has_side_effects=True, vmem_limit_bytes=61 << 20
        ),
    )(tokens, spread, told, later, gate, up, down, router)
    return rows.reshape(slots, width), *others


def on_device(
    hidden_in,
    doc_ids,
    expert_ids,
    attn_gain,
    query_weight,
    key_weight,
    value_weight,
    output_weight,
    query_gain,
    key_gain,
    moe_gain,
    router_weight,
    gate_weight,
    up_weight,
    down_weight,
    cotangent,
):
    both = ("dp", "tensor")
    tok, width = hidden_in.shape
    hd = query_gain.shape[0]
    nkv = key_weight.shape[1] // hd
    nq = query_weight.shape[1] // hd
    group = nq // nkv
    count = router_weight.shape[1]
    routes = expert_ids.shape[1]
    cap = tok * routes // count
    slots = count * cap
    scale = 1.0 / math.sqrt(hd)
    tokens = doc_ids.shape[1]

    lane = lax.broadcasted_iota(jnp.int32, (1, 1, count), 2)
    chosen = jnp.sum((expert_ids[:, :, None] == lane).astype(F32), axis=1)
    below = (
        lax.broadcasted_iota(jnp.int32, (tok, tok), 1)
        < lax.broadcasted_iota(jnp.int32, (tok, tok), 0)
    ).astype(BF16)
    rank = dot_nn(below, chosen.astype(BF16))
    place = jnp.where(chosen > 0, rank, -1.0).T
    spread = (
        place[:, None, :] == lax.broadcasted_iota(jnp.int32, (1, cap, 1), 1).astype(F32)
    ).astype(BF16).reshape(slots, tok)

    hidden = hidden_in.astype(F32)

    in_weights, out_weights, normed, docs, told, later = gather(
        query_weight,
        key_weight,
        value_weight,
        output_weight.T,
        hidden_in,
        attn_gain,
        jnp.broadcast_to(doc_ids, (8, tokens)).astype(F32),
        spread,
        cotangent,
        chosen.astype(BF16),
    )
    later = lax.all_to_all(
        later.reshape(count, cap, later.shape[1]), both, split_axis=0, concat_axis=0, tiled=True
    ).reshape(slots, later.shape[1])

    position, allowed = jax.vmap(layout)(docs[:, 0])
    cosine, sine = rotary(position.reshape(-1), hd)
    cosine = jnp.concatenate([cosine, cosine], axis=1)
    signed = jnp.concatenate([-sine, sine], axis=1)
    bias = jnp.where(allowed, 0.0, MASKED).astype(F32)
    raw = dot_nn(normed, in_weights)
    heads = group * hd
    query, kv, attention, mixed = attend(raw, bias, cosine, signed, query_gain, key_gain, scale)
    attn_out = reduce(dot_nt(mixed, out_weights).astype(BF16), 2)

    residual = hidden + attn_out
    moe_input = rms_scale(residual, moe_gain).astype(BF16)
    moe_input, later = lax.optimization_barrier((moe_input, later))
    gate_mat, up_mat, down_mat = gate_weight[0], up_weight[0], down_weight[0]
    rows, inner_low, grad_gate, grad_up, summed, expert_out = experts(
        moe_input, spread, told, later, gate_mat, up_mat, down_mat, router_weight
    )
    logits = dot_nn(moe_input, router_weight)
    masked = jnp.where(chosen > 0, logits, MASKED)
    probs = jnp.exp(masked - jnp.max(masked, axis=-1, keepdims=True))
    probs = probs / jnp.sum(probs, axis=-1, keepdims=True)

    upstream = cotangent.astype(F32)
    gate_upstream = summed[:, width : width + count] + summed[:, width + count :]
    grad_chosen = probs * (gate_upstream - jnp.sum(probs * gate_upstream, axis=-1, keepdims=True))
    grad_logits = grad_chosen.astype(BF16)
    grad_moe_input = summed[:, :width] + dot_nt(grad_logits, router_weight)
    router_part = dot_tn(moe_input, grad_logits)
    grad_norm, moegain_rows = rms_back(residual, moe_gain, grad_moe_input)
    moegain_part = jnp.sum(moegain_rows, axis=0)
    grad_residual = upstream + grad_norm
    grad_attn, piece = share(grad_residual.astype(BF16), router_part.astype(BF16), 3)
    expert_out, grad_attn = lax.optimization_barrier((expert_out, grad_attn))
    returned = lax.all_to_all(
        expert_out.reshape(count, cap, width), both, split_axis=0, concat_axis=0, tiled=True
    ).reshape(slots, width)

    grad_mixed = dot_nn(grad_attn, out_weights).astype(BF16)
    grad_raw, head_gains = attend_back(
        raw, cosine, signed, query_gain, key_gain, query, kv, attention, grad_mixed, scale
    )
    inner_low, rows, told, later, grad_raw = lax.optimization_barrier(
        (inner_low, rows, told, later, grad_raw)
    )
    cot_rows = jnp.concatenate([told, later[:, : width - told.shape[1]]], axis=1)
    down_grad = dot_tn(inner_low, cot_rows)
    gate_grad = dot_tn(rows, grad_gate)
    up_grad = dot_tn(rows, grad_up)
    normed_part, down_grad, gate_grad, up_grad = lax.optimization_barrier(
        (dot_nt(grad_raw, in_weights).astype(BF16), down_grad, gate_grad, up_grad)
    )
    grad_normed = reduce(normed_part, 4)
    grad_normed, returned = lax.optimization_barrier((grad_normed, returned))
    grad_hidden, attngain_rows = rms_back(hidden, attn_gain, grad_normed)
    input_grad = grad_residual + grad_hidden

    gains = jnp.concatenate([jnp.sum(attngain_rows, axis=0), moegain_part]).reshape(-1, hd)
    gains = jnp.concatenate([gains, head_gains, jnp.zeros((6, hd), F32)], axis=0)

    query_grad, key_grad, value_grad, out_grad, gains, router_grad, layer_out = scatter(
        dot_tn(normed, grad_raw).astype(BF16),
        dot_tn(grad_attn, mixed).astype(BF16),
        gains,
        piece,
        returned,
        spread,
        residual,
        (nq * hd, nkv * hd, nkv * hd, nq * hd),
    )
    at = width // hd
    return (
        layer_out,
        input_grad,
        gains[:at].reshape(-1),
        query_grad,
        key_grad,
        value_grad,
        out_grad.T,
        gains[2 * at],
        gains[2 * at + 1],
        gains[at : 2 * at].reshape(-1),
        router_grad.reshape(width, count).astype(F32),
        gate_grad[None],
        up_grad[None],
        down_grad[None],
    )


def solution(mesh):
    both = ("dp", "tensor")
    in_specs = (
        P(both, None),
        P("dp", None),
        P(both, None),
        P(),
        P("dp", "tensor"),
        P("dp", "tensor"),
        P("dp", "tensor"),
        P("tensor", "dp"),
        P(),
        P(),
        P(),
        P(),
        P(both, None, None),
        P(both, None, None),
        P(both, None, None),
        P(both, None),
    )
    out_specs = (
        P(both, None),
        P(both, None),
        P(),
        P("dp", "tensor"),
        P("dp", "tensor"),
        P("dp", "tensor"),
        P("tensor", "dp"),
        P(),
        P(),
        P(),
        P(),
        P(both, None, None),
        P(both, None, None),
        P(both, None, None),
    )
    return jax.shard_map(
        on_device, mesh=mesh, in_specs=in_specs, out_specs=out_specs, check_vma=False
    )
```
